32 devices in a mesh: ulysses: 4 (over z), blk: 8 (over y, x, core).
Axes of the slice: x: 2, y: 2, z: 4, core: 2. Of those that a mesh axis runs over, the one named last changes fastest.
Arguments:
- tokens: bfloat16 [4096, 768], P(('blk', 'ulysses')), as said below
- cotangent: bfloat16 [4096, 768], P(('blk', 'ulysses')), may hold values from -6 to 6
- doc_starts: int32 [17], replicated, may hold values from 0 to 4095, as said below
- q_weight: bfloat16 [768, 768], P(('ulysses', 'blk')), may hold values from -0.21875 to 0.21875
- k_weight: bfloat16 [768, 768], P(('ulysses', 'blk')), may hold values from -0.21875 to 0.21875
- v_weight: bfloat16 [768, 768], P(('ulysses', 'blk')), may hold values from -0.21875 to 0.21875
- q_bias: bfloat16 [768], P(('ulysses', 'blk')), may hold values from -3 to 3
- v_bias: bfloat16 [768], P(('ulysses', 'blk')), may hold values from -3 to 3
- o_weight: bfloat16 [768, 768], P(('ulysses', 'blk')), may hold values from -3.5 to 3.5
- o_bias: bfloat16 [768], P(('ulysses', 'blk')), may hold values from -3 to 3
- norm1_gain: bfloat16 [768], P(('ulysses', 'blk')), may hold values from 0.25 to 1.75
- norm1_bias: bfloat16 [768], P(('ulysses', 'blk')), may hold values from -3 to 3
- up_weight: bfloat16 [768, 3072], P(('ulysses', 'blk')), may hold values from -0.21875 to 0.21875
- up_bias: bfloat16 [3072], P(('ulysses', 'blk')), may hold values from -3 to 3
- down_weight: bfloat16 [3072, 768], P(('ulysses', 'blk')), may hold values from -0.109375 to 0.109375
- down_bias: bfloat16 [768], P(('ulysses', 'blk')), may hold values from -3 to 3
- norm2_gain: bfloat16 [768], P(('ulysses', 'blk')), may hold values from 0.25 to 1.75
- norm2_bias: bfloat16 [768], P(('ulysses', 'blk')), may hold values from -3 to 3
Outputs:
- layer_out: bfloat16 [4096, 768], P(('blk', 'ulysses'))
- input_grad: float32 [4096, 768], P(('blk', 'ulysses'))
- q_weight_grad: float32 [768, 768], P(('ulysses', 'blk'))
- k_weight_grad: float32 [768, 768], P(('ulysses', 'blk'))
- v_weight_grad: float32 [768, 768], P(('ulysses', 'blk'))
- q_bias_grad: float32 [768], P(('ulysses', 'blk'))
- v_bias_grad: float32 [768], P(('ulysses', 'blk'))
- o_weight_grad: float32 [768, 768], P(('ulysses', 'blk'))
- o_bias_grad: float32 [768], P(('ulysses', 'blk'))
- norm1_gain_grad: float32 [768], P(('ulysses', 'blk'))
- norm1_bias_grad: float32 [768], P(('ulysses', 'blk'))
- up_weight_grad: float32 [768, 3072], P(('ulysses', 'blk'))
- up_bias_grad: float32 [3072], P(('ulysses', 'blk'))
- down_weight_grad: float32 [3072, 768], P(('ulysses', 'blk'))
- down_bias_grad: float32 [768], P(('ulysses', 'blk'))
- norm2_gain_grad: float32 [768], P(('ulysses', 'blk'))
- norm2_bias_grad: float32 [768], P(('ulysses', 'blk'))
The draws below stay inside these ranges and needn't reach their ends.
Inputs may be any that keep to these rules, and one draw needn't show every extreme that they name: `doc_starts`: Sorted, never falling, the first is 0; entries may repeat. Every document, from one start to the next larger one (the last one to 4096), has at most 1024 tokens, and one has exactly 1024. For some s, every position s + k * 1024 below 4096 is a start. `tokens`: each row has mean 0 and mean square 1 over its 768 features.
All inputs are finite; a program needn't handle non-finite values.
Results may differ from the reference program's by a relative error of at most 0.015.
Values may be sent and summed in bfloat16 or wider, within the bound.
A program may use at most 128 MiB of HBM per device.

```python
import jax
import jax.numpy as jnp
from jax import lax

D = 768
H = 12
HD = 64
FF = 3072
TOK_DEV = 128
CUTS = 3
TOKENS = 4096
DOC_MAX = 1024
REACH = 2
SLOTS = 4
N_ULYSSES = 4


def draw_tokens(key, part):
    base = jax.random.normal(key, (TOKENS, D), jnp.float32)
    centered = base - jnp.mean(base, axis=1, keepdims=True)
    scaled = centered * lax.rsqrt(jnp.mean(centered * centered, axis=1, keepdims=True) + 1e-06)
    return scaled.astype(jnp.bfloat16)


def draw_doc_starts(key, part):
    offset = jax.random.randint(jax.random.fold_in(key, 1), (), 0, DOC_MAX)
    forced = jnp.arange(SLOTS, dtype=jnp.int32) * DOC_MAX + offset
    cuts = jax.random.randint(jax.random.fold_in(key, 2), (SLOTS, CUTS), 0, DOC_MAX) + forced[:, None]
    cuts = jnp.minimum(cuts, TOKENS - 1)
    cuts = cuts.at[1].set(jnp.broadcast_to(forced[1], (CUTS,)))
    starts = jnp.concatenate([jnp.zeros((1,), jnp.int32), forced, cuts.reshape(-1)])
    return jnp.sort(starts).astype(jnp.int32)


def levels(own_key, shape, cuts, least, largest):
    level, own = 1.0, jax.random.fold_in(own_key, 6)
    for dim, shards_of in cuts:
        draws = jnp.exp(jax.random.uniform(jax.random.fold_in(own, dim), (shards_of,), jnp.float32, least / len(cuts), largest / len(cuts)))
        level = level * jnp.repeat(draws, shape[dim] // shards_of).reshape([-1 if axis == dim else 1 for axis in range(len(shape))])
    return level


def bell_draw(stream_key, extent, deviation, reach, cuts=(), kind=jnp.bfloat16):
    values = jax.random.normal(stream_key, extent, jnp.float32) * deviation
    if len(cuts) > 0:
        values = levels(stream_key, extent, cuts, -0.22, 0.18) * values
    return jnp.clip(values, min=-reach, max=reach).astype(kind)


def setup_inputs(seed: int = 0) -> dict:
    splits = jax.random.split(jax.random.key(seed), 19)
    tokens = draw_tokens(jax.random.fold_in(splits[18], 71), 0)
    cotangent = bell_draw(splits[1], (TOKENS, D), 1.0, 6.0, ((0, 32),))
    doc_starts = draw_doc_starts(jax.random.fold_in(splits[18], 71), 0)
    q_weight = bell_draw(splits[3], (D, D), D ** -0.5, 0.21875, ((0, 32),))
    k_weight = bell_draw(splits[4], (D, D), D ** -0.5, 0.21875, ((0, 32),))
    v_weight = bell_draw(splits[5], (D, D), D ** -0.5, 0.21875, ((0, 32),))
    q_bias = bell_draw(splits[6], (D,), 0.5, 3.0, ((0, 32),))
    v_bias = bell_draw(splits[7], (D,), 0.5, 3.0, ((0, 32),))
    o_weight = bell_draw(splits[8], (D, D), (max(1, 4 * D // DOC_MAX)) ** -0.5, 3.5, ((0, 32),))
    o_bias = bell_draw(splits[9], (D,), 0.5, 3.0, ((0, 32),))
    norm1_gain = jnp.clip(1.0 + 0.15 * jax.random.normal(splits[10], (D,), jnp.float32), 0.25, 1.75).astype(jnp.bfloat16)
    norm1_bias = bell_draw(splits[11], (D,), 0.5, 3.0, ((0, 32),))
    up_weight = bell_draw(splits[12], (D, FF), D ** -0.5, 0.21875, ((0, 32),))
    up_bias = bell_draw(splits[13], (FF,), 0.5, 3.0, ((0, 32),))
    down_weight = bell_draw(splits[14], (FF, D), FF ** -0.5, 0.109375, ((0, 32),))
    down_bias = bell_draw(splits[15], (D,), 0.5, 3.0, ((0, 32),))
    norm2_gain = jnp.clip(1.0 + 0.15 * jax.random.normal(splits[16], (D,), jnp.float32), 0.25, 1.75).astype(jnp.bfloat16)
    norm2_bias = bell_draw(splits[17], (D,), 0.5, 3.0, ((0, 32),))
    return {"tokens": tokens, "cotangent": cotangent, "doc_starts": doc_starts, "q_weight": q_weight, "k_weight": k_weight, "v_weight": v_weight, "q_bias": q_bias, "v_bias": v_bias, "o_weight": o_weight, "o_bias": o_bias, "norm1_gain": norm1_gain, "norm1_bias": norm1_bias, "up_weight": up_weight, "up_bias": up_bias, "down_weight": down_weight, "down_bias": down_bias, "norm2_gain": norm2_gain, "norm2_bias": norm2_bias}


SCALE = 0.125
EPS = 1e-12

@jax.custom_vjp
def low(v):
    return lax.optimization_barrier(v.astype(jnp.bfloat16)).astype(jnp.float32)

@jax.custom_vjp
def low_back(v):
    return v

def low_keep(v):
    return (low(v), None)

def low_pass(kept, grad):
    return (grad,)

def back_keep(v):
    return (v, None)

def back_low(kept, grad):
    return (low(grad),)
low.defvjp(low_keep, low_pass)
low_back.defvjp(back_keep, back_low)

def matmul(left, right):
    return jnp.dot(left, right, precision=lax.Precision.HIGHEST)

def layer_norm(hidden, gain, shift):
    middle = lax.optimization_barrier(jnp.mean(hidden, axis=-1, keepdims=True))
    centered = hidden - middle
    spread = lax.optimization_barrier(jnp.mean(centered * centered, axis=-1, keepdims=True))
    return centered * lax.rsqrt(spread + EPS) * gain + shift

def segment_ids(doc_starts, positions):
    return lax.optimization_barrier(jnp.sum((doc_starts[None, :] <= positions[:, None]).astype(jnp.int32), axis=1)).astype(jnp.int32)

def attention(query, key_rows, value_rows, segs):
    group = TOK_DEV * N_ULYSSES
    margin = REACH * group
    width = (2 * REACH + 1) * group
    key_pad = jnp.pad(key_rows, ((margin, margin), (0, 0)))
    value_pad = jnp.pad(value_rows, ((margin, margin), (0, 0)))
    seg_pad = jnp.pad(segs, (margin, margin), constant_values=-1)

    def one_block(index):
        start = (index * group).astype(jnp.int32)
        query3 = lax.dynamic_slice_in_dim(query, start, group, 0).reshape(group, H, HD)
        key3 = lax.dynamic_slice_in_dim(key_pad, start, width, 0).reshape(width, H, HD)
        value3 = lax.dynamic_slice_in_dim(value_pad, start, width, 0).reshape(width, H, HD)
        seg_query = lax.dynamic_slice_in_dim(segs, start, group, 0)
        seg_key = lax.dynamic_slice_in_dim(seg_pad, start, width, 0)
        allowed = seg_query[:, None] == seg_key[None, :]
        scores = low_back(jnp.einsum('qhd,khd->hqk', query3, key3, precision=lax.Precision.HIGHEST) * SCALE)
        weights = jnp.where(allowed[None], jnp.exp(scores), 0.0)
        denom = lax.optimization_barrier(jnp.sum(weights, axis=-1))
        numer = jnp.einsum('hqk,khd->qhd', low(weights), value3, precision=lax.Precision.HIGHEST)
        return (numer / jnp.transpose(denom)[:, :, None]).reshape(group, D)
    blocks = lax.map(jax.checkpoint(one_block), jnp.arange(TOKENS // group, dtype=jnp.int32))
    return blocks.reshape(TOKENS, D)

def reference(tokens, cotangent, doc_starts, q_weight, k_weight, v_weight, q_bias, v_bias, o_weight, o_bias, norm1_gain, norm1_bias, up_weight, up_bias, down_weight, down_bias, norm2_gain, norm2_bias):
    positions = jnp.arange(TOKENS, dtype=jnp.int32)
    segs = segment_ids(doc_starts, positions)

    def layer(token_f, w_query, w_key, w_value, b_query, b_value, w_out, b_out, gain_one, shift_one, w_up, b_up, w_down, b_down, gain_two, shift_two):
        query = low(low_back(matmul(token_f, w_query) + b_query))
        key_rows = low(low_back(matmul(token_f, w_key)))
        value_rows = low(low_back(matmul(token_f, w_value) + b_value))
        attn = attention(query, key_rows, value_rows, segs)
        attn_low = low(low_back(attn))
        h_one = token_f + low_back(matmul(attn_low, w_out)) + b_out
        y_one = layer_norm(h_one, gain_one, shift_one)
        pre_act = low_back(matmul(low(y_one), w_up) + b_up)
        act = low(jax.nn.gelu(pre_act, approximate=False))
        h_two = y_one + low_back(matmul(act, w_down)) + b_down
        return layer_norm(h_two, gain_two, shift_two)
    f32 = jnp.float32
    out, pullback = jax.vjp(layer, tokens.astype(f32), q_weight.astype(f32), k_weight.astype(f32), v_weight.astype(f32), q_bias.astype(f32), v_bias.astype(f32), o_weight.astype(f32), o_bias.astype(f32), norm1_gain.astype(f32), norm1_bias.astype(f32), up_weight.astype(f32), up_bias.astype(f32), down_weight.astype(f32), down_bias.astype(f32), norm2_gain.astype(f32), norm2_bias.astype(f32))
    grads = pullback(cotangent.astype(f32))
    return (out.astype(jnp.bfloat16), grads[0], grads[1], grads[2], grads[3], grads[4], grads[5], grads[6], grads[7], grads[8], grads[9], grads[10], grads[11], grads[12], grads[13], grads[14], grads[15])
```

```python
import jax
import jax.numpy as jnp
from jax import lax
from jax.experimental import pallas as pl
from jax.experimental.pallas import tpu as pltpu
from jax.sharding import PartitionSpec as P

HD = 64


SCALE = 0.125
EPS = 1e-12


def passed_along(shard, axis, by):
    length = lax.axis_size(axis)
    return lax.ppermute(shard, axis, [(i, (i + by) % length) for i in range(length)])


def layer_norm(hidden, gain, shift):
    middle = jnp.mean(hidden, axis=-1, keepdims=True)
    centered = hidden - middle
    spread = jnp.mean(centered * centered, axis=-1, keepdims=True)
    return centered * lax.rsqrt(spread + EPS) * gain + shift


def gelu_exact(values):
    return jax.nn.gelu(values, approximate=False)


def doc_ids(doc_starts, positions):
    return jnp.sum((doc_starts[None, :] <= positions[:, None]).astype(jnp.int32), axis=1)


def project(left, right):
    return jnp.dot(left, right, preferred_element_type=jnp.float32)


def project_back(left, right):
    return lax.dot_general(
        left, right, (((1,), (1,)), ((), ())), preferred_element_type=jnp.float32
    )


def outer_sum(left, right):
    return lax.dot_general(
        left, right, (((0,), (0,)), ((), ())), preferred_element_type=jnp.float32
    )


def per_device(
    tokens,
    cotangent,
    doc_starts,
    q_weight,
    k_weight,
    v_weight,
    q_bias,
    v_bias,
    o_weight,
    o_bias,
    norm1_gain,
    norm1_bias,
    up_weight,
    up_bias,
    down_weight,
    down_bias,
    norm2_gain,
    norm2_bias,
):
    f32 = jnp.float32
    bf16 = jnp.bfloat16
    w_query, w_key, w_value, b_query, b_value, w_out, b_out, gain_one, shift_one = (
        lax.all_gather(q_weight, ("ulysses", "blk"), axis=0, tiled=True),
        lax.all_gather(k_weight, ("ulysses", "blk"), axis=0, tiled=True),
        lax.all_gather(v_weight, ("ulysses", "blk"), axis=0, tiled=True),
        lax.all_gather(q_bias, ("ulysses", "blk"), axis=0, tiled=True),
        lax.all_gather(v_bias, ("ulysses", "blk"), axis=0, tiled=True),
        lax.all_gather(o_weight, ("ulysses", "blk"), axis=0, tiled=True),
        lax.all_gather(o_bias, ("ulysses", "blk"), axis=0, tiled=True),
        lax.all_gather(norm1_gain, ("ulysses", "blk"), axis=0, tiled=True),
        lax.all_gather(norm1_bias, ("ulysses", "blk"), axis=0, tiled=True),
    )
    w_up, b_up, w_down, b_down, gain_two, shift_two = (
        lax.all_gather(up_weight, ("ulysses", "blk"), axis=0, tiled=True),
        lax.all_gather(up_bias, ("ulysses", "blk"), axis=0, tiled=True),
        lax.all_gather(down_weight, ("ulysses", "blk"), axis=0, tiled=True),
        lax.all_gather(down_bias, ("ulysses", "blk"), axis=0, tiled=True),
        lax.all_gather(norm2_gain, ("ulysses", "blk"), axis=0, tiled=True),
        lax.all_gather(norm2_bias, ("ulysses", "blk"), axis=0, tiled=True),
    )
    query_tok = (project(tokens, w_query) + b_query.astype(f32)).astype(bf16)
    key_tok = project(tokens, w_key).astype(bf16)
    value_tok = (project(tokens, w_value) + b_value.astype(f32)).astype(bf16)
    query_heads, key_heads, value_heads = (
        lax.all_to_all(query_tok, "ulysses", split_axis=1, concat_axis=0, tiled=True),
        lax.all_to_all(key_tok, "ulysses", split_axis=1, concat_axis=0, tiled=True),
        lax.all_to_all(value_tok, "ulysses", split_axis=1, concat_axis=0, tiled=True),
    )
    group = query_heads.shape[0]
    columns = query_heads.shape[1]
    local_heads = columns // HD
    block_count = lax.axis_size("blk")
    total = group * block_count
    doc_max = min(8192, total // 4, 8 * group)
    reach = (group - 2 + doc_max) // group
    visits = 2 * reach + 1
    block_index = lax.axis_index("blk")
    rows = jnp.arange(group, dtype=jnp.int32)
    query_ids = doc_ids(doc_starts, block_index * group + rows)
    query3 = query_heads.reshape(group, local_heads, HD)

    def block_mask(offset):
        key_pos = (block_index + offset) * group + rows
        inside = (key_pos >= 0) & (key_pos < total)
        key_ids = jnp.where(inside, doc_ids(doc_starts, key_pos), -1)
        allowed = query_ids[:, None] == key_ids[None, :]
        shared = (
            inside[0] & (key_ids[0] <= query_ids[group - 1]) & (key_ids[group - 1] >= query_ids[0])
        )
        return (allowed, shared)

    def exp_scores(pair, allowed):
        key3 = pair[0].reshape(group, local_heads, HD)
        scores = jnp.einsum("qhd,khd->hqk", query3, key3, preferred_element_type=f32) * SCALE
        return jnp.where(allowed[None], jnp.exp(scores), 0.0)

    def forward_terms(pair, offset):
        allowed, shared = block_mask(offset)
        weights = exp_scores(pair, allowed)
        value3 = pair[1].reshape(group, local_heads, HD)
        numer = jnp.einsum("hqk,khd->qhd", weights.astype(bf16), value3, preferred_element_type=f32)
        return (numer, jnp.sum(weights, axis=2))

    pair_own = jnp.stack([key_heads, value_heads])
    pair = passed_along(pair_own, "blk", -reach)
    numer, denom = forward_terms(pair, reach)
    store = jnp.zeros((1,), bf16)

    def forward_step(step, carry):
        pair_now, numer_now, denom_now, store_now = carry
        pair_now = passed_along(pair_now, "blk", 1)
        more_numer, more_denom = forward_terms(pair_now, reach - step)
        return (pair_now, numer_now + more_numer, denom_now + more_denom, store_now)

    pair, numer, denom, store = lax.fori_loop(1, visits, forward_step, (pair, numer, denom, store))
    attn_f = numer / jnp.transpose(denom)[:, :, None]
    attn_b = attn_f.reshape(group, columns).astype(bf16)
    attn_tok = lax.all_to_all(attn_b, "ulysses", split_axis=0, concat_axis=1, tiled=True)
    token_f = tokens.astype(f32)
    h_one = token_f + project(attn_tok, w_out) + b_out.astype(f32)
    y_one, norm_one_back = jax.vjp(layer_norm, h_one, gain_one.astype(f32), shift_one.astype(f32))
    y_one_b = y_one.astype(bf16)
    pre_act = project(y_one_b, w_up) + b_up.astype(f32)
    act, gelu_back = jax.vjp(gelu_exact, pre_act)
    act_b = act.astype(bf16)
    h_two = y_one + project(act_b, w_down) + b_down.astype(f32)
    out_f, norm_two_back = jax.vjp(layer_norm, h_two, gain_two.astype(f32), shift_two.astype(f32))
    layer_out = out_f.astype(bf16)
    d_two, g_gain_two, g_shift_two = norm_two_back(cotangent.astype(f32))
    g_b_down = jnp.sum(d_two, axis=0)
    d_two_b = d_two.astype(bf16)
    g_w_down = outer_sum(act_b, d_two_b)
    d_act = project_back(d_two_b, w_down)
    d_pre = gelu_back(d_act)[0].astype(bf16)
    g_b_up = jnp.sum(d_pre.astype(f32), axis=0)
    g_w_up = outer_sum(y_one_b, d_pre)
    d_y_one = d_two + project_back(d_pre, w_up)
    d_one, g_gain_one, g_shift_one = norm_one_back(d_y_one)
    g_b_out = jnp.sum(d_one, axis=0)
    d_one_b = d_one.astype(bf16)
    g_w_out = outer_sum(attn_tok, d_one_b)
    d_attn_tok = project_back(d_one_b, w_out).astype(bf16)
    d_attn = lax.all_to_all(d_attn_tok, "ulysses", split_axis=1, concat_axis=0, tiled=True)
    d_attn3 = d_attn.reshape(group, local_heads, HD)
    d_attn_f = d_attn3.astype(f32)
    delta = jnp.transpose(jnp.sum(d_attn_f * attn_f, axis=2))
    scaled_grad = d_attn_f / jnp.transpose(denom)[:, :, None]
    grad_high = scaled_grad.astype(bf16)
    grad_rest = (scaled_grad - grad_high.astype(f32)).astype(bf16)

    def backward_terms(pair_in, offset):
        allowed, shared = block_mask(offset)
        weights = exp_scores(pair_in, allowed)
        key3 = pair_in[0].reshape(group, local_heads, HD)
        value3 = pair_in[1].reshape(group, local_heads, HD)
        probs = weights / denom[:, :, None]
        d_prob = jnp.einsum("qhd,khd->hqk", d_attn3, value3, preferred_element_type=f32)
        d_score = (probs * (d_prob - delta[:, :, None]) * SCALE).astype(bf16)
        d_query = jnp.einsum("hqk,khd->qhd", d_score, key3, preferred_element_type=f32)
        d_key = jnp.einsum("hqk,qhd->khd", d_score, query3, preferred_element_type=f32)
        weights_low = weights.astype(bf16)
        d_value = jnp.einsum(
            "hqk,qhd->khd", weights_low, grad_high, preferred_element_type=f32
        ) + jnp.einsum("hqk,qhd->khd", weights_low, grad_rest, preferred_element_type=f32)
        return (d_query, jnp.stack([d_key, d_value]))

    pair = passed_along(pair_own, "blk", -reach)
    d_query_sum, carried = backward_terms(pair, reach)

    def backward_step(step, carry):
        pair_now, d_query_now, carried_now = carry
        pair_now = passed_along(pair_now, "blk", 1)
        more_query, more_kv = backward_terms(pair_now, reach - step)
        carried_now = (
            passed_along(carried_now.astype(jnp.bfloat16), "blk", 1).astype(carried_now.dtype)
            + more_kv
        )
        return (pair_now, d_query_now + more_query, carried_now)

    pair, d_query_sum, carried = lax.fori_loop(
        1, visits, backward_step, (pair, d_query_sum, carried)
    )
    own_grads = passed_along(carried.astype(jnp.bfloat16), "blk", -reach).astype(carried.dtype)
    d_query_b = d_query_sum.reshape(group, columns).astype(bf16)
    d_key_b = own_grads[0].reshape(group, columns).astype(bf16)
    d_value_b = own_grads[1].reshape(group, columns).astype(bf16)
    dq_tok, dk_tok, dv_tok = (
        lax.all_to_all(d_query_b, "ulysses", split_axis=0, concat_axis=1, tiled=True),
        lax.all_to_all(d_key_b, "ulysses", split_axis=0, concat_axis=1, tiled=True),
        lax.all_to_all(d_value_b, "ulysses", split_axis=0, concat_axis=1, tiled=True),
    )
    g_b_query = jnp.sum(dq_tok.astype(f32), axis=0)
    g_b_value = jnp.sum(dv_tok.astype(f32), axis=0)
    g_w_query = outer_sum(tokens, dq_tok)
    g_w_key = outer_sum(tokens, dk_tok)
    g_w_value = outer_sum(tokens, dv_tok)
    input_grad = (
        d_one
        + project_back(dq_tok, w_query)
        + project_back(dk_tok, w_key)
        + project_back(dv_tok, w_value)
    )
    shares = (
        lax.psum_scatter(g_w_query, ("ulysses", "blk"), scatter_dimension=0, tiled=True),
        lax.psum_scatter(g_w_key, ("ulysses", "blk"), scatter_dimension=0, tiled=True),
        lax.psum_scatter(g_w_value, ("ulysses", "blk"), scatter_dimension=0, tiled=True),
        lax.psum_scatter(g_b_query, ("ulysses", "blk"), scatter_dimension=0, tiled=True),
        lax.psum_scatter(g_b_value, ("ulysses", "blk"), scatter_dimension=0, tiled=True),
        lax.psum_scatter(g_w_out, ("ulysses", "blk"), scatter_dimension=0, tiled=True),
        lax.psum_scatter(g_b_out, ("ulysses", "blk"), scatter_dimension=0, tiled=True),
        lax.psum_scatter(g_gain_one, ("ulysses", "blk"), scatter_dimension=0, tiled=True),
        lax.psum_scatter(g_shift_one, ("ulysses", "blk"), scatter_dimension=0, tiled=True),
        lax.psum_scatter(g_w_up, ("ulysses", "blk"), scatter_dimension=0, tiled=True),
        lax.psum_scatter(g_b_up, ("ulysses", "blk"), scatter_dimension=0, tiled=True),
        lax.psum_scatter(g_w_down, ("ulysses", "blk"), scatter_dimension=0, tiled=True),
        lax.psum_scatter(g_b_down, ("ulysses", "blk"), scatter_dimension=0, tiled=True),
        lax.psum_scatter(g_gain_two, ("ulysses", "blk"), scatter_dimension=0, tiled=True),
        lax.psum_scatter(g_shift_two, ("ulysses", "blk"), scatter_dimension=0, tiled=True),
    )
    return (
        layer_out,
        input_grad,
        shares[0],
        shares[1],
        shares[2],
        shares[3],
        shares[4],
        shares[5],
        shares[6],
        shares[7],
        shares[8],
        shares[9],
        shares[10],
        shares[11],
        shares[12],
        shares[13],
        shares[14],
    )


MESH = pl.DeviceIdType.MESH
LOG2E = 1.4426950408889634
RSQRT2 = 0.7071067811865476
PDF0 = 0.3989422804014327

ARGS = ("tok", "cot", "starts", "qw", "kw", "vw", "qb", "vb", "ow", "ob", "g1", "b1", "upw", "upb", "dnw", "dnb", "g2", "b2")
OUTS = (
    ("o_out", (128, 768), jnp.bfloat16),
    ("o_in", (128, 768), jnp.float32),
    ("o_qw", (24, 768), jnp.float32),
    ("o_kw", (24, 768), jnp.float32),
    ("o_vw", (24, 768), jnp.float32),
    ("o_qb", (24,), jnp.float32),
    ("o_vb", (24,), jnp.float32),
    ("o_ow", (24, 768), jnp.float32),
    ("o_ob", (24,), jnp.float32),
    ("o_g1", (24,), jnp.float32),
    ("o_b1", (24,), jnp.float32),
    ("o_upw", (24, 3072), jnp.float32),
    ("o_upb", (96,), jnp.float32),
    ("o_dnw", (96, 768), jnp.float32),
    ("o_dnb", (24,), jnp.float32),
    ("o_g2", (24,), jnp.float32),
    ("o_b2", (24,), jnp.float32),
)
SMALL = ("qb", "vb", "ob", "g1", "b1", "dnb", "g2", "b2")
BF = jnp.bfloat16
F32 = jnp.float32
SCRATCH = (
    ("SM", (24, 128), F32),
    ("WS", (4, 24, 640), BF),
    ("W5", (4, 4, 2, 24, 640), BF),
    ("W2", (768, 640), BF),
    ("US", (4, 24, 768), BF),
    ("UP5", (4, 4, 2, 24, 768), BF),
    ("UP2", (768, 768), BF),
    ("DN4", (4, 2, 96, 768), BF),
    ("OW5", (4, 4, 2, 24, 768), BF),
    ("OW2", (768, 768), BF),
    ("XG", (4, 128, 768), BF),
    ("KV", (5, 4, 128, 384), BF),
    ("KVT", (15, 128, 512), BF),
    ("QP", (3, 4, 128, 128), BF),
    ("GP", (3, 4, 128, 128), BF),
    ("SEGK", (5, 512, 128), jnp.int32),
    ("EL", (15, 512, 512), BF),
    ("DST", (512, 512), BF),
    ("NUM", (3, 64, 512), F32),
    ("DEN", (3, 8, 512), F32),
    ("ATN", (3, 64, 512), F32),
    ("DLT", (3, 8, 512), F32),
    ("AS", (4, 128, 256), BF),
    ("AT", (4, 128, 256), BF),
    ("Y1", (128, 768), F32),
    ("N1", (128, 768), F32),
    ("RSD", (128, 128), F32),
    ("YG", (4, 128, 768), BF),
    ("ACT", (4, 128, 768), BF),
    ("GG", (4, 128, 768), BF),
    ("PS", (4, 128, 768), BF),
    ("PR", (4, 128, 768), BF),
    ("H2", (128, 768), F32),
    ("DH2", (128, 768), F32),
    ("DG", (4, 128, 768), BF),
    ("DU", (4, 128, 768), BF),
    ("DH1", (128, 768), F32),
    ("DAS", (4, 128, 256), BF),
    ("DA", (4, 128, 256), BF),
    ("T1", (768, 512), BF),
    ("DKS", (5, 512, 384), BF),
    ("DKR", (5, 512, 384), BF),
    ("DKO", (512, 384), F32),
    ("DQT", (3, 64, 512), F32),
    ("DQ", (512, 640), BF),
    ("VEC", (16, 768), F32),
    ("VUP", (8, 768), F32),
    ("G1", (4, 4, 2, 24, 640), F32),
    ("R1", (4, 4, 24, 640), F32),
    ("H1", (4, 4, 24, 640), BF),
    ("R1P", (4, 4, 24, 640), BF),
    ("S1", (4, 24, 640), BF),
    ("R1Z", (4, 24, 640), BF),
    ("GU", (4, 4, 2, 24, 768), F32),
    ("RU", (4, 4, 24, 768), F32),
    ("SU", (4, 4, 24, 768), BF),
    ("RUZ", (4, 4, 24, 768), BF),
    ("TU", (4, 24, 768), BF),
    ("RUP", (4, 24, 768), BF),
    ("GD", (4, 2, 96, 768), F32),
    ("RD", (4, 96, 768), F32),
    ("SD", (4, 96, 768), BF),
    ("RDZ", (4, 96, 768), BF),
    ("GO", (4, 4, 2, 24, 768), F32),
    ("RO", (4, 4, 24, 768), F32),
    ("SO", (4, 4, 24, 768), BF),
    ("ROP", (4, 4, 24, 768), BF),
    ("TO", (4, 24, 768), BF),
    ("ROZ", (4, 24, 768), BF),
)


class Semaphores:
    def __init__(self, sizes):
        self.base, at = {}, 0
        for name, size in sizes:
            self.base[name] = at
            at += size
        self.total = at


SEMS = Semaphores(
    (
        ("tok", 4), ("wz", 4), ("wp", 4), ("wc", 1), ("us", 4), ("upz", 4), ("dnz", 4),
        ("oz", 4), ("op", 4), ("cup", 1), ("cdn", 1), ("cow", 1), ("kv", 20), ("at", 4),
        ("yg", 4), ("ps", 4), ("dg", 4), ("qs", 4), ("da", 4), ("dk", 5), ("x", 4),
        ("f1c", 1), ("f1p", 4), ("f1z", 4), ("fuc", 1), ("fuz", 4), ("fup", 4), ("fdc", 1),
        ("fdz", 4), ("foc", 1), ("fop", 4), ("foz", 4), ("own", 4),
    )
)


def mm(left, right):
    return jnp.dot(left, right, preferred_element_type=F32)


def mm_nt(left, right):
    return lax.dot_general(left, right, (((1,), (1,)), ((), ())), preferred_element_type=F32)


def mm_tn(left, right):
    return lax.dot_general(left, right, (((0,), (0,)), ((), ())), preferred_element_type=F32)


def rows_by(shape, axis, flat):
    return lax.broadcasted_iota(jnp.int32, shape, axis).reshape(flat)


class Refs:
    pass


def layer_kernel(*refs):
    R = Refs()
    names = list(ARGS) + [n for n, _, _ in OUTS] + [n for n, _, _ in SCRATCH] + ["SS", "RS"]
    for name, ref in zip(names, refs, strict=True):
        setattr(R, name, ref)
    u = lax.axis_index("ulysses")
    b = lax.axis_index("blk")
    c = lax.rem(b, 2)
    p = lax.div(b, 2)
    other = 1 - c

    def snake(at):
        return at + lax.div(at, 2) * (1 - 2 * lax.rem(at, 2))

    s = snake(p)
    a = 2 * s + c
    far = p >= 2

    def dev(uu, pp, cc):
        return (uu, 2 * pp + cc)

    def block_dev(aa):
        return dev(u, snake(lax.div(aa, 2)), lax.rem(aa, 2))

    def turn(base, k):
        return lax.rem(base + k, 4)

    sends = []

    def copy(src, dst, name, si, ri, device):
        base = SEMS.base[name]
        return pltpu.make_async_remote_copy(
            src_ref=src, dst_ref=dst, send_sem=R.SS.at[base + si], recv_sem=R.RS.at[base + ri],
            device_id=device, device_id_type=MESH,
        )

    def send(*what):
        desc = copy(*what)
        desc.start()
        sends.append((what[2], None, desc))

    def send_if(cond, *what):
        desc = copy(*what)

        @pl.when(cond)
        def _():
            desc.start()

        sends.append((what[2], cond, desc))

    def settle(*wanted):
        for entry in list(sends):
            name, cond, desc = entry
            if wanted and name not in wanted:
                continue
            sends.remove(entry)
            if cond is None:
                desc.wait_send()
            else:

                @pl.when(cond)
                def _():
                    desc.wait_send()

    def arrived(dst, name, ri, device):
        copy(dst, dst, name, 0, ri, device).wait_recv()

    barrier = pltpu.get_barrier_semaphore()

    def greet(device):
        pl.semaphore_signal(barrier, inc=1, device_id=device, device_id_type=MESH)

    for k in range(1, 8):
        greet((u, lax.rem(b + k, 8)))
    for k in range(1, 4):
        greet((turn(u, k), b))

    @pl.when(far)
    def _():
        for k in range(1, 4):
            greet(dev(turn(u, k), s, c))

    R.SM[...] = jnp.zeros_like(R.SM)
    for row, name in enumerate(SMALL):
        R.SM[row : row + 1, 0:24] = getattr(R, name)[...].astype(F32).reshape(1, 24)
    up_bias = R.upb[...].astype(F32).reshape(1, 96)
    for i in range(4):
        R.SM[8 + i : 9 + i, 0:24] = up_bias[:, 24 * i : 24 * i + 24]
    small = R.SM[:, 0:64].astype(BF)
    qw, kw, vw = R.qw[...], R.kw[...], R.vw[...]
    for g in range(4):
        parts = []
        for h in range(3):
            at = 64 * (3 * g + h)
            parts += [kw[:, at : at + 64], vw[:, at : at + 64]]
        for h in range(3):
            at = 64 * (3 * g + h)
            parts.append(qw[:, at : at + 64])
        parts.append(small)
        R.WS[g] = jnp.concatenate(parts, axis=1)

    pl.semaphore_wait(barrier, 10 + 3 * lax.div(p, 2))

    for k in range(1, 4):
        to = turn(u, k)
        send(R.WS.at[to], R.W5.at[u, p, c], "wz", k, u, dev(to, p, c))
    R.W5[u, p, c] = R.WS[u]
    for k in range(1, 4):
        to = turn(u, k)
        send(R.tok, R.XG.at[u], "tok", k, u, dev(to, s, c))
    send_if(far, R.tok, R.XG.at[u], "tok", 0, u, dev(u, s, c))

    @pl.when(jnp.logical_not(far))
    def _():
        R.XG[u] = R.tok[...]

    up = R.upw[...]
    for q in range(4):
        R.US[q] = jnp.concatenate(
            [up[:, 768 * g + 192 * q : 768 * g + 192 * q + 192] for g in range(4)], axis=1
        )
    for k in range(1, 4):
        to = turn(p, k)
        send(R.US.at[to], R.UP5.at[u, p, c], "us", k, p, dev(u, to, c))
    R.UP5[u, p, c] = R.US[p]
    R.DN4[u, c] = R.dnw[...]
    R.OW5[u, p, c] = R.ow[...]
    for k in range(1, 4):
        to = turn(u, k)
        send(R.dnw, R.DN4.at[u, c], "dnz", k, u, dev(to, p, c))
        send(R.ow, R.OW5.at[u, p, c], "oz", k, u, dev(to, p, c))

    row_pos = lax.broadcasted_iota(jnp.int32, (512, 128), 0)
    n_starts = R.starts.shape[0]

    def id_body(j, carry):
        pos = row_pos + (a + j - 2) * 512
        ids = jnp.zeros((512, 128), jnp.int32)
        for i in range(n_starts):
            ids = ids + jnp.where(pos >= R.starts[i], 1, 0)
        R.SEGK[j] = ids
        return carry

    lax.fori_loop(0, 5, id_body, 0)
    q_pos = lax.broadcasted_iota(jnp.int32, (1, 512), 1) + a * 512
    q_ids = jnp.zeros((1, 512), jnp.int32)
    for i in range(n_starts):
        q_ids = q_ids + jnp.where(q_pos >= R.starts[i], 1, 0)
    for ref in (R.QP, R.GP, R.NUM, R.DEN, R.DQT):
        ref[...] = jnp.zeros_like(ref)

    for k in range(1, 4):
        src = turn(u, k)
        arrived(R.W5.at[src, p, c], "wz", src, dev(src, p, c))
    for k in range(1, 4):
        to = turn(p, k)
        send(R.W5.at[:, p, c], R.W5.at[:, p, c], "wp", k, p, dev(u, to, c))
    for k in range(1, 4):
        src = turn(p, k)
        arrived(R.UP5.at[u, src, c], "us", src, dev(u, src, c))
    for k in range(1, 4):
        to = turn(u, k)
        send(R.UP5.at[u, :, c], R.UP5.at[u, :, c], "upz", k, u, dev(to, p, c))
    for k in range(1, 4):
        src = turn(p, k)
        arrived(R.W5.at[:, src, c], "wp", src, dev(u, src, c))
    send(R.W5.at[:, :, c], R.W5.at[:, :, c], "wc", 0, 0, dev(u, p, other))
    arrived(R.W5.at[:, :, other], "wc", 0, dev(u, p, other))
    R.W2[...] = R.W5[...].reshape(768, 640)

    spread = jnp.where(
        rows_by((32, 24, 64), 1, (768, 64)) == lax.broadcasted_iota(jnp.int32, (768, 64), 1), 1.0, 0.0
    ).astype(BF)
    owner = rows_by((32, 24, 768), 0, (768, 768))
    lane = lax.broadcasted_iota(jnp.int32, (1, 768), 1)
    lane_owner = jnp.zeros((1, 768), jnp.int32)
    for i in range(1, 32):
        lane_owner = lane_owner + jnp.where(lane >= 24 * i, 1, 0)
    lane_g = jnp.where(lane >= 192, 1, 0) + jnp.where(lane >= 384, 1, 0) + jnp.where(lane >= 576, 1, 0)
    rest = lane - 192 * lane_g
    lane_c = jnp.where(rest >= 96, 1, 0)
    rest = rest - 96 * lane_c
    lane_r = jnp.where(rest >= 24, 1, 0) + jnp.where(rest >= 48, 1, 0) + jnp.where(rest >= 72, 1, 0)
    up_row = 24 * (8 * lane_g + 2 * p + lane_c) + 8 + lane_r
    row_id = lax.broadcasted_iota(jnp.int32, (768, 768), 0)
    wide = mm_nt(R.W2[:, 576:640], spread)
    mine = jnp.where(owner == lane_owner, wide, 0.0).astype(BF)
    pick = jnp.where(
        lax.broadcasted_iota(jnp.int32, (16, 768), 1) - 24 * lane_owner
        == lax.broadcasted_iota(jnp.int32, (16, 768), 0), 1.0, 0.0
    ).astype(BF)
    R.VEC[...] = mm(pick, mine)
    R.VUP[0:1, :] = jnp.sum(jnp.where(row_id == up_row, wide, 0.0), axis=0, keepdims=True)

    def group_slice(vector):
        out = vector[:, 0:192]
        for g in range(1, 4):
            out = jnp.where(u == g, vector[:, 192 * g : 192 * g + 192], out)
        return out

    qb = group_slice(R.VEC[0:1, :])
    vb = group_slice(R.VEC[1:2, :])
    zero64 = jnp.zeros((1, 64), F32)
    bias = []
    for h in range(3):
        bias += [zero64, vb[:, 64 * h : 64 * h + 64]]
    bias = jnp.concatenate(bias + [qb, zero64], axis=1)

    for k in range(4):
        src = turn(u, k)
        if k == 0:

            @pl.when(far)
            def _():
                arrived(R.XG.at[src], "tok", src, dev(src, s, c))

        else:
            arrived(R.XG.at[src], "tok", src, dev(src, s, c))
        proj = mm(R.XG[src], R.W2[...]) + bias
        R.KV[2, src] = proj[:, 0:384].astype(BF)
        query = proj[:, 384:576].astype(BF) * BF(0.125)
        for h in range(3):
            R.QP[h, src, :, 0:64] = query[:, 64 * h : 64 * h + 64]
        for i, step in enumerate((-2, 2, -1, 1)):
            to = a + step
            ok = jnp.logical_and(to >= 0, to < 8)
            slot = 2 - step
            send_if(
                ok, R.KV.at[2, src], R.KV.at[slot, src], "kv", 4 * k + i, 4 * slot + src, block_dev(to)
            )

    for k in range(1, 4):
        src = turn(u, k)
        arrived(R.OW5.at[src, p, c], "oz", src, dev(src, p, c))
    for k in range(1, 4):
        to = turn(p, k)
        send(R.OW5.at[:, p, c], R.OW5.at[:, p, c], "op", k, p, dev(u, to, c))

    def order(t):
        return 2 + (1 - 2 * c) * lax.div(t + 1, 2) * (1 - 2 * lax.rem(t + 1, 2))

    def forward_block(t, carry):
        j = order(t)
        ok = jnp.logical_and(a + j >= 2, a + j < 10)

        @pl.when(ok)
        def _():
            @pl.when(t > 0)
            def _():
                for r in range(4):
                    arrived(R.KV.at[j, r], "kv", 4 * j + r, block_dev(a + j - 2))

            def head(h, inner):
                lanes = pl.ds(pl.multiple_of(128 * h, 128), 128)
                kv = R.KV[j, :, :, lanes].reshape(512, 128)
                at = 3 * j + h
                R.KVT[at] = kv.T
                query = R.QP[h].reshape(512, 128)
                total = jnp.zeros((1, 512), F32)
                for r in range(4):
                    rows = slice(128 * r, 128 * r + 128)
                    score = mm_nt(kv[rows], query)
                    ids = R.SEGK[j, rows, :]
                    same = jnp.concatenate([ids] * 4, axis=1) == q_ids
                    weight = jnp.where(same, jnp.exp2(score * LOG2E), 0.0)
                    total = total + jnp.sum(weight, axis=0, keepdims=True)
                    R.EL[at, rows, :] = weight.astype(BF)
                R.DEN[h, 0:1, :] += total
                R.NUM[h] += mm(R.KVT[at, 64:128, :], R.EL[at])
                return inner

            lax.fori_loop(0, 3, head, 0)

        return carry

    lax.fori_loop(0, 5, forward_block, 0)

    for h in range(3):
        attn = R.NUM[h] / R.DEN[h, 0:1, :]
        R.ATN[h] = attn
        R.AS[:, :, 64 * h : 64 * h + 64] = attn.T.astype(BF).reshape(4, 128, 64)
    for k in range(1, 4):
        to = turn(u, k)
        send(R.AS.at[to], R.AT.at[u], "at", k, u, dev(to, s, c))
    send_if(far, R.AS.at[u], R.AT.at[u], "at", 0, u, dev(u, s, c))

    @pl.when(jnp.logical_not(far))
    def _():
        R.AT[u] = R.AS[u]

    for k in range(1, 4):
        src = turn(u, k)
        arrived(R.DN4.at[src, c], "dnz", src, dev(src, p, c))
        arrived(R.UP5.at[src, :, c], "upz", src, dev(src, p, c))
        from_p = turn(p, k)
        arrived(R.OW5.at[:, from_p, c], "op", from_p, dev(u, from_p, c))
    mate = dev(u, p, other)
    send(R.OW5.at[:, :, c], R.OW5.at[:, :, c], "cow", 0, 0, mate)
    send(R.UP5.at[:, :, c], R.UP5.at[:, :, c], "cup", 0, 0, mate)
    send(R.DN4.at[:, c], R.DN4.at[:, c], "cdn", 0, 0, mate)
    arrived(R.OW5.at[:, :, other], "cow", 0, mate)
    R.OW2[...] = R.OW5[...].reshape(768, 768)
    arrived(R.UP5.at[:, :, other], "cup", 0, mate)
    R.UP2[...] = R.UP5[...].reshape(768, 768)
    arrived(R.DN4.at[:, other], "cdn", 0, mate)

    def wait_column(ref, name):
        for k in range(1, 4):
            src = turn(u, k)
            arrived(ref.at[src], name, src, dev(src, s, c))

        @pl.when(far)
        def _():
            arrived(ref.at[u], name, u, dev(u, s, c))

    wait_column(R.AT, "at")
    hidden = R.tok[...].astype(F32) + R.VEC[2:3, :]
    for g in range(4):
        hidden = hidden + mm(R.AT[g, :, 0:192], R.OW2[192 * g : 192 * g + 192, :])
    middle = jnp.mean(hidden, axis=-1, keepdims=True)
    hidden = hidden - middle
    rstd = lax.rsqrt(jnp.mean(hidden * hidden, axis=-1, keepdims=True) + EPS)
    normed = hidden * rstd
    R.N1[...] = normed
    R.RSD[...] = jnp.broadcast_to(rstd, (128, 128))
    y_one = normed * R.VEC[3:4, :] + R.VEC[4:5, :]
    R.Y1[...] = y_one

    def gather_plane(ref, value, name):
        ref[p] = value
        for k in range(1, 4):
            send(ref.at[p], ref.at[p], name, k, p, dev(u, turn(p, k), c))

    gather_plane(R.YG, y_one.astype(BF), "yg")
    for k in range(4):
        at = turn(p, k)
        if k > 0:
            arrived(R.YG.at[at], "yg", at, dev(u, at, c))
        pre = mm(R.YG[at], R.UP2[...]) + R.VUP[0:1, :]
        phi = 0.5 * (1.0 + lax.erf(pre * RSQRT2))
        R.GG[at] = (phi + pre * (PDF0 * jnp.exp(-0.5 * pre * pre))).astype(BF)
        act = (pre * phi).astype(BF)
        R.ACT[at] = act
        part = mm(act, R.DN4[...].reshape(768, 768))
        if k == 0:
            R.H2[...] = part
        else:
            R.PS[at] = part.astype(BF)
            send(R.PS.at[at], R.PR.at[p], "ps", k, p, dev(u, at, c))
    hidden = R.Y1[...] + R.H2[...] + R.VEC[5:6, :]
    for k in range(1, 4):
        at = turn(p, k)
        arrived(R.PR.at[at], "ps", at, dev(u, at, c))
        hidden = hidden + R.PR[at].astype(F32)

    middle = jnp.mean(hidden, axis=-1, keepdims=True)
    hidden = hidden - middle
    rstd = lax.rsqrt(jnp.mean(hidden * hidden, axis=-1, keepdims=True) + EPS)
    normed = hidden * rstd
    gain = R.VEC[6:7, :]
    R.o_out[...] = (normed * gain + R.VEC[7:8, :]).astype(BF)
    grad = R.cot[...].astype(F32)
    cg = grad * gain
    d_two = (
        cg - jnp.mean(cg, axis=-1, keepdims=True) - normed * jnp.mean(cg * normed, axis=-1, keepdims=True)
    ) * rstd
    gather_plane(R.DG, d_two.astype(BF), "dg")
    R.DH2[...] = d_two
    g_gain_two = jnp.sum(grad * normed, axis=0, keepdims=True)
    g_shift_two = jnp.sum(grad, axis=0, keepdims=True)
    g_b_down = jnp.sum(d_two, axis=0, keepdims=True)

    settle("ps")
    g_b_up = jnp.zeros((1, 768), F32)
    for k in range(4):
        at = turn(p, k)
        if k > 0:
            arrived(R.DG.at[at], "dg", at, dev(u, at, c))
        d_act = mm_nt(R.DG[at], R.DN4[...].reshape(768, 768))
        d_pre = (d_act * R.GG[at].astype(F32)).astype(BF)
        R.DU[at] = d_pre
        g_b_up = g_b_up + jnp.sum(d_pre.astype(F32), axis=0, keepdims=True)
        part = mm_nt(d_pre, R.UP2[...])
        if k == 0:
            R.H2[...] = part
        else:
            R.PS[at] = part.astype(BF)
            send(R.PS.at[at], R.PR.at[p], "qs", k, p, dev(u, at, c))
    d_y = R.DH2[...] + R.H2[...]
    for k in range(1, 4):
        at = turn(p, k)
        arrived(R.PR.at[at], "qs", at, dev(u, at, c))
        d_y = d_y + R.PR[at].astype(F32)

    normed = R.N1[...]
    cg = d_y * R.VEC[3:4, :]
    d_one = (
        cg - jnp.mean(cg, axis=-1, keepdims=True) - normed * jnp.mean(cg * normed, axis=-1, keepdims=True)
    ) * R.RSD[:, 0:1]
    R.DH1[...] = d_one
    d_one_low = d_one.astype(BF)
    for k in range(4):
        to = turn(u, (k + 1) % 4)
        w_rows = R.OW2[pl.ds(pl.multiple_of(192 * to, 64), 192), :]
        R.DAS[to, :, 0:192] = mm_nt(d_one_low, w_rows).astype(BF)
        if k < 3:
            send(R.DAS.at[to], R.DA.at[u], "da", k + 1, u, dev(to, s, c))
    send_if(far, R.DAS.at[u], R.DA.at[u], "da", 0, u, dev(u, s, c))

    @pl.when(jnp.logical_not(far))
    def _():
        R.DA[u] = R.DAS[u]

    vec = R.VEC
    vec[2:3, :] = jnp.sum(d_one, axis=0, keepdims=True)
    vec[3:4, :] = jnp.sum(d_y * normed, axis=0, keepdims=True)
    vec[4:5, :] = jnp.sum(d_y, axis=0, keepdims=True)
    vec[5:6, :] = g_b_down
    vec[6:7, :] = g_gain_two
    vec[7:8, :] = g_shift_two
    vec[8:16, :] = jnp.zeros((8, 768), F32)
    R.VUP[0:1, :] = g_b_up

    for g in range(4):
        R.GO[g] = mm_tn(R.AT[g, :, 0:192], d_one_low).reshape(4, 2, 24, 768)
    send(R.GO.at[:, :, other], R.RO, "foc", 0, 0, mate)

    def wide_grad(left, right_ref, put):
        R.T1[...] = left.T

        def body(n, carry):
            lanes = pl.ds(pl.multiple_of(256 * n, 256), 256)
            put(lanes, mm(R.T1[...], right_ref[:, :, lanes].reshape(512, 256)))
            return carry

        lax.fori_loop(0, 3, body, 0)

    def put_down(lanes, value):
        R.GD[:, :, :, lanes] = value.reshape(4, 2, 96, 256)

    def put_up(lanes, value):
        R.GU[:, :, :, :, lanes] = value.reshape(4, 4, 2, 24, 256)

    wide_grad(R.ACT[...].reshape(512, 768), R.DG, put_down)
    send(R.GD.at[:, other], R.RD, "fdc", 0, 0, mate)
    wide_grad(R.YG[...].reshape(512, 768), R.DU, put_up)
    send(R.GU.at[:, :, other], R.RU, "fuc", 0, 0, mate)

    wait_column(R.DA, "da")
    for h in range(3):
        d_attn = R.DA[:, :, 64 * h : 64 * h + 64].reshape(512, 64).astype(F32).T
        scaled = (d_attn / R.DEN[h, 0:1, :]).astype(BF)
        R.DLT[h, 0:1, :] = jnp.sum(scaled.astype(F32) * R.ATN[h], axis=0, keepdims=True)
        R.GP[h, :, :, 64:128] = scaled.T.reshape(4, 128, 64)

    def backward_block(t):
        j = order(t)
        ok = jnp.logical_and(a + j >= 2, a + j < 10)

        @pl.when(ok)
        def _():
            def head(h, inner):
                lanes = pl.ds(pl.multiple_of(128 * h, 128), 128)
                at = 3 * j + h
                grad_rows = R.GP[h].reshape(512, 128)
                shift = R.DLT[h, 0:1, :]
                for r in range(4):
                    rows = slice(128 * r, 128 * r + 128)
                    d_prob = mm_nt(R.KV[j, r, :, lanes], grad_rows)
                    R.DST[rows, :] = (R.EL[at, rows, :].astype(F32) * (d_prob - shift)).astype(BF)
                d_kv = mm(R.DST[...], R.QP[h].reshape(512, 128)) + mm(R.EL[at], grad_rows)
                if t == 0:
                    R.DKO[:, lanes] = d_kv
                else:
                    R.DKS[j, :, lanes] = d_kv.astype(BF)
                R.DQT[h] += mm(R.KVT[at, 0:64, :], R.DST[...])
                return inner

            lax.fori_loop(0, 3, head, 0)

        if t > 0:
            send_if(
                ok, R.DKS.at[j], R.DKR.at[4 - j], "dk", t, 4 - j, block_dev(a + j - 2)
            )

    backward_block(4)
    arrived(R.RO, "foc", 0, mate)
    for g in range(4):
        R.SO[g] = (R.GO[g, :, c] + R.RO[g]).astype(BF)
    for k in range(1, 4):
        to = turn(p, k)
        send(R.SO.at[:, to], R.ROP.at[p], "fop", k, p, dev(u, to, c))
    arrived(R.RD, "fdc", 0, mate)
    for g in range(4):
        R.SD[g] = (R.GD[g, c] + R.RD[g]).astype(BF)
    for k in range(1, 4):
        to = turn(u, k)
        send(R.SD.at[to], R.RDZ.at[u], "fdz", k, u, dev(to, p, c))
    arrived(R.RU, "fuc", 0, mate)
    for g in range(4):
        R.SU[g] = (R.GU[g, :, c] + R.RU[g]).astype(BF)
    for k in range(1, 4):
        to = turn(u, k)
        send(R.SU.at[to], R.RUZ.at[u], "fuz", k, u, dev(to, p, c))
    backward_block(3)
    backward_block(2)
    for k in range(1, 4):
        src = turn(p, k)
        arrived(R.ROP.at[src], "fop", src, dev(u, src, c))
    for g in range(4):
        total = R.GO[g, p, c] + R.RO[g, p]
        for k in range(1, 4):
            total = total + R.ROP[turn(p, k), g].astype(F32)
        R.TO[g] = total.astype(BF)
    for k in range(1, 4):
        to = turn(u, k)
        send(R.TO.at[to], R.ROZ.at[u], "foz", k, u, dev(to, p, c))
    backward_block(1)
    backward_block(0)

    for h in range(3):
        R.DQ[:, 384 + 64 * h : 448 + 64 * h] = (R.DQT[h] * 0.125).T.astype(BF)
    R.DQ[:, 576:640] = jnp.zeros((512, 64), BF)
    for t in range(1, 5):
        j = order(t)

        @pl.when(jnp.logical_and(a + j >= 2, a + j < 10))
        def _():
            arrived(R.DKR.at[j], "dk", j, block_dev(a + j - 2))
            R.DKO[...] += R.DKR[j].astype(F32)

    R.DQ[:, 0:384] = R.DKO[...].astype(BF)

    settle("qs")
    for k in range(4):
        to = turn(u, (k + 1) % 4)
        part = mm_nt(R.DQ[pl.ds(pl.multiple_of(128 * to, 128), 128), :], R.W2[...])
        R.PS[to] = part.astype(BF)
        if k < 3:
            send(R.PS.at[to], R.PR.at[u], "x", k + 1, u, dev(to, s, c))
    send_if(far, R.PS.at[u], R.PR.at[u], "x", 0, u, dev(u, s, c))

    @pl.when(jnp.logical_not(far))
    def _():
        R.PR[u] = R.PS[u]

    d_qkv = R.DQ[...].astype(F32)
    sums = jnp.sum(d_qkv, axis=0, keepdims=True)
    sum_v = jnp.concatenate([sums[:, 128 * h + 64 : 128 * h + 128] for h in range(3)], axis=1)
    sum_q = sums[:, 384:576]

    def at_group(piece):
        return jnp.concatenate([jnp.where(u == g, piece, 0.0) for g in range(4)], axis=1)

    vec[0:1, :] = at_group(sum_q)
    vec[1:2, :] = at_group(sum_v)
    choose = jnp.where(
        rows_by((32, 24, 16), 1, (768, 16)) == lax.broadcasted_iota(jnp.int32, (768, 16), 1), 1.0, 0.0
    ).astype(BF)
    laid = jnp.where(owner == lane_owner, mm(choose, vec[...].astype(BF)), 0.0)
    laid = jnp.where(row_id == up_row, R.VUP[0:1, :], laid)
    R.T1[...] = R.XG[...].reshape(512, 768).T
    for n in range(5):
        lanes = slice(128 * n, 128 * n + 128)
        value = mm(R.T1[...], R.DQ[:, lanes])
        if n == 4:
            value = jnp.concatenate([value[:, 0:64], mm(laid.astype(BF), spread)], axis=1)
        R.G1[:, :, :, :, lanes] = value.reshape(4, 4, 2, 24, 128)
    send(R.G1.at[:, :, other], R.R1, "f1c", 0, 0, mate)

    for k in range(1, 4):
        src = turn(u, k)
        arrived(R.RDZ.at[src], "fdz", src, dev(src, p, c))
        arrived(R.RUZ.at[src], "fuz", src, dev(src, p, c))
    total = R.GU[u, :, c] + R.RU[u]
    for k in range(1, 4):
        total = total + R.RUZ[turn(u, k)].astype(F32)
    R.TU[...] = total.astype(BF)
    R.RUP[p] = R.TU[p]
    for k in range(1, 4):
        to = turn(p, k)
        send(R.TU.at[to], R.RUP.at[p], "fup", k, p, dev(u, to, c))

    arrived(R.R1, "f1c", 0, mate)
    for g in range(4):
        R.H1[g] = (R.G1[g, :, c] + R.R1[g]).astype(BF)
    for k in range(1, 4):
        to = turn(p, k)
        send(R.H1.at[:, to], R.R1P.at[p], "f1p", k, p, dev(u, to, c))
    total = R.GD[u, c] + R.RD[u]
    for k in range(1, 4):
        total = total + R.RDZ[turn(u, k)].astype(F32)
    R.o_dnw[...] = total
    for k in range(1, 4):
        src = turn(p, k)
        arrived(R.R1P.at[src], "f1p", src, dev(u, src, c))
    total = R.G1[:, p, c] + R.R1[:, p]
    for k in range(1, 4):
        total = total + R.R1P[turn(p, k)].astype(F32)
    R.S1[...] = total.astype(BF)
    for k in range(1, 4):
        to = turn(u, k)
        send(R.S1.at[to], R.R1Z.at[u], "f1z", k, u, dev(to, p, c))
    R.R1Z[u] = R.S1[u]
    for k in range(1, 4):
        src = turn(u, k)
        arrived(R.ROZ.at[src], "foz", src, dev(src, p, c))
    total = R.TO[u].astype(F32)
    for k in range(1, 4):
        total = total + R.ROZ[turn(u, k)].astype(F32)
    R.o_ow[...] = total
    for k in range(1, 4):
        src = turn(p, k)
        arrived(R.RUP.at[src], "fup", src, dev(u, src, c))
    for q in range(4):
        piece = R.RUP[q].astype(F32)
        for g in range(4):
            R.o_upw[:, 768 * g + 192 * q : 768 * g + 192 * q + 192] = piece[:, 192 * g : 192 * g + 192]
    wait_column(R.PR, "x")
    total = R.DH1[...]
    for g in range(4):
        total = total + R.PR[g].astype(F32)
    R.o_in[...] = total
    for k in range(1, 4):
        src = turn(u, k)
        arrived(R.R1Z.at[src], "f1z", src, dev(src, p, c))
    small = jnp.zeros((24, 64), F32)
    for g in range(4):
        piece = R.R1Z[g].astype(F32)
        at = 192 * g
        R.o_kw[:, at : at + 192] = jnp.concatenate([piece[:, 128 * h : 128 * h + 64] for h in range(3)], axis=1)
        R.o_vw[:, at : at + 192] = jnp.concatenate([piece[:, 128 * h + 64 : 128 * h + 128] for h in range(3)], axis=1)
        R.o_qw[:, at : at + 192] = piece[:, 384:576]
        small = small + piece[:, 576:640]
    for row, name in enumerate(SMALL):
        getattr(R, "o_" + name)[...] = small[row : row + 1, 0:24].reshape(24)
    R.o_upb[...] = jnp.concatenate([small[8 + i : 9 + i, 0:24] for i in range(4)], axis=1).reshape(96)

    settle()


def fused_step(*args):
    vmem = pl.BlockSpec(memory_space=pltpu.VMEM)
    return pl.pallas_call(
        layer_kernel,
        out_shape=[jax.ShapeDtypeStruct(shape, dtype) for _, shape, dtype in OUTS],
        in_specs=[pl.BlockSpec(memory_space=pltpu.SMEM) if n == "starts" else vmem for n in ARGS],
        out_specs=[vmem] * len(OUTS),
        scratch_shapes=[pltpu.VMEM(shape, dtype) for _, shape, dtype in SCRATCH]
        + [pltpu.SemaphoreType.DMA((SEMS.total,))] * 2,
        compiler_params=pltpu.CompilerParams(
            collective_id=0, has_side_effects=True, vmem_limit_bytes=63 << 20
        ),
        name="layer_step",
    )(*args)


def solution(mesh):
    fused = mesh.shape["ulysses"] == 4 and mesh.shape["blk"] == 8
    return jax.shard_map(
        fused_step if fused else per_device,
        mesh=mesh,
        in_specs=(
            P(("blk", "ulysses"), None),
            P(("blk", "ulysses"), None),
            P(),
            P(("ulysses", "blk"), None),
            P(("ulysses", "blk"), None),
            P(("ulysses", "blk"), None),
            P(("ulysses", "blk")),
            P(("ulysses", "blk")),
            P(("ulysses", "blk"), None),
            P(("ulysses", "blk")),
            P(("ulysses", "blk")),
            P(("ulysses", "blk")),
            P(("ulysses", "blk"), None),
            P(("ulysses", "blk")),
            P(("ulysses", "blk"), None),
            P(("ulysses", "blk")),
            P(("ulysses", "blk")),
            P(("ulysses", "blk")),
        ),
        out_specs=(
            P(("blk", "ulysses"), None),
            P(("blk", "ulysses"), None),
            P(("ulysses", "blk"), None),
            P(("ulysses", "blk"), None),
            P(("ulysses", "blk"), None),
            P(("ulysses", "blk")),
            P(("ulysses", "blk")),
            P(("ulysses", "blk"), None),
            P(("ulysses", "blk")),
            P(("ulysses", "blk")),
            P(("ulysses", "blk")),
            P(("ulysses", "blk"), None),
            P(("ulysses", "blk")),
            P(("ulysses", "blk"), None),
            P(("ulysses", "blk")),
            P(("ulysses", "blk")),
            P(("ulysses", "blk")),
        ),
        check_vma=False,
    )
```

```python
import jax
import jax.numpy as jnp
from jax import lax
from jax.experimental import pallas as pl
from jax.experimental.pallas import tpu as pltpu
from jax.sharding import PartitionSpec as P

HD = 64
ULYSSES = "ulysses"
BLK = "blk"
WEIGHT_AXES = (ULYSSES, BLK)
TOKEN_AXES = (BLK, ULYSSES)


SCALE = 0.125
EPS = 1e-12


def passed_along(shard, axis, by):
    length = lax.axis_size(axis)
    return lax.ppermute(shard, axis, [(i, (i + by) % length) for i in range(length)])


def layer_norm(hidden, gain, shift):
    middle = jnp.mean(hidden, axis=-1, keepdims=True)
    centered = hidden - middle
    spread = jnp.mean(centered * centered, axis=-1, keepdims=True)
    return centered * lax.rsqrt(spread + EPS) * gain + shift


def gelu_exact(values):
    return jax.nn.gelu(values, approximate=False)


def doc_ids(doc_starts, positions):
    return jnp.sum((doc_starts[None, :] <= positions[:, None]).astype(jnp.int32), axis=1)


def project(left, right):
    return jnp.dot(left, right, preferred_element_type=jnp.float32)


def project_back(left, right):
    return lax.dot_general(
        left, right, (((1,), (1,)), ((), ())), preferred_element_type=jnp.float32
    )


def outer_sum(left, right):
    return lax.dot_general(
        left, right, (((0,), (0,)), ((), ())), preferred_element_type=jnp.float32
    )


def per_device(
    tokens,
    cotangent,
    doc_starts,
    q_weight,
    k_weight,
    v_weight,
    q_bias,
    v_bias,
    o_weight,
    o_bias,
    norm1_gain,
    norm1_bias,
    up_weight,
    up_bias,
    down_weight,
    down_bias,
    norm2_gain,
    norm2_bias,
):
    f32 = jnp.float32
    bf16 = jnp.bfloat16
    w_query, w_key, w_value, b_query, b_value, w_out, b_out, gain_one, shift_one = (
        lax.all_gather(q_weight, WEIGHT_AXES, axis=0, tiled=True),
        lax.all_gather(k_weight, WEIGHT_AXES, axis=0, tiled=True),
        lax.all_gather(v_weight, WEIGHT_AXES, axis=0, tiled=True),
        lax.all_gather(q_bias, WEIGHT_AXES, axis=0, tiled=True),
        lax.all_gather(v_bias, WEIGHT_AXES, axis=0, tiled=True),
        lax.all_gather(o_weight, WEIGHT_AXES, axis=0, tiled=True),
        lax.all_gather(o_bias, WEIGHT_AXES, axis=0, tiled=True),
        lax.all_gather(norm1_gain, WEIGHT_AXES, axis=0, tiled=True),
        lax.all_gather(norm1_bias, WEIGHT_AXES, axis=0, tiled=True),
    )
    w_up, b_up, w_down, b_down, gain_two, shift_two = (
        lax.all_gather(up_weight, WEIGHT_AXES, axis=0, tiled=True),
        lax.all_gather(up_bias, WEIGHT_AXES, axis=0, tiled=True),
        lax.all_gather(down_weight, WEIGHT_AXES, axis=0, tiled=True),
        lax.all_gather(down_bias, WEIGHT_AXES, axis=0, tiled=True),
        lax.all_gather(norm2_gain, WEIGHT_AXES, axis=0, tiled=True),
        lax.all_gather(norm2_bias, WEIGHT_AXES, axis=0, tiled=True),
    )
    query_tok = (project(tokens, w_query) + b_query.astype(f32)).astype(bf16)
    key_tok = project(tokens, w_key).astype(bf16)
    value_tok = (project(tokens, w_value) + b_value.astype(f32)).astype(bf16)
    query_heads, key_heads, value_heads = (
        lax.all_to_all(query_tok, ULYSSES, split_axis=1, concat_axis=0, tiled=True),
        lax.all_to_all(key_tok, ULYSSES, split_axis=1, concat_axis=0, tiled=True),
        lax.all_to_all(value_tok, ULYSSES, split_axis=1, concat_axis=0, tiled=True),
    )
    group = query_heads.shape[0]
    columns = query_heads.shape[1]
    local_heads = columns // HD
    block_count = lax.axis_size(BLK)
    total = group * block_count
    doc_max = min(8192, total // 4, 8 * group)
    reach = (group - 2 + doc_max) // group
    visits = 2 * reach + 1
    block_index = lax.axis_index(BLK)
    rows = jnp.arange(group, dtype=jnp.int32)
    query_ids = doc_ids(doc_starts, block_index * group + rows)
    query3 = query_heads.reshape(group, local_heads, HD)

    def block_mask(offset):
        key_pos = (block_index + offset) * group + rows
        inside = (key_pos >= 0) & (key_pos < total)
        key_ids = jnp.where(inside, doc_ids(doc_starts, key_pos), -1)
        allowed = query_ids[:, None] == key_ids[None, :]
        shared = (
            inside[0] & (key_ids[0] <= query_ids[group - 1]) & (key_ids[group - 1] >= query_ids[0])
        )
        return (allowed, shared)

    def exp_scores(pair, allowed):
        key3 = pair[0].reshape(group, local_heads, HD)
        scores = jnp.einsum("qhd,khd->hqk", query3, key3, preferred_element_type=f32) * SCALE
        return jnp.where(allowed[None], jnp.exp(scores), 0.0)

    def forward_terms(pair, offset):
        allowed, shared = block_mask(offset)
        weights = exp_scores(pair, allowed)
        value3 = pair[1].reshape(group, local_heads, HD)
        numer = jnp.einsum("hqk,khd->qhd", weights.astype(bf16), value3, preferred_element_type=f32)
        return (numer, jnp.sum(weights, axis=2))

    pair_own = jnp.stack([key_heads, value_heads])
    pair = passed_along(pair_own, BLK, -reach)
    numer, denom = forward_terms(pair, reach)
    store = jnp.zeros((1,), bf16)

    def forward_step(step, carry):
        pair_now, numer_now, denom_now, store_now = carry
        pair_now = passed_along(pair_now, BLK, 1)
        more_numer, more_denom = forward_terms(pair_now, reach - step)
        return (pair_now, numer_now + more_numer, denom_now + more_denom, store_now)

    pair, numer, denom, store = lax.fori_loop(1, visits, forward_step, (pair, numer, denom, store))
    attn_f = numer / jnp.transpose(denom)[:, :, None]
    attn_b = attn_f.reshape(group, columns).astype(bf16)
    attn_tok = lax.all_to_all(attn_b, ULYSSES, split_axis=0, concat_axis=1, tiled=True)
    token_f = tokens.astype(f32)
    h_one = token_f + project(attn_tok, w_out) + b_out.astype(f32)
    y_one, norm_one_back = jax.vjp(layer_norm, h_one, gain_one.astype(f32), shift_one.astype(f32))
    y_one_b = y_one.astype(bf16)
    pre_act = project(y_one_b, w_up) + b_up.astype(f32)
    act, gelu_back = jax.vjp(gelu_exact, pre_act)
    act_b = act.astype(bf16)
    h_two = y_one + project(act_b, w_down) + b_down.astype(f32)
    out_f, norm_two_back = jax.vjp(layer_norm, h_two, gain_two.astype(f32), shift_two.astype(f32))
    layer_out = out_f.astype(bf16)
    d_two, g_gain_two, g_shift_two = norm_two_back(cotangent.astype(f32))
    g_b_down = jnp.sum(d_two, axis=0)
    d_two_b = d_two.astype(bf16)
    g_w_down = outer_sum(act_b, d_two_b)
    d_act = project_back(d_two_b, w_down)
    d_pre = gelu_back(d_act)[0].astype(bf16)
    g_b_up = jnp.sum(d_pre.astype(f32), axis=0)
    g_w_up = outer_sum(y_one_b, d_pre)
    d_y_one = d_two + project_back(d_pre, w_up)
    d_one, g_gain_one, g_shift_one = norm_one_back(d_y_one)
    g_b_out = jnp.sum(d_one, axis=0)
    d_one_b = d_one.astype(bf16)
    g_w_out = outer_sum(attn_tok, d_one_b)
    d_attn_tok = project_back(d_one_b, w_out).astype(bf16)
    d_attn = lax.all_to_all(d_attn_tok, ULYSSES, split_axis=1, concat_axis=0, tiled=True)
    d_attn3 = d_attn.reshape(group, local_heads, HD)
    d_attn_f = d_attn3.astype(f32)
    delta = jnp.transpose(jnp.sum(d_attn_f * attn_f, axis=2))
    scaled_grad = d_attn_f / jnp.transpose(denom)[:, :, None]
    grad_high = scaled_grad.astype(bf16)
    grad_rest = (scaled_grad - grad_high.astype(f32)).astype(bf16)

    def backward_terms(pair_in, offset):
        allowed, shared = block_mask(offset)
        weights = exp_scores(pair_in, allowed)
        key3 = pair_in[0].reshape(group, local_heads, HD)
        value3 = pair_in[1].reshape(group, local_heads, HD)
        probs = weights / denom[:, :, None]
        d_prob = jnp.einsum("qhd,khd->hqk", d_attn3, value3, preferred_element_type=f32)
        d_score = (probs * (d_prob - delta[:, :, None]) * SCALE).astype(bf16)
        d_query = jnp.einsum("hqk,khd->qhd", d_score, key3, preferred_element_type=f32)
        d_key = jnp.einsum("hqk,qhd->khd", d_score, query3, preferred_element_type=f32)
        weights_low = weights.astype(bf16)
        d_value = jnp.einsum(
            "hqk,qhd->khd", weights_low, grad_high, preferred_element_type=f32
        ) + jnp.einsum("hqk,qhd->khd", weights_low, grad_rest, preferred_element_type=f32)
        return (d_query, jnp.stack([d_key, d_value]))

    pair = passed_along(pair_own, BLK, -reach)
    d_query_sum, carried = backward_terms(pair, reach)

    def backward_step(step, carry):
        pair_now, d_query_now, carried_now = carry
        pair_now = passed_along(pair_now, BLK, 1)
        more_query, more_kv = backward_terms(pair_now, reach - step)
        carried_now = (
            passed_along(carried_now.astype(jnp.bfloat16), BLK, 1).astype(carried_now.dtype)
            + more_kv
        )
        return (pair_now, d_query_now + more_query, carried_now)

    pair, d_query_sum, carried = lax.fori_loop(
        1, visits, backward_step, (pair, d_query_sum, carried)
    )
    own_grads = passed_along(carried.astype(jnp.bfloat16), BLK, -reach).astype(carried.dtype)
    d_query_b = d_query_sum.reshape(group, columns).astype(bf16)
    d_key_b = own_grads[0].reshape(group, columns).astype(bf16)
    d_value_b = own_grads[1].reshape(group, columns).astype(bf16)
    dq_tok, dk_tok, dv_tok = (
        lax.all_to_all(d_query_b, ULYSSES, split_axis=0, concat_axis=1, tiled=True),
        lax.all_to_all(d_key_b, ULYSSES, split_axis=0, concat_axis=1, tiled=True),
        lax.all_to_all(d_value_b, ULYSSES, split_axis=0, concat_axis=1, tiled=True),
    )
    g_b_query = jnp.sum(dq_tok.astype(f32), axis=0)
    g_b_value = jnp.sum(dv_tok.astype(f32), axis=0)
    g_w_query = outer_sum(tokens, dq_tok)
    g_w_key = outer_sum(tokens, dk_tok)
    g_w_value = outer_sum(tokens, dv_tok)
    input_grad = (
        d_one
        + project_back(dq_tok, w_query)
        + project_back(dk_tok, w_key)
        + project_back(dv_tok, w_value)
    )
    shares = (
        lax.psum_scatter(g_w_query, WEIGHT_AXES, scatter_dimension=0, tiled=True),
        lax.psum_scatter(g_w_key, WEIGHT_AXES, scatter_dimension=0, tiled=True),
        lax.psum_scatter(g_w_value, WEIGHT_AXES, scatter_dimension=0, tiled=True),
        lax.psum_scatter(g_b_query, WEIGHT_AXES, scatter_dimension=0, tiled=True),
        lax.psum_scatter(g_b_value, WEIGHT_AXES, scatter_dimension=0, tiled=True),
        lax.psum_scatter(g_w_out, WEIGHT_AXES, scatter_dimension=0, tiled=True),
        lax.psum_scatter(g_b_out, WEIGHT_AXES, scatter_dimension=0, tiled=True),
        lax.psum_scatter(g_gain_one, WEIGHT_AXES, scatter_dimension=0, tiled=True),
        lax.psum_scatter(g_shift_one, WEIGHT_AXES, scatter_dimension=0, tiled=True),
        lax.psum_scatter(g_w_up, WEIGHT_AXES, scatter_dimension=0, tiled=True),
        lax.psum_scatter(g_b_up, WEIGHT_AXES, scatter_dimension=0, tiled=True),
        lax.psum_scatter(g_w_down, WEIGHT_AXES, scatter_dimension=0, tiled=True),
        lax.psum_scatter(g_b_down, WEIGHT_AXES, scatter_dimension=0, tiled=True),
        lax.psum_scatter(g_gain_two, WEIGHT_AXES, scatter_dimension=0, tiled=True),
        lax.psum_scatter(g_shift_two, WEIGHT_AXES, scatter_dimension=0, tiled=True),
    )
    return (
        layer_out,
        input_grad,
        shares[0],
        shares[1],
        shares[2],
        shares[3],
        shares[4],
        shares[5],
        shares[6],
        shares[7],
        shares[8],
        shares[9],
        shares[10],
        shares[11],
        shares[12],
        shares[13],
        shares[14],
    )


MESH = pl.DeviceIdType.MESH
LOG2E = 1.4426950408889634
RSQRT2 = 0.7071067811865476
PDF0 = 0.3989422804014327

ARGS = ("tok", "cot", "starts", "qw", "kw", "vw", "qb", "vb", "ow", "ob", "g1", "b1", "upw", "upb", "dnw", "dnb", "g2", "b2")
OUTS = dict(
    o_out=((128, 768), jnp.bfloat16),
    o_in=((128, 768), jnp.float32),
    o_qw=((24, 768), jnp.float32),
    o_kw=((24, 768), jnp.float32),
    o_vw=((24, 768), jnp.float32),
    o_qb=((24,), jnp.float32),
    o_vb=((24,), jnp.float32),
    o_ow=((24, 768), jnp.float32),
    o_ob=((24,), jnp.float32),
    o_g1=((24,), jnp.float32),
    o_b1=((24,), jnp.float32),
    o_upw=((24, 3072), jnp.float32),
    o_upb=((96,), jnp.float32),
    o_dnw=((96, 768), jnp.float32),
    o_dnb=((24,), jnp.float32),
    o_g2=((24,), jnp.float32),
    o_b2=((24,), jnp.float32),
)
RAW = dict(
    t_out=((128, 768), jnp.bfloat16),
    t_in=((128, 768), jnp.float32),
    t_qkv=((4, 24, 640), jnp.bfloat16),
    t_up=((4, 24, 768), jnp.bfloat16),
    t_dn=((96, 768), jnp.float32),
    t_ow=((24, 768), jnp.float32),
)
SMALL = ("qb", "vb", "ob", "g1", "b1", "dnb", "g2", "b2")
BF = jnp.bfloat16
F32 = jnp.float32
SCRATCH = dict(
    SM=((24, 128), F32),
    WS=((4, 24, 640), BF),
    W5=((4, 4, 2, 24, 640), BF),
    W2=((768, 640), BF),
    US=((4, 24, 768), BF),
    UP5=((4, 4, 2, 24, 768), BF),
    UP2=((768, 768), BF),
    DN4=((4, 2, 96, 768), BF),
    OW5=((4, 4, 2, 24, 768), BF),
    OW2=((768, 768), BF),
    XG=((4, 128, 768), BF),
    KV=((5, 4, 128, 384), BF),
    KVT=((15, 128, 512), BF),
    QP=((3, 4, 128, 128), BF),
    GP=((3, 4, 128, 128), BF),
    SEGK=((5, 512, 128), jnp.int32),
    EL=((15, 512, 512), BF),
    DST=((512, 512), BF),
    NUM=((3, 64, 512), F32),
    DEN=((3, 8, 512), F32),
    ATN=((3, 64, 512), F32),
    DLT=((3, 8, 512), F32),
    AS=((4, 192, 128), BF),
    AT=((4, 192, 128), BF),
    Y1=((128, 768), F32),
    N1=((128, 768), F32),
    RSD=((128, 128), F32),
    YG=((4, 128, 768), BF),
    ACT=((4, 128, 768), BF),
    GG=((4, 128, 768), BF),
    PS=((4, 128, 768), BF),
    PR=((4, 128, 768), BF),
    H2=((128, 768), F32),
    DH2=((128, 768), F32),
    DG=((4, 128, 768), BF),
    DU=((4, 128, 768), BF),
    DH1=((128, 768), F32),
    DAS=((4, 192, 128), BF),
    DA=((4, 192, 128), BF),
    T1=((768, 512), BF),
    DKS=((5, 512, 384), BF),
    DKR=((5, 512, 384), BF),
    DKO=((512, 384), F32),
    DQT=((3, 64, 512), F32),
    DQ=((512, 640), BF),
    VEC=((16, 768), F32),
    VUP=((8, 768), F32),
    G1=((4, 4, 2, 24, 640), F32),
    R1=((4, 4, 24, 640), F32),
    H1=((4, 4, 24, 640), BF),
    R1P=((4, 4, 24, 640), BF),
    S1=((4, 24, 640), BF),
    R1Z=((4, 24, 640), BF),
    GU=((4, 4, 2, 24, 768), F32),
    RU=((4, 4, 24, 768), F32),
    SU=((4, 4, 24, 768), BF),
    RUZ=((4, 4, 24, 768), BF),
    TU=((4, 24, 768), BF),
    RUP=((4, 24, 768), BF),
    GD=((4, 2, 96, 768), F32),
    RD=((4, 96, 768), F32),
    SD=((4, 96, 768), BF),
    RDZ=((4, 96, 768), BF),
    GO=((4, 4, 2, 24, 768), F32),
    RO=((4, 4, 24, 768), F32),
    SO=((4, 4, 24, 768), BF),
    ROP=((4, 4, 24, 768), BF),
    TO=((4, 24, 768), BF),
    ROZ=((4, 24, 768), BF),
)


class Slots:
    def __init__(self, **sizes):
        self.total = 0
        for name, size in sizes.items():
            setattr(self, name, self.total)
            self.total += size


SEMS = Slots(
    tok=4, wz=4, wp=4, wc=1, us=4, upz=4, dnz=4, oz=4, op=4, cup=1, cdn=1, cow=1, kv=20, at=4,
    yg=4, ps=4, dg=4, qs=4, da=4, dk=5, x=4, f1c=1, f1p=4, f1z=4, fuc=1, fuz=4, fup=4, fdc=1,
    fdz=4, foc=1, fop=4, foz=4, own=4,
)


def mm(left, right):
    return jnp.dot(left, right, preferred_element_type=F32)


def mm_nt(left, right):
    return lax.dot_general(left, right, (((1,), (1,)), ((), ())), preferred_element_type=F32)


def mm_tn(left, right):
    return lax.dot_general(left, right, (((0,), (0,)), ((), ())), preferred_element_type=F32)


def pack(rows):
    tail = rows[:, 128:192]
    return jnp.concatenate([rows[:, 0:128], jnp.concatenate([tail[0:64], tail[64:128]], axis=1)], axis=0)


def unpack(packed):
    tail = packed[128:192]
    tail = jnp.concatenate([tail[:, 0:64], tail[:, 64:128]], axis=0)
    return jnp.concatenate([packed[0:128], tail], axis=1)


def rows_by(shape, axis, flat):
    return lax.broadcasted_iota(jnp.int32, shape, axis).reshape(flat)


class Refs:
    pass


def layer_kernel(*refs):
    R = Refs()
    names = [*ARGS, *RAW, *SCRATCH, "SS", "RS"]
    for name, ref in zip(names, refs, strict=True):
        setattr(R, name, ref)
    u = lax.axis_index(ULYSSES)
    b = lax.axis_index(BLK)
    c = lax.rem(b, 2)
    p = lax.div(b, 2)
    other = 1 - c

    def snake(at):
        return at + lax.div(at, 2) * (1 - 2 * lax.rem(at, 2))

    s = snake(p)
    a = 2 * s + c
    far = p >= 2

    def dev(uu, pp, cc):
        return (uu, 2 * pp + cc)

    def block_dev(aa):
        return dev(u, snake(lax.div(aa, 2)), lax.rem(aa, 2))

    def turn(base, k):
        low, high = lax.rem(base, 2), lax.div(base, 2)
        if k % 2:
            low = 1 - low
        if k // 2:
            high = 1 - high
        return 2 * high + low

    sends = []

    def copy(src, dst, name, si, ri, device):
        return pltpu.make_async_remote_copy(
            src_ref=src, dst_ref=dst, send_sem=R.SS.at[name + si], recv_sem=R.RS.at[name + ri],
            device_id=device, device_id_type=MESH,
        )

    def send(*what):
        desc = copy(*what)
        desc.start()
        sends.append((what[2], None, desc))

    def send_if(cond, *what):
        desc = copy(*what)

        @pl.when(cond)
        def _():
            desc.start()

        sends.append((what[2], cond, desc))

    def settle(*wanted):
        for entry in list(sends):
            name, cond, desc = entry
            if wanted and name not in wanted:
                continue
            sends.remove(entry)
            if cond is None:
                desc.wait_send()
            else:

                @pl.when(cond)
                def _():
                    desc.wait_send()

    def arrived(dst, name, ri, device):
        copy(dst, dst, name, 0, ri, device).wait_recv()

    barrier = pltpu.get_barrier_semaphore()

    def greet(device):
        pl.semaphore_signal(barrier, inc=1, device_id=device, device_id_type=MESH)

    for k in range(1, 8):
        greet((u, lax.rem(b + k, 8)))
    for k in range(1, 4):
        greet((turn(u, k), b))

    @pl.when(far)
    def _():
        for k in range(1, 4):
            greet(dev(turn(u, k), s, c))

    R.SM[...] = jnp.zeros_like(R.SM)
    for row, name in enumerate(SMALL):
        R.SM[row : row + 1, 0:24] = getattr(R, name)[...].astype(F32).reshape(1, 24)
    up_bias = R.upb[...].astype(F32).reshape(1, 96)
    for i in range(4):
        R.SM[8 + i : 9 + i, 0:24] = up_bias[:, 24 * i : 24 * i + 24]
    small = R.SM[:, 0:64].astype(BF)
    qw, kw, vw = R.qw[...], R.kw[...], R.vw[...]
    for g in range(4):
        parts = []
        for h in range(3):
            at = 64 * (3 * g + h)
            parts += [kw[:, at : at + 64], vw[:, at : at + 64]]
        for h in range(3):
            at = 64 * (3 * g + h)
            parts.append(qw[:, at : at + 64])
        parts.append(small)
        R.WS[g] = jnp.concatenate(parts, axis=1)

    pl.semaphore_wait(barrier, 10 + 3 * lax.div(p, 2))

    for k in range(1, 4):
        to = turn(u, k)
        send(R.WS.at[to], R.W5.at[u, p, c], SEMS.wz, k, u, dev(to, p, c))
    R.W5[u, p, c] = R.WS[u]
    for k in range(1, 4):
        to = turn(u, k)
        send(R.tok, R.XG.at[u], SEMS.tok, k, u, dev(to, s, c))
    send_if(far, R.tok, R.XG.at[u], SEMS.tok, 0, u, dev(u, s, c))

    @pl.when(jnp.logical_not(far))
    def _():
        R.XG[u] = R.tok[...]

    up = R.upw[...]
    for q in range(4):
        R.US[q] = jnp.concatenate(
            [up[:, 768 * g + 192 * q : 768 * g + 192 * q + 192] for g in range(4)], axis=1
        )
    for k in range(1, 4):
        to = turn(p, k)
        send(R.US.at[to], R.UP5.at[u, p, c], SEMS.us, k, p, dev(u, to, c))
    R.UP5[u, p, c] = R.US[p]
    R.DN4[u, c] = R.dnw[...]
    R.OW5[u, p, c] = R.ow[...]
    for k in range(1, 4):
        to = turn(u, k)
        send(R.ow, R.OW5.at[u, p, c], SEMS.oz, k, u, dev(to, p, c))
    near, across = turn(u, 1), turn(u, 2)
    send(R.dnw, R.DN4.at[u, c], SEMS.dnz, 0, u, dev(across, p, c))

    row_pos = lax.broadcasted_iota(jnp.int32, (512, 128), 0)
    n_starts = R.starts.shape[0]

    def id_body(j, carry):
        pos = row_pos + (a + j - 2) * 512
        ids = jnp.zeros((512, 128), jnp.int32)
        for i in range(n_starts):
            ids = ids + jnp.where(pos >= R.starts[i], 1, 0)
        R.SEGK[j] = ids
        return carry

    lax.fori_loop(0, 5, id_body, 0)
    q_pos = lax.broadcasted_iota(jnp.int32, (1, 512), 1) + a * 512
    q_ids = jnp.zeros((1, 512), jnp.int32)
    for i in range(n_starts):
        q_ids = q_ids + jnp.where(q_pos >= R.starts[i], 1, 0)
    for ref in (R.QP, R.GP, R.NUM, R.DEN, R.DQT):
        ref[...] = jnp.zeros_like(ref)

    for k in range(1, 4):
        src = turn(u, k)
        arrived(R.W5.at[src, p, c], SEMS.wz, src, dev(src, p, c))
    for k in range(1, 4):
        to = turn(p, k)
        send(R.W5.at[:, p, c], R.W5.at[:, p, c], SEMS.wp, k, p, dev(u, to, c))
    for k in range(1, 4):
        src = turn(p, k)
        arrived(R.UP5.at[u, src, c], SEMS.us, src, dev(u, src, c))
    send(R.UP5.at[u, :, c], R.UP5.at[u, :, c], SEMS.upz, 0, u, dev(across, p, c))
    for k in range(1, 4):
        src = turn(p, k)
        arrived(R.W5.at[:, src, c], SEMS.wp, src, dev(u, src, c))
    send(R.W5.at[:, :, c], R.W5.at[:, :, c], SEMS.wc, 0, 0, dev(u, p, other))
    arrived(R.W5.at[:, :, other], SEMS.wc, 0, dev(u, p, other))
    R.W2[...] = R.W5[...].reshape(768, 640)

    spread = jnp.where(
        rows_by((32, 24, 64), 1, (768, 64)) == lax.broadcasted_iota(jnp.int32, (768, 64), 1), 1.0, 0.0
    ).astype(BF)
    owner = rows_by((32, 24, 768), 0, (768, 768))
    lane = lax.broadcasted_iota(jnp.int32, (1, 768), 1)
    lane_owner = jnp.zeros((1, 768), jnp.int32)
    for i in range(1, 32):
        lane_owner = lane_owner + jnp.where(lane >= 24 * i, 1, 0)
    lane_g = jnp.where(lane >= 192, 1, 0) + jnp.where(lane >= 384, 1, 0) + jnp.where(lane >= 576, 1, 0)
    rest = lane - 192 * lane_g
    lane_c = jnp.where(rest >= 96, 1, 0)
    rest = rest - 96 * lane_c
    lane_r = jnp.where(rest >= 24, 1, 0) + jnp.where(rest >= 48, 1, 0) + jnp.where(rest >= 72, 1, 0)
    up_row = 24 * (8 * lane_g + 2 * p + lane_c) + 8 + lane_r
    row_id = lax.broadcasted_iota(jnp.int32, (768, 768), 0)
    wide = mm_nt(R.W2[:, 576:640], spread)
    mine = jnp.where(owner == lane_owner, wide, 0.0).astype(BF)
    pick = jnp.where(
        lax.broadcasted_iota(jnp.int32, (16, 768), 1) - 24 * lane_owner
        == lax.broadcasted_iota(jnp.int32, (16, 768), 0), 1.0, 0.0
    ).astype(BF)
    R.VEC[...] = mm(pick, mine)
    R.VUP[0:1, :] = jnp.sum(jnp.where(row_id == up_row, wide, 0.0), axis=0, keepdims=True)

    def group_slice(vector):
        out = vector[:, 0:192]
        for g in range(1, 4):
            out = jnp.where(u == g, vector[:, 192 * g : 192 * g + 192], out)
        return out

    qb = group_slice(R.VEC[0:1, :])
    vb = group_slice(R.VEC[1:2, :])
    zero64 = jnp.zeros((1, 64), F32)
    bias = []
    for h in range(3):
        bias += [zero64, vb[:, 64 * h : 64 * h + 64]]
    bias = jnp.concatenate(bias + [qb, zero64], axis=1)

    for k in range(4):
        src = turn(u, k)
        if k == 0:

            @pl.when(far)
            def _():
                arrived(R.XG.at[src], SEMS.tok, src, dev(src, s, c))

        else:
            arrived(R.XG.at[src], SEMS.tok, src, dev(src, s, c))
        proj = mm(R.XG[src], R.W2[...]) + bias
        R.KV[2, src] = proj[:, 0:384].astype(BF)
        query = proj[:, 384:576].astype(BF) * BF(0.125)
        for h in range(3):
            R.QP[h, src, :, 0:64] = query[:, 64 * h : 64 * h + 64]
        for i, step in enumerate((-2, 2, -1, 1)):
            to = a + step
            ok = jnp.logical_and(to >= 0, to < 8)
            slot = 2 - step
            send_if(
                ok, R.KV.at[2, src], R.KV.at[slot, src], SEMS.kv, 4 * k + i, 4 * slot + src, block_dev(to)
            )

    def order(t):
        return 2 + (1 - 2 * c) * ((t + 1) // 2) * (1 - 2 * ((t + 1) % 2))

    def forward_block(t):
        j = order(t)
        ok = jnp.logical_and(a + j >= 2, a + j < 10)

        @pl.when(ok)
        def _():
            if t > 0:
                for r in range(4):
                    arrived(R.KV.at[j, r], SEMS.kv, 4 * j + r, block_dev(a + j - 2))

            def head(h, inner):
                lanes = pl.ds(pl.multiple_of(128 * h, 128), 128)
                kv = R.KV[j, :, :, lanes].reshape(512, 128)
                at = 3 * j + h
                R.KVT[at] = kv.T
                query = R.QP[h].reshape(512, 128)
                total = jnp.zeros((1, 512), F32)
                for r in range(4):
                    rows = slice(128 * r, 128 * r + 128)
                    score = mm_nt(kv[rows], query)
                    ids = R.SEGK[j, rows, :]
                    same = jnp.concatenate([ids] * 4, axis=1) == q_ids
                    weight = jnp.where(same, jnp.exp2(score * LOG2E), 0.0)
                    total = total + jnp.sum(weight, axis=0, keepdims=True)
                    R.EL[at, rows, :] = weight.astype(BF)
                R.DEN[h, 0:1, :] += total
                R.NUM[h] += mm(R.KVT[at, 64:128, :], R.EL[at])
                return inner

            lax.fori_loop(0, 3, head, 0)

    def relay_out():
        for k in range(1, 4):
            src = turn(u, k)
            arrived(R.OW5.at[src, p, c], SEMS.oz, src, dev(src, p, c))
        for k in range(1, 4):
            to = turn(p, k)
            send(R.OW5.at[:, p, c], R.OW5.at[:, p, c], SEMS.op, k, p, dev(u, to, c))

    forward_block(0)
    relay_out()
    for t in range(1, 5):
        forward_block(t)

    heads = []
    for h in range(3):
        attn = R.NUM[h] / R.DEN[h, 0:1, :]
        R.ATN[h] = attn
        heads.append(attn.T.astype(BF))
    for r in range(4):
        rows = slice(128 * r, 128 * r + 128)
        R.AS[r] = pack(jnp.concatenate([part[rows] for part in heads], axis=1))
    for k in range(1, 4):
        to = turn(u, k)
        send(R.AS.at[to], R.AT.at[u], SEMS.at, k, u, dev(to, s, c))
    send_if(far, R.AS.at[u], R.AT.at[u], SEMS.at, 0, u, dev(u, s, c))

    @pl.when(jnp.logical_not(far))
    def _():
        R.AT[u] = R.AS[u]

    mate = dev(u, p, other)
    there = dev(near, p, c)
    arrived(R.DN4.at[across, c], SEMS.dnz, across, dev(across, p, c))
    for i, src in enumerate((u, across)):
        send(R.DN4.at[src, c], R.DN4.at[src, c], SEMS.dnz, 1 + i, src, there)
    arrived(R.UP5.at[across, :, c], SEMS.upz, across, dev(across, p, c))
    for i, src in enumerate((u, across)):
        send(R.UP5.at[src, :, c], R.UP5.at[src, :, c], SEMS.upz, 1 + i, src, there)
    for k in range(1, 4):
        src = turn(p, k)
        arrived(R.OW5.at[:, src, c], SEMS.op, src, dev(u, src, c))
    send(R.OW5.at[:, :, c], R.OW5.at[:, :, c], SEMS.cow, 0, 0, mate)
    arrived(R.OW5.at[:, :, other], SEMS.cow, 0, mate)
    R.OW2[...] = R.OW5[...].reshape(768, 768)

    def wait_column(ref, name):
        for k in range(1, 4):
            src = turn(u, k)
            arrived(ref.at[src], name, src, dev(src, s, c))

        @pl.when(far)
        def _():
            arrived(ref.at[u], name, u, dev(u, s, c))

    wait_column(R.AT, SEMS.at)
    hidden = R.tok[...].astype(F32) + R.VEC[2:3, :]
    for g in range(4):
        hidden = hidden + mm(unpack(R.AT[g]), R.OW2[192 * g : 192 * g + 192, :])
    middle = jnp.mean(hidden, axis=-1, keepdims=True)
    hidden = hidden - middle
    rstd = lax.rsqrt(jnp.mean(hidden * hidden, axis=-1, keepdims=True) + EPS)
    normed = hidden * rstd
    R.N1[...] = normed
    R.RSD[...] = jnp.broadcast_to(rstd, (128, 128))
    y_one = normed * R.VEC[3:4, :] + R.VEC[4:5, :]
    R.Y1[...] = y_one

    def gather_plane(ref, value, name):
        ref[p] = value
        for k in range(1, 4):
            send(ref.at[p], ref.at[p], name, k, p, dev(u, turn(p, k), c))

    gather_plane(R.YG, y_one.astype(BF), SEMS.yg)
    for src in (near, turn(near, 2)):
        arrived(R.DN4.at[src, c], SEMS.dnz, src, there)
    send(R.DN4.at[:, c], R.DN4.at[:, c], SEMS.cdn, 0, 0, mate)
    for src in (near, turn(near, 2)):
        arrived(R.UP5.at[src, :, c], SEMS.upz, src, there)
    send(R.UP5.at[:, :, c], R.UP5.at[:, :, c], SEMS.cup, 0, 0, mate)
    arrived(R.DN4.at[:, other], SEMS.cdn, 0, mate)
    arrived(R.UP5.at[:, :, other], SEMS.cup, 0, mate)
    R.UP2[...] = R.UP5[...].reshape(768, 768)
    for k in range(4):
        at = turn(p, k)
        if k > 0:
            arrived(R.YG.at[at], SEMS.yg, at, dev(u, at, c))
        pre = mm(R.YG[at], R.UP2[...]) + R.VUP[0:1, :]
        phi = 0.5 * (1.0 + lax.erf(pre * RSQRT2))
        R.GG[at] = (phi + pre * (PDF0 * jnp.exp(-0.5 * pre * pre))).astype(BF)
        act = (pre * phi).astype(BF)
        R.ACT[at] = act
        part = mm(act, R.DN4[...].reshape(768, 768))
        if k == 0:
            R.H2[...] = part
        else:
            R.PS[at] = part.astype(BF)
            send(R.PS.at[at], R.PR.at[p], SEMS.ps, k, p, dev(u, at, c))
    hidden = R.Y1[...] + R.H2[...] + R.VEC[5:6, :]
    for k in range(1, 4):
        at = turn(p, k)
        arrived(R.PR.at[at], SEMS.ps, at, dev(u, at, c))
        hidden = hidden + R.PR[at].astype(F32)

    middle = jnp.mean(hidden, axis=-1, keepdims=True)
    hidden = hidden - middle
    rstd = lax.rsqrt(jnp.mean(hidden * hidden, axis=-1, keepdims=True) + EPS)
    normed = hidden * rstd
    gain = R.VEC[6:7, :]
    R.t_out[...] = (normed * gain + R.VEC[7:8, :]).astype(BF)
    grad = R.cot[...].astype(F32)
    cg = grad * gain
    d_two = (
        cg - jnp.mean(cg, axis=-1, keepdims=True) - normed * jnp.mean(cg * normed, axis=-1, keepdims=True)
    ) * rstd
    gather_plane(R.DG, d_two.astype(BF), SEMS.dg)
    R.DH2[...] = d_two
    g_gain_two = jnp.sum(grad * normed, axis=0, keepdims=True)
    g_shift_two = jnp.sum(grad, axis=0, keepdims=True)
    g_b_down = jnp.sum(d_two, axis=0, keepdims=True)

    settle(SEMS.ps)
    g_b_up = jnp.zeros((1, 768), F32)
    for k in range(4):
        at = turn(p, k)
        if k > 0:
            arrived(R.DG.at[at], SEMS.dg, at, dev(u, at, c))
        d_act = mm_nt(R.DG[at], R.DN4[...].reshape(768, 768))
        d_pre = (d_act * R.GG[at].astype(F32)).astype(BF)
        R.DU[at] = d_pre
        g_b_up = g_b_up + jnp.sum(d_pre.astype(F32), axis=0, keepdims=True)
        part = mm_nt(d_pre, R.UP2[...])
        if k == 0:
            R.H2[...] = part
        else:
            R.PS[at] = part.astype(BF)
            send(R.PS.at[at], R.PR.at[p], SEMS.qs, k, p, dev(u, at, c))
    def wide_grad(left, right_ref, put):
        R.T1[...] = left.T

        def body(n, carry):
            lanes = pl.ds(pl.multiple_of(256 * n, 256), 256)
            put(lanes, mm(R.T1[...], right_ref[:, :, lanes].reshape(512, 256)))
            return carry

        lax.fori_loop(0, 3, body, 0)

    def put_down(lanes, value):
        R.GD[:, :, :, lanes] = value.reshape(4, 2, 96, 256)

    def put_up(lanes, value):
        R.GU[:, :, :, :, lanes] = value.reshape(4, 4, 2, 24, 256)

    wide_grad(R.ACT[...].reshape(512, 768), R.DG, put_down)
    send(R.GD.at[:, other], R.RD, SEMS.fdc, 0, 0, mate)
    wide_grad(R.YG[...].reshape(512, 768), R.DU, put_up)
    send(R.GU.at[:, :, other], R.RU, SEMS.fuc, 0, 0, mate)
    d_y = R.DH2[...] + R.H2[...]
    for k in range(1, 4):
        at = turn(p, k)
        arrived(R.PR.at[at], SEMS.qs, at, dev(u, at, c))
        d_y = d_y + R.PR[at].astype(F32)

    normed = R.N1[...]
    cg = d_y * R.VEC[3:4, :]
    d_one = (
        cg - jnp.mean(cg, axis=-1, keepdims=True) - normed * jnp.mean(cg * normed, axis=-1, keepdims=True)
    ) * R.RSD[:, 0:1]
    R.DH1[...] = d_one
    d_one_low = d_one.astype(BF)
    for k in range(4):
        to = turn(u, (k + 1) % 4)
        w_rows = R.OW2[pl.ds(pl.multiple_of(192 * to, 64), 192), :]
        R.DAS[to] = pack(mm_nt(d_one_low, w_rows).astype(BF))
        if k < 3:
            send(R.DAS.at[to], R.DA.at[u], SEMS.da, k + 1, u, dev(to, s, c))
    send_if(far, R.DAS.at[u], R.DA.at[u], SEMS.da, 0, u, dev(u, s, c))

    @pl.when(jnp.logical_not(far))
    def _():
        R.DA[u] = R.DAS[u]

    vec = R.VEC
    vec[2:3, :] = jnp.sum(d_one, axis=0, keepdims=True)
    vec[3:4, :] = jnp.sum(d_y * normed, axis=0, keepdims=True)
    vec[4:5, :] = jnp.sum(d_y, axis=0, keepdims=True)
    vec[5:6, :] = g_b_down
    vec[6:7, :] = g_gain_two
    vec[7:8, :] = g_shift_two
    vec[8:16, :] = jnp.zeros((8, 768), F32)
    R.VUP[0:1, :] = g_b_up

    for g in range(4):
        R.GO[g] = mm_tn(unpack(R.AT[g]), d_one_low).reshape(4, 2, 24, 768)
    send(R.GO.at[:, :, other], R.RO, SEMS.foc, 0, 0, mate)

    arrived(R.RD, SEMS.fdc, 0, mate)
    for g in range(4):
        R.SD[g] = (R.GD[g, c] + R.RD[g]).astype(BF)
    for k in range(1, 4):
        to = turn(u, k)
        send(R.SD.at[to], R.RDZ.at[u], SEMS.fdz, k, u, dev(to, p, c))
    arrived(R.RU, SEMS.fuc, 0, mate)
    for g in range(4):
        R.SU[g] = (R.GU[g, :, c] + R.RU[g]).astype(BF)
    for k in range(1, 4):
        to = turn(u, k)
        send(R.SU.at[to], R.RUZ.at[u], SEMS.fuz, k, u, dev(to, p, c))
    arrived(R.RO, SEMS.foc, 0, mate)
    for g in range(4):
        R.SO[g] = (R.GO[g, :, c] + R.RO[g]).astype(BF)
    for k in range(1, 4):
        to = turn(p, k)
        send(R.SO.at[:, to], R.ROP.at[p], SEMS.fop, k, p, dev(u, to, c))
    wait_column(R.DA, SEMS.da)
    d_rows = jnp.concatenate([unpack(R.DA[r]) for r in range(4)], axis=0).astype(F32)
    for h in range(3):
        d_attn = d_rows[:, 64 * h : 64 * h + 64].T
        scaled = (d_attn / R.DEN[h, 0:1, :]).astype(BF)
        R.DLT[h, 0:1, :] = jnp.sum(scaled.astype(F32) * R.ATN[h], axis=0, keepdims=True)
        R.GP[h, :, :, 64:128] = scaled.T.reshape(4, 128, 64)

    def backward_block(t):
        j = order(t)
        ok = jnp.logical_and(a + j >= 2, a + j < 10)

        @pl.when(ok)
        def _():
            def head(h, inner):
                lanes = pl.ds(pl.multiple_of(128 * h, 128), 128)
                at = 3 * j + h
                grad_rows = R.GP[h].reshape(512, 128)
                shift = R.DLT[h, 0:1, :]
                for r in range(4):
                    rows = slice(128 * r, 128 * r + 128)
                    d_prob = mm_nt(R.KV[j, r, :, lanes], grad_rows)
                    R.DST[rows, :] = (R.EL[at, rows, :].astype(F32) * (d_prob - shift)).astype(BF)
                d_kv = mm(R.DST[...], R.QP[h].reshape(512, 128)) + mm(R.EL[at], grad_rows)
                if t == 0:
                    R.DKO[:, lanes] = d_kv
                else:
                    R.DKS[j, :, lanes] = d_kv.astype(BF)
                R.DQT[h] += mm(R.KVT[at, 0:64, :], R.DST[...])
                return inner

            lax.fori_loop(0, 3, head, 0)

        if t > 0:
            send_if(
                ok, R.DKS.at[j], R.DKR.at[4 - j], SEMS.dk, t, 4 - j, block_dev(a + j - 2)
            )

    backward_block(4)
    backward_block(3)
    for k in range(1, 4):
        src = turn(p, k)
        arrived(R.ROP.at[src], SEMS.fop, src, dev(u, src, c))
    for g in range(4):
        total = R.GO[g, p, c] + R.RO[g, p]
        for k in range(1, 4):
            total = total + R.ROP[turn(p, k), g].astype(F32)
        R.TO[g] = total.astype(BF)
    for k in range(1, 4):
        to = turn(u, k)
        send(R.TO.at[to], R.ROZ.at[u], SEMS.foz, k, u, dev(to, p, c))
    backward_block(2)
    backward_block(1)
    backward_block(0)

    for h in range(3):
        R.DQ[:, 384 + 64 * h : 448 + 64 * h] = (R.DQT[h] * 0.125).T.astype(BF)
    R.DQ[:, 576:640] = jnp.zeros((512, 64), BF)
    for t in range(1, 5):
        j = order(t)

        @pl.when(jnp.logical_and(a + j >= 2, a + j < 10))
        def _():
            arrived(R.DKR.at[j], SEMS.dk, j, block_dev(a + j - 2))
            R.DKO[...] += R.DKR[j].astype(F32)

    R.DQ[:, 0:384] = R.DKO[...].astype(BF)

    settle(SEMS.qs)
    for k in range(4):
        to = turn(u, (k + 1) % 4)
        part = mm_nt(R.DQ[pl.ds(pl.multiple_of(128 * to, 128), 128), :], R.W2[...])
        R.PS[to] = part.astype(BF)
        if k < 3:
            send(R.PS.at[to], R.PR.at[u], SEMS.x, k + 1, u, dev(to, s, c))
    send_if(far, R.PS.at[u], R.PR.at[u], SEMS.x, 0, u, dev(u, s, c))

    @pl.when(jnp.logical_not(far))
    def _():
        R.PR[u] = R.PS[u]

    d_qkv = R.DQ[...].astype(F32)
    sums = jnp.sum(d_qkv, axis=0, keepdims=True)
    sum_v = jnp.concatenate([sums[:, 128 * h + 64 : 128 * h + 128] for h in range(3)], axis=1)
    sum_q = sums[:, 384:576]

    def at_group(piece):
        return jnp.concatenate([jnp.where(u == g, piece, 0.0) for g in range(4)], axis=1)

    vec[0:1, :] = at_group(sum_q)
    vec[1:2, :] = at_group(sum_v)
    choose = jnp.where(
        rows_by((32, 24, 16), 1, (768, 16)) == lax.broadcasted_iota(jnp.int32, (768, 16), 1), 1.0, 0.0
    ).astype(BF)
    laid = jnp.where(owner == lane_owner, mm(choose, vec[...].astype(BF)), 0.0)
    laid = jnp.where(row_id == up_row, R.VUP[0:1, :], laid)
    R.T1[...] = R.XG[...].reshape(512, 768).T
    for n in range(5):
        lanes = slice(128 * n, 128 * n + 128)
        value = mm(R.T1[...], R.DQ[:, lanes])
        if n == 4:
            value = jnp.concatenate([value[:, 0:64], mm(laid.astype(BF), spread)], axis=1)
        R.G1[:, :, :, :, lanes] = value.reshape(4, 4, 2, 24, 128)
    send(R.G1.at[:, :, other], R.R1, SEMS.f1c, 0, 0, mate)

    arrived(R.R1, SEMS.f1c, 0, mate)
    for g in range(4):
        R.H1[g] = (R.G1[g, :, c] + R.R1[g]).astype(BF)
    for k in range(1, 4):
        to = turn(p, k)
        send(R.H1.at[:, to], R.R1P.at[p], SEMS.f1p, k, p, dev(u, to, c))
    for k in range(1, 4):
        src = turn(u, k)
        arrived(R.RDZ.at[src], SEMS.fdz, src, dev(src, p, c))
        arrived(R.RUZ.at[src], SEMS.fuz, src, dev(src, p, c))
    total = R.GU[u, :, c] + R.RU[u]
    for k in range(1, 4):
        total = total + R.RUZ[turn(u, k)].astype(F32)
    R.TU[...] = total.astype(BF)
    R.RUP[p] = R.TU[p]
    for k in range(1, 4):
        to = turn(p, k)
        send(R.TU.at[to], R.RUP.at[p], SEMS.fup, k, p, dev(u, to, c))

    total = R.GD[u, c] + R.RD[u]
    for k in range(1, 4):
        total = total + R.RDZ[turn(u, k)].astype(F32)
    R.t_dn[...] = total
    for k in range(1, 4):
        src = turn(p, k)
        arrived(R.R1P.at[src], SEMS.f1p, src, dev(u, src, c))
    total = R.G1[:, p, c] + R.R1[:, p]
    for k in range(1, 4):
        total = total + R.R1P[turn(p, k)].astype(F32)
    R.S1[...] = total.astype(BF)
    for k in range(1, 4):
        to = turn(u, k)
        send(R.S1.at[to], R.R1Z.at[u], SEMS.f1z, k, u, dev(to, p, c))
    R.R1Z[u] = R.S1[u]
    for k in range(1, 4):
        src = turn(u, k)
        arrived(R.ROZ.at[src], SEMS.foz, src, dev(src, p, c))
    total = R.TO[u].astype(F32)
    for k in range(1, 4):
        total = total + R.ROZ[turn(u, k)].astype(F32)
    R.t_ow[...] = total
    for k in range(1, 4):
        src = turn(p, k)
        arrived(R.RUP.at[src], SEMS.fup, src, dev(u, src, c))
    R.t_up[...] = R.RUP[...]
    wait_column(R.PR, SEMS.x)
    total = R.DH1[...]
    for g in range(4):
        total = total + R.PR[g].astype(F32)
    R.t_in[...] = total
    for k in range(1, 4):
        src = turn(u, k)
        arrived(R.R1Z.at[src], SEMS.f1z, src, dev(src, p, c))
    R.t_qkv[...] = R.R1Z[...]
    settle()


def finish_kernel(*refs):
    R = Refs()
    for name, ref in zip([*RAW, *OUTS], refs, strict=True):
        setattr(R, name, ref)
    R.o_out[...] = R.t_out[...]
    R.o_in[...] = R.t_in[...]
    R.o_dnw[...] = R.t_dn[...]
    R.o_ow[...] = R.t_ow[...]
    for q in range(4):
        piece = R.t_up[q].astype(F32)
        for g in range(4):
            R.o_upw[:, 768 * g + 192 * q : 768 * g + 192 * q + 192] = piece[:, 192 * g : 192 * g + 192]
    small = jnp.zeros((24, 64), F32)
    for g in range(4):
        piece = R.t_qkv[g].astype(F32)
        at = 192 * g
        R.o_kw[:, at : at + 192] = jnp.concatenate([piece[:, 128 * h : 128 * h + 64] for h in range(3)], axis=1)
        R.o_vw[:, at : at + 192] = jnp.concatenate([piece[:, 128 * h + 64 : 128 * h + 128] for h in range(3)], axis=1)
        R.o_qw[:, at : at + 192] = piece[:, 384:576]
        small = small + piece[:, 576:640]
    for row, name in enumerate(SMALL):
        getattr(R, "o_" + name)[...] = small[row : row + 1, 0:24].reshape(24)
    R.o_upb[...] = jnp.concatenate([small[8 + i : 9 + i, 0:24] for i in range(4)], axis=1).reshape(96)


def fused_step(*args):
    vmem = pl.BlockSpec(memory_space=pltpu.VMEM)
    raw = pl.pallas_call(
        layer_kernel,
        out_shape=[jax.ShapeDtypeStruct(shape, dtype) for shape, dtype in RAW.values()],
        in_specs=[pl.BlockSpec(memory_space=pltpu.SMEM) if n == "starts" else vmem for n in ARGS],
        out_specs=[vmem] * len(RAW),
        scratch_shapes=[pltpu.VMEM(shape, dtype) for shape, dtype in SCRATCH.values()]
        + [pltpu.SemaphoreType.DMA((SEMS.total,))] * 2,
        compiler_params=pltpu.CompilerParams(
            collective_id=0, has_side_effects=True, vmem_limit_bytes=63 << 20
        ),
        name="layer_step",
    )(*args)
    return pl.pallas_call(
        finish_kernel,
        out_shape=[jax.ShapeDtypeStruct(shape, dtype) for shape, dtype in OUTS.values()],
        in_specs=[vmem] * len(RAW),
        out_specs=[vmem] * len(OUTS),
        name="finish",
    )(*raw)


def solution(mesh):
    fused = mesh.shape[ULYSSES] == 4 and mesh.shape[BLK] == 8
    return jax.shard_map(
        fused_step if fused else per_device,
        mesh=mesh,
        in_specs=(
            P(TOKEN_AXES, None),
            P(TOKEN_AXES, None),
            P(),
            P(WEIGHT_AXES, None),
            P(WEIGHT_AXES, None),
            P(WEIGHT_AXES, None),
            P(WEIGHT_AXES),
            P(WEIGHT_AXES),
            P(WEIGHT_AXES, None),
            P(WEIGHT_AXES),
            P(WEIGHT_AXES),
            P(WEIGHT_AXES),
            P(WEIGHT_AXES, None),
            P(WEIGHT_AXES),
            P(WEIGHT_AXES, None),
            P(WEIGHT_AXES),
            P(WEIGHT_AXES),
            P(WEIGHT_AXES),
        ),
        out_specs=(
            P(TOKEN_AXES, None),
            P(TOKEN_AXES, None),
            P(WEIGHT_AXES, None),
            P(WEIGHT_AXES, None),
            P(WEIGHT_AXES, None),
            P(WEIGHT_AXES),
            P(WEIGHT_AXES),
            P(WEIGHT_AXES, None),
            P(WEIGHT_AXES),
            P(WEIGHT_AXES),
            P(WEIGHT_AXES),
            P(WEIGHT_AXES, None),
            P(WEIGHT_AXES),
            P(WEIGHT_AXES, None),
            P(WEIGHT_AXES),
            P(WEIGHT_AXES),
            P(WEIGHT_AXES),
        ),
        check_vma=False,
    )
```

```python
import jax
import jax.numpy as jnp
from jax import lax
from jax.experimental import pallas as pl
from jax.experimental.pallas import tpu as pltpu
from jax.sharding import PartitionSpec as P

HD = 64
ULYSSES = "ulysses"
BLK = "blk"
WEIGHT_AXES = (ULYSSES, BLK)
TOKEN_AXES = (BLK, ULYSSES)


SCALE = 0.125
EPS = 1e-12


def passed_along(shard, axis, by):
    length = lax.axis_size(axis)
    return lax.ppermute(shard, axis, [(i, (i + by) % length) for i in range(length)])


def layer_norm(hidden, gain, shift):
    middle = jnp.mean(hidden, axis=-1, keepdims=True)
    centered = hidden - middle
    spread = jnp.mean(centered * centered, axis=-1, keepdims=True)
    return centered * lax.rsqrt(spread + EPS) * gain + shift


def gelu_exact(values):
    return jax.nn.gelu(values, approximate=False)


def doc_ids(doc_starts, positions):
    return jnp.sum((doc_starts[None, :] <= positions[:, None]).astype(jnp.int32), axis=1)


def project(left, right):
    return jnp.dot(left, right, preferred_element_type=jnp.float32)


def project_back(left, right):
    return lax.dot_general(
        left, right, (((1,), (1,)), ((), ())), preferred_element_type=jnp.float32
    )


def outer_sum(left, right):
    return lax.dot_general(
        left, right, (((0,), (0,)), ((), ())), preferred_element_type=jnp.float32
    )


def per_device(
    tokens,
    cotangent,
    doc_starts,
    q_weight,
    k_weight,
    v_weight,
    q_bias,
    v_bias,
    o_weight,
    o_bias,
    norm1_gain,
    norm1_bias,
    up_weight,
    up_bias,
    down_weight,
    down_bias,
    norm2_gain,
    norm2_bias,
):
    f32 = jnp.float32
    bf16 = jnp.bfloat16
    w_query, w_key, w_value, b_query, b_value, w_out, b_out, gain_one, shift_one = (
        lax.all_gather(q_weight, WEIGHT_AXES, axis=0, tiled=True),
        lax.all_gather(k_weight, WEIGHT_AXES, axis=0, tiled=True),
        lax.all_gather(v_weight, WEIGHT_AXES, axis=0, tiled=True),
        lax.all_gather(q_bias, WEIGHT_AXES, axis=0, tiled=True),
        lax.all_gather(v_bias, WEIGHT_AXES, axis=0, tiled=True),
        lax.all_gather(o_weight, WEIGHT_AXES, axis=0, tiled=True),
        lax.all_gather(o_bias, WEIGHT_AXES, axis=0, tiled=True),
        lax.all_gather(norm1_gain, WEIGHT_AXES, axis=0, tiled=True),
        lax.all_gather(norm1_bias, WEIGHT_AXES, axis=0, tiled=True),
    )
    w_up, b_up, w_down, b_down, gain_two, shift_two = (
        lax.all_gather(up_weight, WEIGHT_AXES, axis=0, tiled=True),
        lax.all_gather(up_bias, WEIGHT_AXES, axis=0, tiled=True),
        lax.all_gather(down_weight, WEIGHT_AXES, axis=0, tiled=True),
        lax.all_gather(down_bias, WEIGHT_AXES, axis=0, tiled=True),
        lax.all_gather(norm2_gain, WEIGHT_AXES, axis=0, tiled=True),
        lax.all_gather(norm2_bias, WEIGHT_AXES, axis=0, tiled=True),
    )
    query_tok = (project(tokens, w_query) + b_query.astype(f32)).astype(bf16)
    key_tok = project(tokens, w_key).astype(bf16)
    value_tok = (project(tokens, w_value) + b_value.astype(f32)).astype(bf16)
    query_heads, key_heads, value_heads = (
        lax.all_to_all(query_tok, ULYSSES, split_axis=1, concat_axis=0, tiled=True),
        lax.all_to_all(key_tok, ULYSSES, split_axis=1, concat_axis=0, tiled=True),
        lax.all_to_all(value_tok, ULYSSES, split_axis=1, concat_axis=0, tiled=True),
    )
    group = query_heads.shape[0]
    columns = query_heads.shape[1]
    local_heads = columns // HD
    block_count = lax.axis_size(BLK)
    total = group * block_count
    doc_max = min(8192, total // 4, 8 * group)
    reach = (group - 2 + doc_max) // group
    visits = 2 * reach + 1
    block_index = lax.axis_index(BLK)
    rows = jnp.arange(group, dtype=jnp.int32)
    query_ids = doc_ids(doc_starts, block_index * group + rows)
    query3 = query_heads.reshape(group, local_heads, HD)

    def block_mask(offset):
        key_pos = (block_index + offset) * group + rows
        inside = (key_pos >= 0) & (key_pos < total)
        key_ids = jnp.where(inside, doc_ids(doc_starts, key_pos), -1)
        allowed = query_ids[:, None] == key_ids[None, :]
        shared = (
            inside[0] & (key_ids[0] <= query_ids[group - 1]) & (key_ids[group - 1] >= query_ids[0])
        )
        return (allowed, shared)

    def exp_scores(pair, allowed):
        key3 = pair[0].reshape(group, local_heads, HD)
        scores = jnp.einsum("qhd,khd->hqk", query3, key3, preferred_element_type=f32) * SCALE
        return jnp.where(allowed[None], jnp.exp(scores), 0.0)

    def forward_terms(pair, offset):
        allowed, shared = block_mask(offset)
        weights = exp_scores(pair, allowed)
        value3 = pair[1].reshape(group, local_heads, HD)
        numer = jnp.einsum("hqk,khd->qhd", weights.astype(bf16), value3, preferred_element_type=f32)
        return (numer, jnp.sum(weights, axis=2))

    pair_own = jnp.stack([key_heads, value_heads])
    pair = passed_along(pair_own, BLK, -reach)
    numer, denom = forward_terms(pair, reach)
    store = jnp.zeros((1,), bf16)

    def forward_step(step, carry):
        pair_now, numer_now, denom_now, store_now = carry
        pair_now = passed_along(pair_now, BLK, 1)
        more_numer, more_denom = forward_terms(pair_now, reach - step)
        return (pair_now, numer_now + more_numer, denom_now + more_denom, store_now)

    pair, numer, denom, store = lax.fori_loop(1, visits, forward_step, (pair, numer, denom, store))
    attn_f = numer / jnp.transpose(denom)[:, :, None]
    attn_b = attn_f.reshape(group, columns).astype(bf16)
    attn_tok = lax.all_to_all(attn_b, ULYSSES, split_axis=0, concat_axis=1, tiled=True)
    token_f = tokens.astype(f32)
    h_one = token_f + project(attn_tok, w_out) + b_out.astype(f32)
    y_one, norm_one_back = jax.vjp(layer_norm, h_one, gain_one.astype(f32), shift_one.astype(f32))
    y_one_b = y_one.astype(bf16)
    pre_act = project(y_one_b, w_up) + b_up.astype(f32)
    act, gelu_back = jax.vjp(gelu_exact, pre_act)
    act_b = act.astype(bf16)
    h_two = y_one + project(act_b, w_down) + b_down.astype(f32)
    out_f, norm_two_back = jax.vjp(layer_norm, h_two, gain_two.astype(f32), shift_two.astype(f32))
    layer_out = out_f.astype(bf16)
    d_two, g_gain_two, g_shift_two = norm_two_back(cotangent.astype(f32))
    g_b_down = jnp.sum(d_two, axis=0)
    d_two_b = d_two.astype(bf16)
    g_w_down = outer_sum(act_b, d_two_b)
    d_act = project_back(d_two_b, w_down)
    d_pre = gelu_back(d_act)[0].astype(bf16)
    g_b_up = jnp.sum(d_pre.astype(f32), axis=0)
    g_w_up = outer_sum(y_one_b, d_pre)
    d_y_one = d_two + project_back(d_pre, w_up)
    d_one, g_gain_one, g_shift_one = norm_one_back(d_y_one)
    g_b_out = jnp.sum(d_one, axis=0)
    d_one_b = d_one.astype(bf16)
    g_w_out = outer_sum(attn_tok, d_one_b)
    d_attn_tok = project_back(d_one_b, w_out).astype(bf16)
    d_attn = lax.all_to_all(d_attn_tok, ULYSSES, split_axis=1, concat_axis=0, tiled=True)
    d_attn3 = d_attn.reshape(group, local_heads, HD)
    d_attn_f = d_attn3.astype(f32)
    delta = jnp.transpose(jnp.sum(d_attn_f * attn_f, axis=2))
    scaled_grad = d_attn_f / jnp.transpose(denom)[:, :, None]
    grad_high = scaled_grad.astype(bf16)
    grad_rest = (scaled_grad - grad_high.astype(f32)).astype(bf16)

    def backward_terms(pair_in, offset):
        allowed, shared = block_mask(offset)
        weights = exp_scores(pair_in, allowed)
        key3 = pair_in[0].reshape(group, local_heads, HD)
        value3 = pair_in[1].reshape(group, local_heads, HD)
        probs = weights / denom[:, :, None]
        d_prob = jnp.einsum("qhd,khd->hqk", d_attn3, value3, preferred_element_type=f32)
        d_score = (probs * (d_prob - delta[:, :, None]) * SCALE).astype(bf16)
        d_query = jnp.einsum("hqk,khd->qhd", d_score, key3, preferred_element_type=f32)
        d_key = jnp.einsum("hqk,qhd->khd", d_score, query3, preferred_element_type=f32)
        weights_low = weights.astype(bf16)
        d_value = jnp.einsum(
            "hqk,qhd->khd", weights_low, grad_high, preferred_element_type=f32
        ) + jnp.einsum("hqk,qhd->khd", weights_low, grad_rest, preferred_element_type=f32)
        return (d_query, jnp.stack([d_key, d_value]))

    pair = passed_along(pair_own, BLK, -reach)
    d_query_sum, carried = backward_terms(pair, reach)

    def backward_step(step, carry):
        pair_now, d_query_now, carried_now = carry
        pair_now = passed_along(pair_now, BLK, 1)
        more_query, more_kv = backward_terms(pair_now, reach - step)
        carried_now = (
            passed_along(carried_now.astype(jnp.bfloat16), BLK, 1).astype(carried_now.dtype)
            + more_kv
        )
        return (pair_now, d_query_now + more_query, carried_now)

    pair, d_query_sum, carried = lax.fori_loop(
        1, visits, backward_step, (pair, d_query_sum, carried)
    )
    own_grads = passed_along(carried.astype(jnp.bfloat16), BLK, -reach).astype(carried.dtype)
    d_query_b = d_query_sum.reshape(group, columns).astype(bf16)
    d_key_b = own_grads[0].reshape(group, columns).astype(bf16)
    d_value_b = own_grads[1].reshape(group, columns).astype(bf16)
    dq_tok, dk_tok, dv_tok = (
        lax.all_to_all(d_query_b, ULYSSES, split_axis=0, concat_axis=1, tiled=True),
        lax.all_to_all(d_key_b, ULYSSES, split_axis=0, concat_axis=1, tiled=True),
        lax.all_to_all(d_value_b, ULYSSES, split_axis=0, concat_axis=1, tiled=True),
    )
    g_b_query = jnp.sum(dq_tok.astype(f32), axis=0)
    g_b_value = jnp.sum(dv_tok.astype(f32), axis=0)
    g_w_query = outer_sum(tokens, dq_tok)
    g_w_key = outer_sum(tokens, dk_tok)
    g_w_value = outer_sum(tokens, dv_tok)
    input_grad = (
        d_one
        + project_back(dq_tok, w_query)
        + project_back(dk_tok, w_key)
        + project_back(dv_tok, w_value)
    )
    shares = (
        lax.psum_scatter(g_w_query, WEIGHT_AXES, scatter_dimension=0, tiled=True),
        lax.psum_scatter(g_w_key, WEIGHT_AXES, scatter_dimension=0, tiled=True),
        lax.psum_scatter(g_w_value, WEIGHT_AXES, scatter_dimension=0, tiled=True),
        lax.psum_scatter(g_b_query, WEIGHT_AXES, scatter_dimension=0, tiled=True),
        lax.psum_scatter(g_b_value, WEIGHT_AXES, scatter_dimension=0, tiled=True),
        lax.psum_scatter(g_w_out, WEIGHT_AXES, scatter_dimension=0, tiled=True),
        lax.psum_scatter(g_b_out, WEIGHT_AXES, scatter_dimension=0, tiled=True),
        lax.psum_scatter(g_gain_one, WEIGHT_AXES, scatter_dimension=0, tiled=True),
        lax.psum_scatter(g_shift_one, WEIGHT_AXES, scatter_dimension=0, tiled=True),
        lax.psum_scatter(g_w_up, WEIGHT_AXES, scatter_dimension=0, tiled=True),
        lax.psum_scatter(g_b_up, WEIGHT_AXES, scatter_dimension=0, tiled=True),
        lax.psum_scatter(g_w_down, WEIGHT_AXES, scatter_dimension=0, tiled=True),
        lax.psum_scatter(g_b_down, WEIGHT_AXES, scatter_dimension=0, tiled=True),
        lax.psum_scatter(g_gain_two, WEIGHT_AXES, scatter_dimension=0, tiled=True),
        lax.psum_scatter(g_shift_two, WEIGHT_AXES, scatter_dimension=0, tiled=True),
    )
    return (
        layer_out,
        input_grad,
        shares[0],
        shares[1],
        shares[2],
        shares[3],
        shares[4],
        shares[5],
        shares[6],
        shares[7],
        shares[8],
        shares[9],
        shares[10],
        shares[11],
        shares[12],
        shares[13],
        shares[14],
    )


MESH = pl.DeviceIdType.MESH
LOG2E = 1.4426950408889634
RSQRT2 = 0.7071067811865476
PDF0 = 0.3989422804014327

ARGS = ("tok", "cot", "starts", "qw", "kw", "vw", "qb", "vb", "ow", "ob", "g1", "b1", "upw", "upb", "dnw", "dnb", "g2", "b2")
OUTS = dict(
    o_out=((128, 768), jnp.bfloat16),
    o_in=((128, 768), jnp.float32),
    o_qw=((24, 768), jnp.float32),
    o_kw=((24, 768), jnp.float32),
    o_vw=((24, 768), jnp.float32),
    o_qb=((24,), jnp.float32),
    o_vb=((24,), jnp.float32),
    o_ow=((24, 768), jnp.float32),
    o_ob=((24,), jnp.float32),
    o_g1=((24,), jnp.float32),
    o_b1=((24,), jnp.float32),
    o_upw=((24, 3072), jnp.float32),
    o_upb=((96,), jnp.float32),
    o_dnw=((96, 768), jnp.float32),
    o_dnb=((24,), jnp.float32),
    o_g2=((24,), jnp.float32),
    o_b2=((24,), jnp.float32),
)
RAW = dict(
    t_out=((128, 768), jnp.bfloat16),
    t_in=((128, 768), jnp.float32),
    t_qkv=((4, 24, 640), jnp.bfloat16),
    t_up=((4, 24, 768), jnp.bfloat16),
    t_dn=((96, 768), jnp.float32),
    t_ow=((24, 768), jnp.float32),
)
SMALL = ("qb", "vb", "ob", "g1", "b1", "dnb", "g2", "b2")
BF = jnp.bfloat16
F32 = jnp.float32
SCRATCH = dict(
    SM=((24, 128), F32),
    WS=((4, 24, 640), BF),
    W5=((4, 4, 2, 24, 640), BF),
    W2=((768, 640), BF),
    US=((4, 24, 768), BF),
    UP5=((4, 4, 2, 24, 768), BF),
    UP2=((768, 768), BF),
    DN4=((4, 2, 96, 768), BF),
    OW5=((4, 4, 2, 24, 768), BF),
    OW2=((768, 768), BF),
    XG=((4, 2, 64, 768), BF),
    KV=((5, 4, 128, 384), BF),
    KVT=((15, 128, 512), BF),
    QP=((3, 4, 128, 128), BF),
    GP=((3, 4, 128, 128), BF),
    SEGK=((5, 512, 128), jnp.int32),
    EL=((15, 512, 512), BF),
    DST=((512, 512), BF),
    NUM=((3, 64, 512), F32),
    DEN=((3, 8, 512), F32),
    ATN=((3, 64, 512), F32),
    DLT=((3, 8, 512), F32),
    AS=((4, 192, 128), BF),
    AT=((4, 192, 128), BF),
    Y1=((128, 768), F32),
    N1=((128, 768), F32),
    RSD=((128, 128), F32),
    YG=((4, 128, 768), BF),
    ACT=((4, 128, 768), BF),
    GG=((4, 128, 768), BF),
    PS=((4, 128, 768), BF),
    PR=((4, 128, 768), BF),
    XN=((128, 768), BF),
    H2=((128, 768), F32),
    DH2=((128, 768), F32),
    DG=((4, 128, 768), BF),
    DU=((4, 128, 768), BF),
    DH1=((128, 768), F32),
    DAS=((4, 192, 128), BF),
    DA=((4, 192, 128), BF),
    T1=((768, 512), BF),
    DKS=((5, 512, 384), BF),
    DKX=((512, 384), BF),
    DKR=((5, 512, 384), BF),
    DKO=((512, 384), F32),
    DQT=((3, 64, 512), F32),
    DQ=((512, 640), BF),
    VEC=((16, 768), F32),
    VUP=((8, 768), F32),
    G1=((4, 4, 2, 24, 640), F32),
    R1=((4, 4, 24, 640), F32),
    H1=((4, 4, 24, 640), BF),
    R1P=((4, 4, 24, 640), BF),
    S1=((4, 24, 640), BF),
    R1Z=((4, 24, 640), BF),
    GU=((4, 4, 2, 24, 768), F32),
    RU=((4, 4, 24, 768), F32),
    SU=((2, 4, 24, 768), BF),
    RU1=((2, 4, 24, 768), BF),
    SU2=((4, 24, 768), BF),
    RU2=((4, 24, 768), BF),
    TU=((4, 24, 768), BF),
    RUP=((4, 24, 768), BF),
    GD=((4, 2, 96, 768), F32),
    RD=((4, 96, 768), F32),
    SD=((2, 96, 768), BF),
    RD1=((2, 96, 768), BF),
    SD2=((96, 768), BF),
    RD2=((96, 768), BF),
    GO=((4, 4, 2, 24, 768), F32),
    RO=((4, 4, 24, 768), F32),
    SO=((4, 4, 24, 768), BF),
    ROP=((4, 4, 24, 768), BF),
    TO=((4, 24, 768), BF),
    ROZ=((4, 24, 768), BF),
)


class Slots:
    def __init__(self, **sizes):
        self.total = 0
        for name, size in sizes.items():
            setattr(self, name, self.total)
            self.total += size


SEMS = Slots(
    tok=8, hop=2, wz=4, wp=4, wc=1, us=4, upz=4, dnz=4, oz=4, op=4, cup=1, cdn=1, cow=1, kv=20, at=4,
    yg=4, ps=4, dg=4, qs=4, da=4, dk=5, dx=1, x=4, f1c=1, f1p=4, f1z=4, fuc=1, fuz=2, fup=4, fdc=1,
    fdz=2, foc=1, fop=4, foz=4, own=4,
)


def mm(left, right):
    return jnp.dot(left, right, preferred_element_type=F32)


def mm_nt(left, right):
    return lax.dot_general(left, right, (((1,), (1,)), ((), ())), preferred_element_type=F32)


def mm_tn(left, right):
    return lax.dot_general(left, right, (((0,), (0,)), ((), ())), preferred_element_type=F32)


def pack(rows):
    tail = rows[:, 128:192]
    return jnp.concatenate([rows[:, 0:128], jnp.concatenate([tail[0:64], tail[64:128]], axis=1)], axis=0)


def unpack(packed):
    tail = packed[128:192]
    tail = jnp.concatenate([tail[:, 0:64], tail[:, 64:128]], axis=0)
    return jnp.concatenate([packed[0:128], tail], axis=1)


def rows_by(shape, axis, flat):
    return lax.broadcasted_iota(jnp.int32, shape, axis).reshape(flat)


class Refs:
    pass


def layer_kernel(*refs):
    R = Refs()
    names = [*ARGS, *RAW, *SCRATCH, "SS", "RS"]
    for name, ref in zip(names, refs, strict=True):
        setattr(R, name, ref)
    u = lax.axis_index(ULYSSES)
    b = lax.axis_index(BLK)
    c = lax.rem(b, 2)
    p = lax.div(b, 2)
    other = 1 - c

    def snake(at):
        return at + lax.div(at, 2) * (1 - 2 * lax.rem(at, 2))

    s = snake(p)
    a = 2 * s + c
    far = p >= 2

    def dev(uu, pp, cc):
        return (uu, 2 * pp + cc)

    def block_dev(aa):
        return dev(u, snake(lax.div(aa, 2)), lax.rem(aa, 2))

    def turn(base, k):
        low, high = lax.rem(base, 2), lax.div(base, 2)
        if k % 2:
            low = 1 - low
        if k // 2:
            high = 1 - high
        return 2 * high + low

    sends = []

    def copy(src, dst, name, si, ri, device):
        return pltpu.make_async_remote_copy(
            src_ref=src, dst_ref=dst, send_sem=R.SS.at[name + si], recv_sem=R.RS.at[name + ri],
            device_id=device, device_id_type=MESH,
        )

    def send(*what):
        desc = copy(*what)
        desc.start()
        sends.append((what[2], None, desc))

    def send_if(cond, *what):
        desc = copy(*what)

        @pl.when(cond)
        def _():
            desc.start()

        sends.append((what[2], cond, desc))

    def settle(*wanted):
        for entry in list(sends):
            name, cond, desc = entry
            if wanted and name not in wanted:
                continue
            sends.remove(entry)
            if cond is None:
                desc.wait_send()
            else:

                @pl.when(cond)
                def _():
                    desc.wait_send()

    def arrived(dst, name, ri, device):
        copy(dst, dst, name, 0, ri, device).wait_recv()

    barrier = pltpu.get_barrier_semaphore()

    def greet(device):
        pl.semaphore_signal(barrier, inc=1, device_id=device, device_id_type=MESH)

    for k in range(1, 8):
        greet((u, lax.rem(b + k, 8)))
    for k in range(1, 4):
        greet((turn(u, k), b))

    @pl.when(far)
    def _():
        for k in range(1, 4):
            greet(dev(turn(u, k), s, c))

    R.SM[...] = jnp.zeros_like(R.SM)
    for row, name in enumerate(SMALL):
        R.SM[row : row + 1, 0:24] = getattr(R, name)[...].astype(F32).reshape(1, 24)
    up_bias = R.upb[...].astype(F32).reshape(1, 96)
    for i in range(4):
        R.SM[8 + i : 9 + i, 0:24] = up_bias[:, 24 * i : 24 * i + 24]
    small = R.SM[:, 0:64].astype(BF)
    qw, kw, vw = R.qw[...], R.kw[...], R.vw[...]
    for g in range(4):
        parts = []
        for h in range(3):
            at = 64 * (3 * g + h)
            parts += [kw[:, at : at + 64], vw[:, at : at + 64]]
        for h in range(3):
            at = 64 * (3 * g + h)
            parts.append(qw[:, at : at + 64])
        parts.append(small)
        R.WS[g] = jnp.concatenate(parts, axis=1)

    pl.semaphore_wait(barrier, 10 + 3 * lax.div(p, 2))

    for k in range(1, 4):
        to = turn(u, k)
        send(R.WS.at[to], R.W5.at[u, p, c], SEMS.wz, k, u, dev(to, p, c))
    R.W5[u, p, c] = R.WS[u]
    halves = (slice(0, 64), slice(64, 128))
    for i in range(2):
        send_if(far, R.tok.at[halves[i]], R.XG.at[u, i], SEMS.hop, i, i, dev(u, s, c))

    @pl.when(jnp.logical_not(far))
    def _():
        for i in range(2):
            R.XG[u, i] = R.tok[halves[i], :]

    near, across = turn(u, 1), turn(u, 2)
    there = dev(near, p, c)
    for i in range(2):
        for k in (2, 1):
            send_if(
                jnp.logical_not(far),
                R.tok.at[halves[i]], R.XG.at[u, i], SEMS.tok, 4 * i + k, 2 * u + i, dev(turn(u, k), p, c),
            )

    up = R.upw[...]
    for q in range(4):
        R.US[q] = jnp.concatenate(
            [up[:, 768 * g + 192 * q : 768 * g + 192 * q + 192] for g in range(4)], axis=1
        )
    for k in range(1, 4):
        to = turn(p, k)
        send(R.US.at[to], R.UP5.at[u, p, c], SEMS.us, k, p, dev(u, to, c))
    R.UP5[u, p, c] = R.US[p]
    R.DN4[u, c] = R.dnw[...]
    R.OW5[u, p, c] = R.ow[...]

    mate = dev(u, p, other)
    row_pos = lax.broadcasted_iota(jnp.int32, (512, 128), 0)
    n_starts = R.starts.shape[0]

    def id_body(j, carry):
        pos = row_pos + (a + j - 2) * 512
        ids = jnp.zeros((512, 128), jnp.int32)
        for i in range(n_starts):
            ids = ids + jnp.where(pos >= R.starts[i], 1, 0)
        R.SEGK[j] = ids
        return carry

    lax.fori_loop(0, 5, id_body, 0)
    q_pos = lax.broadcasted_iota(jnp.int32, (1, 512), 1) + a * 512
    q_ids = jnp.zeros((1, 512), jnp.int32)
    for i in range(n_starts):
        q_ids = q_ids + jnp.where(q_pos >= R.starts[i], 1, 0)
    for ref in (R.QP, R.GP, R.NUM, R.DEN, R.DQT):
        ref[...] = jnp.zeros_like(ref)

    for i in range(2):

        @pl.when(far)
        def _():
            arrived(R.XG.at[u, i], SEMS.hop, i, dev(u, s, c))

        for k in (2, 1):
            send_if(
                far,
                R.XG.at[u, i], R.XG.at[u, i], SEMS.tok, 4 * i + k, 2 * u + i, dev(turn(u, k), p, c),
            )
    for k in range(1, 4):
        src = turn(u, k)
        arrived(R.W5.at[src, p, c], SEMS.wz, src, dev(src, p, c))
    for k in range(1, 4):
        to = turn(p, k)
        send(R.W5.at[:, p, c], R.W5.at[:, p, c], SEMS.wp, k, p, dev(u, to, c))
    for k in range(1, 4):
        src = turn(p, k)
        arrived(R.W5.at[:, src, c], SEMS.wp, src, dev(u, src, c))
    send(R.W5.at[:, :, c], R.W5.at[:, :, c], SEMS.wc, 0, 0, dev(u, p, other))
    for i in range(2):
        arrived(R.XG.at[across, i], SEMS.tok, 2 * across + i, dev(across, p, c))
        send(R.XG.at[across, i], R.XG.at[across, i], SEMS.tok, 4 * i + 3, 2 * across + i, there)
    for k in range(1, 4):
        to = turn(u, k)
        send(R.ow, R.OW5.at[u, p, c], SEMS.oz, k, u, dev(to, p, c))
    send(R.dnw, R.DN4.at[u, c], SEMS.dnz, 0, u, dev(across, p, c))
    for k in range(1, 4):
        src = turn(p, k)
        arrived(R.UP5.at[u, src, c], SEMS.us, src, dev(u, src, c))
    send(R.UP5.at[u, :, c], R.UP5.at[u, :, c], SEMS.upz, 0, u, dev(across, p, c))
    arrived(R.W5.at[:, :, other], SEMS.wc, 0, dev(u, p, other))
    R.W2[...] = R.W5[...].reshape(768, 640)

    spread = jnp.where(
        rows_by((32, 24, 64), 1, (768, 64)) == lax.broadcasted_iota(jnp.int32, (768, 64), 1), 1.0, 0.0
    ).astype(BF)
    owner = rows_by((32, 24, 768), 0, (768, 768))
    lane = lax.broadcasted_iota(jnp.int32, (1, 768), 1)
    lane_owner = jnp.zeros((1, 768), jnp.int32)
    for i in range(1, 32):
        lane_owner = lane_owner + jnp.where(lane >= 24 * i, 1, 0)
    lane_g = jnp.where(lane >= 192, 1, 0) + jnp.where(lane >= 384, 1, 0) + jnp.where(lane >= 576, 1, 0)
    rest = lane - 192 * lane_g
    lane_c = jnp.where(rest >= 96, 1, 0)
    rest = rest - 96 * lane_c
    lane_r = jnp.where(rest >= 24, 1, 0) + jnp.where(rest >= 48, 1, 0) + jnp.where(rest >= 72, 1, 0)
    up_row = 24 * (8 * lane_g + 2 * p + lane_c) + 8 + lane_r
    row_id = lax.broadcasted_iota(jnp.int32, (768, 768), 0)
    wide = mm_nt(R.W2[:, 576:640], spread)
    mine = jnp.where(owner == lane_owner, wide, 0.0).astype(BF)
    pick = jnp.where(
        lax.broadcasted_iota(jnp.int32, (16, 768), 1) - 24 * lane_owner
        == lax.broadcasted_iota(jnp.int32, (16, 768), 0), 1.0, 0.0
    ).astype(BF)
    R.VEC[...] = mm(pick, mine)
    R.VUP[0:1, :] = jnp.sum(jnp.where(row_id == up_row, wide, 0.0), axis=0, keepdims=True)

    def group_slice(vector):
        out = vector[:, 0:192]
        for g in range(1, 4):
            out = jnp.where(u == g, vector[:, 192 * g : 192 * g + 192], out)
        return out

    qb = group_slice(R.VEC[0:1, :])
    vb = group_slice(R.VEC[1:2, :])
    zero64 = jnp.zeros((1, 64), F32)
    bias = []
    for h in range(3):
        bias += [zero64, vb[:, 64 * h : 64 * h + 64]]
    bias = jnp.concatenate(bias + [qb, zero64], axis=1)

    for k in range(4):
        src = turn(u, k)
        if k > 0:
            for i in range(2):
                if k != 2:
                    arrived(R.XG.at[src, i], SEMS.tok, 2 * src + i, there)
        proj = mm(R.XG[src].reshape(128, 768), R.W2[...]) + bias
        R.KV[2, src] = proj[:, 0:384].astype(BF)
        query = proj[:, 384:576].astype(BF) * BF(0.125)
        for h in range(3):
            R.QP[h, src, :, 0:64] = query[:, 64 * h : 64 * h + 64]
        slot = 1 + 2 * c
        send(R.KV.at[2, src], R.KV.at[slot, src], SEMS.kv, 4 * k, 4 * slot + src, mate)
        for i, step in enumerate((-2, 2)):
            to = a + step
            ok = jnp.logical_and(to >= 0, to < 8)
            slot = 2 - step
            send_if(
                ok, R.KV.at[2, src], R.KV.at[slot, src], SEMS.kv, 4 * k + 1 + i, 4 * slot + src, block_dev(to)
            )

    def order(t):
        return 2 + (1 - 2 * c) * ((t + 1) // 2) * (1 - 2 * ((t + 1) % 2))

    def forward_block(t):
        j = order(t)
        ok = jnp.logical_and(a + j >= 2, a + j < 10)

        @pl.when(ok)
        def _():
            if t == 1 or t == 2:
                for r in range(4):
                    arrived(R.KV.at[j, r], SEMS.kv, 4 * j + r, mate)
            if t == 4:
                for r in range(4):
                    arrived(R.KV.at[j, r], SEMS.kv, 4 * j + r, block_dev(a + j - 2))

            def head(h, inner):
                lanes = pl.ds(pl.multiple_of(128 * h, 128), 128)
                kv = R.KV[j, :, :, lanes].reshape(512, 128)
                at = 3 * j + h
                R.KVT[at] = kv.T
                query = R.QP[h].reshape(512, 128)
                total = jnp.zeros((1, 512), F32)
                for r in range(4):
                    rows = slice(128 * r, 128 * r + 128)
                    score = mm_nt(kv[rows], query)
                    ids = R.SEGK[j, rows, :]
                    same = jnp.concatenate([ids] * 4, axis=1) == q_ids
                    weight = jnp.where(same, jnp.exp2(score * LOG2E), 0.0)
                    total = total + jnp.sum(weight, axis=0, keepdims=True)
                    R.EL[at, rows, :] = weight.astype(BF)
                R.DEN[h, 0:1, :] += total
                R.NUM[h] += mm(R.KVT[at, 64:128, :], R.EL[at])
                return inner

            lax.fori_loop(0, 3, head, 0)

    def relay_out():
        for k in range(1, 4):
            src = turn(u, k)
            arrived(R.OW5.at[src, p, c], SEMS.oz, src, dev(src, p, c))
        for k in range(1, 4):
            to = turn(p, k)
            send(R.OW5.at[:, p, c], R.OW5.at[:, p, c], SEMS.op, k, p, dev(u, to, c))

    def share_keys():
        j = order(3)
        ok = jnp.logical_and(a + j >= 2, a + j < 10)
        slot = 1 + 2 * (1 - c)
        for r in range(4):

            @pl.when(ok)
            def _():
                arrived(R.KV.at[j, r], SEMS.kv, 4 * j + r, block_dev(a + j - 2))

            send_if(ok, R.KV.at[j, r], R.KV.at[slot, r], SEMS.kv, 4 * r + 3, 4 * slot + r, mate)

    def relay_down():
        arrived(R.DN4.at[across, c], SEMS.dnz, across, dev(across, p, c))
        for i, src in enumerate((u, across)):
            send(R.DN4.at[src, c], R.DN4.at[src, c], SEMS.dnz, 1 + i, src, there)

    def relay_up():
        arrived(R.UP5.at[across, :, c], SEMS.upz, across, dev(across, p, c))
        for i, src in enumerate((u, across)):
            send(R.UP5.at[src, :, c], R.UP5.at[src, :, c], SEMS.upz, 1 + i, src, there)

    forward_block(0)
    relay_out()
    forward_block(1)
    relay_down()
    share_keys()
    forward_block(3)
    forward_block(2)
    forward_block(4)

    heads = []
    for h in range(3):
        attn = R.NUM[h] / R.DEN[h, 0:1, :]
        R.ATN[h] = attn
        heads.append(attn.T.astype(BF))
    for r in range(4):
        rows = slice(128 * r, 128 * r + 128)
        R.AS[r] = pack(jnp.concatenate([part[rows] for part in heads], axis=1))
    for k in range(1, 4):
        to = turn(u, k)
        send(R.AS.at[to], R.AT.at[u], SEMS.at, k, u, dev(to, s, c))
    send_if(far, R.AS.at[u], R.AT.at[u], SEMS.at, 0, u, dev(u, s, c))

    @pl.when(jnp.logical_not(far))
    def _():
        R.AT[u] = R.AS[u]

    relay_up()
    for k in range(1, 4):
        src = turn(p, k)
        arrived(R.OW5.at[:, src, c], SEMS.op, src, dev(u, src, c))
    send(R.OW5.at[:, :, c], R.OW5.at[:, :, c], SEMS.cow, 0, 0, mate)
    arrived(R.OW5.at[:, :, other], SEMS.cow, 0, mate)
    R.OW2[...] = R.OW5[...].reshape(768, 768)

    def wait_column(ref, name):
        for k in range(1, 4):
            src = turn(u, k)
            arrived(ref.at[src], name, src, dev(src, s, c))

        @pl.when(far)
        def _():
            arrived(ref.at[u], name, u, dev(u, s, c))

    wait_column(R.AT, SEMS.at)
    hidden = R.tok[...].astype(F32) + R.VEC[2:3, :]
    for g in range(4):
        hidden = hidden + mm(unpack(R.AT[g]), R.OW2[192 * g : 192 * g + 192, :])
    middle = jnp.mean(hidden, axis=-1, keepdims=True)
    hidden = hidden - middle
    rstd = lax.rsqrt(jnp.mean(hidden * hidden, axis=-1, keepdims=True) + EPS)
    normed = hidden * rstd
    R.N1[...] = normed
    R.RSD[...] = jnp.broadcast_to(rstd, (128, 128))
    y_one = normed * R.VEC[3:4, :] + R.VEC[4:5, :]
    R.Y1[...] = y_one

    def gather_plane(ref, value, name):
        ref[p] = value
        for k in range(1, 4):
            send(ref.at[p], ref.at[p], name, k, p, dev(u, turn(p, k), c))

    gather_plane(R.YG, y_one.astype(BF), SEMS.yg)
    for src in (near, turn(near, 2)):
        arrived(R.DN4.at[src, c], SEMS.dnz, src, there)
    send(R.DN4.at[:, c], R.DN4.at[:, c], SEMS.cdn, 0, 0, mate)
    for src in (near, turn(near, 2)):
        arrived(R.UP5.at[src, :, c], SEMS.upz, src, there)
    send(R.UP5.at[:, :, c], R.UP5.at[:, :, c], SEMS.cup, 0, 0, mate)
    arrived(R.DN4.at[:, other], SEMS.cdn, 0, mate)
    arrived(R.UP5.at[:, :, other], SEMS.cup, 0, mate)
    R.UP2[...] = R.UP5[...].reshape(768, 768)
    for k in range(4):
        at = turn(p, k)
        if k > 0:
            arrived(R.YG.at[at], SEMS.yg, at, dev(u, at, c))
        pre = mm(R.YG[at], R.UP2[...]) + R.VUP[0:1, :]
        phi = 0.5 * (1.0 + lax.erf(pre * RSQRT2))
        R.GG[at] = (phi + pre * (PDF0 * jnp.exp(-0.5 * pre * pre))).astype(BF)
        act = (pre * phi).astype(BF)
        R.ACT[at] = act
        part = mm(act, R.DN4[...].reshape(768, 768))
        if k == 0:
            R.H2[...] = part
        else:
            R.PS[at] = part.astype(BF)
            send(R.PS.at[at], R.PR.at[p], SEMS.ps, k, p, dev(u, at, c))
    hidden = R.Y1[...] + R.H2[...] + R.VEC[5:6, :]
    for k in range(1, 4):
        at = turn(p, k)
        arrived(R.PR.at[at], SEMS.ps, at, dev(u, at, c))
        hidden = hidden + R.PR[at].astype(F32)

    middle = jnp.mean(hidden, axis=-1, keepdims=True)
    hidden = hidden - middle
    rstd = lax.rsqrt(jnp.mean(hidden * hidden, axis=-1, keepdims=True) + EPS)
    normed = hidden * rstd
    gain = R.VEC[6:7, :]
    R.t_out[...] = (normed * gain + R.VEC[7:8, :]).astype(BF)
    grad = R.cot[...].astype(F32)
    cg = grad * gain
    d_two = (
        cg - jnp.mean(cg, axis=-1, keepdims=True) - normed * jnp.mean(cg * normed, axis=-1, keepdims=True)
    ) * rstd
    gather_plane(R.DG, d_two.astype(BF), SEMS.dg)
    R.DH2[...] = d_two
    g_gain_two = jnp.sum(grad * normed, axis=0, keepdims=True)
    g_shift_two = jnp.sum(grad, axis=0, keepdims=True)
    g_b_down = jnp.sum(d_two, axis=0, keepdims=True)

    settle(SEMS.ps)
    g_b_up = jnp.zeros((1, 768), F32)
    for k in range(4):
        at = turn(p, k)
        if k > 0:
            arrived(R.DG.at[at], SEMS.dg, at, dev(u, at, c))
        d_act = mm_nt(R.DG[at], R.DN4[...].reshape(768, 768))
        d_pre = (d_act * R.GG[at].astype(F32)).astype(BF)
        R.DU[at] = d_pre
        g_b_up = g_b_up + jnp.sum(d_pre.astype(F32), axis=0, keepdims=True)
        part = mm_nt(d_pre, R.UP2[...])
        if k == 0:
            R.H2[...] = part
        else:
            R.PS[at] = part.astype(BF)
            send(R.PS.at[at], R.PR.at[p], SEMS.qs, k, p, dev(u, at, c))
    def wide_grad(left, right_ref, put):
        R.T1[...] = left.T

        def body(n, carry):
            lanes = pl.ds(pl.multiple_of(256 * n, 256), 256)
            put(lanes, mm(R.T1[...], right_ref[:, :, lanes].reshape(512, 256)))
            return carry

        lax.fori_loop(0, 3, body, 0)

    def put_down(lanes, value):
        R.GD[:, :, :, lanes] = value.reshape(4, 2, 96, 256)

    def put_up(lanes, value):
        R.GU[:, :, :, :, lanes] = value.reshape(4, 4, 2, 24, 256)

    wide_grad(R.ACT[...].reshape(512, 768), R.DG, put_down)
    send(R.GD.at[:, other], R.RD, SEMS.fdc, 0, 0, mate)
    wide_grad(R.YG[...].reshape(512, 768), R.DU, put_up)
    send(R.GU.at[:, :, other], R.RU, SEMS.fuc, 0, 0, mate)
    arrived(R.RD, SEMS.fdc, 0, mate)
    for i, g in enumerate((near, turn(near, 2))):
        R.SD[i] = (R.GD[g, c] + R.RD[g]).astype(BF)
    send(R.SD, R.RD1, SEMS.fdz, 0, 0, there)
    d_y = R.DH2[...] + R.H2[...]
    for k in range(1, 4):
        at = turn(p, k)
        arrived(R.PR.at[at], SEMS.qs, at, dev(u, at, c))
        d_y = d_y + R.PR[at].astype(F32)

    normed = R.N1[...]
    cg = d_y * R.VEC[3:4, :]
    d_one = (
        cg - jnp.mean(cg, axis=-1, keepdims=True) - normed * jnp.mean(cg * normed, axis=-1, keepdims=True)
    ) * R.RSD[:, 0:1]
    R.DH1[...] = d_one
    d_one_low = d_one.astype(BF)
    for k in range(4):
        to = turn(u, (k + 1) % 4)
        w_rows = R.OW2[pl.ds(pl.multiple_of(192 * to, 64), 192), :]
        R.DAS[to] = pack(mm_nt(d_one_low, w_rows).astype(BF))
        if k < 3:
            send(R.DAS.at[to], R.DA.at[u], SEMS.da, k + 1, u, dev(to, s, c))
    send_if(far, R.DAS.at[u], R.DA.at[u], SEMS.da, 0, u, dev(u, s, c))

    @pl.when(jnp.logical_not(far))
    def _():
        R.DA[u] = R.DAS[u]

    vec = R.VEC
    vec[2:3, :] = jnp.sum(d_one, axis=0, keepdims=True)
    vec[3:4, :] = jnp.sum(d_y * normed, axis=0, keepdims=True)
    vec[4:5, :] = jnp.sum(d_y, axis=0, keepdims=True)
    vec[5:6, :] = g_b_down
    vec[6:7, :] = g_gain_two
    vec[7:8, :] = g_shift_two
    vec[8:16, :] = jnp.zeros((8, 768), F32)
    R.VUP[0:1, :] = g_b_up

    for g in range(4):
        R.GO[g] = mm_tn(unpack(R.AT[g]), d_one_low).reshape(4, 2, 24, 768)
    send(R.GO.at[:, :, other], R.RO, SEMS.foc, 0, 0, mate)

    arrived(R.RU, SEMS.fuc, 0, mate)
    for i, g in enumerate((near, turn(near, 2))):
        R.SU[i] = (R.GU[g, :, c] + R.RU[g]).astype(BF)
    send(R.SU, R.RU1, SEMS.fuz, 0, 0, there)

    def relay_down_grad():
        arrived(R.RD1, SEMS.fdz, 0, there)
        R.SD2[...] = (R.GD[across, c] + R.RD[across] + R.RD1[1].astype(F32)).astype(BF)
        send(R.SD2, R.RD2, SEMS.fdz, 1, 1, dev(across, p, c))

    def relay_up_grad():
        arrived(R.RU1, SEMS.fuz, 0, there)
        R.SU2[...] = (R.GU[across, :, c] + R.RU[across] + R.RU1[1].astype(F32)).astype(BF)
        send(R.SU2, R.RU2, SEMS.fuz, 1, 1, dev(across, p, c))

    wait_column(R.DA, SEMS.da)
    d_rows = jnp.concatenate([unpack(R.DA[r]) for r in range(4)], axis=0).astype(F32)
    for h in range(3):
        d_attn = d_rows[:, 64 * h : 64 * h + 64].T
        scaled = (d_attn / R.DEN[h, 0:1, :]).astype(BF)
        R.DLT[h, 0:1, :] = jnp.sum(scaled.astype(F32) * R.ATN[h], axis=0, keepdims=True)
        R.GP[h, :, :, 64:128] = scaled.T.reshape(4, 128, 64)

    def backward_block(t):
        j = order(t)
        ok = jnp.logical_and(a + j >= 2, a + j < 10)

        @pl.when(ok)
        def _():
            if t == 3:
                arrived(R.DKX, SEMS.dx, 0, mate)

            def head(h, inner):
                lanes = pl.ds(pl.multiple_of(128 * h, 128), 128)
                at = 3 * j + h
                grad_rows = R.GP[h].reshape(512, 128)
                shift = R.DLT[h, 0:1, :]
                for r in range(4):
                    rows = slice(128 * r, 128 * r + 128)
                    d_prob = mm_nt(R.KV[j, r, :, lanes], grad_rows)
                    R.DST[rows, :] = (R.EL[at, rows, :].astype(F32) * (d_prob - shift)).astype(BF)
                d_kv = mm(R.DST[...], R.QP[h].reshape(512, 128)) + mm(R.EL[at], grad_rows)
                if t == 0:
                    R.DKO[:, lanes] = d_kv
                elif t == 3:
                    R.DKS[j, :, lanes] = (d_kv + R.DKX[:, lanes].astype(F32)).astype(BF)
                else:
                    R.DKS[j, :, lanes] = d_kv.astype(BF)
                R.DQT[h] += mm(R.KVT[at, 0:64, :], R.DST[...])
                return inner

            lax.fori_loop(0, 3, head, 0)

        if t == 2:
            send_if(ok, R.DKS.at[j], R.DKX, SEMS.dx, 0, 0, mate)
        elif t > 0:
            send_if(
                ok, R.DKS.at[j], R.DKR.at[4 - j], SEMS.dk, t, 4 - j, block_dev(a + j - 2)
            )

    backward_block(4)
    relay_down_grad()
    backward_block(2)
    backward_block(3)
    arrived(R.RO, SEMS.foc, 0, mate)
    for g in range(4):
        R.SO[g] = (R.GO[g, :, c] + R.RO[g]).astype(BF)
    for k in range(1, 4):
        to = turn(p, k)
        send(R.SO.at[:, to], R.ROP.at[p], SEMS.fop, k, p, dev(u, to, c))
    backward_block(1)
    relay_up_grad()
    backward_block(0)

    for h in range(3):
        R.DQ[:, 384 + 64 * h : 448 + 64 * h] = (R.DQT[h] * 0.125).T.astype(BF)
    R.DQ[:, 576:640] = jnp.zeros((512, 64), BF)
    for t in (1, 3, 4):
        j = order(t)

        @pl.when(jnp.logical_and(a + j >= 2, a + j < 10))
        def _():
            arrived(R.DKR.at[j], SEMS.dk, j, block_dev(a + j - 2))
            R.DKO[...] += R.DKR[j].astype(F32)

    R.DQ[:, 0:384] = R.DKO[...].astype(BF)

    settle(SEMS.qs)
    def input_part(k):
        rows = pl.ds(pl.multiple_of(128 * turn(u, k), 128), 128)
        return mm_nt(R.DQ[rows, :], R.W2[...])

    R.PS[3] = input_part(3).astype(BF)
    send(R.PS.at[3], R.XN, SEMS.x, 3, 3, there)
    R.PS[1] = input_part(1).astype(BF)
    send(R.PS.at[1], R.PR.at[1], SEMS.x, 1, 1, dev(near, s, c))

    d_qkv = R.DQ[...].astype(F32)
    sums = jnp.sum(d_qkv, axis=0, keepdims=True)
    sum_v = jnp.concatenate([sums[:, 128 * h + 64 : 128 * h + 128] for h in range(3)], axis=1)
    sum_q = sums[:, 384:576]

    def at_group(piece):
        return jnp.concatenate([jnp.where(u == g, piece, 0.0) for g in range(4)], axis=1)

    vec[0:1, :] = at_group(sum_q)
    vec[1:2, :] = at_group(sum_v)
    choose = jnp.where(
        rows_by((32, 24, 16), 1, (768, 16)) == lax.broadcasted_iota(jnp.int32, (768, 16), 1), 1.0, 0.0
    ).astype(BF)
    laid = jnp.where(owner == lane_owner, mm(choose, vec[...].astype(BF)), 0.0)
    laid = jnp.where(row_id == up_row, R.VUP[0:1, :], laid)
    R.T1[...] = R.XG[...].reshape(512, 768).T
    for n in range(5):
        lanes = slice(128 * n, 128 * n + 128)
        value = mm(R.T1[...], R.DQ[:, lanes])
        if n == 4:
            value = jnp.concatenate([value[:, 0:64], mm(laid.astype(BF), spread)], axis=1)
        R.G1[:, :, :, :, lanes] = value.reshape(4, 4, 2, 24, 128)
    send(R.G1.at[:, :, other], R.R1, SEMS.f1c, 0, 0, mate)

    R.PS[0] = input_part(0).astype(BF)
    R.H2[...] = input_part(2)
    arrived(R.R1, SEMS.f1c, 0, mate)
    for g in range(4):
        R.H1[g] = (R.G1[g, :, c] + R.R1[g]).astype(BF)
    for k in range(1, 4):
        to = turn(p, k)
        send(R.H1.at[:, to], R.R1P.at[p], SEMS.f1p, k, p, dev(u, to, c))
    arrived(R.XN, SEMS.x, 3, there)
    R.PS[2] = (R.H2[...] + R.XN[...].astype(F32)).astype(BF)
    send(R.PS.at[2], R.PR.at[2], SEMS.x, 2, 2, dev(across, s, c))
    send_if(far, R.PS.at[0], R.PR.at[0], SEMS.x, 0, 0, dev(u, s, c))

    @pl.when(jnp.logical_not(far))
    def _():
        R.PR[0] = R.PS[0]

    for k in range(1, 4):
        src = turn(p, k)
        arrived(R.ROP.at[src], SEMS.fop, src, dev(u, src, c))
    for g in range(4):
        total = R.GO[g, p, c] + R.RO[g, p]
        for k in range(1, 4):
            total = total + R.ROP[turn(p, k), g].astype(F32)
        R.TO[g] = total.astype(BF)
    for k in range(1, 4):
        to = turn(u, k)
        send(R.TO.at[to], R.ROZ.at[u], SEMS.foz, k, u, dev(to, p, c))
    arrived(R.RD2, SEMS.fdz, 1, dev(across, p, c))
    R.t_dn[...] = R.GD[u, c] + R.RD[u] + R.RD1[0].astype(F32) + R.RD2[...].astype(F32)
    arrived(R.RU2, SEMS.fuz, 1, dev(across, p, c))
    R.TU[...] = (R.GU[u, :, c] + R.RU[u] + R.RU1[0].astype(F32) + R.RU2[...].astype(F32)).astype(BF)
    R.RUP[p] = R.TU[p]
    for k in range(1, 4):
        to = turn(p, k)
        send(R.TU.at[to], R.RUP.at[p], SEMS.fup, k, p, dev(u, to, c))

    for k in range(1, 4):
        src = turn(p, k)
        arrived(R.R1P.at[src], SEMS.f1p, src, dev(u, src, c))
    total = R.G1[:, p, c] + R.R1[:, p]
    for k in range(1, 4):
        total = total + R.R1P[turn(p, k)].astype(F32)
    R.S1[...] = total.astype(BF)
    for k in range(1, 4):
        to = turn(u, k)
        send(R.S1.at[to], R.R1Z.at[u], SEMS.f1z, k, u, dev(to, p, c))
    R.R1Z[u] = R.S1[u]
    for k in range(1, 4):
        src = turn(u, k)
        arrived(R.ROZ.at[src], SEMS.foz, src, dev(src, p, c))
    total = R.TO[u].astype(F32)
    for k in range(1, 4):
        total = total + R.ROZ[turn(u, k)].astype(F32)
    R.t_ow[...] = total
    for k in range(1, 4):
        src = turn(p, k)
        arrived(R.RUP.at[src], SEMS.fup, src, dev(u, src, c))
    R.t_up[...] = R.RUP[...]
    for k in (1, 2):
        arrived(R.PR.at[k], SEMS.x, k, dev(turn(u, k), s, c))

    @pl.when(far)
    def _():
        arrived(R.PR.at[0], SEMS.x, 0, dev(u, s, c))

    total = R.DH1[...]
    for g in range(3):
        total = total + R.PR[g].astype(F32)
    R.t_in[...] = total
    for k in range(1, 4):
        src = turn(u, k)
        arrived(R.R1Z.at[src], SEMS.f1z, src, dev(src, p, c))
    R.t_qkv[...] = R.R1Z[...]
    settle()


def finish_kernel(*refs):
    R = Refs()
    for name, ref in zip([*RAW, *OUTS], refs, strict=True):
        setattr(R, name, ref)
    R.o_out[...] = R.t_out[...]
    R.o_in[...] = R.t_in[...]
    R.o_dnw[...] = R.t_dn[...]
    R.o_ow[...] = R.t_ow[...]
    for q in range(4):
        piece = R.t_up[q].astype(F32)
        for g in range(4):
            R.o_upw[:, 768 * g + 192 * q : 768 * g + 192 * q + 192] = piece[:, 192 * g : 192 * g + 192]
    small = jnp.zeros((24, 64), F32)
    for g in range(4):
        piece = R.t_qkv[g].astype(F32)
        at = 192 * g
        R.o_kw[:, at : at + 192] = jnp.concatenate([piece[:, 128 * h : 128 * h + 64] for h in range(3)], axis=1)
        R.o_vw[:, at : at + 192] = jnp.concatenate([piece[:, 128 * h + 64 : 128 * h + 128] for h in range(3)], axis=1)
        R.o_qw[:, at : at + 192] = piece[:, 384:576]
        small = small + piece[:, 576:640]
    for row, name in enumerate(SMALL):
        getattr(R, "o_" + name)[...] = small[row : row + 1, 0:24].reshape(24)
    R.o_upb[...] = jnp.concatenate([small[8 + i : 9 + i, 0:24] for i in range(4)], axis=1).reshape(96)


def fused_step(*args):
    vmem = pl.BlockSpec(memory_space=pltpu.VMEM)
    raw = pl.pallas_call(
        layer_kernel,
        out_shape=[jax.ShapeDtypeStruct(shape, dtype) for shape, dtype in RAW.values()],
        in_specs=[pl.BlockSpec(memory_space=pltpu.SMEM) if n == "starts" else vmem for n in ARGS],
        out_specs=[vmem] * len(RAW),
        scratch_shapes=[pltpu.VMEM(shape, dtype) for shape, dtype in SCRATCH.values()]
        + [pltpu.SemaphoreType.DMA((SEMS.total,))] * 2,
        compiler_params=pltpu.CompilerParams(
            collective_id=0, has_side_effects=True, vmem_limit_bytes=63 << 20
        ),
        name="layer_step",
    )(*args)
    return pl.pallas_call(
        finish_kernel,
        out_shape=[jax.ShapeDtypeStruct(shape, dtype) for shape, dtype in OUTS.values()],
        in_specs=[vmem] * len(RAW),
        out_specs=[vmem] * len(OUTS),
        name="finish",
    )(*raw)


def solution(mesh):
    fused = mesh.shape[ULYSSES] == 4 and mesh.shape[BLK] == 8
    return jax.shard_map(
        fused_step if fused else per_device,
        mesh=mesh,
        in_specs=(
            P(TOKEN_AXES, None),
            P(TOKEN_AXES, None),
            P(),
            P(WEIGHT_AXES, None),
            P(WEIGHT_AXES, None),
            P(WEIGHT_AXES, None),
            P(WEIGHT_AXES),
            P(WEIGHT_AXES),
            P(WEIGHT_AXES, None),
            P(WEIGHT_AXES),
            P(WEIGHT_AXES),
            P(WEIGHT_AXES),
            P(WEIGHT_AXES, None),
            P(WEIGHT_AXES),
            P(WEIGHT_AXES, None),
            P(WEIGHT_AXES),
            P(WEIGHT_AXES),
            P(WEIGHT_AXES),
        ),
        out_specs=(
            P(TOKEN_AXES, None),
            P(TOKEN_AXES, None),
            P(WEIGHT_AXES, None),
            P(WEIGHT_AXES, None),
            P(WEIGHT_AXES, None),
            P(WEIGHT_AXES),
            P(WEIGHT_AXES),
            P(WEIGHT_AXES, None),
            P(WEIGHT_AXES),
            P(WEIGHT_AXES),
            P(WEIGHT_AXES),
            P(WEIGHT_AXES, None),
            P(WEIGHT_AXES),
            P(WEIGHT_AXES, None),
            P(WEIGHT_AXES),
            P(WEIGHT_AXES),
            P(WEIGHT_AXES),
        ),
        check_vma=False,
    )
```

```python
import jax
import jax.numpy as jnp
from jax import lax
from jax.experimental import pallas as pl
from jax.experimental.pallas import tpu as pltpu
from jax.sharding import PartitionSpec as P

HD = 64
ULYSSES = "ulysses"
BLK = "blk"
WEIGHT_AXES = (ULYSSES, BLK)
TOKEN_AXES = (BLK, ULYSSES)


SCALE = 0.125
EPS = 1e-12


def passed_along(shard, axis, by):
    length = lax.axis_size(axis)
    return lax.ppermute(shard, axis, [(i, (i + by) % length) for i in range(length)])


def layer_norm(hidden, gain, shift):
    middle = jnp.mean(hidden, axis=-1, keepdims=True)
    centered = hidden - middle
    spread = jnp.mean(centered * centered, axis=-1, keepdims=True)
    return centered * lax.rsqrt(spread + EPS) * gain + shift


def gelu_exact(values):
    return jax.nn.gelu(values, approximate=False)


def doc_ids(doc_starts, positions):
    return jnp.sum((doc_starts[None, :] <= positions[:, None]).astype(jnp.int32), axis=1)


def project(left, right):
    return jnp.dot(left, right, preferred_element_type=jnp.float32)


def project_back(left, right):
    return lax.dot_general(
        left, right, (((1,), (1,)), ((), ())), preferred_element_type=jnp.float32
    )


def outer_sum(left, right):
    return lax.dot_general(
        left, right, (((0,), (0,)), ((), ())), preferred_element_type=jnp.float32
    )


def per_device(
    tokens,
    cotangent,
    doc_starts,
    q_weight,
    k_weight,
    v_weight,
    q_bias,
    v_bias,
    o_weight,
    o_bias,
    norm1_gain,
    norm1_bias,
    up_weight,
    up_bias,
    down_weight,
    down_bias,
    norm2_gain,
    norm2_bias,
):
    f32 = jnp.float32
    bf16 = jnp.bfloat16
    w_query, w_key, w_value, b_query, b_value, w_out, b_out, gain_one, shift_one = (
        lax.all_gather(q_weight, WEIGHT_AXES, axis=0, tiled=True),
        lax.all_gather(k_weight, WEIGHT_AXES, axis=0, tiled=True),
        lax.all_gather(v_weight, WEIGHT_AXES, axis=0, tiled=True),
        lax.all_gather(q_bias, WEIGHT_AXES, axis=0, tiled=True),
        lax.all_gather(v_bias, WEIGHT_AXES, axis=0, tiled=True),
        lax.all_gather(o_weight, WEIGHT_AXES, axis=0, tiled=True),
        lax.all_gather(o_bias, WEIGHT_AXES, axis=0, tiled=True),
        lax.all_gather(norm1_gain, WEIGHT_AXES, axis=0, tiled=True),
        lax.all_gather(norm1_bias, WEIGHT_AXES, axis=0, tiled=True),
    )
    w_up, b_up, w_down, b_down, gain_two, shift_two = (
        lax.all_gather(up_weight, WEIGHT_AXES, axis=0, tiled=True),
        lax.all_gather(up_bias, WEIGHT_AXES, axis=0, tiled=True),
        lax.all_gather(down_weight, WEIGHT_AXES, axis=0, tiled=True),
        lax.all_gather(down_bias, WEIGHT_AXES, axis=0, tiled=True),
        lax.all_gather(norm2_gain, WEIGHT_AXES, axis=0, tiled=True),
        lax.all_gather(norm2_bias, WEIGHT_AXES, axis=0, tiled=True),
    )
    query_tok = (project(tokens, w_query) + b_query.astype(f32)).astype(bf16)
    key_tok = project(tokens, w_key).astype(bf16)
    value_tok = (project(tokens, w_value) + b_value.astype(f32)).astype(bf16)
    query_heads, key_heads, value_heads = (
        lax.all_to_all(query_tok, ULYSSES, split_axis=1, concat_axis=0, tiled=True),
        lax.all_to_all(key_tok, ULYSSES, split_axis=1, concat_axis=0, tiled=True),
        lax.all_to_all(value_tok, ULYSSES, split_axis=1, concat_axis=0, tiled=True),
    )
    group = query_heads.shape[0]
    columns = query_heads.shape[1]
    local_heads = columns // HD
    block_count = lax.axis_size(BLK)
    total = group * block_count
    doc_max = min(8192, total // 4, 8 * group)
    reach = (group - 2 + doc_max) // group
    visits = 2 * reach + 1
    block_index = lax.axis_index(BLK)
    rows = jnp.arange(group, dtype=jnp.int32)
    query_ids = doc_ids(doc_starts, block_index * group + rows)
    query3 = query_heads.reshape(group, local_heads, HD)

    def block_mask(offset):
        key_pos = (block_index + offset) * group + rows
        inside = (key_pos >= 0) & (key_pos < total)
        key_ids = jnp.where(inside, doc_ids(doc_starts, key_pos), -1)
        allowed = query_ids[:, None] == key_ids[None, :]
        shared = (
            inside[0] & (key_ids[0] <= query_ids[group - 1]) & (key_ids[group - 1] >= query_ids[0])
        )
        return (allowed, shared)

    def exp_scores(pair, allowed):
        key3 = pair[0].reshape(group, local_heads, HD)
        scores = jnp.einsum("qhd,khd->hqk", query3, key3, preferred_element_type=f32) * SCALE
        return jnp.where(allowed[None], jnp.exp(scores), 0.0)

    def forward_terms(pair, offset):
        allowed, shared = block_mask(offset)
        weights = exp_scores(pair, allowed)
        value3 = pair[1].reshape(group, local_heads, HD)
        numer = jnp.einsum("hqk,khd->qhd", weights.astype(bf16), value3, preferred_element_type=f32)
        return (numer, jnp.sum(weights, axis=2))

    pair_own = jnp.stack([key_heads, value_heads])
    pair = passed_along(pair_own, BLK, -reach)
    numer, denom = forward_terms(pair, reach)
    store = jnp.zeros((1,), bf16)

    def forward_step(step, carry):
        pair_now, numer_now, denom_now, store_now = carry
        pair_now = passed_along(pair_now, BLK, 1)
        more_numer, more_denom = forward_terms(pair_now, reach - step)
        return (pair_now, numer_now + more_numer, denom_now + more_denom, store_now)

    pair, numer, denom, store = lax.fori_loop(1, visits, forward_step, (pair, numer, denom, store))
    attn_f = numer / jnp.transpose(denom)[:, :, None]
    attn_b = attn_f.reshape(group, columns).astype(bf16)
    attn_tok = lax.all_to_all(attn_b, ULYSSES, split_axis=0, concat_axis=1, tiled=True)
    token_f = tokens.astype(f32)
    h_one = token_f + project(attn_tok, w_out) + b_out.astype(f32)
    y_one, norm_one_back = jax.vjp(layer_norm, h_one, gain_one.astype(f32), shift_one.astype(f32))
    y_one_b = y_one.astype(bf16)
    pre_act = project(y_one_b, w_up) + b_up.astype(f32)
    act, gelu_back = jax.vjp(gelu_exact, pre_act)
    act_b = act.astype(bf16)
    h_two = y_one + project(act_b, w_down) + b_down.astype(f32)
    out_f, norm_two_back = jax.vjp(layer_norm, h_two, gain_two.astype(f32), shift_two.astype(f32))
    layer_out = out_f.astype(bf16)
    d_two, g_gain_two, g_shift_two = norm_two_back(cotangent.astype(f32))
    g_b_down = jnp.sum(d_two, axis=0)
    d_two_b = d_two.astype(bf16)
    g_w_down = outer_sum(act_b, d_two_b)
    d_act = project_back(d_two_b, w_down)
    d_pre = gelu_back(d_act)[0].astype(bf16)
    g_b_up = jnp.sum(d_pre.astype(f32), axis=0)
    g_w_up = outer_sum(y_one_b, d_pre)
    d_y_one = d_two + project_back(d_pre, w_up)
    d_one, g_gain_one, g_shift_one = norm_one_back(d_y_one)
    g_b_out = jnp.sum(d_one, axis=0)
    d_one_b = d_one.astype(bf16)
    g_w_out = outer_sum(attn_tok, d_one_b)
    d_attn_tok = project_back(d_one_b, w_out).astype(bf16)
    d_attn = lax.all_to_all(d_attn_tok, ULYSSES, split_axis=1, concat_axis=0, tiled=True)
    d_attn3 = d_attn.reshape(group, local_heads, HD)
    d_attn_f = d_attn3.astype(f32)
    delta = jnp.transpose(jnp.sum(d_attn_f * attn_f, axis=2))
    scaled_grad = d_attn_f / jnp.transpose(denom)[:, :, None]
    grad_high = scaled_grad.astype(bf16)
    grad_rest = (scaled_grad - grad_high.astype(f32)).astype(bf16)

    def backward_terms(pair_in, offset):
        allowed, shared = block_mask(offset)
        weights = exp_scores(pair_in, allowed)
        key3 = pair_in[0].reshape(group, local_heads, HD)
        value3 = pair_in[1].reshape(group, local_heads, HD)
        probs = weights / denom[:, :, None]
        d_prob = jnp.einsum("qhd,khd->hqk", d_attn3, value3, preferred_element_type=f32)
        d_score = (probs * (d_prob - delta[:, :, None]) * SCALE).astype(bf16)
        d_query = jnp.einsum("hqk,khd->qhd", d_score, key3, preferred_element_type=f32)
        d_key = jnp.einsum("hqk,qhd->khd", d_score, query3, preferred_element_type=f32)
        weights_low = weights.astype(bf16)
        d_value = jnp.einsum(
            "hqk,qhd->khd", weights_low, grad_high, preferred_element_type=f32
        ) + jnp.einsum("hqk,qhd->khd", weights_low, grad_rest, preferred_element_type=f32)
        return (d_query, jnp.stack([d_key, d_value]))

    pair = passed_along(pair_own, BLK, -reach)
    d_query_sum, carried = backward_terms(pair, reach)

    def backward_step(step, carry):
        pair_now, d_query_now, carried_now = carry
        pair_now = passed_along(pair_now, BLK, 1)
        more_query, more_kv = backward_terms(pair_now, reach - step)
        carried_now = (
            passed_along(carried_now.astype(jnp.bfloat16), BLK, 1).astype(carried_now.dtype)
            + more_kv
        )
        return (pair_now, d_query_now + more_query, carried_now)

    pair, d_query_sum, carried = lax.fori_loop(
        1, visits, backward_step, (pair, d_query_sum, carried)
    )
    own_grads = passed_along(carried.astype(jnp.bfloat16), BLK, -reach).astype(carried.dtype)
    d_query_b = d_query_sum.reshape(group, columns).astype(bf16)
    d_key_b = own_grads[0].reshape(group, columns).astype(bf16)
    d_value_b = own_grads[1].reshape(group, columns).astype(bf16)
    dq_tok, dk_tok, dv_tok = (
        lax.all_to_all(d_query_b, ULYSSES, split_axis=0, concat_axis=1, tiled=True),
        lax.all_to_all(d_key_b, ULYSSES, split_axis=0, concat_axis=1, tiled=True),
        lax.all_to_all(d_value_b, ULYSSES, split_axis=0, concat_axis=1, tiled=True),
    )
    g_b_query = jnp.sum(dq_tok.astype(f32), axis=0)
    g_b_value = jnp.sum(dv_tok.astype(f32), axis=0)
    g_w_query = outer_sum(tokens, dq_tok)
    g_w_key = outer_sum(tokens, dk_tok)
    g_w_value = outer_sum(tokens, dv_tok)
    input_grad = (
        d_one
        + project_back(dq_tok, w_query)
        + project_back(dk_tok, w_key)
        + project_back(dv_tok, w_value)
    )
    shares = (
        lax.psum_scatter(g_w_query, WEIGHT_AXES, scatter_dimension=0, tiled=True),
        lax.psum_scatter(g_w_key, WEIGHT_AXES, scatter_dimension=0, tiled=True),
        lax.psum_scatter(g_w_value, WEIGHT_AXES, scatter_dimension=0, tiled=True),
        lax.psum_scatter(g_b_query, WEIGHT_AXES, scatter_dimension=0, tiled=True),
        lax.psum_scatter(g_b_value, WEIGHT_AXES, scatter_dimension=0, tiled=True),
        lax.psum_scatter(g_w_out, WEIGHT_AXES, scatter_dimension=0, tiled=True),
        lax.psum_scatter(g_b_out, WEIGHT_AXES, scatter_dimension=0, tiled=True),
        lax.psum_scatter(g_gain_one, WEIGHT_AXES, scatter_dimension=0, tiled=True),
        lax.psum_scatter(g_shift_one, WEIGHT_AXES, scatter_dimension=0, tiled=True),
        lax.psum_scatter(g_w_up, WEIGHT_AXES, scatter_dimension=0, tiled=True),
        lax.psum_scatter(g_b_up, WEIGHT_AXES, scatter_dimension=0, tiled=True),
        lax.psum_scatter(g_w_down, WEIGHT_AXES, scatter_dimension=0, tiled=True),
        lax.psum_scatter(g_b_down, WEIGHT_AXES, scatter_dimension=0, tiled=True),
        lax.psum_scatter(g_gain_two, WEIGHT_AXES, scatter_dimension=0, tiled=True),
        lax.psum_scatter(g_shift_two, WEIGHT_AXES, scatter_dimension=0, tiled=True),
    )
    return (
        layer_out,
        input_grad,
        shares[0],
        shares[1],
        shares[2],
        shares[3],
        shares[4],
        shares[5],
        shares[6],
        shares[7],
        shares[8],
        shares[9],
        shares[10],
        shares[11],
        shares[12],
        shares[13],
        shares[14],
    )


MESH = pl.DeviceIdType.MESH
LOG2E = 1.4426950408889634
RSQRT2 = 0.7071067811865476
FWD_ROWS = 256
BWD_ROWS = 256
KEY_SENDS = 8
SEND_SLOTS = 64
PDF0 = 0.3989422804014327

ARGS = ("tok", "cot", "starts", "qw", "kw", "vw", "qb", "vb", "ow", "ob", "g1", "b1", "upw", "upb", "dnw", "dnb", "g2", "b2")
OUTS = dict(
    o_out=((128, 768), jnp.bfloat16),
    o_in=((128, 768), jnp.float32),
    o_qw=((24, 768), jnp.float32),
    o_kw=((24, 768), jnp.float32),
    o_vw=((24, 768), jnp.float32),
    o_qb=((24,), jnp.float32),
    o_vb=((24,), jnp.float32),
    o_ow=((24, 768), jnp.float32),
    o_ob=((24,), jnp.float32),
    o_g1=((24,), jnp.float32),
    o_b1=((24,), jnp.float32),
    o_upw=((24, 3072), jnp.float32),
    o_upb=((96,), jnp.float32),
    o_dnw=((96, 768), jnp.float32),
    o_dnb=((24,), jnp.float32),
    o_g2=((24,), jnp.float32),
    o_b2=((24,), jnp.float32),
)
RAW = dict(
    t_out=((128, 768), jnp.bfloat16),
    t_in=((128, 768), jnp.float32),
    t_qkv=((4, 24, 640), jnp.bfloat16),
    t_up=((4, 24, 768), jnp.bfloat16),
    t_dn=((96, 768), jnp.float32),
    t_ow=((24, 768), jnp.float32),
)
SMALL = ("qb", "vb", "ob", "g1", "b1", "dnb", "g2", "b2")
BF = jnp.bfloat16
F32 = jnp.float32
SCRATCH = dict(
    SM=((24, 128), F32),
    WS=((4, 24, 640), BF),
    W5=((4, 4, 2, 24, 640), BF),
    W2=((768, 640), BF),
    US=((4, 24, 768), BF),
    UP5=((4, 4, 2, 24, 768), BF),
    UP2=((768, 768), BF),
    DN4=((4, 2, 96, 768), BF),
    OW5=((4, 4, 2, 24, 768), BF),
    OW2=((768, 768), BF),
    XG=((4, 2, 64, 768), BF),
    KV=((5, 4, 128, 384), BF),
    KVT=((15, 144, 512), BF),
    QP=((3, 4, 128, 128), BF),
    GP=((3, 4, 128, 128), BF),
    SEGK=((5, 512, 128), BF),
    EL=((15, 512, 512), BF),
    DST=((512, 512), BF),
    NUM=((3, 80, 512), F32),
    DEN=((3, 8, 512), F32),
    ATN=((3, 64, 512), F32),
    DLT=((3, 8, 512), F32),
    AS=((4, 192, 128), BF),
    AT=((4, 192, 128), BF),
    Y1=((128, 768), F32),
    N1=((128, 768), F32),
    RSD=((128, 128), F32),
    YG=((4, 128, 768), BF),
    ACT=((4, 128, 768), BF),
    GG=((4, 128, 768), BF),
    PS=((4, 128, 768), BF),
    PR=((4, 128, 768), BF),
    XN=((128, 768), BF),
    H2=((128, 768), F32),
    DH2=((128, 768), F32),
    DG=((4, 128, 768), BF),
    DU=((4, 128, 768), BF),
    DH1=((128, 768), F32),
    DAS=((4, 192, 128), BF),
    DA=((4, 192, 128), BF),
    T1=((768, 512), BF),
    MR=((768, 64), F32),
    DKS=((5, 3, 512, 128), BF),
    DKX=((3, 512, 128), BF),
    DKR=((5, 3, 512, 128), BF),
    DKO=((3, 512, 128), F32),
    DQT=((3, 64, 512), F32),
    DQ=((512, 640), BF),
    VEC=((16, 768), F32),
    VUP=((8, 768), F32),
    G1=((4, 4, 2, 24, 640), F32),
    R1=((4, 4, 24, 640), F32),
    H1=((4, 4, 24, 640), BF),
    R1P=((4, 4, 24, 640), BF),
    S1=((4, 24, 640), BF),
    R1Z=((4, 24, 640), BF),
    GU=((4, 4, 2, 24, 768), F32),
    RU=((4, 4, 24, 768), F32),
    SU=((2, 4, 24, 768), BF),
    RU1=((2, 4, 24, 768), BF),
    SU2=((4, 24, 768), BF),
    RU2=((4, 24, 768), BF),
    TU=((4, 24, 768), BF),
    RUP=((4, 24, 768), BF),
    GD=((4, 2, 96, 768), F32),
    RD=((4, 96, 768), F32),
    SD=((2, 96, 768), BF),
    RD1=((2, 96, 768), BF),
    SD2=((96, 768), BF),
    RD2=((96, 768), BF),
    GO=((4, 4, 2, 24, 768), F32),
    RO=((4, 4, 24, 768), F32),
    SO=((4, 4, 24, 768), BF),
    ROP=((4, 4, 24, 768), BF),
    TO=((4, 24, 768), BF),
    ROZ=((4, 24, 768), BF),
)


class Slots:
    def __init__(self, **sizes):
        self.total = 0
        for name, size in sizes.items():
            setattr(self, name, self.total)
            self.total += size


SEMS = Slots(
    tok=6, hop=2, wz=3, wp=3, wc=1, us=3, upz=3, dnz=3, oz=3, op=3, cup=1, cdn=1, cow=1, kv=16, at=4,
    yg=3, ps=3, dg=3, qs=3, da=4, dk=5, dx=3, x=4, f1c=1, f1p=3, f1z=3, fuc=1, fuz=2, fup=3, fdc=1,
    fdz=2, foc=1, fop=3, foz=3,
)


def mm(left, right):
    return jnp.dot(left, right, preferred_element_type=F32)


def mm_nt(left, right):
    return lax.dot_general(left, right, (((1,), (1,)), ((), ())), preferred_element_type=F32)


def mm_tn(left, right):
    return lax.dot_general(left, right, (((0,), (0,)), ((), ())), preferred_element_type=F32)


def pack(rows):
    tail = rows[:, 128:192]
    return jnp.concatenate([rows[:, 0:128], jnp.concatenate([tail[0:64], tail[64:128]], axis=1)], axis=0)


def unpack(packed):
    tail = packed[128:192]
    tail = jnp.concatenate([tail[:, 0:64], tail[:, 64:128]], axis=0)
    return jnp.concatenate([packed[0:128], tail], axis=1)


def rows_by(shape, axis, flat):
    return lax.broadcasted_iota(jnp.int32, shape, axis).reshape(flat)


class Refs:
    pass


def layer_kernel(*refs):
    R = Refs()
    names = [*ARGS, *RAW, *SCRATCH, "SS", "RS"]
    for name, ref in zip(names, refs, strict=True):
        setattr(R, name, ref)
    u = lax.axis_index(ULYSSES)
    b = lax.axis_index(BLK)
    c = lax.rem(b, 2)
    p = lax.div(b, 2)
    other = 1 - c

    def snake(at):
        return at + lax.div(at, 2) * (1 - 2 * lax.rem(at, 2))

    s = snake(p)
    a = 2 * s + c
    far = p >= 2

    def dev(uu, pp, cc):
        return (uu, 2 * pp + cc)

    def block_dev(aa):
        return dev(u, snake(lax.div(aa, 2)), lax.rem(aa, 2))

    def turn(base, k):
        low, high = lax.rem(base, 2), lax.div(base, 2)
        if k % 2:
            low = 1 - low
        if k // 2:
            high = 1 - high
        return 2 * high + low

    sends = []
    free = list(range(KEY_SENDS, SEND_SLOTS))

    def copy(src, dst, slot, ri, device):
        return pltpu.make_async_remote_copy(
            src_ref=src, dst_ref=dst, send_sem=R.SS.at[slot], recv_sem=R.RS.at[ri],
            device_id=device, device_id_type=MESH,
        )

    def send(src, dst, name, ri, device, cond=None):
        slot = free.pop(0)
        desc = copy(src, dst, slot, name + ri, device)
        if cond is None:
            desc.start()
        else:

            @pl.when(cond)
            def _():
                desc.start()

        sends.append((name, cond, desc, slot))

    def send_if(cond, *what):
        send(*what, cond=cond)

    def key_slot(slot, sub):
        return 4 * (slot - lax.div(slot, 3)) + sub

    def settle(*wanted):
        for entry in list(sends):
            name, cond, desc, slot = entry
            if wanted and name not in wanted:
                continue
            sends.remove(entry)
            free.append(slot)
            if cond is None:
                desc.wait_send()
            else:

                @pl.when(cond)
                def _():
                    desc.wait_send()

    def arrived(dst, name, ri, device):
        copy(dst, dst, 0, name + ri, device).wait_recv()

    barrier = pltpu.get_barrier_semaphore()

    def greet(device):
        pl.semaphore_signal(barrier, inc=1, device_id=device, device_id_type=MESH)

    for k in range(1, 8):
        greet((u, lax.rem(b + k, 8)))
    for k in range(1, 4):
        greet((turn(u, k), b))

    @pl.when(far)
    def _():
        for k in range(1, 4):
            greet(dev(turn(u, k), s, c))

    R.SM[...] = jnp.zeros_like(R.SM)
    for row, name in enumerate(SMALL):
        R.SM[row : row + 1, 0:24] = getattr(R, name)[...].astype(F32).reshape(1, 24)
    up_bias = R.upb[...].astype(F32).reshape(1, 96)
    for i in range(4):
        R.SM[8 + i : 9 + i, 0:24] = up_bias[:, 24 * i : 24 * i + 24]
    small = R.SM[:, 0:64].astype(BF)
    qw, kw, vw = R.qw[...], R.kw[...], R.vw[...]
    for g in range(4):
        parts = []
        for h in range(3):
            at = 64 * (3 * g + h)
            parts += [kw[:, at : at + 64], vw[:, at : at + 64]]
        for h in range(3):
            at = 64 * (3 * g + h)
            parts.append(qw[:, at : at + 64])
        parts.append(small)
        R.WS[g] = jnp.concatenate(parts, axis=1)

    pl.semaphore_wait(barrier, 10 + 3 * lax.div(p, 2))

    for k in range(1, 4):
        to = turn(u, k)
        send(R.WS.at[to], R.W5.at[u, p, c], SEMS.wz, k - 1, dev(to, p, c))
    R.W5[u, p, c] = R.WS[u]
    halves = (slice(0, 64), slice(64, 128))
    for i in range(2):
        send_if(far, R.tok.at[halves[i]], R.XG.at[u, i], SEMS.hop, i, dev(u, s, c))

    @pl.when(jnp.logical_not(far))
    def _():
        for i in range(2):
            R.XG[u, i] = R.tok[halves[i], :]

    near, across = turn(u, 1), turn(u, 2)
    there = dev(near, p, c)
    for i in range(2):
        for k in (2, 1):
            send_if(
                jnp.logical_not(far),
                R.tok.at[halves[i]], R.XG.at[u, i], SEMS.tok, 2 * (k - 1) + i, dev(turn(u, k), p, c),
            )

    up = R.upw[...]
    for q in range(4):
        R.US[q] = jnp.concatenate(
            [up[:, 768 * g + 192 * q : 768 * g + 192 * q + 192] for g in range(4)], axis=1
        )
    for k in range(1, 4):
        to = turn(p, k)
        send(R.US.at[to], R.UP5.at[u, p, c], SEMS.us, k - 1, dev(u, to, c))
    R.UP5[u, p, c] = R.US[p]
    R.DN4[u, c] = R.dnw[...]
    R.OW5[u, p, c] = R.ow[...]

    mate = dev(u, p, other)
    row_pos = lax.broadcasted_iota(jnp.int32, (512, 128), 0)
    n_starts = R.starts.shape[0]

    def id_body(j, carry):
        pos = row_pos + (a + j - 2) * 512
        ids = jnp.zeros((512, 128), jnp.int32)
        for i in range(n_starts):
            ids = ids + jnp.where(pos >= R.starts[i], 1, 0)
        R.SEGK[j] = ids.astype(F32).astype(BF)
        return carry

    lax.fori_loop(0, 5, id_body, 0)
    q_pos = lax.broadcasted_iota(jnp.int32, (1, 512), 1) + a * 512
    q_ids = jnp.zeros((1, 512), jnp.int32)
    for i in range(n_starts):
        q_ids = q_ids + jnp.where(q_pos >= R.starts[i], 1, 0)
    q_ids = jnp.broadcast_to(q_ids.astype(F32), (FWD_ROWS, 512)).astype(BF)
    R.KVT[:, 128:144, :] = jnp.ones((15, 16, 512), BF)
    for ref in (R.QP, R.GP, R.NUM, R.DQT):
        ref[...] = jnp.zeros_like(ref)

    for i in range(2):

        @pl.when(far)
        def _():
            arrived(R.XG.at[u, i], SEMS.hop, i, dev(u, s, c))

        for k in (2, 1):
            send_if(
                far,
                R.XG.at[u, i], R.XG.at[u, i], SEMS.tok, 2 * (k - 1) + i, dev(turn(u, k), p, c),
            )
    for k in range(1, 4):
        src = turn(u, k)
        arrived(R.W5.at[src, p, c], SEMS.wz, k - 1, dev(src, p, c))
    for k in range(1, 4):
        to = turn(p, k)
        send(R.W5.at[:, p, c], R.W5.at[:, p, c], SEMS.wp, k - 1, dev(u, to, c))
    def pass_tokens(i):
        arrived(R.XG.at[across, i], SEMS.tok, 2 + i, dev(across, p, c))
        send(R.XG.at[across, i], R.XG.at[across, i], SEMS.tok, 4 + i, there)

    pass_tokens(0)
    for k in range(1, 4):
        src = turn(p, k)
        arrived(R.W5.at[:, src, c], SEMS.wp, k - 1, dev(u, src, c))
    send(R.W5.at[:, :, c], R.W5.at[:, :, c], SEMS.wc, 0, dev(u, p, other))
    pass_tokens(1)
    for k in range(1, 4):
        to = turn(u, k)
        send(R.ow, R.OW5.at[u, p, c], SEMS.oz, k - 1, dev(to, p, c))
    send(R.dnw, R.DN4.at[u, c], SEMS.dnz, 0, dev(across, p, c))
    for k in range(1, 4):
        src = turn(p, k)
        arrived(R.UP5.at[u, src, c], SEMS.us, k - 1, dev(u, src, c))
    send(R.UP5.at[u, :, c], R.UP5.at[u, :, c], SEMS.upz, 0, dev(across, p, c))
    arrived(R.W5.at[:, :, other], SEMS.wc, 0, dev(u, p, other))
    R.W2[...] = R.W5[...].reshape(768, 640)

    spread = jnp.where(
        rows_by((32, 24, 64), 1, (768, 64)) == lax.broadcasted_iota(jnp.int32, (768, 64), 1), 1.0, 0.0
    ).astype(BF)
    owner = rows_by((32, 24, 768), 0, (768, 768))
    lane = lax.broadcasted_iota(jnp.int32, (1, 768), 1)
    lane_owner = jnp.zeros((1, 768), jnp.int32)
    for i in range(1, 32):
        lane_owner = lane_owner + jnp.where(lane >= 24 * i, 1, 0)
    lane_g = jnp.where(lane >= 192, 1, 0) + jnp.where(lane >= 384, 1, 0) + jnp.where(lane >= 576, 1, 0)
    rest = lane - 192 * lane_g
    lane_c = jnp.where(rest >= 96, 1, 0)
    rest = rest - 96 * lane_c
    lane_r = jnp.where(rest >= 24, 1, 0) + jnp.where(rest >= 48, 1, 0) + jnp.where(rest >= 72, 1, 0)
    up_row = 24 * (8 * lane_g + 2 * p + lane_c) + 8 + lane_r
    row_id = lax.broadcasted_iota(jnp.int32, (768, 768), 0)
    wide = mm_nt(R.W2[:, 576:640], spread)
    mine = jnp.where(owner == lane_owner, wide, 0.0).astype(BF)
    pick = jnp.where(
        lax.broadcasted_iota(jnp.int32, (16, 768), 1) - 24 * lane_owner
        == lax.broadcasted_iota(jnp.int32, (16, 768), 0), 1.0, 0.0
    ).astype(BF)
    R.VEC[...] = mm(pick, mine)
    R.VUP[0:1, :] = jnp.sum(jnp.where(row_id == up_row, wide, 0.0), axis=0, keepdims=True)

    def group_slice(vector):
        out = vector[:, 0:192]
        for g in range(1, 4):
            out = jnp.where(u == g, vector[:, 192 * g : 192 * g + 192], out)
        return out

    qb = group_slice(R.VEC[0:1, :])
    vb = group_slice(R.VEC[1:2, :])
    zero64 = jnp.zeros((1, 64), F32)
    bias = []
    for h in range(3):
        bias += [zero64, vb[:, 64 * h : 64 * h + 64]]
    bias = jnp.concatenate(bias + [qb, zero64], axis=1)

    for k in range(4):
        src = turn(u, k)
        if k > 0:
            for i in range(2):
                if k != 2:
                    arrived(R.XG.at[src, i], SEMS.tok, 2 * (k - 1) + i, there)
        proj = mm(R.XG[src].reshape(128, 768), R.W2[...]) + bias
        R.KV[2, src] = proj[:, 0:384].astype(BF)
        query = proj[:, 384:576].astype(BF) * BF(0.125)
        for h in range(3):
            R.QP[h, src, :, 0:64] = query[:, 64 * h : 64 * h + 64]
        slot = 1 + 2 * c
        send(R.KV.at[2, src], R.KV.at[slot, src], SEMS.kv, key_slot(slot, src), mate)
        for i, step in enumerate((-2, 2)):
            to = a + step
            ok = jnp.logical_and(to >= 0, to < 8)
            slot = 2 - step
            send_if(
                ok, R.KV.at[2, src], R.KV.at[slot, src], SEMS.kv, key_slot(slot, src), block_dev(to)
            )

    def order(t):
        return 2 + (1 - 2 * c) * ((t + 1) // 2) * (1 - 2 * ((t + 1) % 2))

    def forward_block(t):
        j = order(t)
        ok = jnp.logical_and(a + j >= 2, a + j < 10)

        @pl.when(ok)
        def _():
            if t == 1 or t == 2:
                for r in range(4):
                    arrived(R.KV.at[j, r], SEMS.kv, key_slot(j, r), mate)
            if t == 4:
                for r in range(4):
                    arrived(R.KV.at[j, r], SEMS.kv, key_slot(j, r), block_dev(a + j - 2))

            def head(h, inner):
                lanes = pl.ds(pl.multiple_of(128 * h, 128), 128)
                kv = R.KV[j, :, :, lanes].reshape(512, 128)
                at = 3 * j + h
                R.KVT[at, 0:128, :] = kv.T
                query = R.QP[h].reshape(512, 128)
                for r in range(512 // FWD_ROWS):
                    rows = slice(FWD_ROWS * r, FWD_ROWS * r + FWD_ROWS)
                    score = mm_nt(kv[rows], query)
                    ids = R.SEGK[j, rows, :]
                    same = jnp.concatenate([ids] * 4, axis=1) == q_ids
                    weight = jnp.exp2(score * LOG2E).astype(BF)
                    R.EL[at, rows, :] = jnp.where(same, weight, jnp.zeros_like(weight))
                R.NUM[h] += mm(R.KVT[at, 64:144, :], R.EL[at])
                return inner

            lax.fori_loop(0, 3, head, 0)

    def relay_out():
        for k in range(1, 4):
            src = turn(u, k)
            arrived(R.OW5.at[src, p, c], SEMS.oz, k - 1, dev(src, p, c))
        for k in range(1, 4):
            to = turn(p, k)
            send(R.OW5.at[:, p, c], R.OW5.at[:, p, c], SEMS.op, k - 1, dev(u, to, c))

    def share_keys():
        j = order(3)
        ok = jnp.logical_and(a + j >= 2, a + j < 10)
        slot = 1 + 2 * (1 - c)
        for r in range(4):

            @pl.when(ok)
            def _():
                arrived(R.KV.at[j, r], SEMS.kv, key_slot(j, r), block_dev(a + j - 2))

            send_if(ok, R.KV.at[j, r], R.KV.at[slot, r], SEMS.kv, key_slot(slot, r), mate)

    def relay_down():
        arrived(R.DN4.at[across, c], SEMS.dnz, 0, dev(across, p, c))
        for i, src in enumerate((u, across)):
            send(R.DN4.at[src, c], R.DN4.at[src, c], SEMS.dnz, 1 + i, there)

    def relay_up():
        arrived(R.UP5.at[across, :, c], SEMS.upz, 0, dev(across, p, c))
        for i, src in enumerate((u, across)):
            send(R.UP5.at[src, :, c], R.UP5.at[src, :, c], SEMS.upz, 1 + i, there)

    forward_block(0)
    relay_out()
    forward_block(1)
    share_keys()
    forward_block(3)
    relay_down()
    forward_block(2)
    forward_block(4)

    heads = []
    for h in range(3):
        R.DEN[h, 0:1, :] = R.NUM[h, 64:65, :]
        attn = R.NUM[h, 0:64, :] / R.DEN[h, 0:1, :]
        R.ATN[h] = attn
        heads.append(attn.T.astype(BF))
    for r in range(4):
        rows = slice(128 * r, 128 * r + 128)
        R.AS[r] = pack(jnp.concatenate([part[rows] for part in heads], axis=1))
    for k in range(1, 4):
        to = turn(u, k)
        send(R.AS.at[to], R.AT.at[u], SEMS.at, k, dev(to, s, c))
    send_if(far, R.AS.at[u], R.AT.at[u], SEMS.at, 0, dev(u, s, c))

    @pl.when(jnp.logical_not(far))
    def _():
        R.AT[u] = R.AS[u]

    relay_up()
    settle(SEMS.tok, SEMS.hop, SEMS.wz, SEMS.wp, SEMS.wc, SEMS.us, SEMS.oz)
    for k in range(1, 4):
        src = turn(p, k)
        arrived(R.OW5.at[:, src, c], SEMS.op, k - 1, dev(u, src, c))
    send(R.OW5.at[:, :, c], R.OW5.at[:, :, c], SEMS.cow, 0, mate)
    arrived(R.OW5.at[:, :, other], SEMS.cow, 0, mate)
    R.OW2[...] = R.OW5[...].reshape(768, 768)

    def wait_column(ref, name):
        for k in range(1, 4):
            src = turn(u, k)
            arrived(ref.at[src], name, k, dev(src, s, c))

        @pl.when(far)
        def _():
            arrived(ref.at[u], name, 0, dev(u, s, c))

    wait_column(R.AT, SEMS.at)
    hidden = R.tok[...].astype(F32) + R.VEC[2:3, :]
    for g in range(4):
        hidden = hidden + mm(unpack(R.AT[g]), R.OW2[192 * g : 192 * g + 192, :])
    middle = jnp.mean(hidden, axis=-1, keepdims=True)
    hidden = hidden - middle
    rstd = lax.rsqrt(jnp.mean(hidden * hidden, axis=-1, keepdims=True) + EPS)
    normed = hidden * rstd
    R.N1[...] = normed
    R.RSD[...] = jnp.broadcast_to(rstd, (128, 128))
    y_one = normed * R.VEC[3:4, :] + R.VEC[4:5, :]
    R.Y1[...] = y_one

    def gather_plane(ref, value, name):
        ref[p] = value
        for k in range(1, 4):
            send(ref.at[p], ref.at[p], name, k - 1, dev(u, turn(p, k), c))

    gather_plane(R.YG, y_one.astype(BF), SEMS.yg)
    settle(SEMS.kv)
    for i, src in enumerate((near, turn(near, 2))):
        arrived(R.DN4.at[src, c], SEMS.dnz, 1 + i, there)
    send(R.DN4.at[:, c], R.DN4.at[:, c], SEMS.cdn, 0, mate)
    for i, src in enumerate((near, turn(near, 2))):
        arrived(R.UP5.at[src, :, c], SEMS.upz, 1 + i, there)
    send(R.UP5.at[:, :, c], R.UP5.at[:, :, c], SEMS.cup, 0, mate)
    arrived(R.DN4.at[:, other], SEMS.cdn, 0, mate)
    arrived(R.UP5.at[:, :, other], SEMS.cup, 0, mate)
    R.UP2[...] = R.UP5[...].reshape(768, 768)
    for k in range(4):
        at = turn(p, k)
        if k > 0:
            arrived(R.YG.at[at], SEMS.yg, k - 1, dev(u, at, c))
        pre = mm(R.YG[at], R.UP2[...]) + R.VUP[0:1, :]
        phi = 0.5 * (1.0 + lax.erf(pre * RSQRT2))
        R.GG[at] = (phi + pre * (PDF0 * jnp.exp(-0.5 * pre * pre))).astype(BF)
        act = (pre * phi).astype(BF)
        R.ACT[at] = act
        part = mm(act, R.DN4[...].reshape(768, 768))
        if k == 0:
            R.H2[...] = part
        else:
            R.PS[at] = part.astype(BF)
            send(R.PS.at[at], R.PR.at[p], SEMS.ps, k - 1, dev(u, at, c))
    hidden = R.Y1[...] + R.H2[...] + R.VEC[5:6, :]
    for k in range(1, 4):
        at = turn(p, k)
        arrived(R.PR.at[at], SEMS.ps, k - 1, dev(u, at, c))
        hidden = hidden + R.PR[at].astype(F32)

    middle = jnp.mean(hidden, axis=-1, keepdims=True)
    hidden = hidden - middle
    rstd = lax.rsqrt(jnp.mean(hidden * hidden, axis=-1, keepdims=True) + EPS)
    normed = hidden * rstd
    gain = R.VEC[6:7, :]
    R.t_out[...] = (normed * gain + R.VEC[7:8, :]).astype(BF)
    grad = R.cot[...].astype(F32)
    cg = grad * gain
    d_two = (
        cg - jnp.mean(cg, axis=-1, keepdims=True) - normed * jnp.mean(cg * normed, axis=-1, keepdims=True)
    ) * rstd
    gather_plane(R.DG, d_two.astype(BF), SEMS.dg)
    R.DH2[...] = d_two
    g_gain_two = jnp.sum(grad * normed, axis=0, keepdims=True)
    g_shift_two = jnp.sum(grad, axis=0, keepdims=True)
    g_b_down = jnp.sum(d_two, axis=0, keepdims=True)

    settle()
    g_b_up = jnp.zeros((1, 768), F32)
    for k in range(4):
        at = turn(p, k)
        if k > 0:
            arrived(R.DG.at[at], SEMS.dg, k - 1, dev(u, at, c))
        d_act = mm_nt(R.DG[at], R.DN4[...].reshape(768, 768))
        d_pre = (d_act * R.GG[at].astype(F32)).astype(BF)
        R.DU[at] = d_pre
        g_b_up = g_b_up + jnp.sum(d_pre.astype(F32), axis=0, keepdims=True)
        part = mm_nt(d_pre, R.UP2[...])
        if k == 0:
            R.H2[...] = part
        else:
            R.PS[at] = part.astype(BF)
            send(R.PS.at[at], R.PR.at[p], SEMS.qs, k - 1, dev(u, at, c))
    def wide_grad(left, right_ref, put):
        R.T1[...] = left.T

        def body(n, carry):
            lanes = pl.ds(pl.multiple_of(256 * n, 256), 256)
            put(lanes, mm(R.T1[...], right_ref[:, :, lanes].reshape(512, 256)))
            return carry

        lax.fori_loop(0, 3, body, 0)

    def put_down(lanes, value):
        R.GD[:, :, :, lanes] = value.reshape(4, 2, 96, 256)

    def put_up(lanes, value):
        R.GU[:, :, :, :, lanes] = value.reshape(4, 4, 2, 24, 256)

    wide_grad(R.ACT[...].reshape(512, 768), R.DG, put_down)
    send(R.GD.at[:, other], R.RD, SEMS.fdc, 0, mate)
    wide_grad(R.YG[...].reshape(512, 768), R.DU, put_up)
    send(R.GU.at[:, :, other], R.RU, SEMS.fuc, 0, mate)
    arrived(R.RD, SEMS.fdc, 0, mate)
    for i, g in enumerate((near, turn(near, 2))):
        R.SD[i] = (R.GD[g, c] + R.RD[g]).astype(BF)
    send(R.SD, R.RD1, SEMS.fdz, 0, there)
    d_y = R.DH2[...] + R.H2[...]
    for k in range(1, 4):
        at = turn(p, k)
        arrived(R.PR.at[at], SEMS.qs, k - 1, dev(u, at, c))
        d_y = d_y + R.PR[at].astype(F32)

    normed = R.N1[...]
    cg = d_y * R.VEC[3:4, :]
    d_one = (
        cg - jnp.mean(cg, axis=-1, keepdims=True) - normed * jnp.mean(cg * normed, axis=-1, keepdims=True)
    ) * R.RSD[:, 0:1]
    R.DH1[...] = d_one
    d_one_low = d_one.astype(BF)
    for k in range(4):
        to = turn(u, (k + 1) % 4)
        w_rows = R.OW2[pl.ds(pl.multiple_of(192 * to, 64), 192), :]
        R.DAS[to] = pack(mm_nt(d_one_low, w_rows).astype(BF))
        if k < 3:
            send(R.DAS.at[to], R.DA.at[u], SEMS.da, k + 1, dev(to, s, c))
    send_if(far, R.DAS.at[u], R.DA.at[u], SEMS.da, 0, dev(u, s, c))

    @pl.when(jnp.logical_not(far))
    def _():
        R.DA[u] = R.DAS[u]

    vec = R.VEC
    vec[2:3, :] = jnp.sum(d_one, axis=0, keepdims=True)
    vec[3:4, :] = jnp.sum(d_y * normed, axis=0, keepdims=True)
    vec[4:5, :] = jnp.sum(d_y, axis=0, keepdims=True)
    vec[5:6, :] = g_b_down
    vec[6:7, :] = g_gain_two
    vec[7:8, :] = g_shift_two
    vec[8:16, :] = jnp.zeros((8, 768), F32)
    R.VUP[0:1, :] = g_b_up

    for g in range(4):
        R.GO[g] = mm_tn(unpack(R.AT[g]), d_one_low).reshape(4, 2, 24, 768)
    send(R.GO.at[:, :, other], R.RO, SEMS.foc, 0, mate)

    arrived(R.RU, SEMS.fuc, 0, mate)
    for i, g in enumerate((near, turn(near, 2))):
        R.SU[i] = (R.GU[g, :, c] + R.RU[g]).astype(BF)
    send(R.SU, R.RU1, SEMS.fuz, 0, there)

    def relay_down_grad():
        arrived(R.RD1, SEMS.fdz, 0, there)
        R.SD2[...] = (R.GD[across, c] + R.RD[across] + R.RD1[1].astype(F32)).astype(BF)
        send(R.SD2, R.RD2, SEMS.fdz, 1, dev(across, p, c))

    def relay_up_grad():
        arrived(R.RU1, SEMS.fuz, 0, there)
        R.SU2[...] = (R.GU[across, :, c] + R.RU[across] + R.RU1[1].astype(F32)).astype(BF)
        send(R.SU2, R.RU2, SEMS.fuz, 1, dev(across, p, c))

    arrived(R.RO, SEMS.foc, 0, mate)
    for g in range(4):
        R.SO[g] = (R.GO[g, :, c] + R.RO[g]).astype(BF)
    for k in range(1, 4):
        to = turn(p, k)
        send(R.SO.at[:, to], R.ROP.at[p], SEMS.fop, k - 1, dev(u, to, c))
    vec[0:2, :] = jnp.zeros((2, 768), F32)
    choose = jnp.where(
        rows_by((32, 24, 16), 1, (768, 16)) == lax.broadcasted_iota(jnp.int32, (768, 16), 1), 1.0, 0.0
    ).astype(BF)
    laid = jnp.where(owner == lane_owner, mm(choose, vec[...].astype(BF)), 0.0)
    laid = jnp.where(row_id == up_row, R.VUP[0:1, :], laid)
    R.MR[...] = mm(laid.astype(BF), spread)
    R.T1[...] = R.XG[...].reshape(512, 768).T
    wait_column(R.DA, SEMS.da)
    d_rows = jnp.concatenate([unpack(R.DA[r]) for r in range(4)], axis=0).astype(F32)
    for h in range(3):
        d_attn = d_rows[:, 64 * h : 64 * h + 64].T
        scaled = (d_attn / R.DEN[h, 0:1, :]).astype(BF)
        R.DLT[h, 0:1, :] = jnp.sum(scaled.astype(F32) * R.ATN[h], axis=0, keepdims=True)
        R.GP[h, :, :, 64:128] = scaled.T.reshape(4, 128, 64)

    def block_copy(t):
        j = order(t)
        there_slot = 0 if t == 1 else 1
        return copy(
            R.DKS.at[j], R.DKR.at[4 - j], there_slot, SEMS.dk + there_slot, block_dev(a + j - 2)
        )

    def key_copy(t, h):
        j = order(t)
        if t == 2:
            return copy(R.DKS.at[j, h], R.DKX.at[h], 2 + h, SEMS.dx + h, mate)
        return copy(
            R.DKS.at[j, h], R.DKR.at[4 - j, h], 5 + h, SEMS.dk + 2 + h, block_dev(a + j - 2)
        )

    def backward_block(t):
        j = order(t)
        ok = jnp.logical_and(a + j >= 2, a + j < 10)

        @pl.when(ok)
        def _():
            def head(h, inner):
                lanes = pl.ds(pl.multiple_of(128 * h, 128), 128)
                at = 3 * j + h
                grad_rows = R.GP[h].reshape(512, 128)
                shift = R.DLT[h, 0:1, :]
                kv = R.KV[j, :, :, lanes].reshape(512, 128)
                for r in range(512 // BWD_ROWS):
                    rows = slice(BWD_ROWS * r, BWD_ROWS * r + BWD_ROWS)
                    d_prob = mm_nt(kv[rows], grad_rows)
                    R.DST[rows, :] = (R.EL[at, rows, :].astype(F32) * (d_prob - shift)).astype(BF)
                d_kv = mm(R.DST[...], R.QP[h].reshape(512, 128)) + mm(R.EL[at], grad_rows)
                if t == 0:
                    R.DKO[h] = d_kv
                elif t == 3:
                    arrived(R.DKX.at[h], SEMS.dx, h, mate)
                    R.DKS[j, h] = (d_kv + R.DKX[h].astype(F32)).astype(BF)
                else:
                    R.DKS[j, h] = d_kv.astype(BF)
                if t == 2 or t == 3:
                    key_copy(t, h).start()
                R.DQT[h] += mm(R.KVT[at, 0:64, :], R.DST[...])
                return inner

            lax.fori_loop(0, 3, head, 0)
            if t == 4 or t == 1:
                block_copy(t).start()

    backward_block(4)
    relay_down_grad()
    backward_block(2)
    backward_block(3)
    backward_block(1)
    relay_up_grad()
    backward_block(0)

    def at_lanes(n, value):
        R.G1[:, :, :, :, 128 * n : 128 * n + 128] = value.reshape(4, 4, 2, 24, 128)

    def query_grads():
        for n in (3, 4):
            value = mm(R.T1[...], R.DQ[:, 128 * n : 128 * n + 128])
            if n == 4:
                value = jnp.concatenate([value[:, 0:64], R.MR[...]], axis=1)
            at_lanes(n, value)

    def key_grads():
        for n in range(3):
            at_lanes(n, mm(R.T1[...], R.DQ[:, 128 * n : 128 * n + 128]))
        sums = mm(jnp.ones((8, 512), BF), R.DQ[...])[0:1]
        sum_v = jnp.concatenate([sums[:, 128 * h + 64 : 128 * h + 128] for h in range(3)], axis=1)
        row = lax.broadcasted_iota(jnp.int32, (192, 192), 0)
        lane_row = 24 * lane_owner[:, 0:192]
        laid = jnp.where(row == lane_row, sums[:, 384:576], jnp.where(row == lane_row + 1, sum_v, 0.0))
        extra = mm(laid.astype(BF), spread[0:192])
        extra = jnp.concatenate([jnp.zeros((192, 64), F32), extra], axis=1)
        R.G1[u, :, :, :, 512:640] += extra.reshape(4, 2, 24, 128)
        send(R.G1.at[:, :, other], R.R1, SEMS.f1c, 0, mate)

    for h in range(3):
        R.DQ[:, 384 + 64 * h : 448 + 64 * h] = (R.DQT[h] * 0.125).T.astype(BF)
    R.DQ[:, 576:640] = jnp.zeros((512, 64), BF)
    query_grads()
    for t in (1, 3, 4):
        j = order(t)

        @pl.when(jnp.logical_and(a + j >= 2, a + j < 10))
        def _():
            if t != 4:
                arrived(R.DKR.at[j], SEMS.dk, 0 if t == 1 else 1, block_dev(a + j - 2))
            for h in range(3):
                if t == 4:
                    arrived(R.DKR.at[j, h], SEMS.dk, 2 + h, block_dev(a + j - 2))
                R.DKO[h] += R.DKR[j, h].astype(F32)

    for h in range(3):
        R.DQ[:, 128 * h : 128 * h + 128] = R.DKO[h].astype(BF)
    key_grads()

    settle(SEMS.qs)
    def input_part(k):
        rows = pl.ds(pl.multiple_of(128 * turn(u, k), 128), 128)
        return mm_nt(R.DQ[rows, :], R.W2[...])

    R.PS[3] = input_part(3).astype(BF)
    send(R.PS.at[3], R.XN, SEMS.x, 3, there)
    R.PS[1] = input_part(1).astype(BF)
    send(R.PS.at[1], R.PR.at[1], SEMS.x, 1, there)
    R.Y1[...] = input_part(0)
    R.H2[...] = input_part(2)
    arrived(R.R1, SEMS.f1c, 0, mate)
    for g in range(4):
        R.H1[g] = (R.G1[g, :, c] + R.R1[g]).astype(BF)
    for k in range(1, 4):
        to = turn(p, k)
        send(R.H1.at[:, to], R.R1P.at[p], SEMS.f1p, k - 1, dev(u, to, c))
    arrived(R.RD2, SEMS.fdz, 1, dev(across, p, c))
    R.t_dn[...] = R.GD[u, c] + R.RD[u] + R.RD1[0].astype(F32) + R.RD2[...].astype(F32)
    arrived(R.RU2, SEMS.fuz, 1, dev(across, p, c))
    R.TU[...] = (R.GU[u, :, c] + R.RU[u] + R.RU1[0].astype(F32) + R.RU2[...].astype(F32)).astype(BF)
    R.RUP[p] = R.TU[p]
    for k in range(1, 4):
        to = turn(p, k)
        send(R.TU.at[to], R.RUP.at[p], SEMS.fup, k - 1, dev(u, to, c))

    arrived(R.XN, SEMS.x, 3, there)
    R.PS[2] = (R.H2[...] + R.XN[...].astype(F32)).astype(BF)
    send(R.PS.at[2], R.PR.at[2], SEMS.x, 2, dev(across, s, c))
    for k in range(1, 4):
        src = turn(p, k)
        arrived(R.ROP.at[src], SEMS.fop, k - 1, dev(u, src, c))
    for g in range(4):
        total = R.GO[g, p, c] + R.RO[g, p]
        for k in range(1, 4):
            total = total + R.ROP[turn(p, k), g].astype(F32)
        R.TO[g] = total.astype(BF)
    for k in range(1, 4):
        to = turn(u, k)
        send(R.TO.at[to], R.ROZ.at[u], SEMS.foz, k - 1, dev(to, p, c))
    arrived(R.PR.at[1], SEMS.x, 1, there)
    R.Y1[...] += R.PR[1].astype(F32)

    @pl.when(far)
    def _():
        R.PS[0] = R.Y1[...].astype(BF)

    send_if(far, R.PS.at[0], R.PR.at[0], SEMS.x, 0, dev(u, s, c))
    for k in range(1, 4):
        src = turn(p, k)
        arrived(R.R1P.at[src], SEMS.f1p, k - 1, dev(u, src, c))
    total = R.G1[:, p, c] + R.R1[:, p]
    for k in range(1, 4):
        total = total + R.R1P[turn(p, k)].astype(F32)
    R.S1[...] = total.astype(BF)
    for k in range(1, 4):
        to = turn(u, k)
        send(R.S1.at[to], R.R1Z.at[u], SEMS.f1z, k - 1, dev(to, p, c))
    R.R1Z[u] = R.S1[u]
    for k in range(1, 4):
        src = turn(u, k)
        arrived(R.ROZ.at[src], SEMS.foz, k - 1, dev(src, p, c))
    total = R.TO[u].astype(F32)
    for k in range(1, 4):
        total = total + R.ROZ[turn(u, k)].astype(F32)
    R.t_ow[...] = total
    for k in range(1, 4):
        src = turn(p, k)
        arrived(R.RUP.at[src], SEMS.fup, k - 1, dev(u, src, c))
    R.t_up[...] = R.RUP[...]
    arrived(R.PR.at[2], SEMS.x, 2, dev(across, s, c))

    @pl.when(far)
    def _():
        arrived(R.PR.at[0], SEMS.x, 0, dev(u, s, c))
        R.Y1[...] = R.PR[0].astype(F32)

    total = R.DH1[...] + R.Y1[...] + R.PR[2].astype(F32)
    R.t_in[...] = total
    for k in range(1, 4):
        src = turn(u, k)
        arrived(R.R1Z.at[src], SEMS.f1z, k - 1, dev(src, p, c))
    R.t_qkv[...] = R.R1Z[...]
    settle()
    for t in range(1, 5):
        j = order(t)

        @pl.when(jnp.logical_and(a + j >= 2, a + j < 10))
        def _():
            if t == 4 or t == 1:
                block_copy(t).wait_send()
            else:
                for h in range(3):
                    key_copy(t, h).wait_send()


def finish_kernel(*refs):
    R = Refs()
    for name, ref in zip([*RAW, *OUTS], refs, strict=True):
        setattr(R, name, ref)
    R.o_out[...] = R.t_out[...]
    R.o_in[...] = R.t_in[...]
    R.o_dnw[...] = R.t_dn[...]
    R.o_ow[...] = R.t_ow[...]
    for q in range(4):
        piece = R.t_up[q].astype(F32)
        for g in range(4):
            R.o_upw[:, 768 * g + 192 * q : 768 * g + 192 * q + 192] = piece[:, 192 * g : 192 * g + 192]
    small = jnp.zeros((24, 64), F32)
    for g in range(4):
        piece = R.t_qkv[g].astype(F32)
        at = 192 * g
        R.o_kw[:, at : at + 192] = jnp.concatenate([piece[:, 128 * h : 128 * h + 64] for h in range(3)], axis=1)
        R.o_vw[:, at : at + 192] = jnp.concatenate([piece[:, 128 * h + 64 : 128 * h + 128] for h in range(3)], axis=1)
        R.o_qw[:, at : at + 192] = piece[:, 384:576]
        small = small + piece[:, 576:640]
    for row, name in enumerate(SMALL):
        getattr(R, "o_" + name)[...] = small[row : row + 1, 0:24].reshape(24)
    R.o_upb[...] = jnp.concatenate([small[8 + i : 9 + i, 0:24] for i in range(4)], axis=1).reshape(96)


def fused_step(*args):
    vmem = pl.BlockSpec(memory_space=pltpu.VMEM)
    raw = pl.pallas_call(
        layer_kernel,
        out_shape=[jax.ShapeDtypeStruct(shape, dtype) for shape, dtype in RAW.values()],
        in_specs=[pl.BlockSpec(memory_space=pltpu.SMEM) if n == "starts" else vmem for n in ARGS],
        out_specs=[vmem] * len(RAW),
        scratch_shapes=[pltpu.VMEM(shape, dtype) for shape, dtype in SCRATCH.values()]
        + [pltpu.SemaphoreType.DMA((n,)) for n in (SEND_SLOTS, SEMS.total)],
        compiler_params=pltpu.CompilerParams(
            collective_id=0, has_side_effects=True, vmem_limit_bytes=63 << 20
        ),
        name="layer_step",
    )(*args)
    return pl.pallas_call(
        finish_kernel,
        out_shape=[jax.ShapeDtypeStruct(shape, dtype) for shape, dtype in OUTS.values()],
        in_specs=[vmem] * len(RAW),
        out_specs=[vmem] * len(OUTS),
        name="finish",
    )(*raw)


def solution(mesh):
    fused = mesh.shape[ULYSSES] == 4 and mesh.shape[BLK] == 8
    return jax.shard_map(
        fused_step if fused else per_device,
        mesh=mesh,
        in_specs=(
            P(TOKEN_AXES, None),
            P(TOKEN_AXES, None),
            P(),
            P(WEIGHT_AXES, None),
            P(WEIGHT_AXES, None),
            P(WEIGHT_AXES, None),
            P(WEIGHT_AXES),
            P(WEIGHT_AXES),
            P(WEIGHT_AXES, None),
            P(WEIGHT_AXES),
            P(WEIGHT_AXES),
            P(WEIGHT_AXES),
            P(WEIGHT_AXES, None),
            P(WEIGHT_AXES),
            P(WEIGHT_AXES, None),
            P(WEIGHT_AXES),
            P(WEIGHT_AXES),
            P(WEIGHT_AXES),
        ),
        out_specs=(
            P(TOKEN_AXES, None),
            P(TOKEN_AXES, None),
            P(WEIGHT_AXES, None),
            P(WEIGHT_AXES, None),
            P(WEIGHT_AXES, None),
            P(WEIGHT_AXES),
            P(WEIGHT_AXES),
            P(WEIGHT_AXES, None),
            P(WEIGHT_AXES),
            P(WEIGHT_AXES),
            P(WEIGHT_AXES),
            P(WEIGHT_AXES, None),
            P(WEIGHT_AXES),
            P(WEIGHT_AXES, None),
            P(WEIGHT_AXES),
            P(WEIGHT_AXES),
            P(WEIGHT_AXES),
        ),
        check_vma=False,
    )
```

```python
import jax
import jax.numpy as jnp
from jax import lax
from jax.experimental import pallas as pl
from jax.experimental.pallas import tpu as pltpu
from jax.sharding import PartitionSpec as P

HD = 64
ULYSSES = "ulysses"
BLK = "blk"
WEIGHT_AXES = (ULYSSES, BLK)
TOKEN_AXES = (BLK, ULYSSES)


SCALE = 0.125
EPS = 1e-12


def passed_along(shard, axis, by):
    length = lax.axis_size(axis)
    return lax.ppermute(shard, axis, [(i, (i + by) % length) for i in range(length)])


def layer_norm(hidden, gain, shift):
    middle = jnp.mean(hidden, axis=-1, keepdims=True)
    centered = hidden - middle
    spread = jnp.mean(centered * centered, axis=-1, keepdims=True)
    return centered * lax.rsqrt(spread + EPS) * gain + shift


def gelu_exact(values):
    return jax.nn.gelu(values, approximate=False)


def doc_ids(doc_starts, positions):
    return jnp.sum((doc_starts[None, :] <= positions[:, None]).astype(jnp.int32), axis=1)


def project(left, right):
    return jnp.dot(left, right, preferred_element_type=jnp.float32)


def project_back(left, right):
    return lax.dot_general(
        left, right, (((1,), (1,)), ((), ())), preferred_element_type=jnp.float32
    )


def outer_sum(left, right):
    return lax.dot_general(
        left, right, (((0,), (0,)), ((), ())), preferred_element_type=jnp.float32
    )


def per_device(
    tokens,
    cotangent,
    doc_starts,
    q_weight,
    k_weight,
    v_weight,
    q_bias,
    v_bias,
    o_weight,
    o_bias,
    norm1_gain,
    norm1_bias,
    up_weight,
    up_bias,
    down_weight,
    down_bias,
    norm2_gain,
    norm2_bias,
):
    f32 = jnp.float32
    bf16 = jnp.bfloat16
    w_query, w_key, w_value, b_query, b_value, w_out, b_out, gain_one, shift_one = (
        lax.all_gather(q_weight, WEIGHT_AXES, axis=0, tiled=True),
        lax.all_gather(k_weight, WEIGHT_AXES, axis=0, tiled=True),
        lax.all_gather(v_weight, WEIGHT_AXES, axis=0, tiled=True),
        lax.all_gather(q_bias, WEIGHT_AXES, axis=0, tiled=True),
        lax.all_gather(v_bias, WEIGHT_AXES, axis=0, tiled=True),
        lax.all_gather(o_weight, WEIGHT_AXES, axis=0, tiled=True),
        lax.all_gather(o_bias, WEIGHT_AXES, axis=0, tiled=True),
        lax.all_gather(norm1_gain, WEIGHT_AXES, axis=0, tiled=True),
        lax.all_gather(norm1_bias, WEIGHT_AXES, axis=0, tiled=True),
    )
    w_up, b_up, w_down, b_down, gain_two, shift_two = (
        lax.all_gather(up_weight, WEIGHT_AXES, axis=0, tiled=True),
        lax.all_gather(up_bias, WEIGHT_AXES, axis=0, tiled=True),
        lax.all_gather(down_weight, WEIGHT_AXES, axis=0, tiled=True),
        lax.all_gather(down_bias, WEIGHT_AXES, axis=0, tiled=True),
        lax.all_gather(norm2_gain, WEIGHT_AXES, axis=0, tiled=True),
        lax.all_gather(norm2_bias, WEIGHT_AXES, axis=0, tiled=True),
    )
    query_tok = (project(tokens, w_query) + b_query.astype(f32)).astype(bf16)
    key_tok = project(tokens, w_key).astype(bf16)
    value_tok = (project(tokens, w_value) + b_value.astype(f32)).astype(bf16)
    query_heads, key_heads, value_heads = (
        lax.all_to_all(query_tok, ULYSSES, split_axis=1, concat_axis=0, tiled=True),
        lax.all_to_all(key_tok, ULYSSES, split_axis=1, concat_axis=0, tiled=True),
        lax.all_to_all(value_tok, ULYSSES, split_axis=1, concat_axis=0, tiled=True),
    )
    group = query_heads.shape[0]
    columns = query_heads.shape[1]
    local_heads = columns // HD
    block_count = lax.axis_size(BLK)
    total = group * block_count
    doc_max = min(8192, total // 4, 8 * group)
    reach = (group - 2 + doc_max) // group
    visits = 2 * reach + 1
    block_index = lax.axis_index(BLK)
    rows = jnp.arange(group, dtype=jnp.int32)
    query_ids = doc_ids(doc_starts, block_index * group + rows)
    query3 = query_heads.reshape(group, local_heads, HD)

    def block_mask(offset):
        key_pos = (block_index + offset) * group + rows
        inside = (key_pos >= 0) & (key_pos < total)
        key_ids = jnp.where(inside, doc_ids(doc_starts, key_pos), -1)
        allowed = query_ids[:, None] == key_ids[None, :]
        shared = (
            inside[0] & (key_ids[0] <= query_ids[group - 1]) & (key_ids[group - 1] >= query_ids[0])
        )
        return (allowed, shared)

    def exp_scores(pair, allowed):
        key3 = pair[0].reshape(group, local_heads, HD)
        scores = jnp.einsum("qhd,khd->hqk", query3, key3, preferred_element_type=f32) * SCALE
        return jnp.where(allowed[None], jnp.exp(scores), 0.0)

    def forward_terms(pair, offset):
        allowed, shared = block_mask(offset)
        weights = exp_scores(pair, allowed)
        value3 = pair[1].reshape(group, local_heads, HD)
        numer = jnp.einsum("hqk,khd->qhd", weights.astype(bf16), value3, preferred_element_type=f32)
        return (numer, jnp.sum(weights, axis=2))

    pair_own = jnp.stack([key_heads, value_heads])
    pair = passed_along(pair_own, BLK, -reach)
    numer, denom = forward_terms(pair, reach)
    store = jnp.zeros((1,), bf16)

    def forward_step(step, carry):
        pair_now, numer_now, denom_now, store_now = carry
        pair_now = passed_along(pair_now, BLK, 1)
        more_numer, more_denom = forward_terms(pair_now, reach - step)
        return (pair_now, numer_now + more_numer, denom_now + more_denom, store_now)

    pair, numer, denom, store = lax.fori_loop(1, visits, forward_step, (pair, numer, denom, store))
    attn_f = numer / jnp.transpose(denom)[:, :, None]
    attn_b = attn_f.reshape(group, columns).astype(bf16)
    attn_tok = lax.all_to_all(attn_b, ULYSSES, split_axis=0, concat_axis=1, tiled=True)
    token_f = tokens.astype(f32)
    h_one = token_f + project(attn_tok, w_out) + b_out.astype(f32)
    y_one, norm_one_back = jax.vjp(layer_norm, h_one, gain_one.astype(f32), shift_one.astype(f32))
    y_one_b = y_one.astype(bf16)
    pre_act = project(y_one_b, w_up) + b_up.astype(f32)
    act, gelu_back = jax.vjp(gelu_exact, pre_act)
    act_b = act.astype(bf16)
    h_two = y_one + project(act_b, w_down) + b_down.astype(f32)
    out_f, norm_two_back = jax.vjp(layer_norm, h_two, gain_two.astype(f32), shift_two.astype(f32))
    layer_out = out_f.astype(bf16)
    d_two, g_gain_two, g_shift_two = norm_two_back(cotangent.astype(f32))
    g_b_down = jnp.sum(d_two, axis=0)
    d_two_b = d_two.astype(bf16)
    g_w_down = outer_sum(act_b, d_two_b)
    d_act = project_back(d_two_b, w_down)
    d_pre = gelu_back(d_act)[0].astype(bf16)
    g_b_up = jnp.sum(d_pre.astype(f32), axis=0)
    g_w_up = outer_sum(y_one_b, d_pre)
    d_y_one = d_two + project_back(d_pre, w_up)
    d_one, g_gain_one, g_shift_one = norm_one_back(d_y_one)
    g_b_out = jnp.sum(d_one, axis=0)
    d_one_b = d_one.astype(bf16)
    g_w_out = outer_sum(attn_tok, d_one_b)
    d_attn_tok = project_back(d_one_b, w_out).astype(bf16)
    d_attn = lax.all_to_all(d_attn_tok, ULYSSES, split_axis=1, concat_axis=0, tiled=True)
    d_attn3 = d_attn.reshape(group, local_heads, HD)
    d_attn_f = d_attn3.astype(f32)
    delta = jnp.transpose(jnp.sum(d_attn_f * attn_f, axis=2))
    scaled_grad = d_attn_f / jnp.transpose(denom)[:, :, None]
    grad_high = scaled_grad.astype(bf16)
    grad_rest = (scaled_grad - grad_high.astype(f32)).astype(bf16)

    def backward_terms(pair_in, offset):
        allowed, shared = block_mask(offset)
        weights = exp_scores(pair_in, allowed)
        key3 = pair_in[0].reshape(group, local_heads, HD)
        value3 = pair_in[1].reshape(group, local_heads, HD)
        probs = weights / denom[:, :, None]
        d_prob = jnp.einsum("qhd,khd->hqk", d_attn3, value3, preferred_element_type=f32)
        d_score = (probs * (d_prob - delta[:, :, None]) * SCALE).astype(bf16)
        d_query = jnp.einsum("hqk,khd->qhd", d_score, key3, preferred_element_type=f32)
        d_key = jnp.einsum("hqk,qhd->khd", d_score, query3, preferred_element_type=f32)
        weights_low = weights.astype(bf16)
        d_value = jnp.einsum(
            "hqk,qhd->khd", weights_low, grad_high, preferred_element_type=f32
        ) + jnp.einsum("hqk,qhd->khd", weights_low, grad_rest, preferred_element_type=f32)
        return (d_query, jnp.stack([d_key, d_value]))

    pair = passed_along(pair_own, BLK, -reach)
    d_query_sum, carried = backward_terms(pair, reach)

    def backward_step(step, carry):
        pair_now, d_query_now, carried_now = carry
        pair_now = passed_along(pair_now, BLK, 1)
        more_query, more_kv = backward_terms(pair_now, reach - step)
        carried_now = (
            passed_along(carried_now.astype(jnp.bfloat16), BLK, 1).astype(carried_now.dtype)
            + more_kv
        )
        return (pair_now, d_query_now + more_query, carried_now)

    pair, d_query_sum, carried = lax.fori_loop(
        1, visits, backward_step, (pair, d_query_sum, carried)
    )
    own_grads = passed_along(carried.astype(jnp.bfloat16), BLK, -reach).astype(carried.dtype)
    d_query_b = d_query_sum.reshape(group, columns).astype(bf16)
    d_key_b = own_grads[0].reshape(group, columns).astype(bf16)
    d_value_b = own_grads[1].reshape(group, columns).astype(bf16)
    dq_tok, dk_tok, dv_tok = (
        lax.all_to_all(d_query_b, ULYSSES, split_axis=0, concat_axis=1, tiled=True),
        lax.all_to_all(d_key_b, ULYSSES, split_axis=0, concat_axis=1, tiled=True),
        lax.all_to_all(d_value_b, ULYSSES, split_axis=0, concat_axis=1, tiled=True),
    )
    g_b_query = jnp.sum(dq_tok.astype(f32), axis=0)
    g_b_value = jnp.sum(dv_tok.astype(f32), axis=0)
    g_w_query = outer_sum(tokens, dq_tok)
    g_w_key = outer_sum(tokens, dk_tok)
    g_w_value = outer_sum(tokens, dv_tok)
    input_grad = (
        d_one
        + project_back(dq_tok, w_query)
        + project_back(dk_tok, w_key)
        + project_back(dv_tok, w_value)
    )
    shares = (
        lax.psum_scatter(g_w_query, WEIGHT_AXES, scatter_dimension=0, tiled=True),
        lax.psum_scatter(g_w_key, WEIGHT_AXES, scatter_dimension=0, tiled=True),
        lax.psum_scatter(g_w_value, WEIGHT_AXES, scatter_dimension=0, tiled=True),
        lax.psum_scatter(g_b_query, WEIGHT_AXES, scatter_dimension=0, tiled=True),
        lax.psum_scatter(g_b_value, WEIGHT_AXES, scatter_dimension=0, tiled=True),
        lax.psum_scatter(g_w_out, WEIGHT_AXES, scatter_dimension=0, tiled=True),
        lax.psum_scatter(g_b_out, WEIGHT_AXES, scatter_dimension=0, tiled=True),
        lax.psum_scatter(g_gain_one, WEIGHT_AXES, scatter_dimension=0, tiled=True),
        lax.psum_scatter(g_shift_one, WEIGHT_AXES, scatter_dimension=0, tiled=True),
        lax.psum_scatter(g_w_up, WEIGHT_AXES, scatter_dimension=0, tiled=True),
        lax.psum_scatter(g_b_up, WEIGHT_AXES, scatter_dimension=0, tiled=True),
        lax.psum_scatter(g_w_down, WEIGHT_AXES, scatter_dimension=0, tiled=True),
        lax.psum_scatter(g_b_down, WEIGHT_AXES, scatter_dimension=0, tiled=True),
        lax.psum_scatter(g_gain_two, WEIGHT_AXES, scatter_dimension=0, tiled=True),
        lax.psum_scatter(g_shift_two, WEIGHT_AXES, scatter_dimension=0, tiled=True),
    )
    return (
        layer_out,
        input_grad,
        shares[0],
        shares[1],
        shares[2],
        shares[3],
        shares[4],
        shares[5],
        shares[6],
        shares[7],
        shares[8],
        shares[9],
        shares[10],
        shares[11],
        shares[12],
        shares[13],
        shares[14],
    )


MESH = pl.DeviceIdType.MESH
LOG2E = 1.4426950408889634
RSQRT2 = 0.7071067811865476
FWD_ROWS = 256
BWD_ROWS = 256
KEY_SENDS = 8
SEND_SLOTS = 62
PDF0 = 0.3989422804014327

ARGS = ("tok", "cot", "starts", "qw", "kw", "vw", "qb", "vb", "ow", "ob", "g1", "b1", "upw", "upb", "dnw", "dnb", "g2", "b2")
OUTS = dict(
    o_out=((128, 768), jnp.bfloat16),
    o_in=((128, 768), jnp.float32),
    o_qw=((24, 768), jnp.float32),
    o_kw=((24, 768), jnp.float32),
    o_vw=((24, 768), jnp.float32),
    o_qb=((24,), jnp.float32),
    o_vb=((24,), jnp.float32),
    o_ow=((24, 768), jnp.float32),
    o_ob=((24,), jnp.float32),
    o_g1=((24,), jnp.float32),
    o_b1=((24,), jnp.float32),
    o_upw=((24, 3072), jnp.float32),
    o_upb=((96,), jnp.float32),
    o_dnw=((96, 768), jnp.float32),
    o_dnb=((24,), jnp.float32),
    o_g2=((24,), jnp.float32),
    o_b2=((24,), jnp.float32),
)
RAW = dict(
    t_out=((128, 768), jnp.bfloat16),
    t_in=((128, 768), jnp.float32),
    t_qkv=((4, 24, 640), jnp.bfloat16),
    t_up=((4, 24, 768), jnp.bfloat16),
    t_dn=((96, 768), jnp.float32),
    t_ow=((24, 768), jnp.float32),
)
SMALL = ("qb", "vb", "ob", "g1", "b1", "dnb", "g2", "b2")
BF = jnp.bfloat16
F32 = jnp.float32
SCRATCH = dict(
    SM=((24, 128), F32),
    WS=((4, 24, 640), BF),
    W5=((4, 4, 2, 24, 640), BF),
    W2=((768, 640), BF),
    US=((4, 24, 768), BF),
    UP5=((4, 4, 2, 24, 768), BF),
    UP2=((768, 768), BF),
    DN4=((4, 2, 96, 768), BF),
    OW5=((4, 4, 2, 24, 768), BF),
    OW2=((768, 768), BF),
    XG=((4, 2, 64, 768), BF),
    KV=((5, 4, 128, 384), BF),
    KVT=((15, 144, 512), BF),
    QP=((3, 4, 128, 128), BF),
    GP=((3, 4, 128, 128), BF),
    SEGK=((5, 512, 128), BF),
    EL=((15, 512, 512), BF),
    DST=((512, 512), BF),
    NUM=((3, 80, 512), F32),
    DEN=((3, 8, 512), F32),
    ATN=((3, 64, 512), F32),
    DLT=((3, 8, 512), F32),
    AS=((4, 192, 128), BF),
    AT=((4, 192, 128), BF),
    Y1=((128, 768), F32),
    N1=((128, 768), F32),
    RSD=((128, 128), F32),
    YG=((4, 128, 768), BF),
    ACT=((4, 128, 768), BF),
    GG=((4, 128, 768), BF),
    PS=((4, 128, 768), BF),
    PR=((4, 128, 768), BF),
    XN=((128, 768), BF),
    H2=((128, 768), F32),
    DH2=((128, 768), F32),
    DG=((4, 128, 768), BF),
    DU=((4, 128, 768), BF),
    DH1=((128, 768), F32),
    DAS=((4, 2, 96, 128), BF),
    DA=((4, 2, 96, 128), BF),
    T1=((768, 512), BF),
    MR=((768, 64), F32),
    DKS=((5, 3, 512, 128), BF),
    DKX=((3, 512, 128), BF),
    DKR=((5, 3, 512, 128), BF),
    DKO=((3, 512, 128), F32),
    DQT=((3, 64, 512), F32),
    DQ=((512, 640), BF),
    VEC=((16, 768), F32),
    VUP=((8, 768), F32),
    G1=((4, 4, 2, 24, 640), F32),
    R1=((4, 4, 24, 640), F32),
    H1=((4, 4, 24, 640), BF),
    R1P=((4, 4, 24, 640), BF),
    S1=((4, 24, 640), BF),
    R1Z=((4, 24, 640), BF),
    GU=((4, 4, 2, 24, 768), F32),
    RU=((4, 4, 24, 768), F32),
    SU=((2, 4, 24, 768), BF),
    RU1=((2, 4, 24, 768), BF),
    SU2=((4, 24, 768), BF),
    RU2=((4, 24, 768), BF),
    TU=((4, 24, 768), BF),
    RUP=((4, 24, 768), BF),
    GD=((4, 2, 96, 768), F32),
    RD=((4, 96, 768), F32),
    SD=((2, 96, 768), BF),
    RD1=((2, 96, 768), BF),
    SD2=((96, 768), BF),
    RD2=((96, 768), BF),
    GO=((4, 4, 2, 24, 768), F32),
    RO=((4, 4, 24, 768), F32),
    SO=((4, 4, 24, 768), BF),
    ROP=((4, 4, 24, 768), BF),
    TO=((4, 24, 768), BF),
    ROZ=((4, 24, 768), BF),
)


class Slots:
    def __init__(self, **sizes):
        self.total = 0
        for name, size in sizes.items():
            setattr(self, name, self.total)
            self.total += size

    def again(self, start, **sizes):
        for name, size in sizes.items():
            setattr(self, name, start)
            start += size
        return start


SEMS = Slots(
    tok=6, hop=2, wz=3, wp=3, wc=1, us=3, kv=7, oz=3, spare=10, cow=1, cup=1, cdn=1, op=3, upz=3, dnz=3,
    at=4, yg=6, ps=6, fdz=2, foz=3,
)
END = SEMS.again(
    SEMS.tok, da=8, dk=5, dx=3, x=4, f1c=1, f1p=3, f1z=3, fuc=1, fuz=2, fup=3, fdc=1, foc=1, fop=3
)
assert END <= SEMS.cow
SEMS.again(SEMS.yg, dg=6, qs=6)


def mm(left, right):
    return jnp.dot(left, right, preferred_element_type=F32)


def mm_nt(left, right):
    return lax.dot_general(left, right, (((1,), (1,)), ((), ())), preferred_element_type=F32)


def mm_tn(left, right):
    return lax.dot_general(left, right, (((0,), (0,)), ((), ())), preferred_element_type=F32)


def pack(rows):
    tail = rows[:, 128:192]
    return jnp.concatenate([rows[:, 0:128], jnp.concatenate([tail[0:64], tail[64:128]], axis=1)], axis=0)


def unpack(packed):
    tail = packed[128:192]
    tail = jnp.concatenate([tail[:, 0:64], tail[:, 64:128]], axis=0)
    return jnp.concatenate([packed[0:128], tail], axis=1)


def unpack_half(packed, i):
    return jnp.concatenate([packed[64 * i : 64 * i + 64], packed[128:192, 64 * i : 64 * i + 64]], axis=1)


def pack_half(rows):
    tail = rows[:, 128:192]
    return jnp.concatenate([rows[:, 0:128], jnp.concatenate([tail[0:32], tail[32:64]], axis=1)], axis=0)


def open_half(packed):
    tail = packed[64:96]
    tail = jnp.concatenate([tail[:, 0:64], tail[:, 64:128]], axis=0)
    return jnp.concatenate([packed[0:64], tail], axis=1)


def rows_by(shape, axis, flat):
    return lax.broadcasted_iota(jnp.int32, shape, axis).reshape(flat)


class Refs:
    pass


def layer_kernel(*refs):
    R = Refs()
    names = [*ARGS, *("g" + n for n in RAW), *RAW, *SCRATCH, "SS", "RS", "LS"]
    for name, ref in zip(names, refs, strict=True):
        setattr(R, name, ref)
    u = lax.axis_index(ULYSSES)
    b = lax.axis_index(BLK)
    c = lax.rem(b, 2)
    p = lax.div(b, 2)
    other = 1 - c

    def snake(at):
        return at + lax.div(at, 2) * (1 - 2 * lax.rem(at, 2))

    s = snake(p)
    a = 2 * s + c
    far = p >= 2

    def dev(uu, pp, cc):
        return (uu, 2 * pp + cc)

    def block_dev(aa):
        return dev(u, snake(lax.div(aa, 2)), lax.rem(aa, 2))

    def turn(base, k):
        low, high = lax.rem(base, 2), lax.div(base, 2)
        if k % 2:
            low = 1 - low
        if k // 2:
            high = 1 - high
        return 2 * high + low

    sends = []
    free = list(range(KEY_SENDS, SEND_SLOTS))

    def copy(src, dst, slot, ri, device):
        return pltpu.make_async_remote_copy(
            src_ref=src, dst_ref=dst, send_sem=R.SS.at[slot], recv_sem=R.RS.at[ri],
            device_id=device, device_id_type=MESH,
        )

    def send(src, dst, name, ri, device, cond=None):
        slot = free.pop(0)
        desc = copy(src, dst, slot, name + ri, device)
        if cond is None:
            desc.start()
        else:

            @pl.when(cond)
            def _():
                desc.start()

        sends.append((name, cond, desc, slot))

    def send_if(cond, *what):
        send(*what, cond=cond)

    leaving = []

    def leave(name):
        out = pltpu.make_async_copy(getattr(R, name), getattr(R, "g" + name), R.LS.at[len(leaving)])
        out.start()
        leaving.append(out)

    def key_slot(t, sub):
        return sub if t == 3 else {1: 4, 2: 5, 4: 6}[t]

    def settle(*wanted):
        for entry in list(sends):
            name, cond, desc, slot = entry
            if wanted and name not in wanted:
                continue
            sends.remove(entry)
            free.append(slot)
            if cond is None:
                desc.wait_send()
            else:

                @pl.when(cond)
                def _():
                    desc.wait_send()

    def arrived(dst, name, ri, device):
        copy(dst, dst, 0, name + ri, device).wait_recv()

    barrier = pltpu.get_barrier_semaphore()

    def greet(device):
        pl.semaphore_signal(barrier, inc=1, device_id=device, device_id_type=MESH)

    for k in range(1, 8):
        greet((u, lax.rem(b + k, 8)))
    for k in range(1, 4):
        greet((turn(u, k), b))

    @pl.when(far)
    def _():
        for k in range(1, 4):
            greet(dev(turn(u, k), s, c))

    R.SM[...] = jnp.zeros_like(R.SM)
    for row, name in enumerate(SMALL):
        R.SM[row : row + 1, 0:24] = getattr(R, name)[...].astype(F32).reshape(1, 24)
    up_bias = R.upb[...].astype(F32).reshape(1, 96)
    for i in range(4):
        R.SM[8 + i : 9 + i, 0:24] = up_bias[:, 24 * i : 24 * i + 24]
    small = R.SM[:, 0:64].astype(BF)
    qw, kw, vw = R.qw[...], R.kw[...], R.vw[...]
    for g in range(4):
        parts = []
        for h in range(3):
            at = 64 * (3 * g + h)
            parts += [kw[:, at : at + 64], vw[:, at : at + 64]]
        for h in range(3):
            at = 64 * (3 * g + h)
            parts.append(qw[:, at : at + 64])
        parts.append(small)
        R.WS[g] = jnp.concatenate(parts, axis=1)

    pl.semaphore_wait(barrier, 10 + 3 * lax.div(p, 2))

    for k in range(1, 4):
        to = turn(u, k)
        send(R.WS.at[to], R.W5.at[u, p, c], SEMS.wz, k - 1, dev(to, p, c))
    R.W5[u, p, c] = R.WS[u]
    halves = (slice(0, 64), slice(64, 128))
    for i in range(2):
        send_if(far, R.tok.at[halves[i]], R.XG.at[u, i], SEMS.hop, i, dev(u, s, c))

    @pl.when(jnp.logical_not(far))
    def _():
        for i in range(2):
            R.XG[u, i] = R.tok[halves[i], :]

    near, across = turn(u, 1), turn(u, 2)
    there = dev(near, p, c)
    for i in range(2):
        for k in (2, 1):
            send_if(
                jnp.logical_not(far),
                R.tok.at[halves[i]], R.XG.at[u, i], SEMS.tok, 2 * (k - 1) + i, dev(turn(u, k), p, c),
            )

    up = R.upw[...]
    for q in range(4):
        R.US[q] = jnp.concatenate(
            [up[:, 768 * g + 192 * q : 768 * g + 192 * q + 192] for g in range(4)], axis=1
        )
    for k in range(1, 4):
        to = turn(p, k)
        send(R.US.at[to], R.UP5.at[u, p, c], SEMS.us, k - 1, dev(u, to, c))
    R.UP5[u, p, c] = R.US[p]
    R.DN4[u, c] = R.dnw[...]
    R.OW5[u, p, c] = R.ow[...]

    mate = dev(u, p, other)
    row_pos = lax.broadcasted_iota(jnp.int32, (512, 128), 0)
    n_starts = R.starts.shape[0]

    def id_body(j, carry):
        pos = row_pos + (a + j - 2) * 512
        ids = jnp.zeros((512, 128), jnp.int32)
        for i in range(n_starts):
            ids = ids + jnp.where(pos >= R.starts[i], 1, 0)
        R.SEGK[j] = ids.astype(F32).astype(BF)
        return carry

    lax.fori_loop(0, 5, id_body, 0)
    q_pos = lax.broadcasted_iota(jnp.int32, (1, 512), 1) + a * 512
    q_ids = jnp.zeros((1, 512), jnp.int32)
    for i in range(n_starts):
        q_ids = q_ids + jnp.where(q_pos >= R.starts[i], 1, 0)
    q_ids = jnp.broadcast_to(q_ids.astype(F32), (FWD_ROWS, 512)).astype(BF)
    R.KVT[:, 128:144, :] = jnp.ones((15, 16, 512), BF)
    for ref in (R.QP, R.GP, R.NUM, R.DQT):
        ref[...] = jnp.zeros_like(ref)

    for i in range(2):

        @pl.when(far)
        def _():
            arrived(R.XG.at[u, i], SEMS.hop, i, dev(u, s, c))

        for k in (2, 1):
            send_if(
                far,
                R.XG.at[u, i], R.XG.at[u, i], SEMS.tok, 2 * (k - 1) + i, dev(turn(u, k), p, c),
            )
    for k in range(1, 4):
        src = turn(u, k)
        arrived(R.W5.at[src, p, c], SEMS.wz, k - 1, dev(src, p, c))
    for k in range(1, 4):
        to = turn(p, k)
        send(R.W5.at[:, p, c], R.W5.at[:, p, c], SEMS.wp, k - 1, dev(u, to, c))
    def pass_tokens(i):
        arrived(R.XG.at[across, i], SEMS.tok, 2 + i, dev(across, p, c))
        send(R.XG.at[across, i], R.XG.at[across, i], SEMS.tok, 4 + i, there)

    pass_tokens(0)
    for k in range(1, 4):
        src = turn(p, k)
        arrived(R.W5.at[:, src, c], SEMS.wp, k - 1, dev(u, src, c))
    send(R.W5.at[:, :, c], R.W5.at[:, :, c], SEMS.wc, 0, dev(u, p, other))
    pass_tokens(1)
    for k in range(1, 4):
        to = turn(u, k)
        send(R.ow, R.OW5.at[u, p, c], SEMS.oz, k - 1, dev(to, p, c))
    send(R.dnw, R.DN4.at[u, c], SEMS.dnz, 0, dev(across, p, c))
    for k in range(1, 4):
        src = turn(p, k)
        arrived(R.UP5.at[u, src, c], SEMS.us, k - 1, dev(u, src, c))
    send(R.UP5.at[u, :, c], R.UP5.at[u, :, c], SEMS.upz, 0, dev(across, p, c))
    arrived(R.W5.at[:, :, other], SEMS.wc, 0, dev(u, p, other))
    R.W2[...] = R.W5[...].reshape(768, 640)

    spread = jnp.where(
        rows_by((32, 24, 64), 1, (768, 64)) == lax.broadcasted_iota(jnp.int32, (768, 64), 1), 1.0, 0.0
    ).astype(BF)
    owner = rows_by((32, 24, 768), 0, (768, 768))
    lane = lax.broadcasted_iota(jnp.int32, (1, 768), 1)
    lane_owner = jnp.zeros((1, 768), jnp.int32)
    for i in range(1, 32):
        lane_owner = lane_owner + jnp.where(lane >= 24 * i, 1, 0)
    lane_g = jnp.where(lane >= 192, 1, 0) + jnp.where(lane >= 384, 1, 0) + jnp.where(lane >= 576, 1, 0)
    rest = lane - 192 * lane_g
    lane_c = jnp.where(rest >= 96, 1, 0)
    rest = rest - 96 * lane_c
    lane_r = jnp.where(rest >= 24, 1, 0) + jnp.where(rest >= 48, 1, 0) + jnp.where(rest >= 72, 1, 0)
    up_row = 24 * (8 * lane_g + 2 * p + lane_c) + 8 + lane_r
    row_id = lax.broadcasted_iota(jnp.int32, (768, 768), 0)
    wide = mm_nt(R.W2[:, 576:640], spread)
    mine = jnp.where(owner == lane_owner, wide, 0.0).astype(BF)
    pick = jnp.where(
        lax.broadcasted_iota(jnp.int32, (16, 768), 1) - 24 * lane_owner
        == lax.broadcasted_iota(jnp.int32, (16, 768), 0), 1.0, 0.0
    ).astype(BF)
    R.VEC[...] = mm(pick, mine)

    def group_slice(vector):
        out = vector[:, 0:192]
        for g in range(1, 4):
            out = jnp.where(u == g, vector[:, 192 * g : 192 * g + 192], out)
        return out

    qb = group_slice(R.VEC[0:1, :])
    vb = group_slice(R.VEC[1:2, :])
    zero64 = jnp.zeros((1, 64), F32)
    bias = []
    for h in range(3):
        bias += [zero64, vb[:, 64 * h : 64 * h + 64]]
    bias = jnp.concatenate(bias + [qb, zero64], axis=1)

    for k in range(4):
        src = turn(u, k)
        if k > 0:
            for i in range(2):
                if k != 2:
                    arrived(R.XG.at[src, i], SEMS.tok, 2 * (k - 1) + i, there)
        proj = mm(R.XG[src].reshape(128, 768), R.W2[...]) + bias
        R.KV[2, src] = proj[:, 0:384].astype(BF)
        query = proj[:, 384:576].astype(BF) * BF(0.125)
        for h in range(3):
            R.QP[h, src, :, 0:64] = query[:, 64 * h : 64 * h + 64]
        slot = 1 + 2 * c
        send(R.KV.at[2, src], R.KV.at[slot, src], SEMS.kv, key_slot(1, src), mate)
        for i, step in enumerate((-2, 2)):
            to = a + step
            ok = jnp.logical_and(to >= 0, to < 8)
            slot = 2 - step
            handed = c if step > 0 else 1 - c
            index = handed * src + (1 - handed) * key_slot(4, src)
            send_if(ok, R.KV.at[2, src], R.KV.at[slot, src], SEMS.kv, index, block_dev(to))

    def order(t):
        return 2 + (1 - 2 * c) * ((t + 1) // 2) * (1 - 2 * ((t + 1) % 2))

    def forward_block(t):
        j = order(t)
        ok = jnp.logical_and(a + j >= 2, a + j < 10)

        @pl.when(ok)
        def _():
            if t == 1 or t == 2 or t == 4:
                arrived(R.KV.at[j], SEMS.kv, key_slot(t, 0), block_dev(a + j - 2) if t == 4 else mate)

            def head(h, inner):
                lanes = pl.ds(pl.multiple_of(128 * h, 128), 128)
                kv = R.KV[j, :, :, lanes].reshape(512, 128)
                at = 3 * j + h
                R.KVT[at, 0:128, :] = kv.T
                query = R.QP[h].reshape(512, 128)
                for r in range(512 // FWD_ROWS):
                    rows = slice(FWD_ROWS * r, FWD_ROWS * r + FWD_ROWS)
                    score = mm_nt(kv[rows], query)
                    ids = R.SEGK[j, rows, :]
                    same = jnp.concatenate([ids] * 4, axis=1) == q_ids
                    weight = jnp.exp2(score * LOG2E).astype(BF)
                    R.EL[at, rows, :] = jnp.where(same, weight, jnp.zeros_like(weight))
                R.NUM[h] += mm(R.KVT[at, 64:144, :], R.EL[at])
                return inner

            lax.fori_loop(0, 3, head, 0)

    def relay_out():
        for k in range(1, 4):
            src = turn(u, k)
            arrived(R.OW5.at[src, p, c], SEMS.oz, k - 1, dev(src, p, c))
        for k in range(1, 4):
            to = turn(p, k)
            send(R.OW5.at[:, p, c], R.OW5.at[:, p, c], SEMS.op, k - 1, dev(u, to, c))

    def share_keys():
        j = order(3)
        ok = jnp.logical_and(a + j >= 2, a + j < 10)
        slot = 1 + 2 * (1 - c)
        for r in range(4):

            @pl.when(ok)
            def _():
                arrived(R.KV.at[j, r], SEMS.kv, key_slot(3, r), block_dev(a + j - 2))

            send_if(ok, R.KV.at[j, r], R.KV.at[slot, r], SEMS.kv, key_slot(2, r), mate)

    def relay_down():
        arrived(R.DN4.at[across, c], SEMS.dnz, 0, dev(across, p, c))
        for i, src in enumerate((u, across)):
            send(R.DN4.at[src, c], R.DN4.at[src, c], SEMS.dnz, 1 + i, there)

    def relay_up():
        arrived(R.UP5.at[across, :, c], SEMS.upz, 0, dev(across, p, c))
        for i, src in enumerate((u, across)):
            send(R.UP5.at[src, :, c], R.UP5.at[src, :, c], SEMS.upz, 1 + i, there)

    forward_block(0)
    relay_out()
    forward_block(1)
    share_keys()
    forward_block(3)
    settle(SEMS.wz, SEMS.hop, SEMS.us, SEMS.wp, SEMS.wc)
    relay_down()
    forward_block(2)
    forward_block(4)

    heads = []
    for h in range(3):
        R.DEN[h, 0:1, :] = R.NUM[h, 64:65, :]
        attn = R.NUM[h, 0:64, :] / R.DEN[h, 0:1, :]
        R.ATN[h] = attn
        heads.append(attn.T.astype(BF))
    for r in range(4):
        rows = slice(128 * r, 128 * r + 128)
        R.AS[r] = pack(jnp.concatenate([part[rows] for part in heads], axis=1))
    for k in range(1, 4):
        to = turn(u, k)
        send(R.AS.at[to], R.AT.at[u], SEMS.at, k, dev(to, s, c))
    send_if(far, R.AS.at[u], R.AT.at[u], SEMS.at, 0, dev(u, s, c))

    @pl.when(jnp.logical_not(far))
    def _():
        R.AT[u] = R.AS[u]

    relay_up()
    wide = mm_nt(R.W2[:, 576:640], spread)
    R.VUP[0:1, :] = jnp.sum(jnp.where(row_id == up_row, wide, 0.0), axis=0, keepdims=True)
    settle(SEMS.tok, SEMS.hop, SEMS.wz, SEMS.wp, SEMS.wc, SEMS.us, SEMS.oz)
    for k in range(1, 4):
        src = turn(p, k)
        arrived(R.OW5.at[:, src, c], SEMS.op, k - 1, dev(u, src, c))
    send(R.OW5.at[:, :, c], R.OW5.at[:, :, c], SEMS.cow, 0, mate)
    arrived(R.OW5.at[:, :, other], SEMS.cow, 0, mate)
    R.OW2[...] = R.OW5[...].reshape(768, 768)

    def wait_column(ref, name):
        for k in range(1, 4):
            src = turn(u, k)
            arrived(ref.at[src], name, k, dev(src, s, c))

        @pl.when(far)
        def _():
            arrived(ref.at[u], name, 0, dev(u, s, c))

    wait_column(R.AT, SEMS.at)

    def gather_half(ref, i, value, name):
        rows = halves[i]
        ref[p, rows, :] = value
        for k in range(1, 4):
            part = ref.at[p, rows]
            send(part, part, name, 2 * (k - 1) + i, dev(u, turn(p, k), c))

    def centered(hidden):
        hidden = hidden - jnp.mean(hidden, axis=-1, keepdims=True)
        rstd = lax.rsqrt(jnp.mean(hidden * hidden, axis=-1, keepdims=True) + EPS)
        return hidden * rstd, rstd

    def norm_back(cg, normed, rstd):
        mean = jnp.mean(cg, axis=-1, keepdims=True)
        return (cg - mean - normed * jnp.mean(cg * normed, axis=-1, keepdims=True)) * rstd

    def down_sum(x):
        return jnp.sum(x, axis=0, keepdims=True)

    for i in range(2):
        rows = halves[i]
        hidden = R.tok[rows, :].astype(F32) + R.VEC[2:3, :]
        for g in range(4):
            hidden = hidden + mm(unpack_half(R.AT[g], i), R.OW2[192 * g : 192 * g + 192, :])
        normed, rstd = centered(hidden)
        R.N1[rows, :] = normed
        R.RSD[rows, :] = jnp.broadcast_to(rstd, (64, 128))
        y_one = normed * R.VEC[3:4, :] + R.VEC[4:5, :]
        R.Y1[rows, :] = y_one
        gather_half(R.YG, i, y_one.astype(BF), SEMS.yg)

    settle(SEMS.kv)
    for i, src in enumerate((near, turn(near, 2))):
        arrived(R.DN4.at[src, c], SEMS.dnz, 1 + i, there)
    send(R.DN4.at[:, c], R.DN4.at[:, c], SEMS.cdn, 0, mate)
    for i, src in enumerate((near, turn(near, 2))):
        arrived(R.UP5.at[src, :, c], SEMS.upz, 1 + i, there)
    send(R.UP5.at[:, :, c], R.UP5.at[:, :, c], SEMS.cup, 0, mate)
    arrived(R.DN4.at[:, other], SEMS.cdn, 0, mate)
    arrived(R.UP5.at[:, :, other], SEMS.cup, 0, mate)
    R.UP2[...] = R.UP5[...].reshape(768, 768)
    turns = ((0, 0), (0, 1), (1, 0), (2, 0), (3, 0), (1, 1), (2, 1), (3, 1))
    for k, i in turns[2:] + turns[:2]:
        at, rows = turn(p, k), halves[i]
        if k > 0:
            arrived(R.YG.at[at, rows], SEMS.yg, 2 * (k - 1) + i, dev(u, at, c))
        pre = mm(R.YG[at, rows, :], R.UP2[...]) + R.VUP[0:1, :]
        phi = 0.5 * (1.0 + lax.erf(pre * RSQRT2))
        R.GG[at, rows, :] = (phi + pre * (PDF0 * jnp.exp(-0.5 * pre * pre))).astype(BF)
        act = (pre * phi).astype(BF)
        R.ACT[at, rows, :] = act
        part = mm(act, R.DN4[...].reshape(768, 768))
        if k == 0:
            R.H2[rows, :] = part
        else:
            R.PS[at, rows, :] = part.astype(BF)
            send(R.PS.at[at, rows], R.PR.at[p, rows], SEMS.ps, 2 * (k - 1) + i, dev(u, at, c))

    g_gain_two = g_shift_two = g_b_down = 0.0
    for i in range(2):
        rows = halves[i]
        hidden = R.Y1[rows, :] + R.H2[rows, :] + R.VEC[5:6, :]
        for k in range(1, 4):
            at = turn(p, k)
            arrived(R.PR.at[at, rows], SEMS.ps, 2 * (k - 1) + i, dev(u, at, c))
            hidden = hidden + R.PR[at, rows, :].astype(F32)
        normed, rstd = centered(hidden)
        gain = R.VEC[6:7, :]
        grad = R.cot[rows, :].astype(F32)
        d_two = norm_back(grad * gain, normed, rstd)
        gather_half(R.DG, i, d_two.astype(BF), SEMS.dg)
        R.DH2[rows, :] = d_two
        R.t_out[rows, :] = (normed * gain + R.VEC[7:8, :]).astype(BF)
        g_gain_two = g_gain_two + down_sum(grad * normed)
        g_shift_two = g_shift_two + down_sum(grad)
        g_b_down = g_b_down + down_sum(d_two)

    leave("t_out")
    settle(SEMS.at, SEMS.op, SEMS.dnz, SEMS.upz, SEMS.cow, SEMS.cup, SEMS.cdn, SEMS.yg, SEMS.ps)
    g_b_up = jnp.zeros((1, 768), F32)
    for k, i in turns:
        at, rows = turn(p, k), halves[i]
        if k > 0:
            arrived(R.DG.at[at, rows], SEMS.dg, 2 * (k - 1) + i, dev(u, at, c))
        d_act = mm_nt(R.DG[at, rows, :], R.DN4[...].reshape(768, 768))
        d_pre = (d_act * R.GG[at, rows, :].astype(F32)).astype(BF)
        R.DU[at, rows, :] = d_pre
        g_b_up = g_b_up + down_sum(d_pre.astype(F32))
        part = mm_nt(d_pre, R.UP2[...])
        if k == 0:
            R.H2[rows, :] = part
        else:
            R.PS[at, rows, :] = part.astype(BF)
            send(R.PS.at[at, rows], R.PR.at[p, rows], SEMS.qs, 2 * (k - 1) + i, dev(u, at, c))

    def wide_grad(left, right_ref, put):
        R.T1[...] = left.T

        def body(n, carry):
            lanes = pl.ds(pl.multiple_of(256 * n, 256), 256)
            put(lanes, mm(R.T1[...], right_ref[:, :, lanes].reshape(512, 256)))
            return carry

        lax.fori_loop(0, 3, body, 0)

    def put_down(lanes, value):
        R.GD[:, :, :, lanes] = value.reshape(4, 2, 96, 256)

    def put_up(lanes, value):
        R.GU[:, :, :, :, lanes] = value.reshape(4, 4, 2, 24, 256)

    wide_grad(R.ACT[...].reshape(512, 768), R.DG, put_down)
    send(R.GD.at[:, other], R.RD, SEMS.fdc, 0, mate)
    wide_grad(R.YG[...].reshape(512, 768), R.DU, put_up)
    send(R.GU.at[:, :, other], R.RU, SEMS.fuc, 0, mate)
    def down_step():
        arrived(R.RD, SEMS.fdc, 0, mate)
        for i, g in enumerate((near, turn(near, 2))):
            R.SD[i] = (R.GD[g, c] + R.RD[g]).astype(BF)
        send(R.SD, R.RD1, SEMS.fdz, 0, there)

    down_step()
    g_b_out = g_gain_one = g_shift_one = 0.0
    for half in range(2):
        rows = halves[half]
        d_y = R.DH2[rows, :] + R.H2[rows, :]
        for k in range(1, 4):
            at = turn(p, k)
            arrived(R.PR.at[at, rows], SEMS.qs, 2 * (k - 1) + half, dev(u, at, c))
            d_y = d_y + R.PR[at, rows, :].astype(F32)
        normed = R.N1[rows, :]
        d_one = norm_back(d_y * R.VEC[3:4, :], normed, R.RSD[rows, 0:1])
        R.DH1[rows, :] = d_one
        for k in (1, 2, 3, 0):
            to = turn(u, k)
            w_rows = R.OW2[pl.ds(pl.multiple_of(192 * to, 64), 192), :]
            R.DAS[to, half] = pack_half(mm_nt(d_one.astype(BF), w_rows).astype(BF))
            if k > 0:
                send(R.DAS.at[to, half], R.DA.at[u, half], SEMS.da, 4 * half + k, dev(to, s, c))
        send_if(far, R.DAS.at[u, half], R.DA.at[u, half], SEMS.da, 4 * half, dev(u, s, c))
        g_b_out = g_b_out + down_sum(d_one)
        g_gain_one = g_gain_one + down_sum(d_y * normed)
        g_shift_one = g_shift_one + down_sum(d_y)

    @pl.when(jnp.logical_not(far))
    def _():
        R.DA[u] = R.DAS[u]

    vec = R.VEC
    vec[2:3, :] = g_b_out
    vec[3:4, :] = g_gain_one
    vec[4:5, :] = g_shift_one
    vec[5:6, :] = g_b_down
    vec[6:7, :] = g_gain_two
    vec[7:8, :] = g_shift_two
    vec[8:16, :] = jnp.zeros((8, 768), F32)
    R.VUP[0:1, :] = g_b_up

    for g in range(4):
        R.GO[g] = mm_tn(unpack(R.AT[g]), R.DH1[...].astype(BF)).reshape(4, 2, 24, 768)
    send(R.GO.at[:, :, other], R.RO, SEMS.foc, 0, mate)

    arrived(R.RU, SEMS.fuc, 0, mate)
    for i, g in enumerate((near, turn(near, 2))):
        R.SU[i] = (R.GU[g, :, c] + R.RU[g]).astype(BF)
    send(R.SU, R.RU1, SEMS.fuz, 0, there)

    def relay_down_grad():
        arrived(R.RD1, SEMS.fdz, 0, there)
        R.SD2[...] = (R.GD[across, c] + R.RD[across] + R.RD1[1].astype(F32)).astype(BF)
        send(R.SD2, R.RD2, SEMS.fdz, 1, dev(across, p, c))

    def relay_up_grad():
        arrived(R.RU1, SEMS.fuz, 0, there)
        R.SU2[...] = (R.GU[across, :, c] + R.RU[across] + R.RU1[1].astype(F32)).astype(BF)
        send(R.SU2, R.RU2, SEMS.fuz, 1, dev(across, p, c))

    arrived(R.RO, SEMS.foc, 0, mate)
    for g in range(4):
        R.SO[g] = (R.GO[g, :, c] + R.RO[g]).astype(BF)
    for k in range(1, 4):
        to = turn(p, k)
        send(R.SO.at[:, to], R.ROP.at[p], SEMS.fop, k - 1, dev(u, to, c))
    settle(SEMS.fdc, SEMS.fuc, SEMS.qs, SEMS.dg)
    vec[0:2, :] = jnp.zeros((2, 768), F32)
    choose = jnp.where(
        rows_by((32, 24, 16), 1, (768, 16)) == lax.broadcasted_iota(jnp.int32, (768, 16), 1), 1.0, 0.0
    ).astype(BF)
    laid = jnp.where(owner == lane_owner, mm(choose, vec[...].astype(BF)), 0.0)
    laid = jnp.where(row_id == up_row, R.VUP[0:1, :], laid)
    R.MR[...] = mm(laid.astype(BF), spread)
    R.T1[...] = R.XG[...].reshape(512, 768).T
    for half in range(2):
        for k in range(1, 4):
            src = turn(u, k)
            arrived(R.DA.at[src, half], SEMS.da, 4 * half + k, dev(src, s, c))

        @pl.when(far)
        def _():
            arrived(R.DA.at[u, half], SEMS.da, 4 * half, dev(u, s, c))

    d_rows = [open_half(R.DA[r, half]) for r in range(4) for half in range(2)]
    d_rows = jnp.concatenate(d_rows, axis=0).astype(F32)
    for h in range(3):
        d_attn = d_rows[:, 64 * h : 64 * h + 64].T
        scaled = (d_attn / R.DEN[h, 0:1, :]).astype(BF)
        R.DLT[h, 0:1, :] = jnp.sum(scaled.astype(F32) * R.ATN[h], axis=0, keepdims=True)
        R.GP[h, :, :, 64:128] = scaled.T.reshape(4, 128, 64)

    def block_copy(t):
        j = order(t)
        there_slot = 0 if t == 1 else 1
        return copy(
            R.DKS.at[j], R.DKR.at[4 - j], there_slot, SEMS.dk + there_slot, block_dev(a + j - 2)
        )

    def key_copy(t, h):
        j = order(t)
        if t == 2:
            return copy(R.DKS.at[j, h], R.DKX.at[h], 2 + h, SEMS.dx + h, mate)
        return copy(
            R.DKS.at[j, h], R.DKR.at[4 - j, h], 5 + h, SEMS.dk + 2 + h, block_dev(a + j - 2)
        )

    def backward_block(t):
        j = order(t)
        ok = jnp.logical_and(a + j >= 2, a + j < 10)

        @pl.when(ok)
        def _():
            def head(h, inner):
                lanes = pl.ds(pl.multiple_of(128 * h, 128), 128)
                at = 3 * j + h
                grad_rows = R.GP[h].reshape(512, 128)
                shift = R.DLT[h, 0:1, :]
                kv = R.KV[j, :, :, lanes].reshape(512, 128)
                for r in range(512 // BWD_ROWS):
                    rows = slice(BWD_ROWS * r, BWD_ROWS * r + BWD_ROWS)
                    d_prob = mm_nt(kv[rows], grad_rows)
                    R.DST[rows, :] = (R.EL[at, rows, :].astype(F32) * (d_prob - shift)).astype(BF)
                d_kv = mm(R.DST[...], R.QP[h].reshape(512, 128)) + mm(R.EL[at], grad_rows)
                if t == 0:
                    R.DKO[h] = d_kv
                elif t == 3:
                    arrived(R.DKX.at[h], SEMS.dx, h, mate)
                    R.DKS[j, h] = (d_kv + R.DKX[h].astype(F32)).astype(BF)
                else:
                    R.DKS[j, h] = d_kv.astype(BF)
                if t == 2 or t == 3:
                    key_copy(t, h).start()
                R.DQT[h] += mm(R.KVT[at, 0:64, :], R.DST[...])
                return inner

            lax.fori_loop(0, 3, head, 0)
            if t == 4 or t == 1:
                block_copy(t).start()

    backward_block(4)
    relay_down_grad()
    backward_block(2)
    backward_block(3)
    relay_up_grad()
    backward_block(1)
    backward_block(0)

    def at_lanes(n, value):
        R.G1[:, :, :, :, 128 * n : 128 * n + 128] = value.reshape(4, 4, 2, 24, 128)

    def query_grads():
        for n in (3, 4):
            value = mm(R.T1[...], R.DQ[:, 128 * n : 128 * n + 128])
            if n == 4:
                value = jnp.concatenate([value[:, 0:64], R.MR[...]], axis=1)
            at_lanes(n, value)

    def key_grads():
        for n in range(3):
            at_lanes(n, mm(R.T1[...], R.DQ[:, 128 * n : 128 * n + 128]))
        sums = mm(jnp.ones((8, 512), BF), R.DQ[...])[0:1]
        sum_v = jnp.concatenate([sums[:, 128 * h + 64 : 128 * h + 128] for h in range(3)], axis=1)
        row = lax.broadcasted_iota(jnp.int32, (192, 192), 0)
        lane_row = 24 * lane_owner[:, 0:192]
        laid = jnp.where(row == lane_row, sums[:, 384:576], jnp.where(row == lane_row + 1, sum_v, 0.0))
        extra = mm(laid.astype(BF), spread[0:192])
        extra = jnp.concatenate([jnp.zeros((192, 64), F32), extra], axis=1)
        R.G1[u, :, :, :, 512:640] += extra.reshape(4, 2, 24, 128)
        send(R.G1.at[:, :, other], R.R1, SEMS.f1c, 0, mate)

    for h in range(3):
        R.DQ[:, 384 + 64 * h : 448 + 64 * h] = (R.DQT[h] * 0.125).T.astype(BF)
    R.DQ[:, 576:640] = jnp.zeros((512, 64), BF)
    query_grads()
    for t in (1, 3, 4):
        j = order(t)

        @pl.when(jnp.logical_and(a + j >= 2, a + j < 10))
        def _():
            if t != 4:
                arrived(R.DKR.at[j], SEMS.dk, 0 if t == 1 else 1, block_dev(a + j - 2))
            for h in range(3):
                if t == 4:
                    arrived(R.DKR.at[j, h], SEMS.dk, 2 + h, block_dev(a + j - 2))
                R.DKO[h] += R.DKR[j, h].astype(F32)

    for h in range(3):
        R.DQ[:, 128 * h : 128 * h + 128] = R.DKO[h].astype(BF)
    key_grads()

    settle(SEMS.qs)
    def input_part(k):
        rows = pl.ds(pl.multiple_of(128 * turn(u, k), 128), 128)
        return mm_nt(R.DQ[rows, :], R.W2[...])

    R.PS[3] = input_part(3).astype(BF)
    send(R.PS.at[3], R.XN, SEMS.x, 3, there)
    R.PS[1] = input_part(1).astype(BF)
    send(R.PS.at[1], R.PR.at[1], SEMS.x, 1, there)
    R.Y1[...] = input_part(0)
    R.H2[...] = input_part(2)
    arrived(R.R1, SEMS.f1c, 0, mate)
    for g in range(4):
        R.H1[g] = (R.G1[g, :, c] + R.R1[g]).astype(BF)
    for k in range(1, 4):
        to = turn(p, k)
        send(R.H1.at[:, to], R.R1P.at[p], SEMS.f1p, k - 1, dev(u, to, c))
    arrived(R.RD2, SEMS.fdz, 1, dev(across, p, c))
    R.t_dn[...] = R.GD[u, c] + R.RD[u] + R.RD1[0].astype(F32) + R.RD2[...].astype(F32)
    leave("t_dn")
    arrived(R.RU2, SEMS.fuz, 1, dev(across, p, c))
    R.TU[...] = (R.GU[u, :, c] + R.RU[u] + R.RU1[0].astype(F32) + R.RU2[...].astype(F32)).astype(BF)
    R.RUP[p] = R.TU[p]
    for k in range(1, 4):
        to = turn(p, k)
        send(R.TU.at[to], R.RUP.at[p], SEMS.fup, k - 1, dev(u, to, c))

    arrived(R.XN, SEMS.x, 3, there)
    R.PS[2] = (R.H2[...] + R.XN[...].astype(F32)).astype(BF)
    send(R.PS.at[2], R.PR.at[2], SEMS.x, 2, dev(across, s, c))
    for k in range(1, 4):
        src = turn(p, k)
        arrived(R.ROP.at[src], SEMS.fop, k - 1, dev(u, src, c))
    for g in range(4):
        total = R.GO[g, p, c] + R.RO[g, p]
        for k in range(1, 4):
            total = total + R.ROP[turn(p, k), g].astype(F32)
        R.TO[g] = total.astype(BF)
    for k in range(1, 4):
        to = turn(u, k)
        send(R.TO.at[to], R.ROZ.at[u], SEMS.foz, k - 1, dev(to, p, c))
    arrived(R.PR.at[1], SEMS.x, 1, there)
    R.Y1[...] += R.PR[1].astype(F32)

    @pl.when(far)
    def _():
        R.PS[0] = R.Y1[...].astype(BF)

    send_if(far, R.PS.at[0], R.PR.at[0], SEMS.x, 0, dev(u, s, c))
    for k in range(1, 4):
        src = turn(p, k)
        arrived(R.R1P.at[src], SEMS.f1p, k - 1, dev(u, src, c))
    total = R.G1[:, p, c] + R.R1[:, p]
    for k in range(1, 4):
        total = total + R.R1P[turn(p, k)].astype(F32)
    R.S1[...] = total.astype(BF)
    for k in range(1, 4):
        to = turn(u, k)
        send(R.S1.at[to], R.R1Z.at[u], SEMS.f1z, k - 1, dev(to, p, c))
    R.R1Z[u] = R.S1[u]
    for k in range(1, 4):
        src = turn(u, k)
        arrived(R.ROZ.at[src], SEMS.foz, k - 1, dev(src, p, c))
    total = R.TO[u].astype(F32)
    for k in range(1, 4):
        total = total + R.ROZ[turn(u, k)].astype(F32)
    R.t_ow[...] = total
    leave("t_ow")
    for k in range(1, 4):
        src = turn(p, k)
        arrived(R.RUP.at[src], SEMS.fup, k - 1, dev(u, src, c))
    R.t_up[...] = R.RUP[...]
    leave("t_up")
    arrived(R.PR.at[2], SEMS.x, 2, dev(across, s, c))

    @pl.when(far)
    def _():
        arrived(R.PR.at[0], SEMS.x, 0, dev(u, s, c))
        R.Y1[...] = R.PR[0].astype(F32)

    total = R.DH1[...] + R.Y1[...] + R.PR[2].astype(F32)
    R.t_in[...] = total
    leave("t_in")
    for k in range(1, 4):
        src = turn(u, k)
        arrived(R.R1Z.at[src], SEMS.f1z, k - 1, dev(src, p, c))
    R.t_qkv[...] = R.R1Z[...]
    leave("t_qkv")
    settle()
    for out in leaving:
        out.wait()
    for t in range(1, 5):
        j = order(t)

        @pl.when(jnp.logical_and(a + j >= 2, a + j < 10))
        def _():
            if t == 4 or t == 1:
                block_copy(t).wait_send()
            else:
                for h in range(3):
                    key_copy(t, h).wait_send()


def finish_kernel(*refs):
    R = Refs()
    for name, ref in zip([*RAW, *OUTS], refs, strict=True):
        setattr(R, name, ref)
    R.o_out[...] = R.t_out[...]
    R.o_in[...] = R.t_in[...]
    R.o_dnw[...] = R.t_dn[...]
    R.o_ow[...] = R.t_ow[...]
    for q in range(4):
        piece = R.t_up[q].astype(F32)
        for g in range(4):
            R.o_upw[:, 768 * g + 192 * q : 768 * g + 192 * q + 192] = piece[:, 192 * g : 192 * g + 192]
    small = jnp.zeros((24, 64), F32)
    for g in range(4):
        piece = R.t_qkv[g].astype(F32)
        at = 192 * g
        R.o_kw[:, at : at + 192] = jnp.concatenate([piece[:, 128 * h : 128 * h + 64] for h in range(3)], axis=1)
        R.o_vw[:, at : at + 192] = jnp.concatenate([piece[:, 128 * h + 64 : 128 * h + 128] for h in range(3)], axis=1)
        R.o_qw[:, at : at + 192] = piece[:, 384:576]
        small = small + piece[:, 576:640]
    for row, name in enumerate(SMALL):
        getattr(R, "o_" + name)[...] = small[row : row + 1, 0:24].reshape(24)
    R.o_upb[...] = jnp.concatenate([small[8 + i : 9 + i, 0:24] for i in range(4)], axis=1).reshape(96)


def fused_step(*args):
    vmem = pl.BlockSpec(memory_space=pltpu.VMEM)
    raw = pl.pallas_call(
        layer_kernel,
        out_shape=[jax.ShapeDtypeStruct(shape, dtype) for shape, dtype in RAW.values()],
        in_specs=[pl.BlockSpec(memory_space=pltpu.SMEM) if n == "starts" else vmem for n in ARGS],
        out_specs=[pl.BlockSpec(memory_space=pl.ANY)] * len(RAW),
        scratch_shapes=[pltpu.VMEM(shape, dtype) for shape, dtype in (RAW | SCRATCH).values()]
        + [pltpu.SemaphoreType.DMA((n,)) for n in (SEND_SLOTS, SEMS.total, len(RAW))],
        compiler_params=pltpu.CompilerParams(
            collective_id=0, has_side_effects=True, vmem_limit_bytes=63 << 20
        ),
        name="layer_step",
    )(*args)
    return pl.pallas_call(
        finish_kernel,
        out_shape=[jax.ShapeDtypeStruct(shape, dtype) for shape, dtype in OUTS.values()],
        in_specs=[vmem] * len(RAW),
        out_specs=[vmem] * len(OUTS),
        name="finish",
    )(*raw)


def solution(mesh):
    fused = mesh.shape[ULYSSES] == 4 and mesh.shape[BLK] == 8
    return jax.shard_map(
        fused_step if fused else per_device,
        mesh=mesh,
        in_specs=(
            P(TOKEN_AXES, None),
            P(TOKEN_AXES, None),
            P(),
            P(WEIGHT_AXES, None),
            P(WEIGHT_AXES, None),
            P(WEIGHT_AXES, None),
            P(WEIGHT_AXES),
            P(WEIGHT_AXES),
            P(WEIGHT_AXES, None),
            P(WEIGHT_AXES),
            P(WEIGHT_AXES),
            P(WEIGHT_AXES),
            P(WEIGHT_AXES, None),
            P(WEIGHT_AXES),
            P(WEIGHT_AXES, None),
            P(WEIGHT_AXES),
            P(WEIGHT_AXES),
            P(WEIGHT_AXES),
        ),
        out_specs=(
            P(TOKEN_AXES, None),
            P(TOKEN_AXES, None),
            P(WEIGHT_AXES, None),
            P(WEIGHT_AXES, None),
            P(WEIGHT_AXES, None),
            P(WEIGHT_AXES),
            P(WEIGHT_AXES),
            P(WEIGHT_AXES, None),
            P(WEIGHT_AXES),
            P(WEIGHT_AXES),
            P(WEIGHT_AXES),
            P(WEIGHT_AXES, None),
            P(WEIGHT_AXES),
            P(WEIGHT_AXES, None),
            P(WEIGHT_AXES),
            P(WEIGHT_AXES),
            P(WEIGHT_AXES),
        ),
        check_vma=False,
    )
```

```python
import jax
import jax.numpy as jnp
from jax import lax
from jax.experimental import pallas as pl
from jax.experimental.pallas import tpu as pltpu
from jax.sharding import PartitionSpec as P

HD = 64
ULYSSES = "ulysses"
BLK = "blk"
WEIGHT_AXES = (ULYSSES, BLK)
TOKEN_AXES = (BLK, ULYSSES)


SCALE = 0.125
EPS = 1e-12


def passed_along(shard, axis, by):
    length = lax.axis_size(axis)
    return lax.ppermute(shard, axis, [(i, (i + by) % length) for i in range(length)])


def layer_norm(hidden, gain, shift):
    middle = jnp.mean(hidden, axis=-1, keepdims=True)
    centered = hidden - middle
    spread = jnp.mean(centered * centered, axis=-1, keepdims=True)
    return centered * lax.rsqrt(spread + EPS) * gain + shift


def gelu_exact(values):
    return jax.nn.gelu(values, approximate=False)


def doc_ids(doc_starts, positions):
    return jnp.sum((doc_starts[None, :] <= positions[:, None]).astype(jnp.int32), axis=1)


def project(left, right):
    return jnp.dot(left, right, preferred_element_type=jnp.float32)


def project_back(left, right):
    return lax.dot_general(
        left, right, (((1,), (1,)), ((), ())), preferred_element_type=jnp.float32
    )


def outer_sum(left, right):
    return lax.dot_general(
        left, right, (((0,), (0,)), ((), ())), preferred_element_type=jnp.float32
    )


def per_device(
    tokens,
    cotangent,
    doc_starts,
    q_weight,
    k_weight,
    v_weight,
    q_bias,
    v_bias,
    o_weight,
    o_bias,
    norm1_gain,
    norm1_bias,
    up_weight,
    up_bias,
    down_weight,
    down_bias,
    norm2_gain,
    norm2_bias,
):
    f32 = jnp.float32
    bf16 = jnp.bfloat16
    w_query, w_key, w_value, b_query, b_value, w_out, b_out, gain_one, shift_one = (
        lax.all_gather(q_weight, WEIGHT_AXES, axis=0, tiled=True),
        lax.all_gather(k_weight, WEIGHT_AXES, axis=0, tiled=True),
        lax.all_gather(v_weight, WEIGHT_AXES, axis=0, tiled=True),
        lax.all_gather(q_bias, WEIGHT_AXES, axis=0, tiled=True),
        lax.all_gather(v_bias, WEIGHT_AXES, axis=0, tiled=True),
        lax.all_gather(o_weight, WEIGHT_AXES, axis=0, tiled=True),
        lax.all_gather(o_bias, WEIGHT_AXES, axis=0, tiled=True),
        lax.all_gather(norm1_gain, WEIGHT_AXES, axis=0, tiled=True),
        lax.all_gather(norm1_bias, WEIGHT_AXES, axis=0, tiled=True),
    )
    w_up, b_up, w_down, b_down, gain_two, shift_two = (
        lax.all_gather(up_weight, WEIGHT_AXES, axis=0, tiled=True),
        lax.all_gather(up_bias, WEIGHT_AXES, axis=0, tiled=True),
        lax.all_gather(down_weight, WEIGHT_AXES, axis=0, tiled=True),
        lax.all_gather(down_bias, WEIGHT_AXES, axis=0, tiled=True),
        lax.all_gather(norm2_gain, WEIGHT_AXES, axis=0, tiled=True),
        lax.all_gather(norm2_bias, WEIGHT_AXES, axis=0, tiled=True),
    )
    query_tok = (project(tokens, w_query) + b_query.astype(f32)).astype(bf16)
    key_tok = project(tokens, w_key).astype(bf16)
    value_tok = (project(tokens, w_value) + b_value.astype(f32)).astype(bf16)
    query_heads, key_heads, value_heads = (
        lax.all_to_all(query_tok, ULYSSES, split_axis=1, concat_axis=0, tiled=True),
        lax.all_to_all(key_tok, ULYSSES, split_axis=1, concat_axis=0, tiled=True),
        lax.all_to_all(value_tok, ULYSSES, split_axis=1, concat_axis=0, tiled=True),
    )
    group = query_heads.shape[0]
    columns = query_heads.shape[1]
    local_heads = columns // HD
    block_count = lax.axis_size(BLK)
    total = group * block_count
    doc_max = min(8192, total // 4, 8 * group)
    reach = (group - 2 + doc_max) // group
    visits = 2 * reach + 1
    block_index = lax.axis_index(BLK)
    rows = jnp.arange(group, dtype=jnp.int32)
    query_ids = doc_ids(doc_starts, block_index * group + rows)
    query3 = query_heads.reshape(group, local_heads, HD)

    def block_mask(offset):
        key_pos = (block_index + offset) * group + rows
        inside = (key_pos >= 0) & (key_pos < total)
        key_ids = jnp.where(inside, doc_ids(doc_starts, key_pos), -1)
        allowed = query_ids[:, None] == key_ids[None, :]
        shared = (
            inside[0] & (key_ids[0] <= query_ids[group - 1]) & (key_ids[group - 1] >= query_ids[0])
        )
        return (allowed, shared)

    def exp_scores(pair, allowed):
        key3 = pair[0].reshape(group, local_heads, HD)
        scores = jnp.einsum("qhd,khd->hqk", query3, key3, preferred_element_type=f32) * SCALE
        return jnp.where(allowed[None], jnp.exp(scores), 0.0)

    def forward_terms(pair, offset):
        allowed, shared = block_mask(offset)
        weights = exp_scores(pair, allowed)
        value3 = pair[1].reshape(group, local_heads, HD)
        numer = jnp.einsum("hqk,khd->qhd", weights.astype(bf16), value3, preferred_element_type=f32)
        return (numer, jnp.sum(weights, axis=2))

    pair_own = jnp.stack([key_heads, value_heads])
    pair = passed_along(pair_own, BLK, -reach)
    numer, denom = forward_terms(pair, reach)
    store = jnp.zeros((1,), bf16)

    def forward_step(step, carry):
        pair_now, numer_now, denom_now, store_now = carry
        pair_now = passed_along(pair_now, BLK, 1)
        more_numer, more_denom = forward_terms(pair_now, reach - step)
        return (pair_now, numer_now + more_numer, denom_now + more_denom, store_now)

    pair, numer, denom, store = lax.fori_loop(1, visits, forward_step, (pair, numer, denom, store))
    attn_f = numer / jnp.transpose(denom)[:, :, None]
    attn_b = attn_f.reshape(group, columns).astype(bf16)
    attn_tok = lax.all_to_all(attn_b, ULYSSES, split_axis=0, concat_axis=1, tiled=True)
    token_f = tokens.astype(f32)
    h_one = token_f + project(attn_tok, w_out) + b_out.astype(f32)
    y_one, norm_one_back = jax.vjp(layer_norm, h_one, gain_one.astype(f32), shift_one.astype(f32))
    y_one_b = y_one.astype(bf16)
    pre_act = project(y_one_b, w_up) + b_up.astype(f32)
    act, gelu_back = jax.vjp(gelu_exact, pre_act)
    act_b = act.astype(bf16)
    h_two = y_one + project(act_b, w_down) + b_down.astype(f32)
    out_f, norm_two_back = jax.vjp(layer_norm, h_two, gain_two.astype(f32), shift_two.astype(f32))
    layer_out = out_f.astype(bf16)
    d_two, g_gain_two, g_shift_two = norm_two_back(cotangent.astype(f32))
    g_b_down = jnp.sum(d_two, axis=0)
    d_two_b = d_two.astype(bf16)
    g_w_down = outer_sum(act_b, d_two_b)
    d_act = project_back(d_two_b, w_down)
    d_pre = gelu_back(d_act)[0].astype(bf16)
    g_b_up = jnp.sum(d_pre.astype(f32), axis=0)
    g_w_up = outer_sum(y_one_b, d_pre)
    d_y_one = d_two + project_back(d_pre, w_up)
    d_one, g_gain_one, g_shift_one = norm_one_back(d_y_one)
    g_b_out = jnp.sum(d_one, axis=0)
    d_one_b = d_one.astype(bf16)
    g_w_out = outer_sum(attn_tok, d_one_b)
    d_attn_tok = project_back(d_one_b, w_out).astype(bf16)
    d_attn = lax.all_to_all(d_attn_tok, ULYSSES, split_axis=1, concat_axis=0, tiled=True)
    d_attn3 = d_attn.reshape(group, local_heads, HD)
    d_attn_f = d_attn3.astype(f32)
    delta = jnp.transpose(jnp.sum(d_attn_f * attn_f, axis=2))
    scaled_grad = d_attn_f / jnp.transpose(denom)[:, :, None]
    grad_high = scaled_grad.astype(bf16)
    grad_rest = (scaled_grad - grad_high.astype(f32)).astype(bf16)

    def backward_terms(pair_in, offset):
        allowed, shared = block_mask(offset)
        weights = exp_scores(pair_in, allowed)
        key3 = pair_in[0].reshape(group, local_heads, HD)
        value3 = pair_in[1].reshape(group, local_heads, HD)
        probs = weights / denom[:, :, None]
        d_prob = jnp.einsum("qhd,khd->hqk", d_attn3, value3, preferred_element_type=f32)
        d_score = (probs * (d_prob - delta[:, :, None]) * SCALE).astype(bf16)
        d_query = jnp.einsum("hqk,khd->qhd", d_score, key3, preferred_element_type=f32)
        d_key = jnp.einsum("hqk,qhd->khd", d_score, query3, preferred_element_type=f32)
        weights_low = weights.astype(bf16)
        d_value = jnp.einsum(
            "hqk,qhd->khd", weights_low, grad_high, preferred_element_type=f32
        ) + jnp.einsum("hqk,qhd->khd", weights_low, grad_rest, preferred_element_type=f32)
        return (d_query, jnp.stack([d_key, d_value]))

    pair = passed_along(pair_own, BLK, -reach)
    d_query_sum, carried = backward_terms(pair, reach)

    def backward_step(step, carry):
        pair_now, d_query_now, carried_now = carry
        pair_now = passed_along(pair_now, BLK, 1)
        more_query, more_kv = backward_terms(pair_now, reach - step)
        carried_now = (
            passed_along(carried_now.astype(jnp.bfloat16), BLK, 1).astype(carried_now.dtype)
            + more_kv
        )
        return (pair_now, d_query_now + more_query, carried_now)

    pair, d_query_sum, carried = lax.fori_loop(
        1, visits, backward_step, (pair, d_query_sum, carried)
    )
    own_grads = passed_along(carried.astype(jnp.bfloat16), BLK, -reach).astype(carried.dtype)
    d_query_b = d_query_sum.reshape(group, columns).astype(bf16)
    d_key_b = own_grads[0].reshape(group, columns).astype(bf16)
    d_value_b = own_grads[1].reshape(group, columns).astype(bf16)
    dq_tok, dk_tok, dv_tok = (
        lax.all_to_all(d_query_b, ULYSSES, split_axis=0, concat_axis=1, tiled=True),
        lax.all_to_all(d_key_b, ULYSSES, split_axis=0, concat_axis=1, tiled=True),
        lax.all_to_all(d_value_b, ULYSSES, split_axis=0, concat_axis=1, tiled=True),
    )
    g_b_query = jnp.sum(dq_tok.astype(f32), axis=0)
    g_b_value = jnp.sum(dv_tok.astype(f32), axis=0)
    g_w_query = outer_sum(tokens, dq_tok)
    g_w_key = outer_sum(tokens, dk_tok)
    g_w_value = outer_sum(tokens, dv_tok)
    input_grad = (
        d_one
        + project_back(dq_tok, w_query)
        + project_back(dk_tok, w_key)
        + project_back(dv_tok, w_value)
    )
    shares = (
        lax.psum_scatter(g_w_query, WEIGHT_AXES, scatter_dimension=0, tiled=True),
        lax.psum_scatter(g_w_key, WEIGHT_AXES, scatter_dimension=0, tiled=True),
        lax.psum_scatter(g_w_value, WEIGHT_AXES, scatter_dimension=0, tiled=True),
        lax.psum_scatter(g_b_query, WEIGHT_AXES, scatter_dimension=0, tiled=True),
        lax.psum_scatter(g_b_value, WEIGHT_AXES, scatter_dimension=0, tiled=True),
        lax.psum_scatter(g_w_out, WEIGHT_AXES, scatter_dimension=0, tiled=True),
        lax.psum_scatter(g_b_out, WEIGHT_AXES, scatter_dimension=0, tiled=True),
        lax.psum_scatter(g_gain_one, WEIGHT_AXES, scatter_dimension=0, tiled=True),
        lax.psum_scatter(g_shift_one, WEIGHT_AXES, scatter_dimension=0, tiled=True),
        lax.psum_scatter(g_w_up, WEIGHT_AXES, scatter_dimension=0, tiled=True),
        lax.psum_scatter(g_b_up, WEIGHT_AXES, scatter_dimension=0, tiled=True),
        lax.psum_scatter(g_w_down, WEIGHT_AXES, scatter_dimension=0, tiled=True),
        lax.psum_scatter(g_b_down, WEIGHT_AXES, scatter_dimension=0, tiled=True),
        lax.psum_scatter(g_gain_two, WEIGHT_AXES, scatter_dimension=0, tiled=True),
        lax.psum_scatter(g_shift_two, WEIGHT_AXES, scatter_dimension=0, tiled=True),
    )
    return (
        layer_out,
        input_grad,
        shares[0],
        shares[1],
        shares[2],
        shares[3],
        shares[4],
        shares[5],
        shares[6],
        shares[7],
        shares[8],
        shares[9],
        shares[10],
        shares[11],
        shares[12],
        shares[13],
        shares[14],
    )


MESH = pl.DeviceIdType.MESH
LOG2E = 1.4426950408889634
RSQRT2 = 0.7071067811865476
FWD_ROWS = 256
BWD_ROWS = 256
KEY_SENDS = 8
SEND_SLOTS = 62
PDF0 = 0.3989422804014327

ARGS = ("tok", "cot", "starts", "qw", "kw", "vw", "qb", "vb", "ow", "ob", "g1", "b1", "upw", "upb", "dnw", "dnb", "g2", "b2")
OUTS = dict(
    o_out=((128, 768), jnp.bfloat16),
    o_in=((128, 768), jnp.float32),
    o_qw=((24, 768), jnp.float32),
    o_kw=((24, 768), jnp.float32),
    o_vw=((24, 768), jnp.float32),
    o_qb=((24,), jnp.float32),
    o_vb=((24,), jnp.float32),
    o_ow=((24, 768), jnp.float32),
    o_ob=((24,), jnp.float32),
    o_g1=((24,), jnp.float32),
    o_b1=((24,), jnp.float32),
    o_upw=((24, 3072), jnp.float32),
    o_upb=((96,), jnp.float32),
    o_dnw=((96, 768), jnp.float32),
    o_dnb=((24,), jnp.float32),
    o_g2=((24,), jnp.float32),
    o_b2=((24,), jnp.float32),
)
RAW = dict(
    t_out=((128, 768), jnp.bfloat16),
    t_in=((128, 768), jnp.float32),
    t_qkv=((4, 24, 640), jnp.bfloat16),
    t_up=((4, 24, 768), jnp.bfloat16),
    t_dn=((96, 768), jnp.float32),
    t_ow=((24, 768), jnp.float32),
)
SMALL = ("qb", "vb", "ob", "g1", "b1", "dnb", "g2", "b2")
BF = jnp.bfloat16
F32 = jnp.float32
SCRATCH = dict(
    SM=((24, 128), F32),
    WS=((4, 24, 640), BF),
    W5=((4, 4, 2, 24, 640), BF),
    W2=((768, 640), BF),
    US=((4, 24, 768), BF),
    UP5=((4, 4, 2, 24, 768), BF),
    UP2=((768, 768), BF),
    DN4=((4, 2, 96, 768), BF),
    OW5=((4, 4, 2, 24, 768), BF),
    OW2=((768, 768), BF),
    XG=((4, 2, 64, 768), BF),
    KV=((5, 4, 128, 384), BF),
    KVT=((15, 144, 512), BF),
    QP=((3, 4, 128, 128), BF),
    GP=((3, 4, 128, 128), BF),
    SEGK=((5, 512, 128), BF),
    EL=((15, 512, 512), BF),
    DST=((512, 512), BF),
    NUM=((3, 80, 512), F32),
    DEN=((3, 8, 512), F32),
    ATN=((3, 64, 512), F32),
    DLT=((3, 8, 512), F32),
    AS=((4, 192, 128), BF),
    AT=((4, 192, 128), BF),
    Y1=((128, 768), F32),
    N1=((128, 768), F32),
    RSD=((128, 128), F32),
    YG=((4, 128, 768), BF),
    ACT=((4, 128, 768), BF),
    GG=((4, 128, 768), BF),
    PS=((4, 128, 768), BF),
    PR=((4, 128, 768), BF),
    XN=((128, 768), BF),
    H2=((128, 768), F32),
    DH2=((128, 768), F32),
    DG=((4, 128, 768), BF),
    DU=((4, 128, 768), BF),
    DH1=((128, 768), F32),
    DAS=((4, 2, 96, 128), BF),
    DA=((4, 2, 96, 128), BF),
    T1=((768, 512), BF),
    MR=((768, 64), F32),
    DKS=((5, 3, 512, 128), BF),
    DKX=((3, 512, 128), BF),
    DKR=((5, 3, 512, 128), BF),
    DKO=((3, 512, 128), F32),
    DQT=((3, 64, 512), F32),
    DQ=((512, 640), BF),
    VEC=((16, 768), F32),
    VUP=((8, 768), F32),
    G1=((4, 4, 2, 24, 640), F32),
    R1=((4, 4, 24, 640), F32),
    H1=((4, 4, 24, 640), BF),
    R1P=((4, 4, 24, 640), BF),
    S1=((4, 24, 640), BF),
    R1Z=((4, 24, 640), BF),
    GU=((4, 4, 2, 24, 768), F32),
    RU=((4, 4, 24, 768), F32),
    SU=((2, 4, 24, 768), BF),
    RU1=((2, 4, 24, 768), BF),
    SU2=((4, 24, 768), BF),
    RU2=((4, 24, 768), BF),
    TU=((4, 24, 768), BF),
    RUP=((4, 24, 768), BF),
    GD=((4, 2, 96, 768), F32),
    RD=((4, 96, 768), F32),
    SD=((2, 96, 768), BF),
    RD1=((2, 96, 768), BF),
    SD2=((96, 768), BF),
    RD2=((96, 768), BF),
    GO=((4, 4, 2, 24, 768), F32),
    RO=((4, 4, 24, 768), F32),
    SO=((4, 4, 24, 768), BF),
    ROP=((4, 4, 24, 768), BF),
    TO=((4, 24, 768), BF),
    ROZ=((4, 24, 768), BF),
)


class Slots:
    def __init__(self, **sizes):
        self.total = 0
        for name, size in sizes.items():
            setattr(self, name, self.total)
            self.total += size

    def again(self, start, **sizes):
        for name, size in sizes.items():
            setattr(self, name, start)
            start += size
        return start


SEMS = Slots(
    tok=6, hop=2, wz=3, wp=3, wc=1, us=3, kv=7, oz=3, spare=10, cow=1, cup=1, cdn=1, op=3, upz=3, dnz=3,
    at=4, yg=6, ps=6, fdz=2, foz=3,
)
END = SEMS.again(
    SEMS.tok, da=8, dk=5, dx=3, x=4, f1c=1, f1p=3, f1z=3, fuc=1, fuz=2, fup=3, fdc=1, foc=1, fop=3
)
assert END <= SEMS.cow
SEMS.again(SEMS.yg, dg=6, qs=6)


def mm(left, right):
    return jnp.dot(left, right, preferred_element_type=F32)


def mm_nt(left, right):
    return lax.dot_general(left, right, (((1,), (1,)), ((), ())), preferred_element_type=F32)


def mm_tn(left, right):
    return lax.dot_general(left, right, (((0,), (0,)), ((), ())), preferred_element_type=F32)


def pack(rows):
    tail = rows[:, 128:192]
    return jnp.concatenate([rows[:, 0:128], jnp.concatenate([tail[0:64], tail[64:128]], axis=1)], axis=0)


def unpack(packed):
    tail = packed[128:192]
    tail = jnp.concatenate([tail[:, 0:64], tail[:, 64:128]], axis=0)
    return jnp.concatenate([packed[0:128], tail], axis=1)


def unpack_half(packed, i):
    return jnp.concatenate([packed[64 * i : 64 * i + 64], packed[128:192, 64 * i : 64 * i + 64]], axis=1)


def pack_half(rows):
    tail = rows[:, 128:192]
    return jnp.concatenate([rows[:, 0:128], jnp.concatenate([tail[0:32], tail[32:64]], axis=1)], axis=0)


def open_half(packed):
    tail = packed[64:96]
    tail = jnp.concatenate([tail[:, 0:64], tail[:, 64:128]], axis=0)
    return jnp.concatenate([packed[0:64], tail], axis=1)


def rows_by(shape, axis, flat):
    return lax.broadcasted_iota(jnp.int32, shape, axis).reshape(flat)


class Refs:
    pass


def layer_kernel(*refs):
    R = Refs()
    names = [*ARGS, *("g" + n for n in RAW), *RAW, *SCRATCH, "SS", "RS", "LS"]
    for name, ref in zip(names, refs, strict=True):
        setattr(R, name, ref)
    u = lax.axis_index(ULYSSES)
    b = lax.axis_index(BLK)
    c = lax.rem(b, 2)
    p = lax.div(b, 2)
    other = 1 - c

    def snake(at):
        return at + lax.div(at, 2) * (1 - 2 * lax.rem(at, 2))

    s = snake(p)
    a = 2 * s + c
    far = p >= 2

    def dev(uu, pp, cc):
        return (uu, 2 * pp + cc)

    def block_dev(aa):
        return dev(u, snake(lax.div(aa, 2)), lax.rem(aa, 2))

    def turn(base, k):
        low, high = lax.rem(base, 2), lax.div(base, 2)
        if k % 2:
            low = 1 - low
        if k // 2:
            high = 1 - high
        return 2 * high + low

    sends = []
    free = list(range(KEY_SENDS, SEND_SLOTS))

    def copy(src, dst, slot, ri, device):
        return pltpu.make_async_remote_copy(
            src_ref=src, dst_ref=dst, send_sem=R.SS.at[slot], recv_sem=R.RS.at[ri],
            device_id=device, device_id_type=MESH,
        )

    def send(src, dst, name, ri, device, cond=None):
        slot = free.pop(0)
        desc = copy(src, dst, slot, name + ri, device)
        if cond is None:
            desc.start()
        else:

            @pl.when(cond)
            def _():
                desc.start()

        sends.append((name, cond, desc, slot))

    def send_if(cond, *what):
        send(*what, cond=cond)

    leaving = []

    def leave(name):
        out = pltpu.make_async_copy(getattr(R, name), getattr(R, "g" + name), R.LS.at[len(leaving)])
        out.start()
        leaving.append(out)

    def key_slot(t, sub):
        return sub if t == 3 else {1: 4, 2: 5, 4: 6}[t]

    def settle(*wanted):
        for entry in list(sends):
            name, cond, desc, slot = entry
            if wanted and name not in wanted:
                continue
            sends.remove(entry)
            free.append(slot)
            if cond is None:
                desc.wait_send()
            else:

                @pl.when(cond)
                def _():
                    desc.wait_send()

    def arrived(dst, name, ri, device):
        copy(dst, dst, 0, name + ri, device).wait_recv()

    barrier = pltpu.get_barrier_semaphore()

    def greet(device):
        pl.semaphore_signal(barrier, inc=1, device_id=device, device_id_type=MESH)

    for k in range(1, 8):
        greet((u, lax.rem(b + k, 8)))
    for k in range(1, 4):
        greet((turn(u, k), b))

    @pl.when(far)
    def _():
        for k in range(1, 4):
            greet(dev(turn(u, k), s, c))

    R.SM[...] = jnp.zeros_like(R.SM)
    for row, name in enumerate(SMALL):
        R.SM[row : row + 1, 0:24] = getattr(R, name)[...].astype(F32).reshape(1, 24)
    up_bias = R.upb[...].astype(F32).reshape(1, 96)
    for i in range(4):
        R.SM[8 + i : 9 + i, 0:24] = up_bias[:, 24 * i : 24 * i + 24]
    small = R.SM[:, 0:64].astype(BF)
    qw, kw, vw = R.qw[...], R.kw[...], R.vw[...]
    for g in range(4):
        parts = []
        for h in range(3):
            at = 64 * (3 * g + h)
            parts += [kw[:, at : at + 64], vw[:, at : at + 64]]
        for h in range(3):
            at = 64 * (3 * g + h)
            parts.append(qw[:, at : at + 64])
        parts.append(small)
        R.WS[g] = jnp.concatenate(parts, axis=1)

    pl.semaphore_wait(barrier, 10 + 3 * lax.div(p, 2))

    for k in range(1, 4):
        to = turn(u, k)
        send(R.WS.at[to], R.W5.at[u, p, c], SEMS.wz, k - 1, dev(to, p, c))
    R.W5[u, p, c] = R.WS[u]
    halves = (slice(0, 64), slice(64, 128))
    for i in range(2):
        send_if(far, R.tok.at[halves[i]], R.XG.at[u, i], SEMS.hop, i, dev(u, s, c))

    @pl.when(jnp.logical_not(far))
    def _():
        for i in range(2):
            R.XG[u, i] = R.tok[halves[i], :]

    near, across = turn(u, 1), turn(u, 2)
    there = dev(near, p, c)
    for i in range(2):
        for k in (2, 1):
            send_if(
                jnp.logical_not(far),
                R.tok.at[halves[i]], R.XG.at[u, i], SEMS.tok, 2 * (k - 1) + i, dev(turn(u, k), p, c),
            )

    up = R.upw[...]
    for q in range(4):
        R.US[q] = jnp.concatenate(
            [up[:, 768 * g + 192 * q : 768 * g + 192 * q + 192] for g in range(4)], axis=1
        )
    for k in range(1, 4):
        to = turn(p, k)
        send(R.US.at[to], R.UP5.at[u, p, c], SEMS.us, k - 1, dev(u, to, c))
    R.UP5[u, p, c] = R.US[p]
    R.DN4[u, c] = R.dnw[...]
    R.OW5[u, p, c] = R.ow[...]

    mate = dev(u, p, other)
    row_pos = lax.broadcasted_iota(jnp.int32, (512, 128), 0)
    n_starts = R.starts.shape[0]

    def id_body(j, carry):
        pos = row_pos + (a + j - 2) * 512
        ids = jnp.zeros((512, 128), jnp.int32)
        for i in range(n_starts):
            ids = ids + jnp.where(pos >= R.starts[i], 1, 0)
        R.SEGK[j] = ids.astype(F32).astype(BF)
        return carry

    lax.fori_loop(0, 5, id_body, 0)
    q_pos = lax.broadcasted_iota(jnp.int32, (1, 512), 1) + a * 512
    q_ids = jnp.zeros((1, 512), jnp.int32)
    for i in range(n_starts):
        q_ids = q_ids + jnp.where(q_pos >= R.starts[i], 1, 0)
    q_ids = jnp.broadcast_to(q_ids.astype(F32), (FWD_ROWS, 512)).astype(BF)
    R.KVT[:, 128:144, :] = jnp.ones((15, 16, 512), BF)
    for ref in (R.QP, R.GP, R.NUM, R.DQT):
        ref[...] = jnp.zeros_like(ref)

    for i in range(2):

        @pl.when(far)
        def _():
            arrived(R.XG.at[u, i], SEMS.hop, i, dev(u, s, c))

        for k in (2, 1):
            send_if(
                far,
                R.XG.at[u, i], R.XG.at[u, i], SEMS.tok, 2 * (k - 1) + i, dev(turn(u, k), p, c),
            )
    for k in range(1, 4):
        src = turn(u, k)
        arrived(R.W5.at[src, p, c], SEMS.wz, k - 1, dev(src, p, c))
    for k in range(1, 4):
        to = turn(p, k)
        send(R.W5.at[:, p, c], R.W5.at[:, p, c], SEMS.wp, k - 1, dev(u, to, c))
    def pass_tokens(i):
        arrived(R.XG.at[across, i], SEMS.tok, 2 + i, dev(across, p, c))
        send(R.XG.at[across, i], R.XG.at[across, i], SEMS.tok, 4 + i, there)

    pass_tokens(0)
    for k in range(1, 4):
        src = turn(p, k)
        arrived(R.W5.at[:, src, c], SEMS.wp, k - 1, dev(u, src, c))
    send(R.W5.at[:, :, c], R.W5.at[:, :, c], SEMS.wc, 0, dev(u, p, other))
    pass_tokens(1)
    for k in range(1, 4):
        to = turn(u, k)
        send(R.ow, R.OW5.at[u, p, c], SEMS.oz, k - 1, dev(to, p, c))
    send(R.dnw, R.DN4.at[u, c], SEMS.dnz, 0, dev(across, p, c))
    for k in range(1, 4):
        src = turn(p, k)
        arrived(R.UP5.at[u, src, c], SEMS.us, k - 1, dev(u, src, c))
    send(R.UP5.at[u, :, c], R.UP5.at[u, :, c], SEMS.upz, 0, dev(across, p, c))
    arrived(R.W5.at[:, :, other], SEMS.wc, 0, dev(u, p, other))
    R.W2[...] = R.W5[...].reshape(768, 640)

    spread = jnp.where(
        rows_by((32, 24, 64), 1, (768, 64)) == lax.broadcasted_iota(jnp.int32, (768, 64), 1), 1.0, 0.0
    ).astype(BF)
    owner = rows_by((32, 24, 768), 0, (768, 768))
    lane = lax.broadcasted_iota(jnp.int32, (1, 768), 1)
    lane_owner = jnp.zeros((1, 768), jnp.int32)
    for i in range(1, 32):
        lane_owner = lane_owner + jnp.where(lane >= 24 * i, 1, 0)
    lane_g = jnp.where(lane >= 192, 1, 0) + jnp.where(lane >= 384, 1, 0) + jnp.where(lane >= 576, 1, 0)
    rest = lane - 192 * lane_g
    lane_c = jnp.where(rest >= 96, 1, 0)
    rest = rest - 96 * lane_c
    lane_r = jnp.where(rest >= 24, 1, 0) + jnp.where(rest >= 48, 1, 0) + jnp.where(rest >= 72, 1, 0)
    up_row = 24 * (8 * lane_g + 2 * p + lane_c) + 8 + lane_r
    row_id = lax.broadcasted_iota(jnp.int32, (768, 768), 0)
    wide = mm_nt(R.W2[:, 576:640], spread)
    mine = jnp.where(owner == lane_owner, wide, 0.0).astype(BF)
    pick = jnp.where(
        lax.broadcasted_iota(jnp.int32, (16, 768), 1) - 24 * lane_owner
        == lax.broadcasted_iota(jnp.int32, (16, 768), 0), 1.0, 0.0
    ).astype(BF)
    R.VEC[...] = mm(pick, mine)

    def group_slice(vector):
        out = vector[:, 0:192]
        for g in range(1, 4):
            out = jnp.where(u == g, vector[:, 192 * g : 192 * g + 192], out)
        return out

    qb = group_slice(R.VEC[0:1, :])
    vb = group_slice(R.VEC[1:2, :])
    zero64 = jnp.zeros((1, 64), F32)
    bias = []
    for h in range(3):
        bias += [zero64, vb[:, 64 * h : 64 * h + 64]]
    bias = jnp.concatenate(bias + [qb, zero64], axis=1)

    for k in range(4):
        src = turn(u, k)
        if k > 0:
            for i in range(2):
                if k != 2:
                    arrived(R.XG.at[src, i], SEMS.tok, 2 * (k - 1) + i, there)
        proj = mm(R.XG[src].reshape(128, 768), R.W2[...]) + bias
        R.KV[2, src] = proj[:, 0:384].astype(BF)
        query = proj[:, 384:576].astype(BF) * BF(0.125)
        for h in range(3):
            R.QP[h, src, :, 0:64] = query[:, 64 * h : 64 * h + 64]
        slot = 1 + 2 * c
        send(R.KV.at[2, src], R.KV.at[slot, src], SEMS.kv, key_slot(1, src), mate)
        for i, step in enumerate((-2, 2)):
            to = a + step
            ok = jnp.logical_and(to >= 0, to < 8)
            slot = 2 - step
            handed = c if step > 0 else 1 - c
            index = handed * src + (1 - handed) * key_slot(4, src)
            send_if(ok, R.KV.at[2, src], R.KV.at[slot, src], SEMS.kv, index, block_dev(to))

    def order(t):
        return 2 + (1 - 2 * c) * ((t + 1) // 2) * (1 - 2 * ((t + 1) % 2))

    def forward_block(t):
        j = order(t)
        ok = jnp.logical_and(a + j >= 2, a + j < 10)

        @pl.when(ok)
        def _():
            if t == 1 or t == 2 or t == 4:
                arrived(R.KV.at[j], SEMS.kv, key_slot(t, 0), block_dev(a + j - 2) if t == 4 else mate)

            def head(h, inner):
                lanes = pl.ds(pl.multiple_of(128 * h, 128), 128)
                kv = R.KV[j, :, :, lanes].reshape(512, 128)
                at = 3 * j + h
                R.KVT[at, 0:128, :] = kv.T
                query = R.QP[h].reshape(512, 128)
                for r in range(512 // FWD_ROWS):
                    rows = slice(FWD_ROWS * r, FWD_ROWS * r + FWD_ROWS)
                    score = mm_nt(kv[rows], query)
                    ids = R.SEGK[j, rows, :]
                    same = jnp.concatenate([ids] * 4, axis=1) == q_ids
                    weight = jnp.exp2(score * LOG2E).astype(BF)
                    R.EL[at, rows, :] = jnp.where(same, weight, jnp.zeros_like(weight))
                R.NUM[h] += mm(R.KVT[at, 64:144, :], R.EL[at])
                return inner

            lax.fori_loop(0, 3, head, 0)

    def relay_out():
        for k in range(1, 4):
            src = turn(u, k)
            arrived(R.OW5.at[src, p, c], SEMS.oz, k - 1, dev(src, p, c))
        for k in range(1, 4):
            to = turn(p, k)
            send(R.OW5.at[:, p, c], R.OW5.at[:, p, c], SEMS.op, k - 1, dev(u, to, c))

    def share_keys():
        j = order(3)
        ok = jnp.logical_and(a + j >= 2, a + j < 10)
        slot = 1 + 2 * (1 - c)
        for r in range(4):

            @pl.when(ok)
            def _():
                arrived(R.KV.at[j, r], SEMS.kv, key_slot(3, r), block_dev(a + j - 2))

            send_if(ok, R.KV.at[j, r], R.KV.at[slot, r], SEMS.kv, key_slot(2, r), mate)

    def relay_down():
        arrived(R.DN4.at[across, c], SEMS.dnz, 0, dev(across, p, c))
        send(R.DN4.at[across, c], R.DN4.at[across, c], SEMS.dnz, 2, there)

    def relay_up():
        arrived(R.UP5.at[across, :, c], SEMS.upz, 0, dev(across, p, c))
        send(R.UP5.at[across, :, c], R.UP5.at[across, :, c], SEMS.upz, 2, there)

    send(R.dnw, R.DN4.at[u, c], SEMS.dnz, 1, there)
    send(R.UP5.at[u, :, c], R.UP5.at[u, :, c], SEMS.upz, 1, there)
    forward_block(0)
    relay_out()
    forward_block(1)
    share_keys()
    forward_block(3)
    settle(SEMS.wz, SEMS.hop, SEMS.us, SEMS.wp, SEMS.wc)
    relay_down()
    forward_block(2)
    forward_block(4)

    heads = []
    for h in range(3):
        R.DEN[h, 0:1, :] = R.NUM[h, 64:65, :]
        attn = R.NUM[h, 0:64, :] / R.DEN[h, 0:1, :]
        R.ATN[h] = attn
        heads.append(attn.T.astype(BF))
    for r in range(4):
        rows = slice(128 * r, 128 * r + 128)
        R.AS[r] = pack(jnp.concatenate([part[rows] for part in heads], axis=1))
    for k in range(1, 4):
        to = turn(u, k)
        send(R.AS.at[to], R.AT.at[u], SEMS.at, k, dev(to, s, c))
    send_if(far, R.AS.at[u], R.AT.at[u], SEMS.at, 0, dev(u, s, c))

    @pl.when(jnp.logical_not(far))
    def _():
        R.AT[u] = R.AS[u]

    relay_up()
    wide = mm_nt(R.W2[:, 576:640], spread)
    R.VUP[0:1, :] = jnp.sum(jnp.where(row_id == up_row, wide, 0.0), axis=0, keepdims=True)
    settle(SEMS.tok, SEMS.hop, SEMS.wz, SEMS.wp, SEMS.wc, SEMS.us, SEMS.oz)
    for k in range(1, 4):
        src = turn(p, k)
        arrived(R.OW5.at[:, src, c], SEMS.op, k - 1, dev(u, src, c))
    send(R.OW5.at[:, :, c], R.OW5.at[:, :, c], SEMS.cow, 0, mate)
    arrived(R.OW5.at[:, :, other], SEMS.cow, 0, mate)
    R.OW2[...] = R.OW5[...].reshape(768, 768)

    def wait_column(ref, name):
        for k in range(1, 4):
            src = turn(u, k)
            arrived(ref.at[src], name, k, dev(src, s, c))

        @pl.when(far)
        def _():
            arrived(ref.at[u], name, 0, dev(u, s, c))

    wait_column(R.AT, SEMS.at)

    def gather_half(ref, i, value, name):
        rows = halves[i]
        ref[p, rows, :] = value
        for k in range(1, 4):
            part = ref.at[p, rows]
            send(part, part, name, 2 * (k - 1) + i, dev(u, turn(p, k), c))

    def centered(hidden):
        hidden = hidden - jnp.mean(hidden, axis=-1, keepdims=True)
        rstd = lax.rsqrt(jnp.mean(hidden * hidden, axis=-1, keepdims=True) + EPS)
        return hidden * rstd, rstd

    def norm_back(cg, normed, rstd):
        mean = jnp.mean(cg, axis=-1, keepdims=True)
        return (cg - mean - normed * jnp.mean(cg * normed, axis=-1, keepdims=True)) * rstd

    def down_sum(x):
        return jnp.sum(x, axis=0, keepdims=True)

    for i in range(2):
        rows = halves[i]
        hidden = R.tok[rows, :].astype(F32) + R.VEC[2:3, :]
        for g in range(4):
            hidden = hidden + mm(unpack_half(R.AT[g], i), R.OW2[192 * g : 192 * g + 192, :])
        normed, rstd = centered(hidden)
        R.N1[rows, :] = normed
        R.RSD[rows, :] = jnp.broadcast_to(rstd, (64, 128))
        y_one = normed * R.VEC[3:4, :] + R.VEC[4:5, :]
        R.Y1[rows, :] = y_one
        gather_half(R.YG, i, y_one.astype(BF), SEMS.yg)

    settle(SEMS.kv)
    for i, src in enumerate((near, turn(near, 2))):
        arrived(R.DN4.at[src, c], SEMS.dnz, 1 + i, there)
    send(R.DN4.at[:, c], R.DN4.at[:, c], SEMS.cdn, 0, mate)
    for i, src in enumerate((near, turn(near, 2))):
        arrived(R.UP5.at[src, :, c], SEMS.upz, 1 + i, there)
    send(R.UP5.at[:, :, c], R.UP5.at[:, :, c], SEMS.cup, 0, mate)
    arrived(R.DN4.at[:, other], SEMS.cdn, 0, mate)
    arrived(R.UP5.at[:, :, other], SEMS.cup, 0, mate)
    R.UP2[...] = R.UP5[...].reshape(768, 768)
    turns = ((0, 0), (0, 1), (1, 0), (2, 0), (3, 0), (1, 1), (2, 1), (3, 1))
    for k, i in turns[2:] + turns[:2]:
        at, rows = turn(p, k), halves[i]
        if k > 0:
            arrived(R.YG.at[at, rows], SEMS.yg, 2 * (k - 1) + i, dev(u, at, c))
        pre = mm(R.YG[at, rows, :], R.UP2[...]) + R.VUP[0:1, :]
        phi = 0.5 * (1.0 + lax.erf(pre * RSQRT2))
        R.GG[at, rows, :] = (phi + pre * (PDF0 * jnp.exp(-0.5 * pre * pre))).astype(BF)
        act = (pre * phi).astype(BF)
        R.ACT[at, rows, :] = act
        part = mm(act, R.DN4[...].reshape(768, 768))
        if k == 0:
            R.H2[rows, :] = part
        else:
            R.PS[at, rows, :] = part.astype(BF)
            send(R.PS.at[at, rows], R.PR.at[p, rows], SEMS.ps, 2 * (k - 1) + i, dev(u, at, c))

    g_gain_two = g_shift_two = g_b_down = 0.0
    for i in range(2):
        rows = halves[i]
        hidden = R.Y1[rows, :] + R.H2[rows, :] + R.VEC[5:6, :]
        for k in range(1, 4):
            at = turn(p, k)
            arrived(R.PR.at[at, rows], SEMS.ps, 2 * (k - 1) + i, dev(u, at, c))
            hidden = hidden + R.PR[at, rows, :].astype(F32)
        normed, rstd = centered(hidden)
        gain = R.VEC[6:7, :]
        grad = R.cot[rows, :].astype(F32)
        d_two = norm_back(grad * gain, normed, rstd)
        gather_half(R.DG, i, d_two.astype(BF), SEMS.dg)
        R.DH2[rows, :] = d_two
        R.t_out[rows, :] = (normed * gain + R.VEC[7:8, :]).astype(BF)
        g_gain_two = g_gain_two + down_sum(grad * normed)
        g_shift_two = g_shift_two + down_sum(grad)
        g_b_down = g_b_down + down_sum(d_two)

    leave("t_out")
    settle(SEMS.at, SEMS.op, SEMS.dnz, SEMS.upz, SEMS.cow, SEMS.cup, SEMS.cdn, SEMS.yg, SEMS.ps)
    g_b_up = jnp.zeros((1, 768), F32)
    for k, i in turns:
        at, rows = turn(p, k), halves[i]
        if k > 0:
            arrived(R.DG.at[at, rows], SEMS.dg, 2 * (k - 1) + i, dev(u, at, c))
        d_act = mm_nt(R.DG[at, rows, :], R.DN4[...].reshape(768, 768))
        d_pre = (d_act * R.GG[at, rows, :].astype(F32)).astype(BF)
        R.DU[at, rows, :] = d_pre
        g_b_up = g_b_up + down_sum(d_pre.astype(F32))
        part = mm_nt(d_pre, R.UP2[...])
        if k == 0:
            R.H2[rows, :] = part
        else:
            R.PS[at, rows, :] = part.astype(BF)
            send(R.PS.at[at, rows], R.PR.at[p, rows], SEMS.qs, 2 * (k - 1) + i, dev(u, at, c))

    def wide_grad(left, right_ref, put):
        R.T1[...] = left.T

        def body(n, carry):
            lanes = pl.ds(pl.multiple_of(256 * n, 256), 256)
            put(lanes, mm(R.T1[...], right_ref[:, :, lanes].reshape(512, 256)))
            return carry

        lax.fori_loop(0, 3, body, 0)

    def put_down(lanes, value):
        R.GD[:, :, :, lanes] = value.reshape(4, 2, 96, 256)

    def put_up(lanes, value):
        R.GU[:, :, :, :, lanes] = value.reshape(4, 4, 2, 24, 256)

    wide_grad(R.ACT[...].reshape(512, 768), R.DG, put_down)
    send(R.GD.at[:, other], R.RD, SEMS.fdc, 0, mate)
    wide_grad(R.YG[...].reshape(512, 768), R.DU, put_up)
    send(R.GU.at[:, :, other], R.RU, SEMS.fuc, 0, mate)
    def down_step():
        arrived(R.RD, SEMS.fdc, 0, mate)
        for i, g in enumerate((near, turn(near, 2))):
            R.SD[i] = (R.GD[g, c] + R.RD[g]).astype(BF)
        send(R.SD, R.RD1, SEMS.fdz, 0, there)

    down_step()
    g_b_out = g_gain_one = g_shift_one = 0.0
    for half in range(2):
        rows = halves[half]
        d_y = R.DH2[rows, :] + R.H2[rows, :]
        for k in range(1, 4):
            at = turn(p, k)
            arrived(R.PR.at[at, rows], SEMS.qs, 2 * (k - 1) + half, dev(u, at, c))
            d_y = d_y + R.PR[at, rows, :].astype(F32)
        normed = R.N1[rows, :]
        d_one = norm_back(d_y * R.VEC[3:4, :], normed, R.RSD[rows, 0:1])
        R.DH1[rows, :] = d_one
        for k in (1, 2, 3, 0):
            to = turn(u, k)
            w_rows = R.OW2[pl.ds(pl.multiple_of(192 * to, 64), 192), :]
            R.DAS[to, half] = pack_half(mm_nt(d_one.astype(BF), w_rows).astype(BF))
            if k > 0:
                send(R.DAS.at[to, half], R.DA.at[u, half], SEMS.da, 4 * half + k, dev(to, s, c))
        send_if(far, R.DAS.at[u, half], R.DA.at[u, half], SEMS.da, 4 * half, dev(u, s, c))
        g_b_out = g_b_out + down_sum(d_one)
        g_gain_one = g_gain_one + down_sum(d_y * normed)
        g_shift_one = g_shift_one + down_sum(d_y)

    @pl.when(jnp.logical_not(far))
    def _():
        R.DA[u] = R.DAS[u]

    vec = R.VEC
    vec[2:3, :] = g_b_out
    vec[3:4, :] = g_gain_one
    vec[4:5, :] = g_shift_one
    vec[5:6, :] = g_b_down
    vec[6:7, :] = g_gain_two
    vec[7:8, :] = g_shift_two
    vec[8:16, :] = jnp.zeros((8, 768), F32)
    R.VUP[0:1, :] = g_b_up

    for g in range(4):
        R.GO[g] = mm_tn(unpack(R.AT[g]), R.DH1[...].astype(BF)).reshape(4, 2, 24, 768)
    send(R.GO.at[:, :, other], R.RO, SEMS.foc, 0, mate)

    arrived(R.RU, SEMS.fuc, 0, mate)
    for i, g in enumerate((near, turn(near, 2))):
        R.SU[i] = (R.GU[g, :, c] + R.RU[g]).astype(BF)
    send(R.SU, R.RU1, SEMS.fuz, 0, there)

    def relay_down_grad():
        arrived(R.RD1, SEMS.fdz, 0, there)
        R.SD2[...] = (R.GD[across, c] + R.RD[across] + R.RD1[1].astype(F32)).astype(BF)
        send(R.SD2, R.RD2, SEMS.fdz, 1, dev(across, p, c))

    def relay_up_grad():
        arrived(R.RU1, SEMS.fuz, 0, there)
        R.SU2[...] = (R.GU[across, :, c] + R.RU[across] + R.RU1[1].astype(F32)).astype(BF)
        send(R.SU2, R.RU2, SEMS.fuz, 1, dev(across, p, c))

    arrived(R.RO, SEMS.foc, 0, mate)
    for g in range(4):
        R.SO[g] = (R.GO[g, :, c] + R.RO[g]).astype(BF)
    for k in range(1, 4):
        to = turn(p, k)
        send(R.SO.at[:, to], R.ROP.at[p], SEMS.fop, k - 1, dev(u, to, c))
    settle(SEMS.fdc, SEMS.fuc, SEMS.qs, SEMS.dg)
    vec[0:2, :] = jnp.zeros((2, 768), F32)
    choose = jnp.where(
        rows_by((32, 24, 16), 1, (768, 16)) == lax.broadcasted_iota(jnp.int32, (768, 16), 1), 1.0, 0.0
    ).astype(BF)
    laid = jnp.where(owner == lane_owner, mm(choose, vec[...].astype(BF)), 0.0)
    laid = jnp.where(row_id == up_row, R.VUP[0:1, :], laid)
    R.MR[...] = mm(laid.astype(BF), spread)
    R.T1[...] = R.XG[...].reshape(512, 768).T
    for half in range(2):
        for k in range(1, 4):
            src = turn(u, k)
            arrived(R.DA.at[src, half], SEMS.da, 4 * half + k, dev(src, s, c))

        @pl.when(far)
        def _():
            arrived(R.DA.at[u, half], SEMS.da, 4 * half, dev(u, s, c))

    d_rows = [open_half(R.DA[r, half]) for r in range(4) for half in range(2)]
    d_rows = jnp.concatenate(d_rows, axis=0).astype(F32)
    for h in range(3):
        d_attn = d_rows[:, 64 * h : 64 * h + 64].T
        scaled = (d_attn / R.DEN[h, 0:1, :]).astype(BF)
        R.DLT[h, 0:1, :] = jnp.sum(scaled.astype(F32) * R.ATN[h], axis=0, keepdims=True)
        R.GP[h, :, :, 64:128] = scaled.T.reshape(4, 128, 64)

    def block_copy(t):
        j = order(t)
        there_slot = 0 if t == 1 else 1
        return copy(
            R.DKS.at[j], R.DKR.at[4 - j], there_slot, SEMS.dk + there_slot, block_dev(a + j - 2)
        )

    def key_copy(t, h):
        j = order(t)
        if t == 2:
            return copy(R.DKS.at[j, h], R.DKX.at[h], 2 + h, SEMS.dx + h, mate)
        return copy(
            R.DKS.at[j, h], R.DKR.at[4 - j, h], 5 + h, SEMS.dk + 2 + h, block_dev(a + j - 2)
        )

    def backward_block(t):
        j = order(t)
        ok = jnp.logical_and(a + j >= 2, a + j < 10)

        @pl.when(ok)
        def _():
            def head(h, inner):
                lanes = pl.ds(pl.multiple_of(128 * h, 128), 128)
                at = 3 * j + h
                grad_rows = R.GP[h].reshape(512, 128)
                shift = R.DLT[h, 0:1, :]
                kv = R.KV[j, :, :, lanes].reshape(512, 128)
                for r in range(512 // BWD_ROWS):
                    rows = slice(BWD_ROWS * r, BWD_ROWS * r + BWD_ROWS)
                    d_prob = mm_nt(kv[rows], grad_rows)
                    R.DST[rows, :] = (R.EL[at, rows, :].astype(F32) * (d_prob - shift)).astype(BF)
                d_kv = mm(R.DST[...], R.QP[h].reshape(512, 128)) + mm(R.EL[at], grad_rows)
                if t == 0:
                    R.DKO[h] = d_kv
                elif t == 3:
                    arrived(R.DKX.at[h], SEMS.dx, h, mate)
                    R.DKS[j, h] = (d_kv + R.DKX[h].astype(F32)).astype(BF)
                else:
                    R.DKS[j, h] = d_kv.astype(BF)
                if t == 2 or t == 3:
                    key_copy(t, h).start()
                R.DQT[h] += mm(R.KVT[at, 0:64, :], R.DST[...])
                return inner

            lax.fori_loop(0, 3, head, 0)
            if t == 4 or t == 1:
                block_copy(t).start()

    backward_block(4)
    relay_down_grad()
    backward_block(2)
    backward_block(3)
    relay_up_grad()
    backward_block(1)
    backward_block(0)

    def at_lanes(n, value):
        R.G1[:, :, :, :, 128 * n : 128 * n + 128] = value.reshape(4, 4, 2, 24, 128)

    def query_grads():
        for n in (3, 4):
            value = mm(R.T1[...], R.DQ[:, 128 * n : 128 * n + 128])
            if n == 4:
                value = jnp.concatenate([value[:, 0:64], R.MR[...]], axis=1)
            at_lanes(n, value)

    def key_grads():
        for n in range(3):
            at_lanes(n, mm(R.T1[...], R.DQ[:, 128 * n : 128 * n + 128]))
        sums = mm(jnp.ones((8, 512), BF), R.DQ[...])[0:1]
        sum_v = jnp.concatenate([sums[:, 128 * h + 64 : 128 * h + 128] for h in range(3)], axis=1)
        row = lax.broadcasted_iota(jnp.int32, (192, 192), 0)
        lane_row = 24 * lane_owner[:, 0:192]
        laid = jnp.where(row == lane_row, sums[:, 384:576], jnp.where(row == lane_row + 1, sum_v, 0.0))
        extra = mm(laid.astype(BF), spread[0:192])
        extra = jnp.concatenate([jnp.zeros((192, 64), F32), extra], axis=1)
        R.G1[u, :, :, :, 512:640] += extra.reshape(4, 2, 24, 128)
        send(R.G1.at[:, :, other], R.R1, SEMS.f1c, 0, mate)

    for h in range(3):
        R.DQ[:, 384 + 64 * h : 448 + 64 * h] = (R.DQT[h] * 0.125).T.astype(BF)
    R.DQ[:, 576:640] = jnp.zeros((512, 64), BF)
    query_grads()
    for t in (1, 3, 4):
        j = order(t)

        @pl.when(jnp.logical_and(a + j >= 2, a + j < 10))
        def _():
            if t != 4:
                arrived(R.DKR.at[j], SEMS.dk, 0 if t == 1 else 1, block_dev(a + j - 2))
            for h in range(3):
                if t == 4:
                    arrived(R.DKR.at[j, h], SEMS.dk, 2 + h, block_dev(a + j - 2))
                R.DKO[h] += R.DKR[j, h].astype(F32)

    for h in range(3):
        R.DQ[:, 128 * h : 128 * h + 128] = R.DKO[h].astype(BF)
    key_grads()

    settle(SEMS.qs)
    def input_part(k):
        rows = pl.ds(pl.multiple_of(128 * turn(u, k), 128), 128)
        return mm_nt(R.DQ[rows, :], R.W2[...])

    R.PS[3] = input_part(3).astype(BF)
    send(R.PS.at[3], R.XN, SEMS.x, 3, there)
    R.PS[1] = input_part(1).astype(BF)
    send(R.PS.at[1], R.PR.at[1], SEMS.x, 1, there)
    R.Y1[...] = input_part(0)
    R.H2[...] = input_part(2)
    arrived(R.R1, SEMS.f1c, 0, mate)
    for g in range(4):
        R.H1[g] = (R.G1[g, :, c] + R.R1[g]).astype(BF)
    for k in range(1, 4):
        to = turn(p, k)
        send(R.H1.at[:, to], R.R1P.at[p], SEMS.f1p, k - 1, dev(u, to, c))
    arrived(R.RD2, SEMS.fdz, 1, dev(across, p, c))
    R.t_dn[...] = R.GD[u, c] + R.RD[u] + R.RD1[0].astype(F32) + R.RD2[...].astype(F32)
    leave("t_dn")
    arrived(R.RU2, SEMS.fuz, 1, dev(across, p, c))
    R.TU[...] = (R.GU[u, :, c] + R.RU[u] + R.RU1[0].astype(F32) + R.RU2[...].astype(F32)).astype(BF)
    R.RUP[p] = R.TU[p]
    for k in range(1, 4):
        to = turn(p, k)
        send(R.TU.at[to], R.RUP.at[p], SEMS.fup, k - 1, dev(u, to, c))

    arrived(R.XN, SEMS.x, 3, there)
    R.PS[2] = (R.H2[...] + R.XN[...].astype(F32)).astype(BF)
    send(R.PS.at[2], R.PR.at[2], SEMS.x, 2, dev(across, s, c))
    for k in range(1, 4):
        src = turn(p, k)
        arrived(R.ROP.at[src], SEMS.fop, k - 1, dev(u, src, c))
    for g in range(4):
        total = R.GO[g, p, c] + R.RO[g, p]
        for k in range(1, 4):
            total = total + R.ROP[turn(p, k), g].astype(F32)
        R.TO[g] = total.astype(BF)
    for k in range(1, 4):
        to = turn(u, k)
        send(R.TO.at[to], R.ROZ.at[u], SEMS.foz, k - 1, dev(to, p, c))
    arrived(R.PR.at[1], SEMS.x, 1, there)
    R.Y1[...] += R.PR[1].astype(F32)

    @pl.when(far)
    def _():
        R.PS[0] = R.Y1[...].astype(BF)

    send_if(far, R.PS.at[0], R.PR.at[0], SEMS.x, 0, dev(u, s, c))
    for k in range(1, 4):
        src = turn(p, k)
        arrived(R.R1P.at[src], SEMS.f1p, k - 1, dev(u, src, c))
    total = R.G1[:, p, c] + R.R1[:, p]
    for k in range(1, 4):
        total = total + R.R1P[turn(p, k)].astype(F32)
    R.S1[...] = total.astype(BF)
    for k in range(1, 4):
        to = turn(u, k)
        send(R.S1.at[to], R.R1Z.at[u], SEMS.f1z, k - 1, dev(to, p, c))
    R.R1Z[u] = R.S1[u]
    for k in range(1, 4):
        src = turn(u, k)
        arrived(R.ROZ.at[src], SEMS.foz, k - 1, dev(src, p, c))
    total = R.TO[u].astype(F32)
    for k in range(1, 4):
        total = total + R.ROZ[turn(u, k)].astype(F32)
    R.t_ow[...] = total
    leave("t_ow")
    for k in range(1, 4):
        src = turn(p, k)
        arrived(R.RUP.at[src], SEMS.fup, k - 1, dev(u, src, c))
    R.t_up[...] = R.RUP[...]
    leave("t_up")
    arrived(R.PR.at[2], SEMS.x, 2, dev(across, s, c))

    @pl.when(far)
    def _():
        arrived(R.PR.at[0], SEMS.x, 0, dev(u, s, c))
        R.Y1[...] = R.PR[0].astype(F32)

    total = R.DH1[...] + R.Y1[...] + R.PR[2].astype(F32)
    R.t_in[...] = total
    leave("t_in")
    for k in range(1, 4):
        src = turn(u, k)
        arrived(R.R1Z.at[src], SEMS.f1z, k - 1, dev(src, p, c))
    R.t_qkv[...] = R.R1Z[...]
    leave("t_qkv")
    settle()
    for out in leaving:
        out.wait()
    for t in range(1, 5):
        j = order(t)

        @pl.when(jnp.logical_and(a + j >= 2, a + j < 10))
        def _():
            if t == 4 or t == 1:
                block_copy(t).wait_send()
            else:
                for h in range(3):
                    key_copy(t, h).wait_send()


def finish_kernel(*refs):
    R = Refs()
    for name, ref in zip([*RAW, *OUTS], refs, strict=True):
        setattr(R, name, ref)
    R.o_out[...] = R.t_out[...]
    R.o_in[...] = R.t_in[...]
    R.o_dnw[...] = R.t_dn[...]
    R.o_ow[...] = R.t_ow[...]
    for q in range(4):
        piece = R.t_up[q].astype(F32)
        for g in range(4):
            R.o_upw[:, 768 * g + 192 * q : 768 * g + 192 * q + 192] = piece[:, 192 * g : 192 * g + 192]
    small = jnp.zeros((24, 64), F32)
    for g in range(4):
        piece = R.t_qkv[g].astype(F32)
        at = 192 * g
        R.o_kw[:, at : at + 192] = jnp.concatenate([piece[:, 128 * h : 128 * h + 64] for h in range(3)], axis=1)
        R.o_vw[:, at : at + 192] = jnp.concatenate([piece[:, 128 * h + 64 : 128 * h + 128] for h in range(3)], axis=1)
        R.o_qw[:, at : at + 192] = piece[:, 384:576]
        small = small + piece[:, 576:640]
    for row, name in enumerate(SMALL):
        getattr(R, "o_" + name)[...] = small[row : row + 1, 0:24].reshape(24)
    R.o_upb[...] = jnp.concatenate([small[8 + i : 9 + i, 0:24] for i in range(4)], axis=1).reshape(96)


def fused_step(*args):
    vmem = pl.BlockSpec(memory_space=pltpu.VMEM)
    raw = pl.pallas_call(
        layer_kernel,
        out_shape=[jax.ShapeDtypeStruct(shape, dtype) for shape, dtype in RAW.values()],
        in_specs=[pl.BlockSpec(memory_space=pltpu.SMEM) if n == "starts" else vmem for n in ARGS],
        out_specs=[pl.BlockSpec(memory_space=pl.ANY)] * len(RAW),
        scratch_shapes=[pltpu.VMEM(shape, dtype) for shape, dtype in (RAW | SCRATCH).values()]
        + [pltpu.SemaphoreType.DMA((n,)) for n in (SEND_SLOTS, SEMS.total, len(RAW))],
        compiler_params=pltpu.CompilerParams(
            collective_id=0, has_side_effects=True, vmem_limit_bytes=63 << 20
        ),
        name="layer_step",
    )(*args)
    return pl.pallas_call(
        finish_kernel,
        out_shape=[jax.ShapeDtypeStruct(shape, dtype) for shape, dtype in OUTS.values()],
        in_specs=[vmem] * len(RAW),
        out_specs=[vmem] * len(OUTS),
        name="finish",
    )(*raw)


def solution(mesh):
    fused = mesh.shape[ULYSSES] == 4 and mesh.shape[BLK] == 8
    return jax.shard_map(
        fused_step if fused else per_device,
        mesh=mesh,
        in_specs=(
            P(TOKEN_AXES, None),
            P(TOKEN_AXES, None),
            P(),
            P(WEIGHT_AXES, None),
            P(WEIGHT_AXES, None),
            P(WEIGHT_AXES, None),
            P(WEIGHT_AXES),
            P(WEIGHT_AXES),
            P(WEIGHT_AXES, None),
            P(WEIGHT_AXES),
            P(WEIGHT_AXES),
            P(WEIGHT_AXES),
            P(WEIGHT_AXES, None),
            P(WEIGHT_AXES),
            P(WEIGHT_AXES, None),
            P(WEIGHT_AXES),
            P(WEIGHT_AXES),
            P(WEIGHT_AXES),
        ),
        out_specs=(
            P(TOKEN_AXES, None),
            P(TOKEN_AXES, None),
            P(WEIGHT_AXES, None),
            P(WEIGHT_AXES, None),
            P(WEIGHT_AXES, None),
            P(WEIGHT_AXES),
            P(WEIGHT_AXES),
            P(WEIGHT_AXES, None),
            P(WEIGHT_AXES),
            P(WEIGHT_AXES),
            P(WEIGHT_AXES),
            P(WEIGHT_AXES, None),
            P(WEIGHT_AXES),
            P(WEIGHT_AXES, None),
            P(WEIGHT_AXES),
            P(WEIGHT_AXES),
            P(WEIGHT_AXES),
        ),
        check_vma=False,
    )
```

```python
import jax
import jax.numpy as jnp
from jax import lax
from jax.experimental import pallas as pl
from jax.experimental.pallas import tpu as pltpu
from jax.sharding import PartitionSpec as P

HD = 64
ULYSSES = "ulysses"
BLK = "blk"
WEIGHT_AXES = (ULYSSES, BLK)
TOKEN_AXES = (BLK, ULYSSES)


SCALE = 0.125
EPS = 1e-12


def passed_along(shard, axis, by):
    length = lax.axis_size(axis)
    return lax.ppermute(shard, axis, [(i, (i + by) % length) for i in range(length)])


def layer_norm(hidden, gain, shift):
    middle = jnp.mean(hidden, axis=-1, keepdims=True)
    centered = hidden - middle
    spread = jnp.mean(centered * centered, axis=-1, keepdims=True)
    return centered * lax.rsqrt(spread + EPS) * gain + shift


def gelu_exact(values):
    return jax.nn.gelu(values, approximate=False)


def doc_ids(doc_starts, positions):
    return jnp.sum((doc_starts[None, :] <= positions[:, None]).astype(jnp.int32), axis=1)


def project(left, right):
    return jnp.dot(left, right, preferred_element_type=jnp.float32)


def project_back(left, right):
    return lax.dot_general(
        left, right, (((1,), (1,)), ((), ())), preferred_element_type=jnp.float32
    )


def outer_sum(left, right):
    return lax.dot_general(
        left, right, (((0,), (0,)), ((), ())), preferred_element_type=jnp.float32
    )


def per_device(
    tokens,
    cotangent,
    doc_starts,
    q_weight,
    k_weight,
    v_weight,
    q_bias,
    v_bias,
    o_weight,
    o_bias,
    norm1_gain,
    norm1_bias,
    up_weight,
    up_bias,
    down_weight,
    down_bias,
    norm2_gain,
    norm2_bias,
):
    f32 = jnp.float32
    bf16 = jnp.bfloat16
    w_query, w_key, w_value, b_query, b_value, w_out, b_out, gain_one, shift_one = (
        lax.all_gather(q_weight, WEIGHT_AXES, axis=0, tiled=True),
        lax.all_gather(k_weight, WEIGHT_AXES, axis=0, tiled=True),
        lax.all_gather(v_weight, WEIGHT_AXES, axis=0, tiled=True),
        lax.all_gather(q_bias, WEIGHT_AXES, axis=0, tiled=True),
        lax.all_gather(v_bias, WEIGHT_AXES, axis=0, tiled=True),
        lax.all_gather(o_weight, WEIGHT_AXES, axis=0, tiled=True),
        lax.all_gather(o_bias, WEIGHT_AXES, axis=0, tiled=True),
        lax.all_gather(norm1_gain, WEIGHT_AXES, axis=0, tiled=True),
        lax.all_gather(norm1_bias, WEIGHT_AXES, axis=0, tiled=True),
    )
    w_up, b_up, w_down, b_down, gain_two, shift_two = (
        lax.all_gather(up_weight, WEIGHT_AXES, axis=0, tiled=True),
        lax.all_gather(up_bias, WEIGHT_AXES, axis=0, tiled=True),
        lax.all_gather(down_weight, WEIGHT_AXES, axis=0, tiled=True),
        lax.all_gather(down_bias, WEIGHT_AXES, axis=0, tiled=True),
        lax.all_gather(norm2_gain, WEIGHT_AXES, axis=0, tiled=True),
        lax.all_gather(norm2_bias, WEIGHT_AXES, axis=0, tiled=True),
    )
    query_tok = (project(tokens, w_query) + b_query.astype(f32)).astype(bf16)
    key_tok = project(tokens, w_key).astype(bf16)
    value_tok = (project(tokens, w_value) + b_value.astype(f32)).astype(bf16)
    query_heads, key_heads, value_heads = (
        lax.all_to_all(query_tok, ULYSSES, split_axis=1, concat_axis=0, tiled=True),
        lax.all_to_all(key_tok, ULYSSES, split_axis=1, concat_axis=0, tiled=True),
        lax.all_to_all(value_tok, ULYSSES, split_axis=1, concat_axis=0, tiled=True),
    )
    group = query_heads.shape[0]
    columns = query_heads.shape[1]
    local_heads = columns // HD
    block_count = lax.axis_size(BLK)
    total = group * block_count
    doc_max = min(8192, total // 4, 8 * group)
    reach = (group - 2 + doc_max) // group
    visits = 2 * reach + 1
    block_index = lax.axis_index(BLK)
    rows = jnp.arange(group, dtype=jnp.int32)
    query_ids = doc_ids(doc_starts, block_index * group + rows)
    query3 = query_heads.reshape(group, local_heads, HD)

    def block_mask(offset):
        key_pos = (block_index + offset) * group + rows
        inside = (key_pos >= 0) & (key_pos < total)
        key_ids = jnp.where(inside, doc_ids(doc_starts, key_pos), -1)
        allowed = query_ids[:, None] == key_ids[None, :]
        shared = (
            inside[0] & (key_ids[0] <= query_ids[group - 1]) & (key_ids[group - 1] >= query_ids[0])
        )
        return (allowed, shared)

    def exp_scores(pair, allowed):
        key3 = pair[0].reshape(group, local_heads, HD)
        scores = jnp.einsum("qhd,khd->hqk", query3, key3, preferred_element_type=f32) * SCALE
        return jnp.where(allowed[None], jnp.exp(scores), 0.0)

    def forward_terms(pair, offset):
        allowed, shared = block_mask(offset)
        weights = exp_scores(pair, allowed)
        value3 = pair[1].reshape(group, local_heads, HD)
        numer = jnp.einsum("hqk,khd->qhd", weights.astype(bf16), value3, preferred_element_type=f32)
        return (numer, jnp.sum(weights, axis=2))

    pair_own = jnp.stack([key_heads, value_heads])
    pair = passed_along(pair_own, BLK, -reach)
    numer, denom = forward_terms(pair, reach)
    store = jnp.zeros((1,), bf16)

    def forward_step(step, carry):
        pair_now, numer_now, denom_now, store_now = carry
        pair_now = passed_along(pair_now, BLK, 1)
        more_numer, more_denom = forward_terms(pair_now, reach - step)
        return (pair_now, numer_now + more_numer, denom_now + more_denom, store_now)

    pair, numer, denom, store = lax.fori_loop(1, visits, forward_step, (pair, numer, denom, store))
    attn_f = numer / jnp.transpose(denom)[:, :, None]
    attn_b = attn_f.reshape(group, columns).astype(bf16)
    attn_tok = lax.all_to_all(attn_b, ULYSSES, split_axis=0, concat_axis=1, tiled=True)
    token_f = tokens.astype(f32)
    h_one = token_f + project(attn_tok, w_out) + b_out.astype(f32)
    y_one, norm_one_back = jax.vjp(layer_norm, h_one, gain_one.astype(f32), shift_one.astype(f32))
    y_one_b = y_one.astype(bf16)
    pre_act = project(y_one_b, w_up) + b_up.astype(f32)
    act, gelu_back = jax.vjp(gelu_exact, pre_act)
    act_b = act.astype(bf16)
    h_two = y_one + project(act_b, w_down) + b_down.astype(f32)
    out_f, norm_two_back = jax.vjp(layer_norm, h_two, gain_two.astype(f32), shift_two.astype(f32))
    layer_out = out_f.astype(bf16)
    d_two, g_gain_two, g_shift_two = norm_two_back(cotangent.astype(f32))
    g_b_down = jnp.sum(d_two, axis=0)
    d_two_b = d_two.astype(bf16)
    g_w_down = outer_sum(act_b, d_two_b)
    d_act = project_back(d_two_b, w_down)
    d_pre = gelu_back(d_act)[0].astype(bf16)
    g_b_up = jnp.sum(d_pre.astype(f32), axis=0)
    g_w_up = outer_sum(y_one_b, d_pre)
    d_y_one = d_two + project_back(d_pre, w_up)
    d_one, g_gain_one, g_shift_one = norm_one_back(d_y_one)
    g_b_out = jnp.sum(d_one, axis=0)
    d_one_b = d_one.astype(bf16)
    g_w_out = outer_sum(attn_tok, d_one_b)
    d_attn_tok = project_back(d_one_b, w_out).astype(bf16)
    d_attn = lax.all_to_all(d_attn_tok, ULYSSES, split_axis=1, concat_axis=0, tiled=True)
    d_attn3 = d_attn.reshape(group, local_heads, HD)
    d_attn_f = d_attn3.astype(f32)
    delta = jnp.transpose(jnp.sum(d_attn_f * attn_f, axis=2))
    scaled_grad = d_attn_f / jnp.transpose(denom)[:, :, None]
    grad_high = scaled_grad.astype(bf16)
    grad_rest = (scaled_grad - grad_high.astype(f32)).astype(bf16)

    def backward_terms(pair_in, offset):
        allowed, shared = block_mask(offset)
        weights = exp_scores(pair_in, allowed)
        key3 = pair_in[0].reshape(group, local_heads, HD)
        value3 = pair_in[1].reshape(group, local_heads, HD)
        probs = weights / denom[:, :, None]
        d_prob = jnp.einsum("qhd,khd->hqk", d_attn3, value3, preferred_element_type=f32)
        d_score = (probs * (d_prob - delta[:, :, None]) * SCALE).astype(bf16)
        d_query = jnp.einsum("hqk,khd->qhd", d_score, key3, preferred_element_type=f32)
        d_key = jnp.einsum("hqk,qhd->khd", d_score, query3, preferred_element_type=f32)
        weights_low = weights.astype(bf16)
        d_value = jnp.einsum(
            "hqk,qhd->khd", weights_low, grad_high, preferred_element_type=f32
        ) + jnp.einsum("hqk,qhd->khd", weights_low, grad_rest, preferred_element_type=f32)
        return (d_query, jnp.stack([d_key, d_value]))

    pair = passed_along(pair_own, BLK, -reach)
    d_query_sum, carried = backward_terms(pair, reach)

    def backward_step(step, carry):
        pair_now, d_query_now, carried_now = carry
        pair_now = passed_along(pair_now, BLK, 1)
        more_query, more_kv = backward_terms(pair_now, reach - step)
        carried_now = (
            passed_along(carried_now.astype(jnp.bfloat16), BLK, 1).astype(carried_now.dtype)
            + more_kv
        )
        return (pair_now, d_query_now + more_query, carried_now)

    pair, d_query_sum, carried = lax.fori_loop(
        1, visits, backward_step, (pair, d_query_sum, carried)
    )
    own_grads = passed_along(carried.astype(jnp.bfloat16), BLK, -reach).astype(carried.dtype)
    d_query_b = d_query_sum.reshape(group, columns).astype(bf16)
    d_key_b = own_grads[0].reshape(group, columns).astype(bf16)
    d_value_b = own_grads[1].reshape(group, columns).astype(bf16)
    dq_tok, dk_tok, dv_tok = (
        lax.all_to_all(d_query_b, ULYSSES, split_axis=0, concat_axis=1, tiled=True),
        lax.all_to_all(d_key_b, ULYSSES, split_axis=0, concat_axis=1, tiled=True),
        lax.all_to_all(d_value_b, ULYSSES, split_axis=0, concat_axis=1, tiled=True),
    )
    g_b_query = jnp.sum(dq_tok.astype(f32), axis=0)
    g_b_value = jnp.sum(dv_tok.astype(f32), axis=0)
    g_w_query = outer_sum(tokens, dq_tok)
    g_w_key = outer_sum(tokens, dk_tok)
    g_w_value = outer_sum(tokens, dv_tok)
    input_grad = (
        d_one
        + project_back(dq_tok, w_query)
        + project_back(dk_tok, w_key)
        + project_back(dv_tok, w_value)
    )
    shares = (
        lax.psum_scatter(g_w_query, WEIGHT_AXES, scatter_dimension=0, tiled=True),
        lax.psum_scatter(g_w_key, WEIGHT_AXES, scatter_dimension=0, tiled=True),
        lax.psum_scatter(g_w_value, WEIGHT_AXES, scatter_dimension=0, tiled=True),
        lax.psum_scatter(g_b_query, WEIGHT_AXES, scatter_dimension=0, tiled=True),
        lax.psum_scatter(g_b_value, WEIGHT_AXES, scatter_dimension=0, tiled=True),
        lax.psum_scatter(g_w_out, WEIGHT_AXES, scatter_dimension=0, tiled=True),
        lax.psum_scatter(g_b_out, WEIGHT_AXES, scatter_dimension=0, tiled=True),
        lax.psum_scatter(g_gain_one, WEIGHT_AXES, scatter_dimension=0, tiled=True),
        lax.psum_scatter(g_shift_one, WEIGHT_AXES, scatter_dimension=0, tiled=True),
        lax.psum_scatter(g_w_up, WEIGHT_AXES, scatter_dimension=0, tiled=True),
        lax.psum_scatter(g_b_up, WEIGHT_AXES, scatter_dimension=0, tiled=True),
        lax.psum_scatter(g_w_down, WEIGHT_AXES, scatter_dimension=0, tiled=True),
        lax.psum_scatter(g_b_down, WEIGHT_AXES, scatter_dimension=0, tiled=True),
        lax.psum_scatter(g_gain_two, WEIGHT_AXES, scatter_dimension=0, tiled=True),
        lax.psum_scatter(g_shift_two, WEIGHT_AXES, scatter_dimension=0, tiled=True),
    )
    return (
        layer_out,
        input_grad,
        shares[0],
        shares[1],
        shares[2],
        shares[3],
        shares[4],
        shares[5],
        shares[6],
        shares[7],
        shares[8],
        shares[9],
        shares[10],
        shares[11],
        shares[12],
        shares[13],
        shares[14],
    )


MESH = pl.DeviceIdType.MESH
LOG2E = 1.4426950408889634
RSQRT2 = 0.7071067811865476
FWD_ROWS = 256
BWD_ROWS = 256
KEY_SENDS = 8
SEND_SLOTS = 62
PDF0 = 0.3989422804014327

ARGS = ("tok", "cot", "starts", "qw", "kw", "vw", "qb", "vb", "ow", "ob", "g1", "b1", "upw", "upb", "dnw", "dnb", "g2", "b2")
OUTS = dict(
    o_out=((128, 768), jnp.bfloat16),
    o_in=((128, 768), jnp.float32),
    o_qw=((24, 768), jnp.float32),
    o_kw=((24, 768), jnp.float32),
    o_vw=((24, 768), jnp.float32),
    o_qb=((24,), jnp.float32),
    o_vb=((24,), jnp.float32),
    o_ow=((24, 768), jnp.float32),
    o_ob=((24,), jnp.float32),
    o_g1=((24,), jnp.float32),
    o_b1=((24,), jnp.float32),
    o_upw=((24, 3072), jnp.float32),
    o_upb=((96,), jnp.float32),
    o_dnw=((96, 768), jnp.float32),
    o_dnb=((24,), jnp.float32),
    o_g2=((24,), jnp.float32),
    o_b2=((24,), jnp.float32),
)
RAW = dict(
    t_out=((128, 768), jnp.bfloat16),
    t_in=((128, 768), jnp.float32),
    t_qkv=((4, 24, 640), jnp.bfloat16),
    t_up=((4, 24, 768), jnp.bfloat16),
    t_dn=((96, 768), jnp.float32),
    t_ow=((24, 768), jnp.float32),
)
SMALL = ("qb", "vb", "ob", "g1", "b1", "dnb", "g2", "b2")
BF = jnp.bfloat16
F32 = jnp.float32
SCRATCH = dict(
    SM=((24, 128), F32),
    WS=((4, 24, 640), BF),
    W5=((4, 4, 2, 24, 640), BF),
    W2=((768, 640), BF),
    US=((4, 24, 768), BF),
    UP5=((4, 4, 2, 24, 768), BF),
    UP2=((768, 768), BF),
    DN4=((4, 2, 96, 768), BF),
    OW5=((4, 4, 2, 24, 768), BF),
    OW2=((768, 768), BF),
    XG=((4, 2, 64, 768), BF),
    KV=((5, 4, 128, 384), BF),
    KVT=((15, 144, 512), BF),
    QP=((3, 4, 128, 128), BF),
    GP=((3, 4, 128, 128), BF),
    SEGK=((5, 512, 128), BF),
    EL=((15, 512, 512), BF),
    DST=((512, 512), BF),
    NUM=((3, 80, 512), F32),
    DEN=((3, 8, 512), F32),
    ATN=((3, 64, 512), F32),
    DLT=((3, 8, 512), F32),
    AS=((4, 192, 128), BF),
    AT=((4, 192, 128), BF),
    Y1=((128, 768), F32),
    N1=((128, 768), F32),
    RSD=((128, 128), F32),
    YG=((4, 128, 768), BF),
    ACT=((4, 128, 768), BF),
    GG=((4, 128, 768), BF),
    PS=((4, 128, 768), BF),
    PR=((4, 128, 768), BF),
    XN=((128, 768), BF),
    H2=((128, 768), F32),
    DH2=((128, 768), F32),
    DG=((4, 128, 768), BF),
    DU=((4, 128, 768), BF),
    DH1=((128, 768), F32),
    DAS=((4, 2, 96, 128), BF),
    DA=((4, 2, 96, 128), BF),
    T1=((768, 512), BF),
    MR=((768, 64), F32),
    DKS=((5, 3, 512, 128), BF),
    DKX=((3, 512, 128), BF),
    DKR=((5, 3, 512, 128), BF),
    DKO=((3, 512, 128), F32),
    DQT=((3, 64, 512), F32),
    DQ=((512, 640), BF),
    VEC=((16, 768), F32),
    VUP=((8, 768), F32),
    G1=((4, 4, 2, 24, 640), F32),
    R1=((4, 4, 24, 640), F32),
    H1=((4, 4, 24, 640), BF),
    R1P=((4, 4, 24, 640), BF),
    S1=((4, 24, 640), BF),
    R1Z=((4, 24, 640), BF),
    GU=((4, 4, 2, 24, 768), F32),
    RU=((4, 4, 24, 768), F32),
    SU=((2, 4, 24, 768), BF),
    RU1=((2, 4, 24, 768), BF),
    SU2=((4, 24, 768), BF),
    RU2=((4, 24, 768), BF),
    TU=((4, 24, 768), BF),
    RUP=((4, 24, 768), BF),
    GD=((4, 2, 96, 768), F32),
    RD=((4, 96, 768), F32),
    SD=((2, 96, 768), BF),
    RD1=((2, 96, 768), BF),
    SD2=((96, 768), BF),
    RD2=((96, 768), BF),
    GO=((4, 4, 2, 24, 768), F32),
    RO=((4, 4, 24, 768), F32),
    SO=((4, 4, 24, 768), BF),
    ROP=((4, 4, 24, 768), BF),
    TO=((4, 24, 768), BF),
    ROZ=((4, 24, 768), BF),
)


class Slots:
    def __init__(self, **sizes):
        self.total = 0
        for name, size in sizes.items():
            setattr(self, name, self.total)
            self.total += size

    def again(self, start, **sizes):
        for name, size in sizes.items():
            setattr(self, name, start)
            start += size
        return start


SEMS = Slots(
    tok=6, hop=2, wz=3, wp=3, wc=1, us=3, kv=7, oz=3, spare=10, cow=1, cup=1, cdn=1, op=3, upz=3, dnz=3,
    at=4, yg=6, ps=6, fdz=2, foz=3,
)
END = SEMS.again(
    SEMS.tok, da=8, dk=5, dx=3, x=4, f1c=1, f1p=3, f1z=3, fuc=1, fuz=2, fup=3, fdc=1, foc=1, fop=3
)
assert END <= SEMS.cow
SEMS.again(SEMS.yg, dg=6, qs=6)


def mm(left, right):
    return jnp.dot(left, right, preferred_element_type=F32)


def mm_nt(left, right):
    return lax.dot_general(left, right, (((1,), (1,)), ((), ())), preferred_element_type=F32)


def mm_tn(left, right):
    return lax.dot_general(left, right, (((0,), (0,)), ((), ())), preferred_element_type=F32)


def pack(rows):
    tail = rows[:, 128:192]
    return jnp.concatenate([rows[:, 0:128], jnp.concatenate([tail[0:64], tail[64:128]], axis=1)], axis=0)


def unpack(packed):
    tail = packed[128:192]
    tail = jnp.concatenate([tail[:, 0:64], tail[:, 64:128]], axis=0)
    return jnp.concatenate([packed[0:128], tail], axis=1)


def unpack_half(packed, i):
    return jnp.concatenate([packed[64 * i : 64 * i + 64], packed[128:192, 64 * i : 64 * i + 64]], axis=1)


def pack_half(rows):
    tail = rows[:, 128:192]
    return jnp.concatenate([rows[:, 0:128], jnp.concatenate([tail[0:32], tail[32:64]], axis=1)], axis=0)


def open_half(packed):
    tail = packed[64:96]
    tail = jnp.concatenate([tail[:, 0:64], tail[:, 64:128]], axis=0)
    return jnp.concatenate([packed[0:64], tail], axis=1)


def rows_by(shape, axis, flat):
    return lax.broadcasted_iota(jnp.int32, shape, axis).reshape(flat)


class Refs:
    pass


def layer_kernel(*refs):
    R = Refs()
    names = [*ARGS, *("g" + n for n in RAW), *RAW, *SCRATCH, "SS", "RS", "LS"]
    for name, ref in zip(names, refs, strict=True):
        setattr(R, name, ref)
    u = lax.axis_index(ULYSSES)
    b = lax.axis_index(BLK)
    c = lax.rem(b, 2)
    p = lax.div(b, 2)
    other = 1 - c

    def snake(at):
        return at + lax.div(at, 2) * (1 - 2 * lax.rem(at, 2))

    s = snake(p)
    a = 2 * s + c
    far = p >= 2

    def dev(uu, pp, cc):
        return (uu, 2 * pp + cc)

    def block_dev(aa):
        return dev(u, snake(lax.div(aa, 2)), lax.rem(aa, 2))

    def turn(base, k):
        low, high = lax.rem(base, 2), lax.div(base, 2)
        if k % 2:
            low = 1 - low
        if k // 2:
            high = 1 - high
        return 2 * high + low

    sends = []
    free = list(range(KEY_SENDS, SEND_SLOTS))

    def copy(src, dst, slot, ri, device):
        return pltpu.make_async_remote_copy(
            src_ref=src, dst_ref=dst, send_sem=R.SS.at[slot], recv_sem=R.RS.at[ri],
            device_id=device, device_id_type=MESH,
        )

    def send(src, dst, name, ri, device, cond=None):
        slot = free.pop(0)
        desc = copy(src, dst, slot, name + ri, device)
        if cond is None:
            desc.start()
        else:

            @pl.when(cond)
            def _():
                desc.start()

        sends.append((name, cond, desc, slot))

    def send_if(cond, *what):
        send(*what, cond=cond)

    leaving = []

    def leave(name):
        out = pltpu.make_async_copy(getattr(R, name), getattr(R, "g" + name), R.LS.at[len(leaving)])
        out.start()
        leaving.append(out)

    def key_slot(t, sub):
        return sub if t == 3 else {1: 4, 2: 5, 4: 6}[t]

    def settle(*wanted):
        for entry in list(sends):
            name, cond, desc, slot = entry
            if wanted and name not in wanted:
                continue
            sends.remove(entry)
            free.append(slot)
            if cond is None:
                desc.wait_send()
            else:

                @pl.when(cond)
                def _():
                    desc.wait_send()

    def arrived(dst, name, ri, device):
        copy(dst, dst, 0, name + ri, device).wait_recv()

    barrier = pltpu.get_barrier_semaphore()

    def greet(device):
        pl.semaphore_signal(barrier, inc=1, device_id=device, device_id_type=MESH)

    for k in range(1, 8):
        greet((u, lax.rem(b + k, 8)))
    for k in range(1, 4):
        greet((turn(u, k), b))

    @pl.when(far)
    def _():
        for k in range(1, 4):
            greet(dev(turn(u, k), s, c))

    R.SM[...] = jnp.zeros_like(R.SM)
    for row, name in enumerate(SMALL):
        R.SM[row : row + 1, 0:24] = getattr(R, name)[...].astype(F32).reshape(1, 24)
    up_bias = R.upb[...].astype(F32).reshape(1, 96)
    for i in range(4):
        R.SM[8 + i : 9 + i, 0:24] = up_bias[:, 24 * i : 24 * i + 24]
    small = R.SM[:, 0:64].astype(BF)
    qw, kw, vw = R.qw[...], R.kw[...], R.vw[...]
    for g in range(4):
        parts = []
        for h in range(3):
            at = 64 * (3 * g + h)
            parts += [kw[:, at : at + 64], vw[:, at : at + 64]]
        for h in range(3):
            at = 64 * (3 * g + h)
            parts.append(qw[:, at : at + 64])
        parts.append(small)
        R.WS[g] = jnp.concatenate(parts, axis=1)

    pl.semaphore_wait(barrier, 10 + 3 * lax.div(p, 2))

    for k in range(1, 4):
        to = turn(u, k)
        send(R.WS.at[to], R.W5.at[u, p, c], SEMS.wz, k - 1, dev(to, p, c))
    R.W5[u, p, c] = R.WS[u]
    halves = (slice(0, 64), slice(64, 128))
    for i in range(2):
        send_if(far, R.tok.at[halves[i]], R.XG.at[u, i], SEMS.hop, i, dev(u, s, c))

    @pl.when(jnp.logical_not(far))
    def _():
        for i in range(2):
            R.XG[u, i] = R.tok[halves[i], :]

    near, across = turn(u, 1), turn(u, 2)
    there = dev(near, p, c)
    for i in range(2):
        for k in (2, 1):
            send_if(
                jnp.logical_not(far),
                R.tok.at[halves[i]], R.XG.at[u, i], SEMS.tok, 2 * (k - 1) + i, dev(turn(u, k), p, c),
            )

    up = R.upw[...]
    for q in range(4):
        R.US[q] = jnp.concatenate(
            [up[:, 768 * g + 192 * q : 768 * g + 192 * q + 192] for g in range(4)], axis=1
        )
    for k in range(1, 4):
        to = turn(p, k)
        send(R.US.at[to], R.UP5.at[u, p, c], SEMS.us, k - 1, dev(u, to, c))
    R.UP5[u, p, c] = R.US[p]
    R.DN4[u, c] = R.dnw[...]
    R.OW5[u, p, c] = R.ow[...]

    mate = dev(u, p, other)
    row_pos = lax.broadcasted_iota(jnp.int32, (512, 128), 0)
    n_starts = R.starts.shape[0]

    def id_body(j, carry):
        pos = row_pos + (a + j - 2) * 512
        ids = jnp.zeros((512, 128), jnp.int32)
        for i in range(n_starts):
            ids = ids + jnp.where(pos >= R.starts[i], 1, 0)
        R.SEGK[j] = ids.astype(F32).astype(BF)
        return carry

    lax.fori_loop(0, 5, id_body, 0)
    q_pos = lax.broadcasted_iota(jnp.int32, (1, 512), 1) + a * 512
    q_ids = jnp.zeros((1, 512), jnp.int32)
    for i in range(n_starts):
        q_ids = q_ids + jnp.where(q_pos >= R.starts[i], 1, 0)
    q_ids = jnp.broadcast_to(q_ids.astype(F32), (FWD_ROWS, 512)).astype(BF)
    R.KVT[:, 128:144, :] = jnp.ones((15, 16, 512), BF)
    for ref in (R.QP, R.GP, R.NUM, R.DQT):
        ref[...] = jnp.zeros_like(ref)

    for i in range(2):

        @pl.when(far)
        def _():
            arrived(R.XG.at[u, i], SEMS.hop, i, dev(u, s, c))

        for k in (2, 1):
            send_if(
                far,
                R.XG.at[u, i], R.XG.at[u, i], SEMS.tok, 2 * (k - 1) + i, dev(turn(u, k), p, c),
            )
    for k in range(1, 4):
        src = turn(u, k)
        arrived(R.W5.at[src, p, c], SEMS.wz, k - 1, dev(src, p, c))
    for k in range(1, 4):
        to = turn(p, k)
        send(R.W5.at[:, p, c], R.W5.at[:, p, c], SEMS.wp, k - 1, dev(u, to, c))
    def pass_tokens(i):
        arrived(R.XG.at[across, i], SEMS.tok, 2 + i, dev(across, p, c))
        send(R.XG.at[across, i], R.XG.at[across, i], SEMS.tok, 4 + i, there)

    pass_tokens(0)
    for k in range(1, 4):
        src = turn(p, k)
        arrived(R.W5.at[:, src, c], SEMS.wp, k - 1, dev(u, src, c))
    send(R.W5.at[:, :, c], R.W5.at[:, :, c], SEMS.wc, 0, dev(u, p, other))
    pass_tokens(1)
    for k in range(1, 4):
        to = turn(u, k)
        send(R.ow, R.OW5.at[u, p, c], SEMS.oz, k - 1, dev(to, p, c))
    send(R.dnw, R.DN4.at[u, c], SEMS.dnz, 0, dev(across, p, c))
    for k in range(1, 4):
        src = turn(p, k)
        arrived(R.UP5.at[u, src, c], SEMS.us, k - 1, dev(u, src, c))
    send(R.UP5.at[u, :, c], R.UP5.at[u, :, c], SEMS.upz, 0, dev(across, p, c))
    arrived(R.W5.at[:, :, other], SEMS.wc, 0, dev(u, p, other))
    R.W2[...] = R.W5[...].reshape(768, 640)

    spread = jnp.where(
        rows_by((32, 24, 64), 1, (768, 64)) == lax.broadcasted_iota(jnp.int32, (768, 64), 1), 1.0, 0.0
    ).astype(BF)
    owner = rows_by((32, 24, 768), 0, (768, 768))
    lane = lax.broadcasted_iota(jnp.int32, (1, 768), 1)
    lane_owner = jnp.zeros((1, 768), jnp.int32)
    for i in range(1, 32):
        lane_owner = lane_owner + jnp.where(lane >= 24 * i, 1, 0)
    lane_g = jnp.where(lane >= 192, 1, 0) + jnp.where(lane >= 384, 1, 0) + jnp.where(lane >= 576, 1, 0)
    rest = lane - 192 * lane_g
    lane_c = jnp.where(rest >= 96, 1, 0)
    rest = rest - 96 * lane_c
    lane_r = jnp.where(rest >= 24, 1, 0) + jnp.where(rest >= 48, 1, 0) + jnp.where(rest >= 72, 1, 0)
    up_row = 24 * (8 * lane_g + 2 * p + lane_c) + 8 + lane_r
    row_id = lax.broadcasted_iota(jnp.int32, (768, 768), 0)
    wide = mm_nt(R.W2[:, 576:640], spread)
    mine = jnp.where(owner == lane_owner, wide, 0.0).astype(BF)
    pick = jnp.where(
        lax.broadcasted_iota(jnp.int32, (16, 768), 1) - 24 * lane_owner
        == lax.broadcasted_iota(jnp.int32, (16, 768), 0), 1.0, 0.0
    ).astype(BF)
    R.VEC[...] = mm(pick, mine)

    def group_slice(vector):
        out = vector[:, 0:192]
        for g in range(1, 4):
            out = jnp.where(u == g, vector[:, 192 * g : 192 * g + 192], out)
        return out

    qb = group_slice(R.VEC[0:1, :])
    vb = group_slice(R.VEC[1:2, :])
    zero64 = jnp.zeros((1, 64), F32)
    bias = []
    for h in range(3):
        bias += [zero64, vb[:, 64 * h : 64 * h + 64]]
    bias = jnp.concatenate(bias + [qb, zero64], axis=1)

    for k in range(4):
        src = turn(u, k)
        if k > 0:
            for i in range(2):
                if k != 2:
                    arrived(R.XG.at[src, i], SEMS.tok, 2 * (k - 1) + i, there)
        proj = mm(R.XG[src].reshape(128, 768), R.W2[...]) + bias
        R.KV[2, src] = proj[:, 0:384].astype(BF)
        query = proj[:, 384:576].astype(BF) * BF(0.125)
        for h in range(3):
            R.QP[h, src, :, 0:64] = query[:, 64 * h : 64 * h + 64]
        slot = 1 + 2 * c
        send(R.KV.at[2, src], R.KV.at[slot, src], SEMS.kv, key_slot(1, src), mate)
        for i, step in enumerate((-2, 2)):
            to = a + step
            ok = jnp.logical_and(to >= 0, to < 8)
            slot = 2 - step
            handed = c if step > 0 else 1 - c
            index = handed * src + (1 - handed) * key_slot(4, src)
            send_if(ok, R.KV.at[2, src], R.KV.at[slot, src], SEMS.kv, index, block_dev(to))

    def order(t):
        return 2 + (1 - 2 * c) * ((t + 1) // 2) * (1 - 2 * ((t + 1) % 2))

    def forward_block(t):
        j = order(t)
        ok = jnp.logical_and(a + j >= 2, a + j < 10)

        @pl.when(ok)
        def _():
            if t == 1 or t == 2 or t == 4:
                arrived(R.KV.at[j], SEMS.kv, key_slot(t, 0), block_dev(a + j - 2) if t == 4 else mate)

            def head(h, inner):
                lanes = pl.ds(pl.multiple_of(128 * h, 128), 128)
                kv = R.KV[j, :, :, lanes].reshape(512, 128)
                at = 3 * j + h
                R.KVT[at, 0:128, :] = kv.T
                query = R.QP[h].reshape(512, 128)
                for r in range(512 // FWD_ROWS):
                    rows = slice(FWD_ROWS * r, FWD_ROWS * r + FWD_ROWS)
                    score = mm_nt(kv[rows], query)
                    ids = R.SEGK[j, rows, :]
                    same = jnp.concatenate([ids] * 4, axis=1) == q_ids
                    weight = jnp.exp2(score * LOG2E).astype(BF)
                    R.EL[at, rows, :] = jnp.where(same, weight, jnp.zeros_like(weight))
                R.NUM[h] += mm(R.KVT[at, 64:144, :], R.EL[at])
                return inner

            lax.fori_loop(0, 3, head, 0)

    def relay_out():
        for k in range(1, 4):
            src = turn(u, k)
            arrived(R.OW5.at[src, p, c], SEMS.oz, k - 1, dev(src, p, c))
        for k in range(1, 4):
            to = turn(p, k)
            send(R.OW5.at[:, p, c], R.OW5.at[:, p, c], SEMS.op, k - 1, dev(u, to, c))

    def share_keys():
        j = order(3)
        ok = jnp.logical_and(a + j >= 2, a + j < 10)
        slot = 1 + 2 * (1 - c)
        for r in range(4):

            @pl.when(ok)
            def _():
                arrived(R.KV.at[j, r], SEMS.kv, key_slot(3, r), block_dev(a + j - 2))

            send_if(ok, R.KV.at[j, r], R.KV.at[slot, r], SEMS.kv, key_slot(2, r), mate)

    def relay_down():
        arrived(R.DN4.at[across, c], SEMS.dnz, 0, dev(across, p, c))
        send(R.DN4.at[across, c], R.DN4.at[across, c], SEMS.dnz, 2, there)

    def relay_up():
        arrived(R.UP5.at[across, :, c], SEMS.upz, 0, dev(across, p, c))
        send(R.UP5.at[across, :, c], R.UP5.at[across, :, c], SEMS.upz, 2, there)

    send(R.dnw, R.DN4.at[u, c], SEMS.dnz, 1, there)
    send(R.UP5.at[u, :, c], R.UP5.at[u, :, c], SEMS.upz, 1, there)
    forward_block(0)
    relay_out()
    forward_block(1)
    share_keys()
    forward_block(3)
    settle(SEMS.wz, SEMS.hop, SEMS.us, SEMS.wp, SEMS.wc)
    relay_down()
    forward_block(2)
    forward_block(4)

    heads = []
    for h in range(3):
        R.DEN[h, 0:1, :] = R.NUM[h, 64:65, :]
        attn = R.NUM[h, 0:64, :] / R.DEN[h, 0:1, :]
        R.ATN[h] = attn
        heads.append(attn.T.astype(BF))
    for r in range(4):
        rows = slice(128 * r, 128 * r + 128)
        R.AS[r] = pack(jnp.concatenate([part[rows] for part in heads], axis=1))
    for k in (2, 3, 1):
        to = turn(u, k)
        send(R.AS.at[to], R.AT.at[u], SEMS.at, k, dev(to, s, c))
    send_if(far, R.AS.at[u], R.AT.at[u], SEMS.at, 0, dev(u, s, c))

    @pl.when(jnp.logical_not(far))
    def _():
        R.AT[u] = R.AS[u]

    relay_up()
    wide = mm_nt(R.W2[:, 576:640], spread)
    R.VUP[0:1, :] = jnp.sum(jnp.where(row_id == up_row, wide, 0.0), axis=0, keepdims=True)
    settle(SEMS.tok, SEMS.hop, SEMS.wz, SEMS.wp, SEMS.wc, SEMS.us, SEMS.oz)
    for k in range(1, 4):
        src = turn(p, k)
        arrived(R.OW5.at[:, src, c], SEMS.op, k - 1, dev(u, src, c))
    send(R.OW5.at[:, :, c], R.OW5.at[:, :, c], SEMS.cow, 0, mate)
    arrived(R.OW5.at[:, :, other], SEMS.cow, 0, mate)
    R.OW2[...] = R.OW5[...].reshape(768, 768)

    def wait_column(ref, name):
        for k in range(1, 4):
            src = turn(u, k)
            arrived(ref.at[src], name, k, dev(src, s, c))

        @pl.when(far)
        def _():
            arrived(ref.at[u], name, 0, dev(u, s, c))

    wait_column(R.AT, SEMS.at)

    def gather_half(ref, i, value, name):
        rows = halves[i]
        ref[p, rows, :] = value
        for k in range(1, 4):
            part = ref.at[p, rows]
            send(part, part, name, 2 * (k - 1) + i, dev(u, turn(p, k), c))

    def centered(hidden):
        hidden = hidden - jnp.mean(hidden, axis=-1, keepdims=True)
        rstd = lax.rsqrt(jnp.mean(hidden * hidden, axis=-1, keepdims=True) + EPS)
        return hidden * rstd, rstd

    def norm_back(cg, normed, rstd):
        mean = jnp.mean(cg, axis=-1, keepdims=True)
        return (cg - mean - normed * jnp.mean(cg * normed, axis=-1, keepdims=True)) * rstd

    def down_sum(x):
        return jnp.sum(x, axis=0, keepdims=True)

    for i in range(2):
        rows = halves[i]
        hidden = R.tok[rows, :].astype(F32) + R.VEC[2:3, :]
        for g in range(4):
            hidden = hidden + mm(unpack_half(R.AT[g], i), R.OW2[192 * g : 192 * g + 192, :])
        normed, rstd = centered(hidden)
        R.N1[rows, :] = normed
        R.RSD[rows, :] = jnp.broadcast_to(rstd, (64, 128))
        y_one = normed * R.VEC[3:4, :] + R.VEC[4:5, :]
        R.Y1[rows, :] = y_one
        gather_half(R.YG, i, y_one.astype(BF), SEMS.yg)

    settle(SEMS.kv)
    for i, src in enumerate((near, turn(near, 2))):
        arrived(R.DN4.at[src, c], SEMS.dnz, 1 + i, there)
    send(R.DN4.at[:, c], R.DN4.at[:, c], SEMS.cdn, 0, mate)
    for i, src in enumerate((near, turn(near, 2))):
        arrived(R.UP5.at[src, :, c], SEMS.upz, 1 + i, there)
    send(R.UP5.at[:, :, c], R.UP5.at[:, :, c], SEMS.cup, 0, mate)
    arrived(R.DN4.at[:, other], SEMS.cdn, 0, mate)
    arrived(R.UP5.at[:, :, other], SEMS.cup, 0, mate)
    R.UP2[...] = R.UP5[...].reshape(768, 768)
    turns = ((0, 0), (0, 1), (1, 0), (2, 0), (3, 0), (1, 1), (2, 1), (3, 1))
    for k, i in turns[2:] + turns[:2]:
        at, rows = turn(p, k), halves[i]
        if k > 0:
            arrived(R.YG.at[at, rows], SEMS.yg, 2 * (k - 1) + i, dev(u, at, c))
        pre = mm(R.YG[at, rows, :], R.UP2[...]) + R.VUP[0:1, :]
        phi = 0.5 * (1.0 + lax.erf(pre * RSQRT2))
        R.GG[at, rows, :] = (phi + pre * (PDF0 * jnp.exp(-0.5 * pre * pre))).astype(BF)
        act = (pre * phi).astype(BF)
        R.ACT[at, rows, :] = act
        part = mm(act, R.DN4[...].reshape(768, 768))
        if k == 0:
            R.H2[rows, :] = part
        else:
            R.PS[at, rows, :] = part.astype(BF)
            send(R.PS.at[at, rows], R.PR.at[p, rows], SEMS.ps, 2 * (k - 1) + i, dev(u, at, c))

    g_gain_two = g_shift_two = g_b_down = 0.0
    for i in range(2):
        rows = halves[i]
        hidden = R.Y1[rows, :] + R.H2[rows, :] + R.VEC[5:6, :]
        for k in range(1, 4):
            at = turn(p, k)
            arrived(R.PR.at[at, rows], SEMS.ps, 2 * (k - 1) + i, dev(u, at, c))
            hidden = hidden + R.PR[at, rows, :].astype(F32)
        normed, rstd = centered(hidden)
        gain = R.VEC[6:7, :]
        grad = R.cot[rows, :].astype(F32)
        d_two = norm_back(grad * gain, normed, rstd)
        gather_half(R.DG, i, d_two.astype(BF), SEMS.dg)
        R.DH2[rows, :] = d_two
        R.t_out[rows, :] = (normed * gain + R.VEC[7:8, :]).astype(BF)
        g_gain_two = g_gain_two + down_sum(grad * normed)
        g_shift_two = g_shift_two + down_sum(grad)
        g_b_down = g_b_down + down_sum(d_two)

    leave("t_out")
    settle(SEMS.at, SEMS.op, SEMS.dnz, SEMS.upz, SEMS.cow, SEMS.cup, SEMS.cdn, SEMS.yg, SEMS.ps)
    g_b_up = jnp.zeros((1, 768), F32)
    for k, i in turns:
        at, rows = turn(p, k), halves[i]
        if k > 0:
            arrived(R.DG.at[at, rows], SEMS.dg, 2 * (k - 1) + i, dev(u, at, c))
        d_act = mm_nt(R.DG[at, rows, :], R.DN4[...].reshape(768, 768))
        d_pre = (d_act * R.GG[at, rows, :].astype(F32)).astype(BF)
        R.DU[at, rows, :] = d_pre
        g_b_up = g_b_up + down_sum(d_pre.astype(F32))
        part = mm_nt(d_pre, R.UP2[...])
        if k == 0:
            R.H2[rows, :] = part
        else:
            R.PS[at, rows, :] = part.astype(BF)
            send(R.PS.at[at, rows], R.PR.at[p, rows], SEMS.qs, 2 * (k - 1) + i, dev(u, at, c))

    def wide_grad(left, right_ref, put):
        R.T1[...] = left.T

        def body(n, carry):
            lanes = pl.ds(pl.multiple_of(256 * n, 256), 256)
            put(lanes, mm(R.T1[...], right_ref[:, :, lanes].reshape(512, 256)))
            return carry

        lax.fori_loop(0, 3, body, 0)

    def put_down(lanes, value):
        R.GD[:, :, :, lanes] = value.reshape(4, 2, 96, 256)

    def put_up(lanes, value):
        R.GU[:, :, :, :, lanes] = value.reshape(4, 4, 2, 24, 256)

    wide_grad(R.ACT[...].reshape(512, 768), R.DG, put_down)
    send(R.GD.at[:, other], R.RD, SEMS.fdc, 0, mate)
    wide_grad(R.YG[...].reshape(512, 768), R.DU, put_up)
    send(R.GU.at[:, :, other], R.RU, SEMS.fuc, 0, mate)
    def down_step():
        arrived(R.RD, SEMS.fdc, 0, mate)
        for i, g in enumerate((near, turn(near, 2))):
            R.SD[i] = (R.GD[g, c] + R.RD[g]).astype(BF)
        send(R.SD, R.RD1, SEMS.fdz, 0, there)

    down_step()
    g_b_out = g_gain_one = g_shift_one = 0.0
    for half in range(2):
        rows = halves[half]
        d_y = R.DH2[rows, :] + R.H2[rows, :]
        for k in range(1, 4):
            at = turn(p, k)
            arrived(R.PR.at[at, rows], SEMS.qs, 2 * (k - 1) + half, dev(u, at, c))
            d_y = d_y + R.PR[at, rows, :].astype(F32)
        normed = R.N1[rows, :]
        d_one = norm_back(d_y * R.VEC[3:4, :], normed, R.RSD[rows, 0:1])
        R.DH1[rows, :] = d_one
        for k in (2, 3, 1, 0):
            to = turn(u, k)
            w_rows = R.OW2[pl.ds(pl.multiple_of(192 * to, 64), 192), :]
            R.DAS[to, half] = pack_half(mm_nt(d_one.astype(BF), w_rows).astype(BF))
            if k > 0:
                send(R.DAS.at[to, half], R.DA.at[u, half], SEMS.da, 4 * half + k, dev(to, s, c))
        send_if(far, R.DAS.at[u, half], R.DA.at[u, half], SEMS.da, 4 * half, dev(u, s, c))
        g_b_out = g_b_out + down_sum(d_one)
        g_gain_one = g_gain_one + down_sum(d_y * normed)
        g_shift_one = g_shift_one + down_sum(d_y)

    @pl.when(jnp.logical_not(far))
    def _():
        R.DA[u] = R.DAS[u]

    vec = R.VEC
    vec[2:3, :] = g_b_out
    vec[3:4, :] = g_gain_one
    vec[4:5, :] = g_shift_one
    vec[5:6, :] = g_b_down
    vec[6:7, :] = g_gain_two
    vec[7:8, :] = g_shift_two
    vec[8:16, :] = jnp.zeros((8, 768), F32)
    R.VUP[0:1, :] = g_b_up

    for g in range(4):
        R.GO[g] = mm_tn(unpack(R.AT[g]), R.DH1[...].astype(BF)).reshape(4, 2, 24, 768)
    send(R.GO.at[:, :, other], R.RO, SEMS.foc, 0, mate)

    arrived(R.RU, SEMS.fuc, 0, mate)
    for i, g in enumerate((near, turn(near, 2))):
        R.SU[i] = (R.GU[g, :, c] + R.RU[g]).astype(BF)
    send(R.SU, R.RU1, SEMS.fuz, 0, there)

    def relay_down_grad():
        arrived(R.RD1, SEMS.fdz, 0, there)
        R.SD2[...] = (R.GD[across, c] + R.RD[across] + R.RD1[1].astype(F32)).astype(BF)
        send(R.SD2, R.RD2, SEMS.fdz, 1, dev(across, p, c))

    def relay_up_grad():
        arrived(R.RU1, SEMS.fuz, 0, there)
        R.SU2[...] = (R.GU[across, :, c] + R.RU[across] + R.RU1[1].astype(F32)).astype(BF)
        send(R.SU2, R.RU2, SEMS.fuz, 1, dev(across, p, c))

    arrived(R.RO, SEMS.foc, 0, mate)
    for g in range(4):
        R.SO[g] = (R.GO[g, :, c] + R.RO[g]).astype(BF)
    for k in range(1, 4):
        to = turn(p, k)
        send(R.SO.at[:, to], R.ROP.at[p], SEMS.fop, k - 1, dev(u, to, c))
    settle(SEMS.fdc, SEMS.fuc, SEMS.qs, SEMS.dg)
    vec[0:2, :] = jnp.zeros((2, 768), F32)
    choose = jnp.where(
        rows_by((32, 24, 16), 1, (768, 16)) == lax.broadcasted_iota(jnp.int32, (768, 16), 1), 1.0, 0.0
    ).astype(BF)
    laid = jnp.where(owner == lane_owner, mm(choose, vec[...].astype(BF)), 0.0)
    laid = jnp.where(row_id == up_row, R.VUP[0:1, :], laid)
    R.MR[...] = mm(laid.astype(BF), spread)
    R.T1[...] = R.XG[...].reshape(512, 768).T
    for half in range(2):
        for k in range(1, 4):
            src = turn(u, k)
            arrived(R.DA.at[src, half], SEMS.da, 4 * half + k, dev(src, s, c))

        @pl.when(far)
        def _():
            arrived(R.DA.at[u, half], SEMS.da, 4 * half, dev(u, s, c))

    d_rows = [open_half(R.DA[r, half]) for r in range(4) for half in range(2)]
    d_rows = jnp.concatenate(d_rows, axis=0).astype(F32)
    for h in range(3):
        d_attn = d_rows[:, 64 * h : 64 * h + 64].T
        scaled = (d_attn / R.DEN[h, 0:1, :]).astype(BF)
        R.DLT[h, 0:1, :] = jnp.sum(scaled.astype(F32) * R.ATN[h], axis=0, keepdims=True)
        R.GP[h, :, :, 64:128] = scaled.T.reshape(4, 128, 64)

    def block_copy(t):
        j = order(t)
        there_slot = 0 if t == 1 else 1
        return copy(
            R.DKS.at[j], R.DKR.at[4 - j], there_slot, SEMS.dk + there_slot, block_dev(a + j - 2)
        )

    def key_copy(t, h):
        j = order(t)
        if t == 2:
            return copy(R.DKS.at[j, h], R.DKX.at[h], 2 + h, SEMS.dx + h, mate)
        return copy(
            R.DKS.at[j, h], R.DKR.at[4 - j, h], 5 + h, SEMS.dk + 2 + h, block_dev(a + j - 2)
        )

    def backward_block(t):
        j = order(t)
        ok = jnp.logical_and(a + j >= 2, a + j < 10)

        @pl.when(ok)
        def _():
            def head(h, inner):
                lanes = pl.ds(pl.multiple_of(128 * h, 128), 128)
                at = 3 * j + h
                grad_rows = R.GP[h].reshape(512, 128)
                shift = R.DLT[h, 0:1, :]
                kv = R.KV[j, :, :, lanes].reshape(512, 128)
                for r in range(512 // BWD_ROWS):
                    rows = slice(BWD_ROWS * r, BWD_ROWS * r + BWD_ROWS)
                    d_prob = mm_nt(kv[rows], grad_rows)
                    R.DST[rows, :] = (R.EL[at, rows, :].astype(F32) * (d_prob - shift)).astype(BF)
                d_kv = mm(R.DST[...], R.QP[h].reshape(512, 128)) + mm(R.EL[at], grad_rows)
                if t == 0:
                    R.DKO[h] = d_kv
                elif t == 3:
                    arrived(R.DKX.at[h], SEMS.dx, h, mate)
                    R.DKS[j, h] = (d_kv + R.DKX[h].astype(F32)).astype(BF)
                else:
                    R.DKS[j, h] = d_kv.astype(BF)
                if t == 2 or t == 3:
                    key_copy(t, h).start()
                R.DQT[h] += mm(R.KVT[at, 0:64, :], R.DST[...])
                return inner

            lax.fori_loop(0, 3, head, 0)
            if t == 4 or t == 1:
                block_copy(t).start()

    backward_block(4)
    relay_down_grad()
    backward_block(2)
    backward_block(3)
    relay_up_grad()
    backward_block(1)
    backward_block(0)

    def at_lanes(n, value):
        R.G1[:, :, :, :, 128 * n : 128 * n + 128] = value.reshape(4, 4, 2, 24, 128)

    def query_grads():
        for n in (3, 4):
            value = mm(R.T1[...], R.DQ[:, 128 * n : 128 * n + 128])
            if n == 4:
                value = jnp.concatenate([value[:, 0:64], R.MR[...]], axis=1)
            at_lanes(n, value)

    def key_grads():
        for n in range(3):
            at_lanes(n, mm(R.T1[...], R.DQ[:, 128 * n : 128 * n + 128]))
        sums = mm(jnp.ones((8, 512), BF), R.DQ[...])[0:1]
        sum_v = jnp.concatenate([sums[:, 128 * h + 64 : 128 * h + 128] for h in range(3)], axis=1)
        row = lax.broadcasted_iota(jnp.int32, (192, 192), 0)
        lane_row = 24 * lane_owner[:, 0:192]
        laid = jnp.where(row == lane_row, sums[:, 384:576], jnp.where(row == lane_row + 1, sum_v, 0.0))
        extra = mm(laid.astype(BF), spread[0:192])
        extra = jnp.concatenate([jnp.zeros((192, 64), F32), extra], axis=1)
        R.G1[u, :, :, :, 512:640] += extra.reshape(4, 2, 24, 128)
        send(R.G1.at[:, :, other], R.R1, SEMS.f1c, 0, mate)

    for h in range(3):
        R.DQ[:, 384 + 64 * h : 448 + 64 * h] = (R.DQT[h] * 0.125).T.astype(BF)
    R.DQ[:, 576:640] = jnp.zeros((512, 64), BF)
    query_grads()
    for t in (1, 3, 4):
        j = order(t)

        @pl.when(jnp.logical_and(a + j >= 2, a + j < 10))
        def _():
            if t != 4:
                arrived(R.DKR.at[j], SEMS.dk, 0 if t == 1 else 1, block_dev(a + j - 2))
            for h in range(3):
                if t == 4:
                    arrived(R.DKR.at[j, h], SEMS.dk, 2 + h, block_dev(a + j - 2))
                R.DKO[h] += R.DKR[j, h].astype(F32)

    for h in range(3):
        R.DQ[:, 128 * h : 128 * h + 128] = R.DKO[h].astype(BF)
    key_grads()

    settle(SEMS.qs)
    def input_part(k):
        rows = pl.ds(pl.multiple_of(128 * turn(u, k), 128), 128)
        return mm_nt(R.DQ[rows, :], R.W2[...])

    R.PS[3] = input_part(3).astype(BF)
    send(R.PS.at[3], R.XN, SEMS.x, 3, there)
    R.PS[1] = input_part(1).astype(BF)
    send(R.PS.at[1], R.PR.at[1], SEMS.x, 1, there)
    R.Y1[...] = input_part(0)
    R.H2[...] = input_part(2)
    arrived(R.R1, SEMS.f1c, 0, mate)
    for g in range(4):
        R.H1[g] = (R.G1[g, :, c] + R.R1[g]).astype(BF)
    for k in range(1, 4):
        to = turn(p, k)
        send(R.H1.at[:, to], R.R1P.at[p], SEMS.f1p, k - 1, dev(u, to, c))
    arrived(R.RD2, SEMS.fdz, 1, dev(across, p, c))
    R.t_dn[...] = R.GD[u, c] + R.RD[u] + R.RD1[0].astype(F32) + R.RD2[...].astype(F32)
    leave("t_dn")
    arrived(R.RU2, SEMS.fuz, 1, dev(across, p, c))
    R.TU[...] = (R.GU[u, :, c] + R.RU[u] + R.RU1[0].astype(F32) + R.RU2[...].astype(F32)).astype(BF)
    R.RUP[p] = R.TU[p]
    for k in range(1, 4):
        to = turn(p, k)
        send(R.TU.at[to], R.RUP.at[p], SEMS.fup, k - 1, dev(u, to, c))

    arrived(R.XN, SEMS.x, 3, there)
    R.PS[2] = (R.H2[...] + R.XN[...].astype(F32)).astype(BF)
    send(R.PS.at[2], R.PR.at[2], SEMS.x, 2, dev(across, s, c))
    for k in range(1, 4):
        src = turn(p, k)
        arrived(R.ROP.at[src], SEMS.fop, k - 1, dev(u, src, c))
    for g in range(4):
        total = R.GO[g, p, c] + R.RO[g, p]
        for k in range(1, 4):
            total = total + R.ROP[turn(p, k), g].astype(F32)
        R.TO[g] = total.astype(BF)
    for k in range(1, 4):
        to = turn(u, k)
        send(R.TO.at[to], R.ROZ.at[u], SEMS.foz, k - 1, dev(to, p, c))
    arrived(R.PR.at[1], SEMS.x, 1, there)
    R.Y1[...] += R.PR[1].astype(F32)

    @pl.when(far)
    def _():
        R.PS[0] = R.Y1[...].astype(BF)

    send_if(far, R.PS.at[0], R.PR.at[0], SEMS.x, 0, dev(u, s, c))
    for k in range(1, 4):
        src = turn(p, k)
        arrived(R.R1P.at[src], SEMS.f1p, k - 1, dev(u, src, c))
    total = R.G1[:, p, c] + R.R1[:, p]
    for k in range(1, 4):
        total = total + R.R1P[turn(p, k)].astype(F32)
    R.S1[...] = total.astype(BF)
    for k in range(1, 4):
        to = turn(u, k)
        send(R.S1.at[to], R.R1Z.at[u], SEMS.f1z, k - 1, dev(to, p, c))
    R.R1Z[u] = R.S1[u]
    for k in range(1, 4):
        src = turn(u, k)
        arrived(R.ROZ.at[src], SEMS.foz, k - 1, dev(src, p, c))
    total = R.TO[u].astype(F32)
    for k in range(1, 4):
        total = total + R.ROZ[turn(u, k)].astype(F32)
    R.t_ow[...] = total
    leave("t_ow")
    for k in range(1, 4):
        src = turn(p, k)
        arrived(R.RUP.at[src], SEMS.fup, k - 1, dev(u, src, c))
    R.t_up[...] = R.RUP[...]
    leave("t_up")
    arrived(R.PR.at[2], SEMS.x, 2, dev(across, s, c))

    @pl.when(far)
    def _():
        arrived(R.PR.at[0], SEMS.x, 0, dev(u, s, c))
        R.Y1[...] = R.PR[0].astype(F32)

    total = R.DH1[...] + R.Y1[...] + R.PR[2].astype(F32)
    R.t_in[...] = total
    leave("t_in")
    for k in range(1, 4):
        src = turn(u, k)
        arrived(R.R1Z.at[src], SEMS.f1z, k - 1, dev(src, p, c))
    R.t_qkv[...] = R.R1Z[...]
    leave("t_qkv")
    settle()
    for out in leaving:
        out.wait()
    for t in range(1, 5):
        j = order(t)

        @pl.when(jnp.logical_and(a + j >= 2, a + j < 10))
        def _():
            if t == 4 or t == 1:
                block_copy(t).wait_send()
            else:
                for h in range(3):
                    key_copy(t, h).wait_send()


def finish_kernel(*refs):
    R = Refs()
    for name, ref in zip([*RAW, *OUTS], refs, strict=True):
        setattr(R, name, ref)
    R.o_out[...] = R.t_out[...]
    R.o_in[...] = R.t_in[...]
    R.o_dnw[...] = R.t_dn[...]
    R.o_ow[...] = R.t_ow[...]
    for q in range(4):
        piece = R.t_up[q].astype(F32)
        for g in range(4):
            R.o_upw[:, 768 * g + 192 * q : 768 * g + 192 * q + 192] = piece[:, 192 * g : 192 * g + 192]
    small = jnp.zeros((24, 64), F32)
    for g in range(4):
        piece = R.t_qkv[g].astype(F32)
        at = 192 * g
        R.o_kw[:, at : at + 192] = jnp.concatenate([piece[:, 128 * h : 128 * h + 64] for h in range(3)], axis=1)
        R.o_vw[:, at : at + 192] = jnp.concatenate([piece[:, 128 * h + 64 : 128 * h + 128] for h in range(3)], axis=1)
        R.o_qw[:, at : at + 192] = piece[:, 384:576]
        small = small + piece[:, 576:640]
    for row, name in enumerate(SMALL):
        getattr(R, "o_" + name)[...] = small[row : row + 1, 0:24].reshape(24)
    R.o_upb[...] = jnp.concatenate([small[8 + i : 9 + i, 0:24] for i in range(4)], axis=1).reshape(96)


def fused_step(*args):
    vmem = pl.BlockSpec(memory_space=pltpu.VMEM)
    raw = pl.pallas_call(
        layer_kernel,
        out_shape=[jax.ShapeDtypeStruct(shape, dtype) for shape, dtype in RAW.values()],
        in_specs=[pl.BlockSpec(memory_space=pltpu.SMEM) if n == "starts" else vmem for n in ARGS],
        out_specs=[pl.BlockSpec(memory_space=pl.ANY)] * len(RAW),
        scratch_shapes=[pltpu.VMEM(shape, dtype) for shape, dtype in (RAW | SCRATCH).values()]
        + [pltpu.SemaphoreType.DMA((n,)) for n in (SEND_SLOTS, SEMS.total, len(RAW))],
        compiler_params=pltpu.CompilerParams(
            collective_id=0, has_side_effects=True, vmem_limit_bytes=63 << 20
        ),
        name="layer_step",
    )(*args)
    return pl.pallas_call(
        finish_kernel,
        out_shape=[jax.ShapeDtypeStruct(shape, dtype) for shape, dtype in OUTS.values()],
        in_specs=[vmem] * len(RAW),
        out_specs=[vmem] * len(OUTS),
        name="finish",
    )(*raw)


def solution(mesh):
    fused = mesh.shape[ULYSSES] == 4 and mesh.shape[BLK] == 8
    return jax.shard_map(
        fused_step if fused else per_device,
        mesh=mesh,
        in_specs=(
            P(TOKEN_AXES, None),
            P(TOKEN_AXES, None),
            P(),
            P(WEIGHT_AXES, None),
            P(WEIGHT_AXES, None),
            P(WEIGHT_AXES, None),
            P(WEIGHT_AXES),
            P(WEIGHT_AXES),
            P(WEIGHT_AXES, None),
            P(WEIGHT_AXES),
            P(WEIGHT_AXES),
            P(WEIGHT_AXES),
            P(WEIGHT_AXES, None),
            P(WEIGHT_AXES),
            P(WEIGHT_AXES, None),
            P(WEIGHT_AXES),
            P(WEIGHT_AXES),
            P(WEIGHT_AXES),
        ),
        out_specs=(
            P(TOKEN_AXES, None),
            P(TOKEN_AXES, None),
            P(WEIGHT_AXES, None),
            P(WEIGHT_AXES, None),
            P(WEIGHT_AXES, None),
            P(WEIGHT_AXES),
            P(WEIGHT_AXES),
            P(WEIGHT_AXES, None),
            P(WEIGHT_AXES),
            P(WEIGHT_AXES),
            P(WEIGHT_AXES),
            P(WEIGHT_AXES, None),
            P(WEIGHT_AXES),
            P(WEIGHT_AXES, None),
            P(WEIGHT_AXES),
            P(WEIGHT_AXES),
            P(WEIGHT_AXES),
        ),
        check_vma=False,
    )
```
